32 devices in a mesh: dp: 8 (over z, y), tensor: 4 (over x, core).
Axes of the slice: x: 2, y: 2, z: 4, core: 2. Of those that a mesh axis runs over, the one named last changes fastest.
Arguments:
- hidden_in: bfloat16 [16384, 768], P(('dp', 'tensor')), may hold values from -6 to 6
- grad_out: bfloat16 [16384, 768], P(('dp', 'tensor')), may hold values from -6 to 6
- w_query: bfloat16 [768, 768], P('dp', 'tensor'), may hold values from -0.21875 to 0.21875
- b_query: float32 [768], P('tensor'), may hold values from -1.75 to 1.75
- w_key: bfloat16 [768, 768], P('dp', 'tensor'), may hold values from -0.21875 to 0.21875
- w_value: bfloat16 [768, 768], P('dp', 'tensor'), may hold values from -0.21875 to 0.21875
- b_value: float32 [768], P('tensor'), may hold values from -0.3125 to 0.3125
- w_out: bfloat16 [768, 768], P('tensor', 'dp'), may hold values from -3 to 3
- b_out: float32 [768], replicated, may hold values from -1.75 to 1.75
- gain_one: float32 [768], replicated, may hold values from 0.25 to 1.75
- shift_one: float32 [768], replicated, may hold values from -1.75 to 1.75
- w_up: bfloat16 [768, 3072], P('dp', 'tensor'), may hold values from -0.21875 to 0.21875
- b_up: float32 [3072], replicated, may hold values from -1.75 to 1.75
- w_down: bfloat16 [3072, 768], P('tensor', 'dp'), may hold values from -0.109375 to 0.109375
- b_down: float32 [768], replicated, may hold values from -1.75 to 1.75
- gain_two: float32 [768], replicated, may hold values from 0.25 to 1.75
- shift_two: float32 [768], replicated, may hold values from -1.75 to 1.75
- lengths: int32 [8], P('dp'), may hold values from 1024 to 2048, as said below
- global_raw: int32 [8, 2], P('dp'), may hold values from 0 to 65535
- random_raw: int32 [8, 32, 3], P('dp'), may hold values from 0 to 65535
Outputs:
- layer_out: bfloat16 [16384, 768], P(('dp', 'tensor'))
- grad_in: float32 [16384, 768], P(('dp', 'tensor'))
- grad_w_query: float32 [768, 768], P('dp', 'tensor')
- grad_b_query: float32 [768], P('tensor')
- grad_w_key: float32 [768, 768], P('dp', 'tensor')
- grad_w_value: float32 [768, 768], P('dp', 'tensor')
- grad_b_value: float32 [768], P('tensor')
- grad_w_out: float32 [768, 768], P('tensor', 'dp')
- grad_b_out: float32 [768], replicated
- grad_gain_one: float32 [768], replicated
- grad_shift_one: float32 [768], replicated
- grad_w_up: float32 [768, 3072], P('dp', 'tensor')
- grad_b_up: float32 [3072], P('tensor')
- grad_w_down: float32 [3072, 768], P('tensor', 'dp')
- grad_b_down: float32 [768], replicated
- grad_gain_two: float32 [768], replicated
- grad_shift_two: float32 [768], replicated
The draws below stay inside these ranges and needn't reach their ends.
Inputs may be any that keep to these rules, and one draw needn't show every extreme that they name: `lengths`: the first sequence has 2048 live tokens.
All inputs are finite; a program needn't handle non-finite values.
Results may differ from the reference program's by a relative error of at most 0.015.
Values may be sent and summed in bfloat16 or wider, within the bound.
No kernel may reach another device: no remote copies, remote signals or barrier semaphores. Data moves between devices by JAX's collectives and lax.ppermute only.
A program may use at most 192 MiB of HBM per device.

```python
import jax
import jax.numpy as jnp
from jax import lax

D = 768
H = 12
HD = 64
FF = 3072
BLK = 64
GLOB = 2
RAND = 3
QROWS = 512
LMAX = 2048
MINLEN = 1024
NB = 32
SEQS = 8
TOKENS = 16384


def draw_lengths(key, part):
    drawn_lengths = jax.random.randint(key, (SEQS,), MINLEN, LMAX + 1, dtype=jnp.int32)
    return drawn_lengths.at[0].set(LMAX)


def plant(values, own_key, low, top_value):
    index_at = [jax.random.randint(jax.random.fold_in(own_key, axis), (), 0, length) for axis, length in enumerate(values.shape)]
    widest = values.shape.index(max(values.shape))
    next_to = index_at[:widest] + [(index_at[widest] + 1) % values.shape[widest]] + index_at[widest + 1:]
    return values.at[tuple(index_at)].set(low).at[tuple(next_to)].set(top_value)


def block_scale(rng, extent, shards, smallest, high):
    level = 1.0
    for axis_at, shards_of in shards:
        draws = jax.random.uniform(jax.random.fold_in(jax.random.fold_in(rng, 6), axis_at), (shards_of,), jnp.float32, smallest / len(shards), high / len(shards))
        level = level * jnp.repeat(jnp.exp(draws), extent[axis_at] // shards_of).reshape((-1,) + (1,) * (len(extent) - 1 - axis_at))
    return level


def noise(own_key, extent, width, limit, shards=(), held_as=jnp.bfloat16):
    values = width * jax.random.normal(own_key, extent, jnp.float32)
    if shards:
        values = values * block_scale(own_key, extent, shards, -0.22, 0.18)
    return jnp.clip(values, -limit, limit).astype(held_as)


def setup_inputs(seed: int = 0) -> dict:
    arg_keys = jax.random.split(jax.random.key(seed), 21)
    return {
        "hidden_in": noise(arg_keys[0], (TOKENS, D), 1.0, 6.0, ((0, 32),)),
        "grad_out": noise(arg_keys[1], (TOKENS, D), 1.0, 6.0, ((0, 32),)),
        "w_query": noise(arg_keys[2], (D, D), D ** -0.5, 0.21875, ((0, 8), (1, 4))),
        "b_query": noise(arg_keys[3], (D,), 0.3, 1.75, ((0, 4),), jnp.float32),
        "w_key": noise(arg_keys[4], (D, D), D ** -0.5, 0.21875, ((0, 8), (1, 4))),
        "w_value": noise(arg_keys[5], (D, D), D ** -0.5, 0.21875, ((0, 8), (1, 4))),
        "b_value": noise(arg_keys[6], (D,), 0.05, 0.3125, ((0, 4),), jnp.float32),
        "w_out": noise(arg_keys[7], (D, D), 4 ** -0.5, 3.0, ((0, 4), (1, 8))),
        "b_out": noise(arg_keys[8], (D,), 0.3, 1.75, (), jnp.float32),
        "gain_one": jnp.clip(1.0 + 0.15 * jax.random.normal(arg_keys[9], (D,), jnp.float32), 0.25, 1.75),
        "shift_one": noise(arg_keys[10], (D,), 0.3, 1.75, (), jnp.float32),
        "w_up": noise(arg_keys[11], (D, FF), D ** -0.5, 0.21875, ((0, 8), (1, 4))),
        "b_up": noise(arg_keys[12], (FF,), 0.3, 1.75, (), jnp.float32),
        "w_down": noise(arg_keys[13], (FF, D), FF ** -0.5, 0.109375, ((0, 4), (1, 8))),
        "b_down": noise(arg_keys[14], (D,), 0.3, 1.75, (), jnp.float32),
        "gain_two": jnp.clip(1.0 + 0.15 * jax.random.normal(arg_keys[15], (D,), jnp.float32), 0.25, 1.75),
        "shift_two": noise(arg_keys[16], (D,), 0.3, 1.75, (), jnp.float32),
        "lengths": draw_lengths(jax.random.fold_in(arg_keys[20], 71), 0),
        "global_raw": plant(jax.random.randint(arg_keys[18], (SEQS, GLOB), 0, 65536), jax.random.fold_in(arg_keys[18], 1), 0, 65535).astype(jnp.int32),
        "random_raw": plant(jax.random.randint(arg_keys[19], (SEQS, NB, RAND), 0, 65536), jax.random.fold_in(arg_keys[19], 1), 0, 65535).astype(jnp.int32),
    }


@jax.custom_vjp
def low(v):
    return lax.optimization_barrier(v.astype(jnp.bfloat16)).astype(jnp.float32)

@jax.custom_vjp
def low_back(v):
    return v

def low_keep(v):
    return (low(v), None)

def low_pass(kept, grad):
    return (grad,)

def back_keep(v):
    return (v, None)

def back_low(kept, grad):
    return (low(grad),)
low.defvjp(low_keep, low_pass)
low_back.defvjp(back_keep, back_low)
highest = lax.Precision.HIGHEST
masked_score = -1e+30
EPSILON = 1e-12

def matmul(a, b):
    return jnp.dot(a, b, precision=highest)

def layer_norm(values, gain_vec, shift_vec):
    centred = values - lax.optimization_barrier(jnp.mean(values, axis=-1, keepdims=True))
    spread = lax.optimization_barrier(jnp.mean(centred * centred, axis=-1, keepdims=True))
    return centred * lax.rsqrt(spread + EPSILON) * gain_vec + shift_vec

def block_tables(length, global_row, random_rows):
    live_count = (length + BLK - 1) // BLK
    block_ids = jnp.arange(NB, dtype=jnp.int32)
    left_block = jnp.maximum(block_ids - 1, 0)
    right_block = jnp.minimum(block_ids + 1, NB - 1)
    global_ids = jnp.broadcast_to((global_row % live_count)[None, :], (NB, GLOB))
    key_table = jnp.concatenate([left_block[:, None], block_ids[:, None], right_block[:, None], global_ids, random_rows % live_count], axis=1).astype(jnp.int32)
    block_ok = jnp.concatenate([(block_ids >= 1)[:, None], (block_ids >= 0)[:, None], (block_ids + 1 < NB)[:, None], jnp.ones((NB, GLOB + RAND), dtype=jnp.bool_)], axis=1)
    position = key_table[:, :, None] * BLK + jnp.arange(BLK, dtype=jnp.int32)[None, None, :]
    key_valid = block_ok[:, :, None] & (position < length)
    return (key_table, key_valid.reshape(NB, (3 + GLOB + RAND) * BLK))

def attend(queries, key_seq, value_seq, key_table, key_valid):
    group_size = QROWS // BLK
    score_scale = HD ** (-0.5)

    def one_group(pieces):
        q_part, table_part, valid_part = pieces
        k_part = key_seq[table_part].reshape(group_size, -1, H, HD)
        v_part = value_seq[table_part].reshape(group_size, -1, H, HD)
        scores = jnp.einsum('gqhd,gkhd->ghqk', q_part, k_part, precision=highest) * score_scale
        scores = low_back(scores)
        scores = jnp.where(valid_part[:, None, None, :], scores, masked_score)
        row_max = lax.optimization_barrier(jnp.max(scores, axis=-1, keepdims=True))
        weights = jnp.exp(scores - row_max)
        weights = weights / lax.optimization_barrier(jnp.sum(weights, axis=-1, keepdims=True))
        return jnp.einsum('ghqk,gkhd->gqhd', low(weights), v_part, precision=highest)
    group_count = NB // group_size
    result = lax.map(jax.checkpoint(one_group), (queries.reshape(group_count, group_size, BLK, H, HD), key_table.reshape(group_count, group_size, -1), key_valid.reshape(group_count, group_size, -1)))
    return result.reshape(LMAX, H * HD)

def sequence_layer(inputs, params, key_table, key_valid):
    w_query, b_query, w_key, w_value, b_value, w_out, b_out, gain_one, shift_one, w_up, b_up, w_down, b_down, gain_two, shift_two = params
    queries = low_back(low(matmul(inputs, w_query) + b_query))
    key_rows = low_back(low(matmul(inputs, w_key)))
    value_rows = low_back(low(matmul(inputs, w_value) + b_value))
    mixed_out = attend(queries.reshape(NB, BLK, H, HD), key_rows.reshape(NB, BLK, H, HD), value_rows.reshape(NB, BLK, H, HD), key_table, key_valid)
    mixed_out = low_back(low(mixed_out))
    after_attn = low_back(inputs + matmul(mixed_out, w_out) + b_out)
    normed = layer_norm(after_attn, gain_one, shift_one)
    hidden_pre = low_back(matmul(low(normed), w_up) + b_up)
    activated = low(jax.nn.gelu(hidden_pre, approximate=True))
    summed = low_back(normed + matmul(activated, w_down) + b_down)
    return layer_norm(summed, gain_two, shift_two)

def reference(hidden_in, grad_out, w_query, b_query, w_key, w_value, b_value, w_out, b_out, gain_one, shift_one, w_up, b_up, w_down, b_down, gain_two, shift_two, lengths, global_raw, random_raw):
    params = tuple((p.astype(jnp.float32) for p in (w_query, b_query, w_key, w_value, b_value, w_out, b_out, gain_one, shift_one, w_up, b_up, w_down, b_down, gain_two, shift_two)))
    inputs = hidden_in.astype(jnp.float32).reshape(SEQS, LMAX, D)
    cotangent = grad_out.astype(jnp.float32).reshape(SEQS, LMAX, D)

    def per_sequence(totals, pieces):
        seq_in, seq_cot, length, global_row, random_rows = pieces
        key_table, key_valid = block_tables(length, global_row, random_rows)
        keep_rows = (jnp.arange(LMAX, dtype=jnp.int32) < length)[:, None]
        result, pullback = jax.vjp(lambda a, b: sequence_layer(a, b, key_table, key_valid), seq_in, params)
        grad_seq, grad_params = pullback(jnp.where(keep_rows, seq_cot, jnp.zeros_like(seq_cot)))
        totals = jax.tree.map(lambda t, g: t + g, totals, grad_params)
        return (totals, (result.astype(jnp.bfloat16), grad_seq))
    zero_grads = jax.tree.map(jnp.zeros_like, params)
    totals, (seq_outs, grad_rows) = lax.scan(per_sequence, zero_grads, (inputs, cotangent, lengths, global_raw, random_raw))
    return (seq_outs.reshape(TOKENS, D), grad_rows.reshape(TOKENS, D), totals[0], totals[1], totals[2], totals[3], totals[4], totals[5], totals[6], totals[7], totals[8], totals[9], totals[10], totals[11], totals[12], totals[13], totals[14])
```

```python
from functools import partial

import jax
import jax.numpy as jnp
from jax import lax
from jax.experimental import pallas as pl
from jax.experimental.pallas import tpu as pltpu
from jax.sharding import PartitionSpec as P

D = 768
HD = 64
FF = 3072
BLK = 64
GLOB = 2
RAND = 3
LMAX = 2048
NB = 32
KEYS = (3 + GLOB + RAND) * BLK
PAD = 256
LANES = 128

masked_score = -1e30
EPSILON = 1e-12
f32 = jnp.float32
bf16 = jnp.bfloat16


def swap(array, bit):
    size = lax.axis_size("tensor")
    return lax.ppermute(array, "tensor", [(t, t ^ bit) for t in range(size)])


def dp_swap(array, bit):
    size = lax.axis_size("dp")
    return lax.ppermute(array, "dp", [(t, t ^ bit) for t in range(size)])


def ring_order(size):
    return list(range(0, size, 2)) + list(range(size - 1, 0, -2))


def ring_member(steps):
    size = lax.axis_size("dp")
    me = lax.axis_index("dp")
    place = jnp.where(me % 2 == 0, me // 2, size - 1 - me // 2)
    place = (place + steps + size) % size
    return jnp.where(place < size // 2, 2 * place, 2 * (size - 1 - place) + 1)


def ring_send(array, step):
    size = lax.axis_size("dp")
    order = ring_order(size)
    return lax.ppermute(
        array, "dp", [(order[i], order[(i + step) % size]) for i in range(size)]
    )


def gather_rows(shard):
    size = lax.axis_size("dp")
    if size != 8:
        return lax.all_gather(shard, "dp", axis=0, tiled=True)
    rows, width = shard.shape
    whole = jnp.zeros((size, rows, width), shard.dtype)

    def put(whole, piece, steps):
        return lax.dynamic_update_slice(whole, piece[None], (ring_member(steps), 0, 0))

    whole = put(whole, shard, 0)
    ahead, behind = shard, shard
    for step in range(1, size // 2 + 1):
        ahead = ring_send(ahead, 1)
        if step < size // 2:
            behind = ring_send(behind, -1)
        whole = put(whole, ahead, -step)
        if step < size // 2:
            whole = put(whole, behind, step)
    return whole.reshape(size * rows, width)


def scatter_sum(partial_sums):
    size = lax.axis_size("dp")
    if size != 8:
        return lax.psum_scatter(partial_sums, "dp", scatter_dimension=0, tiled=True).astype(f32)
    width = partial_sums.shape[1]
    blocks = partial_sums.reshape(size, -1, width)

    def part(steps):
        return lax.dynamic_index_in_dim(blocks, ring_member(steps), 0, keepdims=False)

    half = size // 2
    ahead = ring_send(part(half), 1)
    behind = ring_send(part(1 - half), -1)
    for left in range(half - 1, 0, -1):
        ahead = ring_send((ahead.astype(f32) + part(left).astype(f32)).astype(bf16), 1)
        if left > 1:
            behind = ring_send(
                (behind.astype(f32) + part(1 - left).astype(f32)).astype(bf16), -1
            )
    return ahead.astype(f32) + behind.astype(f32) + part(0).astype(f32)


def sum_over(vector, dp_only=False):
    if not dp_only:
        bit = 1
        while bit < lax.axis_size("tensor"):
            vector = vector + swap(vector, bit)
            bit *= 2
    bit = 1
    while bit < lax.axis_size("dp"):
        vector = vector + dp_swap(vector, bit)
        bit *= 2
    return vector


def layer_norm(values, gain_vec, shift_vec):
    centred = values - jnp.mean(values, axis=-1, keepdims=True)
    inv_std = lax.rsqrt(jnp.mean(centred * centred, axis=-1, keepdims=True) + EPSILON)
    scaled = centred * inv_std
    return (scaled * gain_vec + shift_vec, scaled, inv_std)


def norm_backward(upstream, scaled, inv_std, gain_vec):
    weighted = upstream * gain_vec
    inner_sum = jnp.mean(weighted * scaled, axis=-1, keepdims=True)
    grad_values = inv_std * (
        weighted - jnp.mean(weighted, axis=-1, keepdims=True) - scaled * inner_sum
    )
    return (grad_values, jnp.sum(upstream * scaled, axis=0), jnp.sum(upstream, axis=0))


def block_tables(lengths, global_raw, random_raw, own_blocks):
    seq_count = lengths.shape[0]
    me = lax.axis_index("tensor")
    live_count = (lengths + BLK - 1) // BLK
    block_ids = jnp.arange(NB, dtype=jnp.int32)
    left_block = jnp.maximum(block_ids - 1, 0)
    right_block = jnp.minimum(block_ids + 1, NB - 1)
    near_ids = jnp.broadcast_to(
        jnp.stack([left_block, block_ids, right_block], axis=1)[None], (seq_count, NB, 3)
    )
    global_ids = jnp.broadcast_to(
        (global_raw % live_count[:, None])[:, None, :], (seq_count, NB, GLOB)
    )
    random_ids = random_raw % live_count[:, None, None]
    key_table = jnp.concatenate([near_ids, global_ids, random_ids], axis=2)
    near_ok = jnp.stack([block_ids >= 1, block_ids >= 0, block_ids + 1 < NB], axis=1)
    block_ok = jnp.concatenate([near_ok, jnp.ones((NB, GLOB + RAND), dtype=jnp.bool_)], axis=1)
    position = key_table[..., None] * BLK + jnp.arange(BLK, dtype=jnp.int32)
    key_valid = block_ok[None, :, :, None] & (position < lengths[:, None, None, None])
    bias = jnp.where(key_valid, 0.0, masked_score).astype(f32).reshape(seq_count * NB, KEYS)
    offsets = jnp.arange(seq_count, dtype=jnp.int32)[:, None, None] * NB
    table = (key_table + offsets).reshape(seq_count * NB, -1)
    table = ((table // own_blocks) ^ me) * own_blocks + table % own_blocks
    pieces = seq_count * NB // own_blocks
    order = jnp.arange(pieces, dtype=jnp.int32) ^ me
    table = jnp.take(table.reshape(pieces, own_blocks, -1), order, axis=0)
    bias = jnp.take(bias.reshape(pieces, own_blocks, KEYS), order, axis=0)
    return table.reshape(pieces * own_blocks, -1), bias.reshape(pieces * own_blocks, KEYS)


def head_masks(heads, scale, dtype):
    lane = lax.broadcasted_iota(jnp.int32, (1, PAD), 1)
    return [
        jnp.where((lane >= h * HD) & (lane < (h + 1) * HD), scale, 0.0).astype(dtype)
        for h in range(heads)
    ]


def stacked_heads(rows, masks):
    return jnp.concatenate([rows * mask for mask in masks], axis=0)


def unstacked_heads(stacked, masks):
    rows = stacked.shape[0] // len(masks)
    total = stacked[:rows] * masks[0]
    for h in range(1, len(masks)):
        total = total + stacked[h * rows : (h + 1) * rows] * masks[h]
    return total


def key_blocks(ref, table, block, column):
    return jnp.concatenate(
        [
            ref[pl.ds(pl.multiple_of(table[block, j] * BLK, BLK), BLK), column : column + PAD]
            for j in range(KEYS // BLK)
        ],
        axis=0,
    )


def contract(a, b, dims):
    return lax.dot_general(a, b, ((dims[:1], dims[1:]), ((), ())), preferred_element_type=f32)


def attend_kernel(heads, chosen, pieces, own_blocks, table, *refs):
    parts = refs[:pieces]
    bias = refs[pieces]
    outs = refs[pieces + 1 : pieces + 1 + len(chosen)]
    totals = refs[pieces + 1 + len(chosen) : pieces + 1 + 2 * len(chosen)]
    rows, sems = refs[pieces + 1 + 2 * len(chosen) :]
    own_rows = own_blocks * BLK
    copies = [
        pltpu.make_async_copy(
            parts[s], rows.at[pl.ds(s * own_rows, own_rows)], sems.at[s]
        )
        for s in range(pieces)
    ]
    for copy in copies:
        copy.start()
    for copy in copies:
        copy.wait()
    query_masks = head_masks(heads, HD**-0.5, bf16)
    out_masks = head_masks(heads, 1.0, f32)
    lane = lax.broadcasted_iota(jnp.int32, (BLK, LANES), 1)

    def step(i, carry):
        for at, s in enumerate(chosen):
            block = s * own_blocks + i
            start = pl.multiple_of(i * BLK, BLK)
            queries = stacked_heads(
                rows[pl.ds(pl.multiple_of(block * BLK, BLK), BLK), 0:PAD], query_masks
            )
            keys = key_blocks(rows, table, block, PAD)
            values = key_blocks(rows, table, block, 2 * PAD)
            scores = contract(queries, keys, (1, 1)) + bias[pl.ds(block, 1), :]
            top = jnp.max(scores, axis=-1, keepdims=True)
            weights = jnp.exp(scores - top)
            total = jnp.sum(weights, axis=-1, keepdims=True)
            mixed = contract(weights.astype(bf16), values, (1, 0)) / total
            outs[at][pl.ds(start, BLK), :] = unstacked_heads(mixed, out_masks).astype(bf16)
            log_total = top + jnp.log(total)
            kept = jnp.zeros((BLK, LANES), f32)
            for h in range(heads):
                kept = jnp.where(lane == h, log_total[h * BLK : (h + 1) * BLK], kept)
            totals[at][pl.ds(start, BLK), :] = kept
        return carry

    lax.fori_loop(0, own_blocks, step, 0)


def attend_forward(parts, table, bias, heads, chosen):
    own_rows = parts[0].shape[0]
    pieces = len(parts)
    own_blocks = own_rows // BLK
    n = len(chosen)
    vmem = pl.BlockSpec(memory_space=pltpu.VMEM)
    work = n * own_rows * KEYS * heads
    results = pl.pallas_call(
        partial(attend_kernel, heads, chosen, pieces, own_blocks),
        out_shape=[jax.ShapeDtypeStruct((own_rows, PAD), bf16)] * n
        + [jax.ShapeDtypeStruct((own_rows, LANES), f32)] * n,
        in_specs=[pl.BlockSpec(memory_space=pltpu.SMEM)]
        + [pl.BlockSpec(memory_space=pl.ANY)] * pieces
        + [vmem],
        out_specs=[vmem] * (2 * n),
        scratch_shapes=[
            pltpu.VMEM((pieces * own_rows, 3 * PAD), bf16),
            pltpu.SemaphoreType.DMA((pieces,)),
        ],
        cost_estimate=pl.CostEstimate(
            flops=12 * work * HD, bytes_accessed=4 << 20, transcendentals=work
        ),
        name="attend_forward",
    )(table, *parts, bias)
    return results[:n], results[n:]


def attend_back_kernel(heads, pieces, own_blocks, table, *refs):
    parts = refs[:pieces]
    ups = refs[pieces : 2 * pieces]
    totals = refs[2 * pieces : 3 * pieces]
    bias = refs[3 * pieces]
    outs = refs[3 * pieces + 1 : 4 * pieces + 1]
    rows, up_rows, key_sum, value_sum, sems = refs[4 * pieces + 1 :]
    own_rows = own_blocks * BLK
    copies = [
        pltpu.make_async_copy(
            parts[s], rows.at[pl.ds(s * own_rows, own_rows)], sems.at[s]
        )
        for s in range(pieces)
    ] + [
        pltpu.make_async_copy(
            ups[s], up_rows.at[pl.ds(s * own_rows, own_rows)], sems.at[pieces + s]
        )
        for s in range(pieces)
    ]
    for copy in copies:
        copy.start()
    key_sum[...] = jnp.zeros_like(key_sum)
    value_sum[...] = jnp.zeros_like(value_sum)
    for copy in copies:
        copy.wait()
    query_masks = head_masks(heads, HD**-0.5, bf16)
    up_masks = head_masks(heads, 1.0, bf16)
    out_masks = head_masks(heads, HD**-0.5, f32)
    for s in range(pieces):

        def step(i, carry, s=s):
            block = s * own_blocks + i
            start = pl.multiple_of(i * BLK, BLK)
            at = pl.ds(pl.multiple_of(block * BLK, BLK), BLK)
            queries = stacked_heads(rows[at, 0:PAD], query_masks)
            upstream = stacked_heads(up_rows[at, :], up_masks)
            keys = key_blocks(rows, table, block, PAD)
            values = key_blocks(rows, table, block, 2 * PAD)
            kept = totals[s][pl.ds(start, BLK), :]
            log_total = jnp.concatenate([kept[:, h : h + 1] for h in range(heads)], axis=0)
            scores = contract(queries, keys, (1, 1)) + bias[pl.ds(block, 1), :]
            weights = jnp.exp(scores - log_total)
            grad_weights = contract(upstream, values, (1, 1))
            inner = jnp.sum(weights * grad_weights, axis=-1, keepdims=True)
            grad_scores = (weights * (grad_weights - inner)).astype(bf16)
            grad_query = contract(grad_scores, keys, (1, 0))
            outs[s][pl.ds(start, BLK), 0:PAD] = unstacked_heads(grad_query, out_masks).astype(bf16)
            key_part = contract(grad_scores, queries, (0, 0))
            value_part = contract(weights.astype(bf16), upstream, (0, 0))
            for j in range(KEYS // BLK):
                there = pl.ds(pl.multiple_of(table[block, j] * BLK, BLK), BLK)
                key_sum[there, :] += key_part[j * BLK : (j + 1) * BLK]
                value_sum[there, :] += value_part[j * BLK : (j + 1) * BLK]
            return carry

        lax.fori_loop(0, own_blocks, step, 0)
    for s in range(pieces):
        span = pl.ds(s * own_rows, own_rows)
        outs[s][:, PAD : 2 * PAD] = key_sum[span, :].astype(bf16)
        outs[s][:, 2 * PAD : 3 * PAD] = value_sum[span, :].astype(bf16)


def attend_backward(parts, ups, totals, table, bias, heads):
    own_rows = parts[0].shape[0]
    pieces = len(parts)
    own_blocks = own_rows // BLK
    vmem = pl.BlockSpec(memory_space=pltpu.VMEM)
    work = pieces * own_rows * KEYS * heads
    return pl.pallas_call(
        partial(attend_back_kernel, heads, pieces, own_blocks),
        out_shape=[jax.ShapeDtypeStruct((own_rows, 3 * PAD), bf16)] * pieces,
        in_specs=[pl.BlockSpec(memory_space=pltpu.SMEM)]
        + [pl.BlockSpec(memory_space=pl.ANY)] * (2 * pieces)
        + [vmem] * (pieces + 1),
        out_specs=[vmem] * pieces,
        scratch_shapes=[
            pltpu.VMEM((pieces * own_rows, 3 * PAD), bf16),
            pltpu.VMEM((pieces * own_rows, PAD), bf16),
            pltpu.VMEM((pieces * own_rows, PAD), f32),
            pltpu.VMEM((pieces * own_rows, PAD), f32),
            pltpu.SemaphoreType.DMA((2 * pieces,)),
        ],
        cost_estimate=pl.CostEstimate(
            flops=30 * work * HD, bytes_accessed=12 << 20, transcendentals=work
        ),
        name="attend_backward",
    )(table, *parts, *ups, *totals, bias)


def padded(array):
    return jnp.pad(array, ((0, 0), (0, PAD - array.shape[1])))


def dot(a, b, dims=(1, 0)):
    return contract(a, b, dims)


def per_device(
    hidden_in,
    grad_out,
    w_query,
    b_query,
    w_key,
    w_value,
    b_value,
    w_out,
    b_out,
    gain_one,
    shift_one,
    w_up,
    b_up,
    w_down,
    b_down,
    gain_two,
    shift_two,
    lengths,
    global_raw,
    random_raw,
):
    own_rows = hidden_in.shape[0]
    me = lax.axis_index("tensor")
    width = w_query.shape[1]
    heads = width // HD
    hidden = w_up.shape[1]

    table, bias = block_tables(lengths, global_raw, random_raw, own_rows // BLK)

    x2 = swap(hidden_in, 2)
    x1 = swap(hidden_in, 1)
    x3 = swap(x2, 1)
    x_parts = [hidden_in, x1, x2, x3]

    qkv_w = gather_rows(jnp.concatenate([padded(w_query), padded(w_key), padded(w_value)], axis=1))
    out_t = padded(w_out.T)
    down_t = w_down.T
    up_far, out_far, down_far = swap(w_up, 2), swap(out_t, 2), swap(down_t, 2)
    up_out = gather_rows(jnp.concatenate([w_up, up_far, out_t, out_far], axis=1))
    up_w = up_out[:, : 2 * hidden]
    out_near = up_out[:, 2 * hidden :]
    down_w = gather_rows(jnp.concatenate([down_t, down_far], axis=1))
    out_other = swap(out_near, 1)
    out_ws = [
        out_near[:, :PAD],
        out_other[:, :PAD],
        out_near[:, PAD:],
        out_other[:, PAD:],
    ]
    b_up_parts = b_up.reshape(-1, hidden)
    b_up_used = jnp.concatenate([jnp.take(b_up_parts, me, axis=0), jnp.take(b_up_parts, me ^ 2, axis=0)])

    qkv_b = jnp.concatenate(
        [jnp.pad(b_query, (0, PAD - width)), jnp.zeros((PAD,), f32), jnp.pad(b_value, (0, PAD - width))]
    )
    qkv = [(dot(x, qkv_w) + qkv_b).astype(bf16) for x in x_parts]

    (o2, o3), (t2, t3) = attend_forward(qkv, table, bias, heads, (2, 3))
    r2 = swap(o2, 2)
    r3 = swap(o3, 3)
    (o0, o1), (t0, t1) = attend_forward(qkv, table, bias, heads, (0, 1))
    r1 = swap(o1, 1)
    mixed = [o0, r1, r2, r3]

    after = hidden_in.astype(f32) + b_out
    for o, w in zip(mixed, out_ws):
        after = after + dot(o, w, (1, 1))
    normed, scaled_one, inv_one = layer_norm(after, gain_one, shift_one)
    normed_low = normed.astype(bf16)
    rows_low = jnp.concatenate([normed_low, swap(normed_low, 1)], axis=0)
    up_pre = dot(rows_low, up_w) + b_up_used
    activated, gelu_pull = jax.vjp(partial(jax.nn.gelu, approximate=True), up_pre)
    activated = activated.astype(bf16)
    ffn = dot(activated, down_w, (1, 1))
    summed = normed + b_down + ffn[:own_rows] + swap(ffn[own_rows:], 1)
    layer_out, scaled_two, inv_two = layer_norm(summed, gain_two, shift_two)

    row_ids = me * own_rows + jnp.arange(own_rows, dtype=jnp.int32)
    keep_rows = row_ids % LMAX < jnp.take(lengths, row_ids // LMAX)
    upstream = jnp.where(keep_rows[:, None], grad_out.astype(f32), 0.0)
    grad_summed, grad_gain_two, grad_shift_two = norm_backward(
        upstream, scaled_two, inv_two, gain_two
    )
    grad_low = grad_summed.astype(bf16)
    grad_b_down = jnp.sum(grad_low.astype(f32), axis=0)
    grads_low = jnp.concatenate([grad_low, swap(grad_low, 1)], axis=0)
    down_sums = dot(grads_low, activated, (0, 0)).astype(bf16)
    grad_up = gelu_pull(dot(grads_low, down_w))[0].astype(bf16)
    grad_b_up = jnp.sum(grad_up.astype(f32), axis=0)
    back = dot(grad_up, up_w, (1, 1))
    up_sums = dot(rows_low, grad_up, (0, 0)).astype(bf16)
    grad_normed = grad_low.astype(f32) + back[:own_rows] + swap(back[own_rows:], 1)
    grad_after, grad_gain_one, grad_shift_one = norm_backward(
        grad_normed, scaled_one, inv_one, gain_one
    )
    after_low = grad_after.astype(bf16)
    grad_b_out = jnp.sum(after_low.astype(f32), axis=0)

    grad_mixed = [dot(after_low, w).astype(bf16) for w in out_ws]
    ups = [grad_mixed[0]] + [swap(grad_mixed[s], s) for s in range(1, 4)]
    out_sums = [dot(after_low, o, (0, 0)).astype(bf16) for o in mixed]
    out_pair = jnp.concatenate([out_sums[0], out_sums[2]], axis=1).astype(f32) + swap(
        jnp.concatenate([out_sums[1], out_sums[3]], axis=1), 1
    ).astype(f32)

    down_part = scatter_sum(down_sums)
    up_part = scatter_sum(jnp.concatenate([up_sums, out_pair.astype(bf16)], axis=1))

    grads = attend_backward(qkv, ups, [t0, t1, t2, t3], table, bias, heads)
    parts = [dot(g, qkv_w, (1, 1)) for g in grads]
    far = parts[2] + swap(parts[3].astype(bf16), 1).astype(f32)
    far = swap(far.astype(bf16), 2)
    near = parts[0] + swap(parts[1].astype(bf16), 1).astype(f32)
    grad_in = after_low.astype(f32) + near + far.astype(f32)

    qkv_sums = dot(x_parts[0], grads[0], (0, 0))
    for s in range(1, 4):
        qkv_sums = qkv_sums + dot(x_parts[s], grads[s], (0, 0))
    qkv_part = scatter_sum(qkv_sums.astype(bf16))

    def far_sum(part, cut):
        return part[:, :cut] + swap(part[:, cut:].astype(bf16), 2).astype(f32)

    grad_w_down = far_sum(down_part, hidden).T
    grad_w_up = far_sum(up_part[:, : 2 * hidden], hidden)
    grad_w_out = far_sum(up_part[:, 2 * hidden :], PAD)[:, :width].T

    up_slots = jnp.zeros((FF // hidden, hidden), f32)
    up_slots = lax.dynamic_update_slice(up_slots, grad_b_up[None, :hidden], (me, 0))
    up_slots = lax.dynamic_update_slice(up_slots, grad_b_up[None, hidden:], (me ^ 2, 0))
    rows = [grad_gain_two, grad_shift_two, grad_b_down, grad_gain_one, grad_shift_one, grad_b_out]
    small = sum_over(jnp.concatenate([jnp.stack(rows).reshape(-1), up_slots.reshape(-1)]))
    small_rows = small[: 6 * D].reshape(6, D)
    bias_up = jnp.take(small[6 * D :].reshape(-1, hidden), me, axis=0)
    row_sums = sum(jnp.sum(g.astype(f32), axis=0) for g in grads)
    bias_pair = sum_over(jnp.concatenate([row_sums[:PAD], row_sums[2 * PAD :]]), dp_only=True)

    return (
        layer_out.astype(bf16),
        grad_in,
        qkv_part[:, :width],
        bias_pair[:width],
        qkv_part[:, PAD : PAD + width],
        qkv_part[:, 2 * PAD : 2 * PAD + width],
        bias_pair[PAD : PAD + width],
        grad_w_out,
        small_rows[5],
        small_rows[3],
        small_rows[4],
        grad_w_up,
        bias_up,
        grad_w_down,
        small_rows[2],
        small_rows[0],
        small_rows[1],
    )


def solution(mesh):
    in_specs = (
        P(("dp", "tensor"), None),
        P(("dp", "tensor"), None),
        P("dp", "tensor"),
        P("tensor"),
        P("dp", "tensor"),
        P("dp", "tensor"),
        P("tensor"),
        P("tensor", "dp"),
        P(),
        P(),
        P(),
        P("dp", "tensor"),
        P(),
        P("tensor", "dp"),
        P(),
        P(),
        P(),
        P("dp"),
        P("dp", None),
        P("dp", None, None),
    )
    out_specs = (
        P(("dp", "tensor"), None),
        P(("dp", "tensor"), None),
        P("dp", "tensor"),
        P("tensor"),
        P("dp", "tensor"),
        P("dp", "tensor"),
        P("tensor"),
        P("tensor", "dp"),
        P(),
        P(),
        P(),
        P("dp", "tensor"),
        P("tensor"),
        P("tensor", "dp"),
        P(),
        P(),
        P(),
    )
    return jax.shard_map(
        per_device, mesh=mesh, in_specs=in_specs, out_specs=out_specs, check_vma=False
    )
```

```python
from functools import partial

import jax
import jax.numpy as jnp
from jax import lax
from jax.experimental import pallas as pl
from jax.experimental.pallas import tpu as pltpu
from jax.sharding import PartitionSpec as P

D = 768
HD = 64
FF = 3072
BLK = 64
GLOB = 2
RAND = 3
LMAX = 2048
NB = 32
KEYS = (3 + GLOB + RAND) * BLK
PAD = 256
LANES = 128
SUM_ROW = 10

masked_score = -1e30
EPSILON = 1e-12
f32 = jnp.float32
bf16 = jnp.bfloat16


def swap(array, bit):
    size = lax.axis_size("tensor")
    return lax.ppermute(array, "tensor", [(t, t ^ bit) for t in range(size)])


def dp_swap(array, bit):
    size = lax.axis_size("dp")
    return lax.ppermute(array, "dp", [(t, t ^ bit) for t in range(size)])


def ring_order(size):
    return list(range(0, size, 2)) + list(range(size - 1, 0, -2))


def ring_member(steps):
    size = lax.axis_size("dp")
    me = lax.axis_index("dp")
    place = jnp.where(me % 2 == 0, me // 2, size - 1 - me // 2)
    place = (place + steps + size) % size
    return jnp.where(place < size // 2, 2 * place, 2 * (size - 1 - place) + 1)


def ring_send(array, step):
    size = lax.axis_size("dp")
    order = ring_order(size)
    return lax.ppermute(
        array, "dp", [(order[i], order[(i + step) % size]) for i in range(size)]
    )


RING_STEPS = (0, -1, 1, -2, 2, -3, 3, -4)


def ring_pieces(shard, gate=None):
    pieces = [shard]
    ahead, behind = shard, shard
    for step in range(1, 5):
        if gate is not None:
            ahead, behind = gate(step, ahead, behind)
        ahead = ring_send(ahead, 1)
        pieces.append(ahead)
        if step < 4:
            behind = ring_send(behind, -1)
            pieces.append(behind)
    return pieces


def dp_scatter_sum(sums):
    size = lax.axis_size("dp")
    if size != 8:
        return lax.psum_scatter(sums, "dp", scatter_dimension=0, tiled=True).astype(f32)
    blocks = lax.all_to_all(sums.reshape(size, -1, sums.shape[1]), "dp", 0, 0, tiled=True)
    return jnp.sum(blocks.astype(f32), axis=0)


def sum_over(vector, dp_only=False):
    if not dp_only:
        bit = 1
        while bit < lax.axis_size("tensor"):
            vector = vector + swap(vector, bit)
            bit *= 2
    bit = 1
    while bit < lax.axis_size("dp"):
        vector = vector + dp_swap(vector, bit)
        bit *= 2
    return vector


def block_tables(lengths, global_raw, random_raw, own_blocks, pieces):
    count = own_blocks * pieces
    per_block = KEYS // BLK

    def kernel(length_ref, global_ref, random_ref, table, bias):
        me = lax.axis_index("tensor")
        lane = lax.broadcasted_iota(jnp.int32, (1, KEYS), 1)
        slot = lane // BLK
        within = lane % BLK

        def step(i, carry):
            block = ((i // own_blocks) ^ me) * own_blocks + i % own_blocks
            seq = block // NB
            block = block % NB
            length = length_ref[seq]
            live = (length + BLK - 1) // BLK
            ids = [jnp.maximum(block - 1, 0), block, jnp.minimum(block + 1, NB - 1)]
            ids += [lax.rem(global_ref[seq, j], live) for j in range(GLOB)]
            ids += [lax.rem(random_ref[seq, block, r], live) for r in range(RAND)]
            spread_ids = jnp.zeros((1, KEYS), jnp.int32)
            for j in range(per_block):
                spread_ids = jnp.where(slot == j, ids[j], spread_ids)
                there = ids[j] + seq * NB
                table[i, j] = ((there // own_blocks) ^ me) * own_blocks + there % own_blocks
            position = spread_ids * BLK + within
            lost = (position >= length) | ((slot == 0) & (block == 0))
            lost = lost | ((slot == 2) & (block == NB - 1))
            bias[pl.ds(i, 1), :] = jnp.where(lost, masked_score, 0.0).astype(f32)
            return carry

        lax.fori_loop(0, count, step, 0)

    smem = pl.BlockSpec(memory_space=pltpu.SMEM)
    return pl.pallas_call(
        kernel,
        out_shape=[
            jax.ShapeDtypeStruct((count, per_block), jnp.int32),
            jax.ShapeDtypeStruct((count, KEYS), f32),
        ],
        in_specs=[smem] * 3,
        out_specs=[smem, pl.BlockSpec(memory_space=pltpu.VMEM)],
        cost_estimate=cost(count * KEYS * 16, count * KEYS * 4),
        name="block_tables",
    )(lengths, global_raw, random_raw)


def head_masks(heads, scale, dtype):
    lane = lax.broadcasted_iota(jnp.int32, (1, PAD), 1)
    return [
        jnp.where((lane >= h * HD) & (lane < (h + 1) * HD), scale, 0.0).astype(dtype)
        for h in range(heads)
    ]


def stacked_heads(rows, masks):
    return jnp.concatenate([rows * mask for mask in masks], axis=0)


def unstacked_heads(stacked, masks):
    rows = stacked.shape[0] // len(masks)
    total = stacked[:rows] * masks[0]
    for h in range(1, len(masks)):
        total = total + stacked[h * rows : (h + 1) * rows] * masks[h]
    return total


def key_blocks(ref, table, block, column):
    return jnp.concatenate(
        [
            ref[pl.ds(pl.multiple_of(table[block, j] * BLK, BLK), BLK), column : column + PAD]
            for j in range(KEYS // BLK)
        ],
        axis=0,
    )


def contract(a, b, dims):
    return lax.dot_general(a, b, ((dims[:1], dims[1:]), ((), ())), preferred_element_type=f32)


def attend_kernel(heads, chosen, pieces, own_blocks, table, *refs):
    parts = refs[:pieces]
    bias = refs[pieces]
    outs = refs[pieces + 1 : pieces + 1 + len(chosen)]
    totals = refs[pieces + 1 + len(chosen) : pieces + 1 + 2 * len(chosen)]
    rows, sems = refs[pieces + 1 + 2 * len(chosen) :]
    own_rows = own_blocks * BLK
    copies = [
        pltpu.make_async_copy(
            parts[s], rows.at[pl.ds(s * own_rows, own_rows)], sems.at[s]
        )
        for s in range(pieces)
    ]
    for copy in copies:
        copy.start()
    for copy in copies:
        copy.wait()
    query_masks = head_masks(heads, HD**-0.5, bf16)
    out_masks = head_masks(heads, 1.0, f32)
    lane = lax.broadcasted_iota(jnp.int32, (BLK, LANES), 1)

    def step(i, carry):
        for at, s in enumerate(chosen):
            block = s * own_blocks + i
            start = pl.multiple_of(i * BLK, BLK)
            queries = stacked_heads(
                rows[pl.ds(pl.multiple_of(block * BLK, BLK), BLK), 0:PAD], query_masks
            )
            keys = key_blocks(rows, table, block, PAD)
            values = key_blocks(rows, table, block, 2 * PAD)
            scores = contract(queries, keys, (1, 1)) + bias[pl.ds(block, 1), :]
            top = jnp.max(scores, axis=-1, keepdims=True)
            weights = jnp.exp(scores - top)
            total = jnp.sum(weights, axis=-1, keepdims=True)
            mixed = contract(weights.astype(bf16), values, (1, 0)) / total
            outs[at][pl.ds(start, BLK), :] = unstacked_heads(mixed, out_masks).astype(bf16)
            log_total = top + jnp.log(total)
            kept = jnp.zeros((BLK, LANES), f32)
            for h in range(heads):
                kept = jnp.where(lane == h, log_total[h * BLK : (h + 1) * BLK], kept)
            totals[at][pl.ds(start, BLK), :] = kept
        return carry

    lax.fori_loop(0, own_blocks, step, 0)


def attend_forward(parts, table, bias, heads, chosen):
    own_rows = parts[0].shape[0]
    pieces = len(parts)
    own_blocks = own_rows // BLK
    n = len(chosen)
    vmem = pl.BlockSpec(memory_space=pltpu.VMEM)
    work = n * own_rows * KEYS * heads
    results = pl.pallas_call(
        partial(attend_kernel, heads, chosen, pieces, own_blocks),
        out_shape=[jax.ShapeDtypeStruct((own_rows, PAD), bf16)] * n
        + [jax.ShapeDtypeStruct((own_rows, LANES), f32)] * n,
        in_specs=[pl.BlockSpec(memory_space=pltpu.SMEM)]
        + [pl.BlockSpec(memory_space=pl.ANY)] * pieces
        + [vmem],
        out_specs=[vmem] * (2 * n),
        scratch_shapes=[
            pltpu.VMEM((pieces * own_rows, 3 * PAD), bf16),
            pltpu.SemaphoreType.DMA((pieces,)),
        ],
        cost_estimate=cost(12 * work * HD, 4 << 20, work),
        name="attend_forward",
    )(table, *parts, bias)
    return results[:n], results[n:]


def attend_back_kernel(heads, chosen, pieces, own_blocks, waited, carried, table, *refs):
    refs = list(refs)

    def take(count):
        taken = refs[:count]
        del refs[:count]
        return taken

    parts = take(pieces)
    ups = take(len(chosen))
    totals = take(len(chosen))
    (bias,) = take(1)
    take(waited)
    if carried:
        key_before, value_before = take(2)
        query_before = take(pieces - len(chosen))
        (small,) = take(1)
        outs = take(pieces)
        (tail,) = take(1)
        key_sum, value_sum, key_kept, value_kept, row_sums = take(5)
    else:
        outs = take(len(chosen))
        key_sum, value_sum = take(2)
    rows, up_rows, sems = refs
    own_rows = own_blocks * BLK
    copies = [
        pltpu.make_async_copy(parts[s], rows.at[pl.ds(s * own_rows, own_rows)], sems.at[s])
        for s in range(pieces)
    ] + [
        pltpu.make_async_copy(ups[at], up_rows.at[at], sems.at[pieces + at])
        for at in range(len(chosen))
    ]
    late = []
    if carried:
        late = [
            pltpu.make_async_copy(key_before, key_kept, sems.at[pieces + len(chosen)]),
            pltpu.make_async_copy(value_before, value_kept, sems.at[pieces + len(chosen) + 1]),
        ]
    for copy in copies + late:
        copy.start()
    key_sum[...] = jnp.zeros_like(key_sum)
    value_sum[...] = jnp.zeros_like(value_sum)
    for copy in copies:
        copy.wait()
    query_masks = head_masks(heads, HD**-0.5, bf16)
    up_masks = head_masks(heads, 1.0, bf16)
    out_masks = head_masks(heads, HD**-0.5, f32)

    def step(i, carry):
        for at, s in enumerate(chosen):
            block = s * own_blocks + i
            start = pl.multiple_of(i * BLK, BLK)
            here = pl.ds(pl.multiple_of(block * BLK, BLK), BLK)
            queries = stacked_heads(rows[here, 0:PAD], query_masks)
            upstream = stacked_heads(up_rows[at, pl.ds(start, BLK), :], up_masks)
            keys = key_blocks(rows, table, block, PAD)
            values = key_blocks(rows, table, block, 2 * PAD)
            kept = totals[at][pl.ds(start, BLK), :]
            log_total = jnp.concatenate([kept[:, h : h + 1] for h in range(heads)], axis=0)
            scores = contract(queries, keys, (1, 1)) + bias[pl.ds(block, 1), :]
            weights = jnp.exp(scores - log_total)
            grad_weights = contract(upstream, values, (1, 1))
            inner = jnp.sum(weights * grad_weights, axis=-1, keepdims=True)
            grad_scores = (weights * (grad_weights - inner)).astype(bf16)
            grad_query = contract(grad_scores, keys, (1, 0))
            to = outs[s] if carried else outs[at]
            to[pl.ds(start, BLK), 0:PAD] = unstacked_heads(grad_query, out_masks).astype(bf16)
            key_part = contract(grad_scores, queries, (0, 0))
            value_part = contract(weights.astype(bf16), upstream, (0, 0))
            for j in range(KEYS // BLK):
                there = pl.ds(pl.multiple_of(table[block, j] * BLK, BLK), BLK)
                key_sum[there, :] += key_part[j * BLK : (j + 1) * BLK]
                value_sum[there, :] += value_part[j * BLK : (j + 1) * BLK]
        return carry

    lax.fori_loop(0, own_blocks, step, 0)
    if not carried:
        return
    for copy in late:
        copy.wait()
    before = [s for s in range(pieces) if s not in chosen]
    for at, s in enumerate(before):
        outs[s][:, 0:PAD] = query_before[at][...]
    row_sums[...] = jnp.zeros_like(row_sums)
    for s in range(pieces):

        def finish(i, carry, s=s):
            at = pl.ds(pl.multiple_of(i * BLK, BLK), BLK)
            span = pl.ds(pl.multiple_of(s * own_rows + i * BLK, BLK), BLK)
            outs[s][at, PAD : 2 * PAD] = (key_sum[span, :] + key_kept[span, :]).astype(bf16)
            outs[s][at, 2 * PAD : 3 * PAD] = (value_sum[span, :] + value_kept[span, :]).astype(bf16)
            whole = outs[s][at, :].astype(f32)
            row_sums[...] += jnp.sum(whole.reshape(BLK // 8, 8, 3 * PAD), axis=0)
            return carry

        lax.fori_loop(0, own_blocks, finish, 0)
    slot = lax.broadcasted_iota(jnp.int32, small.shape, 0)
    whole = jnp.sum(row_sums[...], axis=0, keepdims=True)
    tail[...] = jnp.where(slot == SUM_ROW, whole, small[...]).astype(bf16)


def attend_backward(parts, ups, totals, table, bias, heads, chosen, waited=(), before=None):
    own_rows = parts[0].shape[0]
    pieces = len(parts)
    n = len(chosen)
    own_blocks = own_rows // BLK
    vmem = pl.BlockSpec(memory_space=pltpu.VMEM)
    anyspace = pl.BlockSpec(memory_space=pl.ANY)
    work = n * own_rows * KEYS * heads
    sum_shape = (pieces * own_rows, PAD)
    if before is None:
        outs = [((own_rows, PAD), bf16)] * n + [(sum_shape, f32)] * 2
        extra, extra_specs, scratch = [], [], []
    else:
        outs = [((own_rows, 3 * PAD), bf16)] * pieces + [((16, 3 * PAD), bf16)]
        extra = list(before)
        extra_specs = [anyspace] * 2 + [vmem] * (len(before) - 2)
        scratch = [pltpu.VMEM(sum_shape, f32)] * 4 + [pltpu.VMEM((8, 3 * PAD), f32)]
    return pl.pallas_call(
        partial(
            attend_back_kernel, heads, chosen, pieces, own_blocks, len(waited), before is not None
        ),
        out_shape=[jax.ShapeDtypeStruct(*out) for out in outs],
        in_specs=[pl.BlockSpec(memory_space=pltpu.SMEM)]
        + [anyspace] * (pieces + n)
        + [vmem] * (n + 1)
        + [anyspace] * len(waited)
        + extra_specs,
        out_specs=[vmem] * len(outs),
        scratch_shapes=scratch
        + [
            pltpu.VMEM((pieces * own_rows, 3 * PAD), bf16),
            pltpu.VMEM((n, own_rows, PAD), bf16),
            pltpu.SemaphoreType.DMA((pieces + n + 2,)),
        ],
        cost_estimate=cost(30 * work * HD, 12 << 20, work),
        name="attend_backward",
    )(table, *parts, *ups, *totals, bias, *waited, *extra)


VMEM_SPEC = pl.BlockSpec(memory_space=pltpu.VMEM)
ANY_SPEC = pl.BlockSpec(memory_space=pl.ANY)
SMEM_SPEC = pl.BlockSpec(memory_space=pltpu.SMEM)
COST_CUT = 64
GELU_A = 0.7978845608028654
GELU_B = 0.044715


def cost(flops, size, transcendentals=0):
    return pl.CostEstimate(
        flops=flops // COST_CUT, bytes_accessed=size // COST_CUT, transcendentals=transcendentals // COST_CUT
    )


def struct(shape, dtype):
    return jax.ShapeDtypeStruct(shape, dtype)


def row_stats(values):
    centred = values - jnp.mean(values, axis=-1, keepdims=True)
    inv_std = lax.rsqrt(jnp.mean(centred * centred, axis=-1, keepdims=True) + EPSILON)
    return centred * inv_std, inv_std


def norm_backward(upstream, scaled, inv_std, gain):
    weighted = upstream * gain
    inner = jnp.mean(weighted * scaled, axis=-1, keepdims=True)
    return inv_std * (weighted - jnp.mean(weighted, axis=-1, keepdims=True) - scaled * inner)


def column_sum(array):
    return jnp.sum(array.reshape(array.shape[0] // 8, 8, array.shape[1]), axis=0)


def rows_kernel(teams, sources, length, *refs):
    refs = list(refs)

    def take(count):
        taken = refs[:count]
        del refs[:count]
        return taken

    mixed = take(teams)
    x_in, g_in = take(2)
    weights = take(sources)
    vectors, b_up = take(2)
    b_out, g1, c1, b_down, g2, c2 = [vectors.at[k : k + 1, :] for k in range(6)]
    layer_out, low_out, grad_out, act_near, act_far, up_near, up_far = take(7)
    back_out = take(teams)
    after_out, after_turned, small = take(3)
    (
        o_buf,
        x_buf,
        g_buf,
        out_w,
        up_w,
        down_w,
        scaled_buf,
        inv_buf,
        wide_buf,
        low_buf,
        act_buf,
        slope_buf,
        last_buf,
        turned_buf,
        sums,
        up_sums,
        in_sems,
        w_sems,
        out_sems,
    ) = refs
    rows = x_in.shape[0]
    hidden = up_w.shape[2]
    tile, cut = 64, 256
    me = lax.axis_index("tensor")
    ring = sources > 1

    first = []
    for s in range(teams):
        first.append(pltpu.make_async_copy(mixed[s], o_buf.at[s], in_sems.at[s]))
    first.append(pltpu.make_async_copy(x_in, x_buf, in_sems.at[teams]))
    upstream_copy = pltpu.make_async_copy(g_in, g_buf, in_sems.at[teams + 1])
    fetched = ([], [], [])

    def fetch(kind, source, to):
        sem = w_sems.at[kind, len(fetched[kind])]
        fetched[kind].append(pltpu.make_async_copy(source, to, sem))

    wholes = (out_w, up_w, down_w)
    if ring:
        part = weights[0].shape[0]
        spans = ((2 * hidden, PAD), (0, hidden), (2 * hidden + 2 * PAD, hidden))
        for at, piece in enumerate(weights):
            row = pl.multiple_of(ring_member(RING_STEPS[at % 8]) * part, 16)
            for kind, (start, size) in enumerate(spans):
                for pair in range(2):
                    fetch(
                        kind,
                        piece.at[:, pl.ds(start + pair * size, size)],
                        wholes[kind].at[2 * pair + at // 8, pl.ds(row, part), :],
                    )
    else:
        spans = ((hidden, PAD), (0, hidden), (hidden + PAD, hidden))
        for kind, (start, size) in enumerate(spans):
            for s in range(teams):
                fetch(kind, weights[0].at[me ^ s, :, pl.ds(start, size)], wholes[kind].at[s])
    for copy in first + fetched[0] + fetched[1] + fetched[2] + [upstream_copy]:
        copy.start()
    sums[...] = jnp.zeros_like(sums)
    up_sums[...] = jnp.zeros_like(up_sums)
    leaving = []

    def leave(ref, to):
        copy = pltpu.make_async_copy(ref, to, out_sems.at[len(leaving)])
        copy.start()
        leaving.append(copy)

    def leave_turned(k, source, to):
        for n in range(D // LANES):
            span = slice(n * LANES, (n + 1) * LANES)
            turned_buf[k, span, :] = source[:, span].T
        bits, far, part, _ = to.shape
        here = lax.axis_index("dp")
        for b in range(bits):
            for z in range(far):
                row = (here ^ (2 * z + b)) * part if ring else 0
                leave(turned_buf.at[k, pl.ds(pl.multiple_of(row, 16), part), :], to.at[b, z])

    def tiles(body):
        def step(i, carry):
            body(i, pl.ds(pl.multiple_of(i * tile, tile), tile))
            return carry

        lax.fori_loop(0, rows // tile, step, 0)

    for copy in first + fetched[0]:
        copy.wait()
    for n in range(D // cut):
        cols = slice(n * cut, (n + 1) * cut)
        total = contract(o_buf[0], out_w[0, cols, :], (1, 1))
        for s in range(1, teams):
            total = total + contract(o_buf[s], out_w[s, cols, :], (1, 1))
        wide_buf[:, cols] = total

    def first_norm(i, at):
        after = x_buf[at, :].astype(f32) + wide_buf[at, :] + b_out[...]
        scaled, inv_std = row_stats(after)
        scaled_buf[at, :] = scaled
        inv_buf[at, :] = jnp.broadcast_to(inv_std, (tile, LANES))
        low_buf[at, :] = (scaled * g1[...] + c1[...]).astype(bf16)

    tiles(first_norm)
    leave_turned(0, low_buf, low_out)
    for copy in fetched[1]:
        copy.wait()

    def up_step(s, carry):
        bias = b_up[pl.ds(s ^ me, 1), :]
        for c in range(hidden // cut):
            cols = slice(c * cut, (c + 1) * cut)
            u = contract(low_buf[...], up_w[s, :, cols], (1, 0)) + bias[:, cols]
            square = u * u
            t = jnp.tanh(u * (GELU_A + GELU_A * GELU_B * square))
            half = 0.5 + 0.5 * t
            act_buf[s, :, cols] = (u * half).astype(bf16)
            slope_buf[s, :, cols] = (
                half + (0.5 * u) * (1.0 - t * t) * (GELU_A + 3.0 * GELU_A * GELU_B * square)
            ).astype(bf16)
        return carry

    lax.fori_loop(0, teams, up_step, 0)
    for s in range(teams):
        leave(act_buf.at[s], (act_far if s % 2 else act_near).at[s // 2])
    for copy in fetched[2]:
        copy.wait()
    upstream_copy.wait()
    for n in range(D // cut):
        cols = slice(n * cut, (n + 1) * cut)
        total = contract(act_buf[0], down_w[0, cols, :], (1, 1))
        for s in range(1, teams):
            total = total + contract(act_buf[s], down_w[s, cols, :], (1, 1))
        wide_buf[:, cols] = total
    start = me * rows
    seq = start // LMAX
    live = length[seq] - (start - seq * LMAX)

    def second_norm(i, at):
        z = (scaled_buf[at, :] * g1[...] + c1[...]) + wide_buf[at, :] + b_down[...]
        scaled, inv_std = row_stats(z)
        x_buf[at, :] = (scaled * g2[...] + c2[...]).astype(bf16)
        row = lax.broadcasted_iota(jnp.int32, (tile, D), 0) + i * tile
        upstream = jnp.where(row < live, g_buf[at, :].astype(f32), 0.0)
        grad = norm_backward(upstream, scaled, inv_std, g2[...]).astype(bf16)
        g_buf[at, :] = grad
        sums[0:8, :] += column_sum(upstream * scaled)
        sums[8:16, :] += column_sum(upstream)
        sums[16:24, :] += column_sum(grad.astype(f32))

    tiles(second_norm)
    leave(x_buf, layer_out)
    leave_turned(1, g_buf, grad_out)

    def down_back(s, carry):
        for c in range(hidden // cut):
            cols = slice(c * cut, (c + 1) * cut)
            g = contract(g_buf[...], down_w[s, :, cols], (1, 0))
            g = (g * slope_buf[s, :, cols].astype(f32)).astype(bf16)
            slope_buf[s, :, cols] = g
            up_sums[pl.ds(pl.multiple_of(s * 8, 8), 8), cols] = column_sum(g.astype(f32))
        return carry

    lax.fori_loop(0, teams, down_back, 0)
    for s in range(teams):
        leave(slope_buf.at[s], (up_far if s % 2 else up_near).at[s // 2])
    for n in range(D // cut):
        cols = slice(n * cut, (n + 1) * cut)
        total = contract(slope_buf[0], up_w[0, cols, :], (1, 1))
        for s in range(1, teams):
            total = total + contract(slope_buf[s], up_w[s, cols, :], (1, 1))
        wide_buf[:, cols] = total

    def first_back(i, at):
        upstream = g_buf[at, :].astype(f32) + wide_buf[at, :]
        scaled = scaled_buf[at, :]
        grad = norm_backward(upstream, scaled, inv_buf[at, :][:, :1], g1[...]).astype(bf16)
        last_buf[at, :] = grad
        sums[24:32, :] += column_sum(upstream * scaled)
        sums[32:40, :] += column_sum(upstream)
        sums[40:48, :] += column_sum(grad.astype(f32))

    tiles(first_back)
    leave(last_buf, after_out)
    leave_turned(2, last_buf, after_turned)
    for s in (2, 3, 1, 0):
        o_buf[s] = contract(last_buf[...], out_w[s], (1, 0)).astype(bf16)
        leave(o_buf.at[s], back_out[s])
    small[...] = jnp.zeros_like(small)
    for k in range(6):
        small[k : k + 1, :] = jnp.sum(sums[8 * k : 8 * k + 8, :], axis=0, keepdims=True)
    for s in range(teams):
        small[pl.ds(6 + (s ^ me), 1), :] = jnp.sum(
            up_sums[8 * s : 8 * s + 8, :], axis=0, keepdims=True
        )
    for copy in leaving:
        copy.wait()


def layer_rows(mixed, hidden_in, grad_out, weights, vectors, lengths):
    teams = len(mixed)
    rows = hidden_in.shape[0]
    rows_of, b_up = vectors
    hidden = b_up.shape[1]
    half = teams // 2
    low = struct((rows, D), bf16)
    pair = struct((half, rows, hidden), bf16)
    ring = len(weights) > 1
    turned = struct((2, 4, D // 8, rows) if ring else (1, 1, D, rows), bf16)
    return pl.pallas_call(
        partial(rows_kernel, teams, len(weights)),
        out_shape=[low, turned, turned, pair, pair, pair, pair]
        + [struct((rows, PAD), bf16)] * teams
        + [low, turned, struct((16, D), f32)],
        in_specs=[SMEM_SPEC] + [ANY_SPEC] * (teams + 2 + len(weights)) + [VMEM_SPEC] * 2,
        out_specs=[ANY_SPEC] * (9 + teams) + [VMEM_SPEC],
        scratch_shapes=[
            pltpu.VMEM((teams, rows, PAD), bf16),
            pltpu.VMEM((rows, D), bf16),
            pltpu.VMEM((rows, D), bf16),
            pltpu.VMEM((teams, D, PAD), bf16),
            pltpu.VMEM((teams, D, hidden), bf16),
            pltpu.VMEM((teams, D, hidden), bf16),
            pltpu.VMEM((rows, D), f32),
            pltpu.VMEM((rows, LANES), f32),
            pltpu.VMEM((rows, D), f32),
            pltpu.VMEM((rows, D), bf16),
            pltpu.VMEM((teams, rows, hidden), bf16),
            pltpu.VMEM((teams, rows, hidden), bf16),
            pltpu.VMEM((rows, D), bf16),
            pltpu.VMEM((3, D, rows), bf16),
            pltpu.VMEM((48, D), f32),
            pltpu.VMEM((8 * teams, hidden), f32),
            pltpu.SemaphoreType.DMA((teams + 2,)),
            pltpu.SemaphoreType.DMA((3, 32)),
            pltpu.SemaphoreType.DMA((2 + 3 * teams + 24,)),
        ],
        cost_estimate=cost(8 * rows * D * (teams * hidden) + 4 * rows * D * teams * PAD, 24 << 20),
        compiler_params=pltpu.CompilerParams(vmem_limit_bytes=60 << 20),
        name="layer_rows",
    )(
        lengths,
        *mixed,
        hidden_in,
        grad_out,
        *weights,
        rows_of,
        b_up,
    )


def row_dot(groups, cut_by=None, waited=(), tail=None):
    sets = len(groups[0][0])
    bits, far, part, rows = groups[0][0][0].shape
    count = groups[0][1][0].shape[0]
    cut = 256
    lows = [0]
    for _, rights in groups:
        lows.append(lows[-1] + rights[0].shape[2] // cut)
    high = bits * far * part
    below = 0 if tail is None else tail.shape[0]
    cuts = 1 if cut_by is None else 2

    def kernel(*refs):
        refs = list(refs)
        ins = [[refs.pop(0) for _ in range(sets)] for _ in groups]
        others = [[refs.pop(0) for _ in range(sets)] for _ in groups]
        if below:
            tail_ref = refs.pop(0)
        outs = refs[len(waited) :]
        j = pl.program_id(0)
        for g in range(len(groups)):

            @pl.when((j >= lows[g]) & (j < lows[g + 1]))
            def _(g=g):
                for i in range(count):
                    total = contract(ins[g][0][...].reshape(high, rows), others[g][0][i], (1, 0))
                    for k in range(1, sets):
                        total = total + contract(
                            ins[g][k][...].reshape(high, rows), others[g][k][i], (1, 0)
                        )
                    total = total.astype(bf16).reshape(bits, far, part, cut)
                    for b in range(bits):
                        if cut_by == "bits":
                            to = outs[b].at[i, 0]
                        elif cut_by == "rights":
                            to = outs[i].at[0, b]
                        else:
                            to = outs[0].at[i, b]
                        if below:
                            to[:, :part, :] = total[b]
                            to[:, part:, :] = jnp.broadcast_to(
                                tail_ref[...][None], (far, below, cut)
                            )
                        else:
                            to[...] = total[b]

    def column(g):
        return lambda j: (0, 0, jnp.clip(j - lows[g], 0, lows[g + 1] - lows[g] - 1))

    specs, arrays = [], []
    for lefts, _ in groups:
        specs += [pl.BlockSpec((bits, far, part, rows), lambda j: (0, 0, 0, 0))] * sets
        arrays += list(lefts)
    for g, (_, rights) in enumerate(groups):
        specs += [pl.BlockSpec((count, rows, cut), column(g))] * sets
        arrays += list(rights)
    if below:
        specs.append(pl.BlockSpec((below, cut), lambda j: (0, j)))
        arrays.append(tail)
    width = lows[-1] * cut
    lead = (count // 2 if cut_by == "rights" else count, bits // 2 if cut_by == "bits" else bits)
    return pl.pallas_call(
        kernel,
        grid=(lows[-1],),
        out_shape=[struct((*lead, far, part + below, width), bf16)] * cuts,
        in_specs=specs + [ANY_SPEC] * len(waited),
        out_specs=[
            pl.BlockSpec((*lead, far, part + below, cut), lambda j: (0, 0, 0, 0, j))
        ]
        * cuts,
        cost_estimate=cost(2 * sets * rows * high * count * width, 8 << 20),
        name="row_dot",
    )(*arrays, *waited)


def plus(a, b, waited=(), cuts=1, dtype=bf16):
    lead = a.shape[0] // cuts

    def kernel(a_ref, b_ref, *refs):
        for k in range(cuts):
            span = slice(k * lead, (k + 1) * lead)
            refs[len(waited) + k][...] = (
                a_ref[span].astype(f32) + b_ref[span].astype(f32)
            ).astype(dtype)

    return pl.pallas_call(
        kernel,
        out_shape=[struct((lead, *a.shape[1:]), dtype)] * cuts,
        in_specs=[VMEM_SPEC] * 2 + [ANY_SPEC] * len(waited),
        out_specs=[VMEM_SPEC] * cuts,
        cost_estimate=cost(a.size, 6 * a.size),
        name="plus",
    )(a, b, *waited)


def joined_sums(pairs, waited=()):
    rows = pairs[0][0].shape[1]
    widths = [a.shape[2] for a, _ in pairs]
    count = 2 * len(pairs)

    def kernel(*refs):
        outs = refs[count + len(waited) :]
        for z in range(4):
            at = 0
            for k, width in enumerate(widths):
                outs[z][:, at : at + width] = (
                    refs[2 * k][z].astype(f32) + refs[2 * k + 1][z].astype(f32)
                ).astype(bf16)
                at += width

    return pl.pallas_call(
        kernel,
        out_shape=[struct((rows, sum(widths)), bf16)] * 4,
        in_specs=[VMEM_SPEC] * count + [ANY_SPEC] * len(waited),
        out_specs=[VMEM_SPEC] * 4,
        cost_estimate=cost(rows * sum(widths) * 4, rows * sum(widths) * 24),
        name="joined_sums",
    )(*[array for pair in pairs for array in pair], *waited)


def held(array, waited):
    def kernel(a_ref, *refs):
        refs[-1][...] = a_ref[...]

    return pl.pallas_call(
        kernel,
        out_shape=struct(array.shape, array.dtype),
        in_specs=[VMEM_SPEC] + [ANY_SPEC] * len(waited),
        out_specs=VMEM_SPEC,
        cost_estimate=cost(array.size, 8 * array.size),
        name="held",
    )(array, *waited)


def spread(grads, weight, added=None, after=None, waited=()):
    rows = grads[0].shape[0]

    def kernel(first, second, w, *refs):
        if added is None:
            out = refs[-1]
            out[0] = contract(first[...], w[...], (1, 1)).astype(bf16)
            out[1] = contract(second[...], w[...], (1, 1)).astype(bf16)
            return
        plus_ref, after_ref = refs[:2]
        away, here = refs[-2:]
        away[...] = (contract(first[...], w[...], (1, 1)) + plus_ref[0].astype(f32)).astype(bf16)
        here[...] = contract(second[...], w[...], (1, 1)) + (
            plus_ref[1].astype(f32) + after_ref[...].astype(f32)
        )

    if added is None:
        outs, more = struct((2, rows, D), bf16), []
    else:
        outs, more = [struct((rows, D), bf16), struct((rows, D), f32)], [added, after]
    return pl.pallas_call(
        kernel,
        out_shape=outs,
        in_specs=[VMEM_SPEC] * (3 + len(more)) + [ANY_SPEC] * len(waited),
        out_specs=VMEM_SPEC if added is None else [VMEM_SPEC] * 2,
        cost_estimate=cost(4 * rows * D * weight.shape[1], 5 << 20),
        name="spread",
    )(*grads, weight, *more, *waited)


def pack_weights(w_query, w_key, w_value, w_up, w_out, w_down):
    rows, width = w_query.shape
    hidden = w_up.shape[1]

    def kernel(q, k, v, up, out, down, qkv, own):
        for at, ref in enumerate((q, k, v)):
            qkv[:, at * PAD : (at + 1) * PAD] = jnp.zeros((rows, PAD), bf16)
            qkv[:, at * PAD : at * PAD + width] = ref[...]
        own[:, :hidden] = up[...]
        own[:, hidden : hidden + PAD] = jnp.zeros((rows, PAD), bf16)
        own[:, hidden : hidden + width] = out[...].T
        own[:, hidden + PAD :] = down[...].T

    return pl.pallas_call(
        kernel,
        out_shape=[
            struct((rows, 3 * PAD), bf16),
            struct((rows, 2 * hidden + PAD), bf16),
        ],
        in_specs=[VMEM_SPEC] * 6,
        out_specs=[VMEM_SPEC] * 2,
        cost_estimate=cost(rows * hidden, 4 << 20),
        name="pack_weights",
    )(w_query, w_key, w_value, w_up, w_out, w_down)


def pair_weights(own, beyond, hidden):
    rows, width = own.shape
    starts = (0, hidden, hidden + PAD, width)

    def kernel(a, b, out):
        for at, end in zip(starts, starts[1:]):
            out[:, 2 * at : at + end] = a[:, at:end]
            out[:, at + end : 2 * end] = b[:, at:end]

    return pl.pallas_call(
        kernel,
        out_shape=struct((rows, 2 * width), bf16),
        in_specs=[VMEM_SPEC] * 2,
        out_specs=VMEM_SPEC,
        cost_estimate=cost(rows * width, 4 * rows * width),
        name="pair_weights",
    )(own, beyond)


def project_in(xs, weights, bias):
    rows = xs[0].shape[0]
    pieces = len(xs)
    sources = len(weights)
    ordered = sources > 1
    bits, far = (2, 4) if ordered else (1, 1)
    part = D // (bits * far)
    wide = weights[0].shape[1]

    def kernel(*refs):
        refs = list(refs)
        ins = [refs.pop(0) for _ in range(pieces)]
        shards = [refs.pop(0) for _ in range(sources)]
        b = refs.pop(0)
        outs = [refs.pop(0) for _ in range(pieces)]
        turned_outs = [refs.pop(0) for _ in range(pieces)]
        whole_out, x_buf, w, out_buf, turned, sems, w_sems, out_sems = refs
        here = lax.axis_index("dp") if ordered else 0
        copies = [
            pltpu.make_async_copy(ins[s], x_buf.at[s], sems.at[s]) for s in range(pieces)
        ]
        fetched = []
        for at in range(sources):
            row = ring_member(RING_STEPS[at]) * part if ordered else 0
            fetched.append(
                pltpu.make_async_copy(
                    shards[at],
                    w.at[pl.ds(pl.multiple_of(row, 16), shards[at].shape[0]), :],
                    w_sems.at[at],
                )
            )
        for copy in fetched + copies:
            copy.start()
        for copy in fetched:
            copy.wait()
        leaving = []

        def leave(ref, to):
            copy = pltpu.make_async_copy(ref, to, out_sems.at[len(leaving)])
            copy.start()
            leaving.append(copy)

        leave(w, whole_out)
        for s in range(pieces):
            copies[s].wait()
            for c in range(0, wide, PAD):
                cols = slice(c, c + PAD)
                out_buf[s, :, cols] = (
                    contract(x_buf[s], w[:, cols], (1, 0)) + b[:, cols]
                ).astype(bf16)
            leave(out_buf.at[s], outs[s])
            for n in range(D // LANES):
                span = slice(n * LANES, (n + 1) * LANES)
                turned[s, span, :] = x_buf[s, :, span].T
            for k in range(bits):
                for z in range(far):
                    row = (here ^ (2 * z + k)) * part if ordered else 0
                    leave(
                        turned.at[s, pl.ds(pl.multiple_of(row, 16), part), :],
                        turned_outs[s].at[k, z],
                    )
        for copy in leaving:
            copy.wait()

    results = pl.pallas_call(
        kernel,
        out_shape=[struct((rows, wide), bf16)] * pieces
        + [struct((bits, far, part, rows), bf16)] * pieces
        + [struct((D, wide), bf16)],
        in_specs=[ANY_SPEC] * (pieces + sources) + [VMEM_SPEC],
        out_specs=[ANY_SPEC] * (2 * pieces + 1),
        scratch_shapes=[
            pltpu.VMEM((pieces, rows, D), bf16),
            pltpu.VMEM((D, wide), bf16),
            pltpu.VMEM((pieces, rows, wide), bf16),
            pltpu.VMEM((pieces, D, rows), bf16),
            pltpu.SemaphoreType.DMA((pieces,)),
            pltpu.SemaphoreType.DMA((sources,)),
            pltpu.SemaphoreType.DMA((1 + pieces * (1 + bits * far),)),
        ],
        cost_estimate=cost(2 * pieces * rows * D * wide, 12 << 20),
        name="project_in",
    )(*xs, *weights, bias)
    return results[:pieces], results[pieces : 2 * pieces], results[2 * pieces]


def padded(array):
    return jnp.pad(array, ((0, 0), (0, PAD - array.shape[1])))


def dot(a, b, dims=(1, 0)):
    return contract(a, b, dims)


def per_device(
    hidden_in,
    grad_out,
    w_query,
    b_query,
    w_key,
    w_value,
    b_value,
    w_out,
    b_out,
    gain_one,
    shift_one,
    w_up,
    b_up,
    w_down,
    b_down,
    gain_two,
    shift_two,
    lengths,
    global_raw,
    random_raw,
):
    own_rows = hidden_in.shape[0]
    me = lax.axis_index("tensor")
    teams = lax.axis_size("tensor")
    members = lax.axis_size("dp")
    width = w_query.shape[1]
    heads = width // HD
    hidden = w_up.shape[1]

    table, bias = block_tables(lengths, global_raw, random_raw, own_rows // BLK, teams)

    x2 = swap(hidden_in, 2)
    x1 = swap(hidden_in, 1)
    x3 = swap(x2, 1)
    x_parts = [hidden_in, x1, x2, x3]

    qkv_b = jnp.concatenate(
        [jnp.pad(b_query, (0, PAD - width)), jnp.zeros((PAD,), f32), jnp.pad(b_value, (0, PAD - width))]
    )
    halved = members == 8
    if halved:
        qkv_shard, own = pack_weights(w_query, w_key, w_value, w_up, w_out, w_down)
        shard = pair_weights(own, swap(own, 2), hidden)
        qkv_pieces = ring_pieces(qkv_shard)
    else:
        qkv_shard = jnp.concatenate([padded(w_query), padded(w_key), padded(w_value)], axis=1)
        qkv_pieces = [lax.all_gather(qkv_shard, "dp", axis=0, tiled=True)]
        shard = jnp.concatenate([w_up, padded(w_out.T), w_down.T], axis=1)
        weights = lax.all_gather(shard, ("dp", "tensor"), axis=0, tiled=False)
        weights = jnp.swapaxes(weights.reshape(members, teams, *shard.shape), 0, 1)
        weights = [weights.reshape(teams, D, shard.shape[1])]

    qkv, x_turned, qkv_w = project_in(x_parts, qkv_pieces, qkv_b[None])
    (o2, o3), (t2, t3) = attend_forward(qkv, table, bias, heads, (2, 3))
    r2 = swap(o2, 2)
    r3 = swap(o3, 3)
    (o0, o1), (t0, t1) = attend_forward(qkv, table, bias, heads, (0, 1))
    r1 = swap(o1, 1)
    if halved:

        def gate(step, ahead, behind):
            waited = {3: qkv[0], 4: o2}.get(step)
            if waited is None:
                return ahead, behind
            ahead = held(ahead, (waited,))
            if step < 4:
                behind = held(behind, (waited,))
            return ahead, behind

        weights = ring_pieces(shard, gate)
        weights = weights + [swap(piece, 1) for piece in weights]

    results = layer_rows(
        [o0, r1, r2, r3],
        hidden_in,
        grad_out,
        weights,
        (
            jnp.stack([b_out, gain_one, shift_one, b_down, gain_two, shift_two]),
            b_up.reshape(teams, hidden),
        ),
        lengths,
    )
    layer_out, low, grad_low, act_near, act_far, up_near, up_far = results[:7]
    backs = results[7 : 7 + teams]
    after_low, after_turned, small = results[7 + teams :]
    ups = [backs[0]] + [swap(backs[s], s) for s in range(1, teams)]
    small = small + swap(small, 1)
    small = small + swap(small, 2)

    down_group = ([grad_low, swap(grad_low, 1)], [act_near, swap(act_far, 1)])
    up_group = ([low, swap(low, 1)], [up_near, swap(up_far, 1)])
    out_group = (
        [after_turned, swap(after_turned, 1)],
        [jnp.stack([o0, r2]), jnp.stack([o1, swap(r3, 1)])],
    )
    if halved:
        up_kept, up_gone = row_dot([up_group, out_group], "bits")
        up_away = dp_swap(up_gone, 1)
        down_kept, down_gone = row_dot([down_group], "rights", (up_gone, ups[2], ups[3], small))
        down_away = swap(down_gone, 2)
        waited = (down_gone,)
    else:
        down_sums = row_dot([down_group])[0].reshape(2, D, -1)
        up_sums = row_dot([up_group, out_group])[0].reshape(2, D, -1)
        waited = ()

    totals = [t0, t1, t2, t3]
    before = attend_backward(qkv, ups[:2], totals[:2], table, bias, heads, (0, 1), waited)
    if halved:
        down_here, down_next = plus(down_kept[0], down_away[0], (before[0],), 2)
        down_away = dp_swap(down_next, 1)
        up_here, up_next = plus(up_kept, up_away, (before[0],), 2)
        up_away = swap(up_next, 2)
        waited = (down_next, up_next)
    results = attend_backward(
        qkv,
        ups[2:],
        totals[2:],
        table,
        bias,
        heads,
        (2, 3),
        waited,
        (before[2], before[3], before[0], before[1], small),
    )
    grads, tail = results[:4], results[4]
    waited = ()
    if halved:
        sums = joined_sums(
            [(down_here[0], down_away[0]), (up_here[0, 0], up_away[0, 0])], (grads[0],)
        )
        waited = (sums[0],)
    parts = spread([grads[3], grads[1]], qkv_w, waited=waited)
    spread_away = swap(parts, 1)
    qkv_group = (x_turned, [g[None] for g in grads])
    if halved:
        kept, gone = row_dot([qkv_group], "bits", (parts,), tail)
        away = dp_swap(gone, 1)
        beyond, here = spread([grads[2], grads[0]], qkv_w, spread_away, after_low, (kept,))
        total = sums[0].astype(f32)
        for z in range(1, 4):
            total = total + dp_swap(sums[z], 2 * z).astype(f32)
        down_part, up_part = total[:, :hidden], total[:, hidden:]
        blocks = joined_sums([(kept[0, 0], away[0, 0])], (beyond,))
        beyond = swap(beyond, 2)
        qkv_part = blocks[0].astype(f32)
        for z in range(1, 4):
            qkv_part = qkv_part + dp_swap(blocks[z], 2 * z).astype(f32)
        qkv_part, small = qkv_part[:-16], qkv_part[-16:]
    else:
        blocks = row_dot([qkv_group])[0].reshape(D, -1)
        qkv_part = dp_scatter_sum(blocks)
        small = lax.psum(tail.astype(f32), "dp")
        beyond, here = spread([grads[2], grads[0]], qkv_w, spread_away, after_low)
        beyond = swap(beyond, 2)
        down_part = dp_scatter_sum(down_sums[0] + swap(down_sums[1], 2))
        up_part = dp_scatter_sum(up_sums[0] + swap(up_sums[1], 2))
    grad_in = here + beyond.astype(f32)

    bias_row = small[SUM_ROW]
    return (
        layer_out,
        grad_in,
        qkv_part[:, :width],
        bias_row[:width],
        qkv_part[:, PAD : PAD + width],
        qkv_part[:, 2 * PAD : 2 * PAD + width],
        bias_row[2 * PAD : 2 * PAD + width],
        up_part[:, hidden : hidden + width].T,
        small[5],
        small[3],
        small[4],
        up_part[:, :hidden],
        jnp.take(small[6 : 6 + teams], me, axis=0),
        down_part.T,
        small[2],
        small[0],
        small[1],
    )


def solution(mesh):
    in_specs = (
        P(("dp", "tensor"), None),
        P(("dp", "tensor"), None),
        P("dp", "tensor"),
        P("tensor"),
        P("dp", "tensor"),
        P("dp", "tensor"),
        P("tensor"),
        P("tensor", "dp"),
        P(),
        P(),
        P(),
        P("dp", "tensor"),
        P(),
        P("tensor", "dp"),
        P(),
        P(),
        P(),
        P("dp"),
        P("dp", None),
        P("dp", None, None),
    )
    out_specs = (
        P(("dp", "tensor"), None),
        P(("dp", "tensor"), None),
        P("dp", "tensor"),
        P("tensor"),
        P("dp", "tensor"),
        P("dp", "tensor"),
        P("tensor"),
        P("tensor", "dp"),
        P(),
        P(),
        P(),
        P("dp", "tensor"),
        P("tensor"),
        P("tensor", "dp"),
        P(),
        P(),
        P(),
    )
    return jax.shard_map(
        per_device, mesh=mesh, in_specs=in_specs, out_specs=out_specs, check_vma=False
    )
```

```python
from functools import partial

import jax
import jax.numpy as jnp
from jax import lax
from jax.experimental import pallas as pl
from jax.experimental.pallas import tpu as pltpu
from jax.sharding import PartitionSpec as P

D = 768
HD = 64
FF = 3072
BLK = 64
GLOB = 2
RAND = 3
LMAX = 2048
NB = 32
KEYS = (3 + GLOB + RAND) * BLK
PAD = 256
LANES = 128
SUM_ROW = 10
GATE = 6

masked_score = -1e30
EPSILON = 1e-12
f32 = jnp.float32
bf16 = jnp.bfloat16


def swap(array, bit):
    size = lax.axis_size("tensor")
    return lax.ppermute(array, "tensor", [(t, t ^ bit) for t in range(size)])


def dp_swap(array, bit):
    size = lax.axis_size("dp")
    return lax.ppermute(array, "dp", [(t, t ^ bit) for t in range(size)])


def ring_order(size):
    return list(range(0, size, 2)) + list(range(size - 1, 0, -2))


def ring_member(steps):
    size = lax.axis_size("dp")
    me = lax.axis_index("dp")
    place = jnp.where(me % 2 == 0, me // 2, size - 1 - me // 2)
    place = (place + steps + size) % size
    return jnp.where(place < size // 2, 2 * place, 2 * (size - 1 - place) + 1)


def ring_send(array, step):
    size = lax.axis_size("dp")
    order = ring_order(size)
    return lax.ppermute(
        array, "dp", [(order[i], order[(i + step) % size]) for i in range(size)]
    )


RING_STEPS = (0, -1, 1, -2, 2, -3, 3, -4)


def ring_pieces(shard):
    pieces = [shard]
    ahead, behind = shard, shard
    for step in range(1, 5):
        ahead = ring_send(ahead, 1)
        pieces.append(ahead)
        if step < 4:
            behind = ring_send(behind, -1)
            pieces.append(behind)
    return pieces


def far_exchange(blocks):
    groups = [[2 * f + n for f in range(4)] for n in range(2)]
    return lax.all_to_all(blocks, "dp", 0, 0, axis_index_groups=groups, tiled=True)


def dp_scatter_sum(sums):
    size = lax.axis_size("dp")
    if size != 8:
        return lax.psum_scatter(sums, "dp", scatter_dimension=0, tiled=True).astype(f32)
    blocks = lax.all_to_all(sums.reshape(size, -1, sums.shape[1]), "dp", 0, 0, tiled=True)
    return jnp.sum(blocks.astype(f32), axis=0)


def sum_over(vector, dp_only=False):
    if not dp_only:
        bit = 1
        while bit < lax.axis_size("tensor"):
            vector = vector + swap(vector, bit)
            bit *= 2
    bit = 1
    while bit < lax.axis_size("dp"):
        vector = vector + dp_swap(vector, bit)
        bit *= 2
    return vector


def block_tables(lengths, global_raw, random_raw, own_blocks, pieces):
    count = own_blocks * pieces

    def kernel(length_ref, global_ref, random_ref, table, bias):
        me = lax.axis_index("tensor")
        lane = lax.broadcasted_iota(jnp.int32, (1, KEYS), 1)
        slot = lane // BLK
        within = lane % BLK
        wide = lax.broadcasted_iota(jnp.int32, (own_blocks, LANES), 1)
        row = lax.broadcasted_iota(jnp.int32, (own_blocks, 1), 0)
        for s in range(pieces):
            first = (s ^ me) * own_blocks
            seq = first // NB
            start = first - seq * NB
            length = length_ref[seq]
            live = (length + BLK - 1) // BLK
            raw = random_ref[seq, pl.ds(pl.multiple_of(start, 8), own_blocks), :]
            rest = raw - live * jnp.floor(raw.astype(f32) / live.astype(f32)).astype(jnp.int32)
            rest = jnp.where(rest < 0, rest + live, rest)
            rest = jnp.where(rest >= live, rest - live, rest)
            block = row + start
            ids = [jnp.maximum(block - 1, 0), block, jnp.minimum(block + 1, NB - 1)]
            ids += [jnp.full((own_blocks, 1), lax.rem(global_ref[seq, j], live)) for j in range(GLOB)]
            ids += [rest[:, r : r + 1] for r in range(RAND)]
            spread_ids = jnp.zeros((own_blocks, KEYS), jnp.int32)
            packed = jnp.zeros((own_blocks, LANES), jnp.int32)
            for j, own in enumerate(ids):
                spread_ids = jnp.where(slot == j, own, spread_ids)
                there = own + seq * NB
                there = ((there // own_blocks) ^ me) * own_blocks + there % own_blocks
                packed = jnp.where(wide == j, there, packed)
            table[s * own_blocks : (s + 1) * own_blocks, :] = packed
            lost = (spread_ids * BLK + within) >= length
            lost = lost | ((slot == 0) & (block == 0)) | ((slot == 2) & (block == NB - 1))
            bias[s * own_blocks : (s + 1) * own_blocks, :] = jnp.where(lost, masked_score, 0.0).astype(f32)

    smem = pl.BlockSpec(memory_space=pltpu.SMEM)
    vmem = pl.BlockSpec(memory_space=pltpu.VMEM)
    return pl.pallas_call(
        kernel,
        out_shape=[
            jax.ShapeDtypeStruct((count, LANES), jnp.int32),
            jax.ShapeDtypeStruct((count, KEYS), f32),
        ],
        in_specs=[smem, smem, vmem],
        out_specs=[vmem, vmem],
        cost_estimate=cost(count * KEYS * 16, count * KEYS * 4),
        name="block_tables",
    )(lengths, global_raw, random_raw)


def head_masks(heads, scale, dtype):
    lane = lax.broadcasted_iota(jnp.int32, (1, PAD), 1)
    return [
        jnp.where((lane >= h * HD) & (lane < (h + 1) * HD), scale, 0.0).astype(dtype)
        for h in range(heads)
    ]


def stacked_heads(rows, masks):
    return jnp.concatenate([rows * mask for mask in masks], axis=0)


def unstacked_heads(stacked, masks):
    rows = stacked.shape[0] // len(masks)
    total = stacked[:rows] * masks[0]
    for h in range(1, len(masks)):
        total = total + stacked[h * rows : (h + 1) * rows] * masks[h]
    return total


def key_blocks(ref, table, block, column):
    return jnp.concatenate(
        [
            ref[pl.ds(pl.multiple_of(table[block, j] * BLK, BLK), BLK), column : column + PAD]
            for j in range(KEYS // BLK)
        ],
        axis=0,
    )


def contract(a, b, dims):
    return lax.dot_general(a, b, ((dims[:1], dims[1:]), ((), ())), preferred_element_type=f32)


def attend_kernel(heads, chosen, pieces, own_blocks, table, *refs):
    parts = refs[:pieces]
    bias = refs[pieces]
    out = refs[pieces + 1]
    totals = refs[pieces + 2 : pieces + 2 + len(chosen)]
    rows, sems = refs[pieces + 2 + len(chosen) :]
    own_rows = own_blocks * BLK
    copies = [
        pltpu.make_async_copy(
            parts[s], rows.at[pl.ds(s * own_rows, own_rows)], sems.at[s]
        )
        for s in range(pieces)
    ]
    for copy in copies:
        copy.start()
    for copy in copies:
        copy.wait()
    query_masks = head_masks(heads, HD**-0.5, bf16)
    out_masks = head_masks(heads, 1.0, f32)
    lane = lax.broadcasted_iota(jnp.int32, (BLK, LANES), 1)

    def step(i, carry):
        for at, s in enumerate(chosen):
            block = s * own_blocks + i
            start = pl.multiple_of(i * BLK, BLK)
            queries = stacked_heads(
                rows[pl.ds(pl.multiple_of(block * BLK, BLK), BLK), 0:PAD], query_masks
            )
            keys = key_blocks(rows, table, block, PAD)
            values = key_blocks(rows, table, block, 2 * PAD)
            scores = contract(queries, keys, (1, 1)) + bias[pl.ds(block, 1), :]
            top = jnp.max(scores, axis=-1, keepdims=True)
            weights = jnp.exp(scores - top)
            total = jnp.sum(weights, axis=-1, keepdims=True)
            mixed = contract(weights.astype(bf16), values, (1, 0)) / total
            out[at, pl.ds(start, BLK), :] = unstacked_heads(mixed, out_masks).astype(bf16)
            log_total = top + jnp.log(total)
            kept = jnp.zeros((BLK, LANES), f32)
            for h in range(heads):
                kept = jnp.where(lane == h, log_total[h * BLK : (h + 1) * BLK], kept)
            totals[at][pl.ds(start, BLK), :] = kept
        return carry

    lax.fori_loop(0, own_blocks, step, 0)


def attend_forward(parts, table, bias, heads, chosen):
    own_rows = parts[0].shape[0]
    pieces = len(parts)
    own_blocks = own_rows // BLK
    n = len(chosen)
    vmem = pl.BlockSpec(memory_space=pltpu.VMEM)
    work = n * own_rows * KEYS * heads
    results = pl.pallas_call(
        partial(attend_kernel, heads, chosen, pieces, own_blocks),
        out_shape=[jax.ShapeDtypeStruct((n, own_rows, PAD), bf16)]
        + [jax.ShapeDtypeStruct((own_rows, LANES), f32)] * n,
        in_specs=[pl.BlockSpec(memory_space=pltpu.SMEM)]
        + [pl.BlockSpec(memory_space=pl.ANY)] * pieces
        + [vmem],
        out_specs=[vmem] * (1 + n),
        scratch_shapes=[
            pltpu.VMEM((pieces * own_rows, 3 * PAD), bf16),
            pltpu.SemaphoreType.DMA((pieces,)),
        ],
        cost_estimate=cost(48 * work * HD, 16 << 20, 4 * work, 1),
        name="attend_forward",
    )(table, *parts, bias)
    return results[0], results[1:]


def attend_back_kernel(heads, chosen, pieces, own_blocks, waited, carried, table, *refs):
    refs = list(refs)

    def take(count):
        taken = refs[:count]
        del refs[:count]
        return taken

    parts = take(pieces)
    ups = take(len(chosen))
    totals = take(len(chosen))
    (bias,) = take(1)
    take(waited)
    if carried:
        key_before, value_before = take(2)
        query_before = take(pieces - len(chosen))
        (small,) = take(1)
        outs = take(pieces)
        (tail,) = take(1)
        key_sum, value_sum, key_kept, value_kept, row_sums = take(5)
    else:
        (small,) = take(1)
        outs = take(len(chosen))
        key_sum, value_sum = take(2)
        (small_out,) = take(1)
        small_out[...] = small[...]
    rows, up_rows, sems = refs
    own_rows = own_blocks * BLK
    copies = [
        pltpu.make_async_copy(parts[s], rows.at[pl.ds(s * own_rows, own_rows)], sems.at[s])
        for s in range(pieces)
    ] + [
        pltpu.make_async_copy(ups[at], up_rows.at[at], sems.at[pieces + at])
        for at in range(len(chosen))
    ]
    late = []
    if carried:
        late = [
            pltpu.make_async_copy(key_before, key_kept, sems.at[pieces + len(chosen)]),
            pltpu.make_async_copy(value_before, value_kept, sems.at[pieces + len(chosen) + 1]),
        ]
    for copy in copies + late:
        copy.start()
    key_sum[...] = jnp.zeros_like(key_sum)
    value_sum[...] = jnp.zeros_like(value_sum)
    for copy in copies:
        copy.wait()
    query_masks = head_masks(heads, HD**-0.5, bf16)
    up_masks = head_masks(heads, 1.0, bf16)
    out_masks = head_masks(heads, HD**-0.5, f32)

    side = 2 if len(chosen) == 1 else 1

    def step(step_at, carry):
        for at, s in enumerate(chosen * side):
            i = step_at * side + at // len(chosen)
            at = at % len(chosen)
            block = s * own_blocks + i
            start = pl.multiple_of(i * BLK, BLK)
            here = pl.ds(pl.multiple_of(block * BLK, BLK), BLK)
            queries = stacked_heads(rows[here, 0:PAD], query_masks)
            upstream = stacked_heads(up_rows[at, pl.ds(start, BLK), :], up_masks)
            keys = key_blocks(rows, table, block, PAD)
            values = key_blocks(rows, table, block, 2 * PAD)
            kept = totals[at][pl.ds(start, BLK), :]
            log_total = jnp.concatenate([kept[:, h : h + 1] for h in range(heads)], axis=0)
            scores = contract(queries, keys, (1, 1)) + bias[pl.ds(block, 1), :]
            weights = jnp.exp(scores - log_total)
            grad_weights = contract(upstream, values, (1, 1))
            inner = jnp.sum(weights * grad_weights, axis=-1, keepdims=True)
            grad_scores = (weights * (grad_weights - inner)).astype(bf16)
            grad_query = contract(grad_scores, keys, (1, 0))
            to = outs[s] if carried else outs[at]
            to[pl.ds(start, BLK), 0:PAD] = unstacked_heads(grad_query, out_masks).astype(bf16)
            key_part = contract(grad_scores, queries, (0, 0))
            value_part = contract(weights.astype(bf16), upstream, (0, 0))
            for j in range(KEYS // BLK):
                there = pl.ds(pl.multiple_of(table[block, j] * BLK, BLK), BLK)
                key_sum[there, :] += key_part[j * BLK : (j + 1) * BLK]
                value_sum[there, :] += value_part[j * BLK : (j + 1) * BLK]
        return carry

    lax.fori_loop(0, own_blocks // side, step, 0)
    if not carried:
        return
    for copy in late:
        copy.wait()
    before = [s for s in range(pieces) if s not in chosen]
    for at, s in enumerate(before):
        outs[s][:, 0:PAD] = query_before[at][...]
    row_sums[...] = jnp.zeros_like(row_sums)
    for s in range(pieces):

        def finish(i, carry, s=s):
            at = pl.ds(pl.multiple_of(i * BLK, BLK), BLK)
            span = pl.ds(pl.multiple_of(s * own_rows + i * BLK, BLK), BLK)
            outs[s][at, PAD : 2 * PAD] = (key_sum[span, :] + key_kept[span, :]).astype(bf16)
            outs[s][at, 2 * PAD : 3 * PAD] = (value_sum[span, :] + value_kept[span, :]).astype(bf16)
            whole = outs[s][at, :].astype(f32)
            row_sums[...] += jnp.sum(whole.reshape(BLK // 8, 8, 3 * PAD), axis=0)
            return carry

        lax.fori_loop(0, own_blocks, finish, 0)
    slot = lax.broadcasted_iota(jnp.int32, small.shape, 0)
    whole = jnp.sum(row_sums[...], axis=0, keepdims=True)
    tail[...] = jnp.where(slot == SUM_ROW, whole, small[...]).astype(bf16)


def attend_backward(parts, ups, totals, table, bias, heads, chosen, small, waited=(), before=None):
    own_rows = parts[0].shape[0]
    pieces = len(parts)
    n = len(chosen)
    own_blocks = own_rows // BLK
    vmem = pl.BlockSpec(memory_space=pltpu.VMEM)
    anyspace = pl.BlockSpec(memory_space=pl.ANY)
    work = n * own_rows * KEYS * heads
    sum_shape = (pieces * own_rows, PAD)
    if before is None:
        outs = [((own_rows, PAD), bf16)] * n + [(sum_shape, f32)] * 2 + [((16, 3 * PAD), f32)]
        extra, extra_specs, scratch = [small], [vmem], []
    else:
        outs = [((own_rows, 3 * PAD), bf16)] * pieces + [((16, 3 * PAD), bf16)]
        extra = [*before, small]
        extra_specs = [anyspace] * 2 + [vmem] * (len(before) - 1)
        scratch = [pltpu.VMEM(sum_shape, f32)] * 4 + [pltpu.VMEM((8, 3 * PAD), f32)]
    return pl.pallas_call(
        partial(
            attend_back_kernel, heads, chosen, pieces, own_blocks, len(waited), before is not None
        ),
        out_shape=[jax.ShapeDtypeStruct(*out) for out in outs],
        in_specs=[pl.BlockSpec(memory_space=pltpu.SMEM)]
        + [anyspace] * (pieces + n)
        + [vmem] * (n + 1)
        + [anyspace] * len(waited)
        + extra_specs,
        out_specs=[vmem] * len(outs),
        scratch_shapes=scratch
        + [
            pltpu.VMEM((pieces * own_rows, 3 * PAD), bf16),
            pltpu.VMEM((n, own_rows, PAD), bf16),
            pltpu.SemaphoreType.DMA((pieces + n + 2,)),
        ],
        cost_estimate=cost(30 * work * HD, 12 << 20, work),
        name="attend_backward",
    )(table, *parts, *ups, *totals, bias, *waited, *extra)


VMEM_SPEC = pl.BlockSpec(memory_space=pltpu.VMEM)
ANY_SPEC = pl.BlockSpec(memory_space=pl.ANY)
SMEM_SPEC = pl.BlockSpec(memory_space=pltpu.SMEM)
COST_CUT = 64
GELU_A = 0.7978845608028654
GELU_B = 0.044715


def cost(flops, size, transcendentals=0, cut=None):
    cut = cut or COST_CUT
    return pl.CostEstimate(
        flops=flops // cut, bytes_accessed=size // cut, transcendentals=transcendentals // cut
    )


def struct(shape, dtype):
    return jax.ShapeDtypeStruct(shape, dtype)


def row_stats(values):
    centred = values - jnp.mean(values, axis=-1, keepdims=True)
    inv_std = lax.rsqrt(jnp.mean(centred * centred, axis=-1, keepdims=True) + EPSILON)
    return centred * inv_std, inv_std


def norm_backward(upstream, scaled, inv_std, gain):
    weighted = upstream * gain
    inner = jnp.mean(weighted * scaled, axis=-1, keepdims=True)
    return inv_std * (weighted - jnp.mean(weighted, axis=-1, keepdims=True) - scaled * inner)


def column_sum(array):
    return jnp.sum(array.reshape(array.shape[0] // 8, 8, array.shape[1]), axis=0)


def rows_kernel(places, sources, length, *refs):
    teams = len(places)
    refs = list(refs)

    def take(count):
        taken = refs[:count]
        del refs[:count]
        return taken

    mixed = take(teams)
    x_in, g_in = take(2)
    weights = take(sources)
    vectors, b_up = take(2)
    b_out, g1, c1, b_down, g2, c2 = [vectors.at[k : k + 1, :] for k in range(6)]
    layer_out, near_out, far_out, turned_out = take(4)
    back_out = take(teams)
    after_out, small = take(2)
    (
        o_buf,
        x_buf,
        g_buf,
        out_w,
        up_w,
        down_w,
        scaled_buf,
        inv_buf,
        wide_buf,
        low_buf,
        act_buf,
        slope_buf,
        last_buf,
        turned_buf,
        sums,
        up_sums,
        in_sems,
        w_sems,
        out_sems,
    ) = refs
    rows = x_in.shape[0]
    hidden = up_w.shape[2]
    tile, cut = 64, 256
    me = lax.axis_index("tensor")
    ring = sources > 1

    first = []
    for s in range(teams):
        source = mixed[s] if places[s] is None else mixed[s].at[places[s]]
        first.append(pltpu.make_async_copy(source, o_buf.at[s], in_sems.at[s]))
    first.append(pltpu.make_async_copy(x_in, x_buf, in_sems.at[teams]))
    upstream_copy = pltpu.make_async_copy(g_in, g_buf, in_sems.at[teams + 1])
    fetched = ([], [], [])

    def fetch(kind, source, to):
        sem = w_sems.at[kind, len(fetched[kind])]
        fetched[kind].append(pltpu.make_async_copy(source, to, sem))

    wholes = (out_w, up_w, down_w)
    if ring:
        part = weights[0].shape[0]
        spans = ((2 * hidden, PAD), (0, hidden), (2 * hidden + 2 * PAD, hidden))
        for at, piece in enumerate(weights):
            row = pl.multiple_of(ring_member(RING_STEPS[at % 8]) * part, 16)
            for kind, (start, size) in enumerate(spans):
                for pair in range(2):
                    fetch(
                        kind,
                        piece.at[:, pl.ds(start + pair * size, size)],
                        wholes[kind].at[2 * pair + at // 8, pl.ds(row, part), :],
                    )
    else:
        spans = ((hidden, PAD), (0, hidden), (hidden + PAD, hidden))
        for kind, (start, size) in enumerate(spans):
            for s in range(teams):
                fetch(kind, weights[0].at[me ^ s, :, pl.ds(start, size)], wholes[kind].at[s])
    for copy in first + fetched[0] + fetched[1] + fetched[2] + [upstream_copy]:
        copy.start()
    sums[...] = jnp.zeros_like(sums)
    up_sums[...] = jnp.zeros_like(up_sums)
    leaving = []

    def leave(ref, to):
        copy = pltpu.make_async_copy(ref, to, out_sems.at[len(leaving)])
        copy.start()
        leaving.append(copy)

    def leave_turned(k, source, to):
        for n in range(D // LANES):
            span = slice(n * LANES, (n + 1) * LANES)
            turned_buf[k, span, :] = source[:, span].T
        bits, far, part, _ = to.shape
        here = lax.axis_index("dp")
        for b in range(bits):
            for z in range(far):
                row = (here ^ (2 * z + b)) * part if ring else 0
                leave(turned_buf.at[k, pl.ds(pl.multiple_of(row, 16), part), :], to.at[b, z])

    def tiles(body):
        def step(i, carry):
            body(i, pl.ds(pl.multiple_of(i * tile, tile), tile))
            return carry

        lax.fori_loop(0, rows // tile, step, 0)

    for copy in first + fetched[0]:
        copy.wait()
    for n in range(D // cut):
        cols = slice(n * cut, (n + 1) * cut)
        total = contract(o_buf[0], out_w[0, cols, :], (1, 1))
        for s in range(1, teams):
            total = total + contract(o_buf[s], out_w[s, cols, :], (1, 1))
        wide_buf[:, cols] = total

    def first_norm(i, at):
        after = x_buf[at, :].astype(f32) + wide_buf[at, :] + b_out[...]
        scaled, inv_std = row_stats(after)
        scaled_buf[at, :] = scaled
        inv_buf[at, :] = jnp.broadcast_to(inv_std, (tile, LANES))
        low_buf[at, :] = (scaled * g1[...] + c1[...]).astype(bf16)

    tiles(first_norm)
    leave_turned(0, low_buf, turned_out.at[0])
    for copy in fetched[1]:
        copy.wait()

    def up_step(s, carry):
        bias = b_up[pl.ds(s ^ me, 1), :]
        for c in range(hidden // cut):
            cols = slice(c * cut, (c + 1) * cut)
            u = contract(low_buf[...], up_w[s, :, cols], (1, 0)) + bias[:, cols]
            square = u * u
            t = jnp.tanh(u * (GELU_A + GELU_A * GELU_B * square))
            half = 0.5 + 0.5 * t
            act_buf[s, :, cols] = (u * half).astype(bf16)
            slope_buf[s, :, cols] = (
                half + (0.5 * u) * (1.0 - t * t) * (GELU_A + 3.0 * GELU_A * GELU_B * square)
            ).astype(bf16)
        return carry

    lax.fori_loop(0, teams, up_step, 0)
    for s in range(teams):
        leave(act_buf.at[s], (far_out if s % 2 else near_out).at[s // 2])
    for copy in fetched[2]:
        copy.wait()
    upstream_copy.wait()
    for n in range(D // cut):
        cols = slice(n * cut, (n + 1) * cut)
        total = contract(act_buf[0], down_w[0, cols, :], (1, 1))
        for s in range(1, teams):
            total = total + contract(act_buf[s], down_w[s, cols, :], (1, 1))
        wide_buf[:, cols] = total
    start = me * rows
    seq = start // LMAX
    live = length[seq] - (start - seq * LMAX)

    def second_norm(i, at):
        z = (scaled_buf[at, :] * g1[...] + c1[...]) + wide_buf[at, :] + b_down[...]
        scaled, inv_std = row_stats(z)
        x_buf[at, :] = (scaled * g2[...] + c2[...]).astype(bf16)
        row = lax.broadcasted_iota(jnp.int32, (tile, D), 0) + i * tile
        upstream = jnp.where(row < live, g_buf[at, :].astype(f32), 0.0)
        grad = norm_backward(upstream, scaled, inv_std, g2[...]).astype(bf16)
        g_buf[at, :] = grad
        sums[0:8, :] += column_sum(upstream * scaled)
        sums[8:16, :] += column_sum(upstream)
        sums[16:24, :] += column_sum(grad.astype(f32))

    tiles(second_norm)
    leave(x_buf, layer_out)
    leave_turned(1, g_buf, turned_out.at[1])

    def down_back(s, carry):
        for c in range(hidden // cut):
            cols = slice(c * cut, (c + 1) * cut)
            g = contract(g_buf[...], down_w[s, :, cols], (1, 0))
            g = (g * slope_buf[s, :, cols].astype(f32)).astype(bf16)
            slope_buf[s, :, cols] = g
            up_sums[pl.ds(pl.multiple_of(s * 8, 8), 8), cols] = column_sum(g.astype(f32))
        return carry

    lax.fori_loop(0, teams, down_back, 0)
    for s in range(teams):
        leave(slope_buf.at[s], (far_out if s % 2 else near_out).at[2 + s // 2])
    for n in range(D // cut):
        cols = slice(n * cut, (n + 1) * cut)
        total = contract(slope_buf[0], up_w[0, cols, :], (1, 1))
        for s in range(1, teams):
            total = total + contract(slope_buf[s], up_w[s, cols, :], (1, 1))
        wide_buf[:, cols] = total

    def first_back(i, at):
        upstream = g_buf[at, :].astype(f32) + wide_buf[at, :]
        scaled = scaled_buf[at, :]
        grad = norm_backward(upstream, scaled, inv_buf[at, :][:, :1], g1[...]).astype(bf16)
        last_buf[at, :] = grad
        sums[24:32, :] += column_sum(upstream * scaled)
        sums[32:40, :] += column_sum(upstream)
        sums[40:48, :] += column_sum(grad.astype(f32))

    tiles(first_back)
    leave(last_buf, after_out)
    leave_turned(2, last_buf, turned_out.at[2])
    for s in (2, 3, 1, 0):
        o_buf[s] = contract(last_buf[...], out_w[s], (1, 0)).astype(bf16)
        leave(o_buf.at[s], back_out[s])
    small[...] = jnp.zeros_like(small)
    for k in range(6):
        small[k : k + 1, :] = jnp.sum(sums[8 * k : 8 * k + 8, :], axis=0, keepdims=True)
    for s in range(teams):
        small[pl.ds(6 + (s ^ me), 1), :] = jnp.sum(
            up_sums[8 * s : 8 * s + 8, :], axis=0, keepdims=True
        )
    for copy in leaving:
        copy.wait()


def layer_rows(mixed, hidden_in, grad_out, weights, vectors, lengths):
    teams = len(mixed)
    rows = hidden_in.shape[0]
    rows_of, b_up = vectors
    hidden = b_up.shape[1]
    half = teams // 2
    low = struct((rows, D), bf16)
    pair = struct((2 * half, rows, hidden), bf16)
    ring = len(weights) > 1
    turned = struct((3, 2, 4, D // 8, rows) if ring else (3, 1, 1, D, rows), bf16)
    return pl.pallas_call(
        partial(rows_kernel, [at for _, at in mixed], len(weights)),
        out_shape=[low, pair, pair, turned]
        + [struct((rows, PAD), bf16)] * teams
        + [low, struct((16, D), f32)],
        in_specs=[SMEM_SPEC]
        + [ANY_SPEC] * (teams + 2 + len(weights))
        + [VMEM_SPEC] * 2,
        out_specs=[ANY_SPEC] * (5 + teams) + [VMEM_SPEC],
        scratch_shapes=[
            pltpu.VMEM((teams, rows, PAD), bf16),
            pltpu.VMEM((rows, D), bf16),
            pltpu.VMEM((rows, D), bf16),
            pltpu.VMEM((teams, D, PAD), bf16),
            pltpu.VMEM((teams, D, hidden), bf16),
            pltpu.VMEM((teams, D, hidden), bf16),
            pltpu.VMEM((rows, D), f32),
            pltpu.VMEM((rows, LANES), f32),
            pltpu.VMEM((rows, D), f32),
            pltpu.VMEM((rows, D), bf16),
            pltpu.VMEM((teams, rows, hidden), bf16),
            pltpu.VMEM((teams, rows, hidden), bf16),
            pltpu.VMEM((rows, D), bf16),
            pltpu.VMEM((3, D, rows), bf16),
            pltpu.VMEM((48, D), f32),
            pltpu.VMEM((8 * teams, hidden), f32),
            pltpu.SemaphoreType.DMA((teams + 2,)),
            pltpu.SemaphoreType.DMA((3, 32)),
            pltpu.SemaphoreType.DMA((2 + 3 * teams + 24,)),
        ],
        cost_estimate=cost(8 * rows * D * (teams * hidden) + 4 * rows * D * teams * PAD, 24 << 20),
        compiler_params=pltpu.CompilerParams(vmem_limit_bytes=60 << 20),
        name="layer_rows",
    )(
        lengths,
        *[array for array, _ in mixed],
        hidden_in,
        grad_out,
        *weights,
        rows_of,
        b_up,
    )


def row_dot(groups, count, cut_by=None, waited=(), tail=None):
    sets = len(groups[0][0])
    bits, far, part, rows = groups[0][0][0][0].shape[1:]
    cut = 256
    lows = [0]
    for _, rights in groups:
        lows.append(lows[-1] + rights[0][0][0].shape[2] // cut)
    high = bits * far * part
    below = 0 if tail is None else tail.shape[0]
    cuts = 2 if cut_by in ("bits", "rights") else 1

    def kernel(*refs):
        refs = list(refs)
        ins = [[refs.pop(0) for _ in range(sets)] for _ in groups]
        others = [[[refs.pop(0) for _ in range(count)] for _ in range(sets)] for _ in groups]
        if below:
            tail_ref = refs.pop(0)
        outs = refs[len(waited) :]
        j = pl.program_id(0)
        for g in range(len(groups)):

            @pl.when((j >= lows[g]) & (j < lows[g + 1]))
            def _(g=g):
                for i in range(count):
                    total = contract(ins[g][0][...].reshape(high, rows), others[g][0][i][...], (1, 0))
                    for k in range(1, sets):
                        total = total + contract(
                            ins[g][k][...].reshape(high, rows), others[g][k][i][...], (1, 0)
                        )
                    total = total.astype(bf16).reshape(bits, far, part, cut)
                    if cut_by == "far":
                        mine = lax.axis_index("dp") // 2
                        for z in range(far):
                            outs[0][z ^ mine, i] = total[:, z]
                        continue
                    for b in range(bits):
                        if cut_by == "bits":
                            to = outs[b].at[i, 0]
                        elif cut_by == "rights":
                            to = outs[i].at[0, b]
                        else:
                            to = outs[0].at[i, b]
                        if below:
                            to[:, :part, :] = total[b]
                            to[:, part:, :] = jnp.broadcast_to(
                                tail_ref[...][None], (far, below, cut)
                            )
                        else:
                            to[...] = total[b]

    def column(g, at):
        return lambda j: (at, 0, jnp.clip(j - lows[g], 0, lows[g + 1] - lows[g] - 1))

    specs, arrays = [], []
    for lefts, _ in groups:
        for array, at in lefts:
            specs.append(
                pl.BlockSpec((None, bits, far, part, rows), lambda j, at=at: (at, 0, 0, 0, 0))
            )
            arrays.append(array)
    for g, (_, rights) in enumerate(groups):
        for pairs in rights:
            for array, at in pairs:
                specs.append(pl.BlockSpec((None, rows, cut), column(g, at)))
                arrays.append(array)
    if below:
        specs.append(pl.BlockSpec((below, cut), lambda j: (0, j)))
        arrays.append(tail)
    width = lows[-1] * cut
    lead = (count // 2 if cut_by == "rights" else count, bits // 2 if cut_by == "bits" else bits)
    return pl.pallas_call(
        kernel,
        grid=(lows[-1],),
        out_shape=[
            struct((far, *lead, part, width) if cut_by == "far" else (*lead, far, part + below, width), bf16)
        ]
        * cuts,
        in_specs=specs + [ANY_SPEC] * len(waited),
        out_specs=[
            pl.BlockSpec(
                (far, *lead, part, cut) if cut_by == "far" else (*lead, far, part + below, cut),
                lambda j: (0, 0, 0, 0, j),
            )
        ]
        * cuts,
        cost_estimate=cost(2 * sets * rows * high * count * width, 8 << 20),
        name="row_dot",
    )(*arrays, *waited)


def plus(a, b, waited=(), cuts=1, dtype=bf16):
    lead = a.shape[0] // cuts

    def kernel(a_ref, b_ref, *refs):
        for k in range(cuts):
            span = slice(k * lead, (k + 1) * lead)
            refs[len(waited) + k][...] = (
                a_ref[span].astype(f32) + b_ref[span].astype(f32)
            ).astype(dtype)

    return pl.pallas_call(
        kernel,
        out_shape=[struct((lead, *a.shape[1:]), dtype)] * cuts,
        in_specs=[VMEM_SPEC] * 2 + [ANY_SPEC] * len(waited),
        out_specs=[VMEM_SPEC] * cuts,
        cost_estimate=cost(a.size, 6 * a.size),
        name="plus",
    )(a, b, *waited)


def fold(blocks, waited=()):
    def kernel(ref, *refs):
        for k in range(2):
            total = ref[0, k].astype(f32)
            for z in range(1, 4):
                total = total + ref[z, k].astype(f32)
            refs[len(waited) + k][...] = total.astype(bf16)

    return pl.pallas_call(
        kernel,
        out_shape=[struct(blocks.shape[2:], bf16)] * 2,
        in_specs=[VMEM_SPEC] + [ANY_SPEC] * len(waited),
        out_specs=[VMEM_SPEC] * 2,
        cost_estimate=cost(blocks.size, 3 * blocks.size),
        name="fold",
    )(blocks, *waited)


def joined_sums(pairs, waited=()):
    heights = [a.shape[1] for a, _ in pairs]
    rows = max(heights)
    widths = [a.shape[2] for a, _ in pairs]
    count = 2 * len(pairs)

    def kernel(*refs):
        out = refs[-1]
        mine = lax.axis_index("dp") // 2
        for z in range(4):
            at = 0
            to = out.at[z ^ mine]
            for k, width in enumerate(widths):
                if heights[k] < rows:
                    to[heights[k] :, at : at + width] = jnp.zeros((rows - heights[k], width), bf16)
                to[: heights[k], at : at + width] = (
                    refs[2 * k][z].astype(f32) + refs[2 * k + 1][z].astype(f32)
                ).astype(bf16)
                at += width

    return pl.pallas_call(
        kernel,
        out_shape=struct((4, rows, sum(widths)), bf16),
        in_specs=[VMEM_SPEC] * count + [ANY_SPEC] * len(waited),
        out_specs=VMEM_SPEC,
        cost_estimate=cost(rows * sum(widths) * 4, rows * sum(widths) * 24),
        name="joined_sums",
    )(*[array for pair in pairs for array in pair], *waited)


def spread(grads, weight, added=None, after=None, waited=()):
    rows = grads[0].shape[0]

    def kernel(first, second, w, *refs):
        if added is None:
            out = refs[-1]
            out[0] = contract(first[...], w[...], (1, 1)).astype(bf16)
            out[1] = contract(second[...], w[...], (1, 1)).astype(bf16)
            return
        plus_ref, after_ref = refs[:2]
        away, here = refs[-2:]
        away[...] = (contract(first[...], w[...], (1, 1)) + plus_ref[0].astype(f32)).astype(bf16)
        here[...] = contract(second[...], w[...], (1, 1)) + (
            plus_ref[1].astype(f32) + after_ref[...].astype(f32)
        )

    if added is None:
        outs, more = struct((2, rows, D), bf16), []
    else:
        outs, more = [struct((rows, D), bf16), struct((rows, D), f32)], [added, after]
    return pl.pallas_call(
        kernel,
        out_shape=outs,
        in_specs=[VMEM_SPEC] * (3 + len(more)) + [ANY_SPEC] * len(waited),
        out_specs=VMEM_SPEC if added is None else [VMEM_SPEC] * 2,
        cost_estimate=cost(4 * rows * D * weight.shape[1], 5 << 20),
        name="spread",
    )(*grads, weight, *more, *waited)


def pack_queries(w_query, w_key, w_value):
    rows, width = w_query.shape

    def kernel(q, k, v, qkv):
        qkv[...] = jnp.zeros_like(qkv)
        for at, ref in enumerate((q, k, v)):
            qkv[:, at * PAD : at * PAD + width] = ref[...]

    return pl.pallas_call(
        kernel,
        out_shape=struct((rows, 3 * PAD), bf16),
        in_specs=[VMEM_SPEC] * 3,
        out_specs=VMEM_SPEC,
        cost_estimate=cost(rows * PAD, rows * PAD * 8),
        name="pack_queries",
    )(w_query, w_key, w_value)


def pack_weights(w_up, w_out, w_down):
    rows, hidden = w_up.shape
    width = w_out.shape[0]

    def kernel(up, out, down, own):
        own[:, :hidden] = up[...]
        own[:, hidden : hidden + PAD] = jnp.zeros((rows, PAD), bf16)
        own[:, hidden : hidden + width] = out[...].T
        own[:, hidden + PAD :] = down[...].T

    return pl.pallas_call(
        kernel,
        out_shape=struct((rows, 2 * hidden + PAD), bf16),
        in_specs=[VMEM_SPEC] * 3,
        out_specs=VMEM_SPEC,
        cost_estimate=cost(rows * hidden, 2 << 20),
        name="pack_weights",
    )(w_up, w_out, w_down)


def pair_weights(own, beyond, hidden, waited):
    rows, width = own.shape
    starts = (0, hidden, hidden + PAD, width)

    def kernel(a, b, *refs):
        out = refs[-1]
        for at, end in zip(starts, starts[1:]):
            out[:, 2 * at : at + end] = a[:, at:end]
            out[:, at + end : 2 * end] = b[:, at:end]

    return pl.pallas_call(
        kernel,
        out_shape=struct((rows, 2 * width), bf16),
        in_specs=[VMEM_SPEC] * 2 + [ANY_SPEC] * len(waited),
        out_specs=VMEM_SPEC,
        cost_estimate=cost(rows * width, 4 * rows * width),
        name="pair_weights",
    )(own, beyond, *waited)


def project_in(xs, weights, bias):
    rows = xs[0].shape[0]
    pieces = len(xs)
    sources = len(weights)
    ordered = sources > 1
    bits, far = (2, 4) if ordered else (1, 1)
    part = D // (bits * far)
    wide = weights[0].shape[1]

    def kernel(*refs):
        refs = list(refs)
        ins = [refs.pop(0) for _ in range(pieces)]
        shards = [refs.pop(0) for _ in range(sources)]
        b = refs.pop(0)
        outs = [refs.pop(0) for _ in range(pieces)]
        turned_outs = [refs.pop(0) for _ in range(pieces)]
        whole_out, x_buf, w, out_buf, turned, sems, w_sems, out_sems = refs
        here = lax.axis_index("dp") if ordered else 0
        copies = [
            pltpu.make_async_copy(ins[s], x_buf.at[s], sems.at[s]) for s in range(pieces)
        ]
        fetched = []
        for at in range(sources):
            row = ring_member(RING_STEPS[at]) * part if ordered else 0
            fetched.append(
                pltpu.make_async_copy(
                    shards[at],
                    w.at[pl.ds(pl.multiple_of(row, 16), shards[at].shape[0]), :],
                    w_sems.at[at],
                )
            )
        for copy in fetched + copies:
            copy.start()
        for copy in fetched:
            copy.wait()
        leaving = []

        def leave(ref, to):
            copy = pltpu.make_async_copy(ref, to, out_sems.at[len(leaving)])
            copy.start()
            leaving.append(copy)

        leave(w, whole_out)
        for s in range(pieces):
            copies[s].wait()
            for c in range(0, wide, PAD):
                cols = slice(c, c + PAD)
                out_buf[s, :, cols] = (
                    contract(x_buf[s], w[:, cols], (1, 0)) + b[:, cols]
                ).astype(bf16)
            leave(out_buf.at[s], outs[s])
            for n in range(D // LANES):
                span = slice(n * LANES, (n + 1) * LANES)
                turned[s, span, :] = x_buf[s, :, span].T
            for k in range(bits):
                for z in range(far):
                    row = (here ^ (2 * z + k)) * part if ordered else 0
                    leave(
                        turned.at[s, pl.ds(pl.multiple_of(row, 16), part), :],
                        turned_outs[s].at[k, z],
                    )
        for copy in leaving:
            copy.wait()

    results = pl.pallas_call(
        kernel,
        out_shape=[struct((rows, wide), bf16)] * pieces
        + [struct((bits, far, part, rows), bf16)] * pieces
        + [struct((D, wide), bf16)],
        in_specs=[ANY_SPEC] * (pieces + sources) + [VMEM_SPEC],
        out_specs=[ANY_SPEC] * (2 * pieces + 1),
        scratch_shapes=[
            pltpu.VMEM((pieces, rows, D), bf16),
            pltpu.VMEM((D, wide), bf16),
            pltpu.VMEM((pieces, rows, wide), bf16),
            pltpu.VMEM((pieces, D, rows), bf16),
            pltpu.SemaphoreType.DMA((pieces,)),
            pltpu.SemaphoreType.DMA((sources,)),
            pltpu.SemaphoreType.DMA((1 + pieces * (1 + bits * far),)),
        ],
        cost_estimate=cost(4 * pieces * rows * D * wide, 24 << 20, 0, 1),
        name="project_in",
    )(*xs, *weights, bias)
    return results[:pieces], results[pieces : 2 * pieces], results[2 * pieces]


def padded(array):
    return jnp.pad(array, ((0, 0), (0, PAD - array.shape[1])))


def dot(a, b, dims=(1, 0)):
    return contract(a, b, dims)


def per_device(
    hidden_in,
    grad_out,
    w_query,
    b_query,
    w_key,
    w_value,
    b_value,
    w_out,
    b_out,
    gain_one,
    shift_one,
    w_up,
    b_up,
    w_down,
    b_down,
    gain_two,
    shift_two,
    lengths,
    global_raw,
    random_raw,
):
    own_rows = hidden_in.shape[0]
    me = lax.axis_index("tensor")
    teams = lax.axis_size("tensor")
    members = lax.axis_size("dp")
    width = w_query.shape[1]
    heads = width // HD
    hidden = w_up.shape[1]

    table, bias = block_tables(lengths, global_raw, random_raw, own_rows // BLK, teams)

    x2 = swap(hidden_in, 2)
    x1 = swap(hidden_in, 1)
    x3 = swap(x2, 1)
    x_parts = [hidden_in, x1, x2, x3]

    qkv_b = jnp.concatenate(
        [jnp.pad(b_query, (0, PAD - width)), jnp.zeros((PAD,), f32), jnp.pad(b_value, (0, PAD - width))]
    )
    halved = members == 8
    if halved:
        qkv_pieces = ring_pieces(pack_queries(w_query, w_key, w_value))
        own = pack_weights(w_up, w_out, w_down)
        shard = pair_weights(own, swap(own, 2), hidden, qkv_pieces[GATE:])
    else:
        qkv_shard = jnp.concatenate([padded(w_query), padded(w_key), padded(w_value)], axis=1)
        qkv_pieces = [lax.all_gather(qkv_shard, "dp", axis=0, tiled=True)]
        shard = jnp.concatenate([w_up, padded(w_out.T), w_down.T], axis=1)
        weights = lax.all_gather(shard, ("dp", "tensor"), axis=0, tiled=False)
        weights = jnp.swapaxes(weights.reshape(members, teams, *shard.shape), 0, 1)
        weights = [weights.reshape(teams, D, shard.shape[1])]

    qkv, x_turned, qkv_w = project_in(x_parts, qkv_pieces, qkv_b[None])
    far_mixed, (t2, t3) = attend_forward(qkv, table, bias, heads, (2, 3))
    far_mixed = swap(far_mixed, 2)
    near_mixed, (t0, t1) = attend_forward(qkv, table, bias, heads, (0, 1))
    r1 = swap(near_mixed[1], 1)
    r3 = swap(far_mixed[1], 1)
    if halved:

        weights = ring_pieces(shard)
        weights = weights + [swap(piece, 1) for piece in weights]

    results = layer_rows(
        [(near_mixed, 0), (r1, None), (far_mixed, 0), (r3, None)],
        hidden_in,
        grad_out,
        weights,
        (
            jnp.stack([b_out, gain_one, shift_one, b_down, gain_two, shift_two]),
            b_up.reshape(teams, hidden),
        ),
        lengths,
    )
    layer_out, near_rows, far_rows, turned = results[:4]
    backs = results[4 : 4 + teams]
    after_low, small = results[4 + teams :]
    ups = [backs[0]] + [swap(backs[s], s) for s in range(1, teams)]
    totals = [t0, t1, t2, t3]
    before = attend_backward(qkv, ups[:1], totals[:1], table, bias, heads, (0,), small)
    small = before[3]
    small = small + swap(small, 1)
    small = small + swap(small, 2)

    next_rows, next_turned = swap(far_rows, 1), swap(turned, 1)
    down_group = (
        [(turned, 1), (next_turned, 1)],
        [[(near_rows, 0), (near_rows, 1)], [(next_rows, 0), (next_rows, 1)]],
    )
    up_group = (
        [(turned, 0), (next_turned, 0)],
        [[(near_rows, 2), (near_rows, 3)], [(next_rows, 2), (next_rows, 3)]],
    )
    out_group = (
        [(turned, 2), (next_turned, 2)],
        [[(near_mixed, 0), (far_mixed, 0)], [(near_mixed, 1), (far_mixed, 1)]],
    )
    if halved:
        (down_gone,) = row_dot([down_group], 2, "far", (before[0], *ups[1:]))
        down_blocks = far_exchange(down_gone)
        up_kept, up_gone = row_dot([up_group, out_group], 2, "bits", (down_gone,))
        up_away = dp_swap(up_gone, 1)
        waited = (up_gone,)
    else:
        down_sums = row_dot([down_group], 2)[0].reshape(2, D, -1)
        up_sums = row_dot([up_group, out_group], 2)[0].reshape(2, D, -1)
        waited = ()
    results = attend_backward(
        qkv,
        ups[1:],
        totals[1:],
        table,
        bias,
        heads,
        (1, 2, 3),
        small,
        waited,
        (before[1], before[2], before[0]),
    )
    grads, tail = results[:4], results[4]
    waited = ()
    if halved:
        up_here, up_next = plus(up_kept, up_away, (grads[0],), 2)
        up_away = swap(up_next, 2)
        waited = (up_next,)
    parts = spread([grads[3], grads[1]], qkv_w, waited=waited)
    spread_away = swap(parts, 1)
    qkv_group = ([(x[None], 0) for x in x_turned], [[(g[None], 0)] for g in grads])
    if halved:
        kept, gone = row_dot([qkv_group], 1, "bits", (parts,), tail)
        away = dp_swap(gone, 1)
        beyond, here = spread([grads[2], grads[0]], qkv_w, spread_away, after_low, (gone,))
        beyond_away = swap(beyond, 2)
        down_here, down_next = fold(down_blocks, (beyond,))
        down_away = swap(down_next, 2)
        blocks = joined_sums(
            [(kept[0, 0], away[0, 0]), (up_here[0, 0], up_away[0, 0])], (down_next,)
        )
        total = far_exchange(blocks)
        down_here, down_next = plus(down_here, down_away, (blocks,), 2)
        down_away = dp_swap(down_next, 1)
        down_part = down_here[0].astype(f32) + down_away[0].astype(f32)
        total = jnp.sum(total.astype(f32), axis=0)
        qkv_part, up_part = total[:, : 3 * PAD], total[:-16, 3 * PAD :]
        qkv_part, small = qkv_part[:-16], qkv_part[-16:]
    else:
        blocks = row_dot([qkv_group], 1)[0].reshape(D, -1)
        qkv_part = dp_scatter_sum(blocks)
        small = lax.psum(tail.astype(f32), "dp")
        beyond, here = spread([grads[2], grads[0]], qkv_w, spread_away, after_low)
        beyond_away = swap(beyond, 2)
        down_part = dp_scatter_sum(down_sums[0] + swap(down_sums[1], 2))
        up_part = dp_scatter_sum(up_sums[0] + swap(up_sums[1], 2))
    grad_in = here + beyond_away.astype(f32)

    bias_row = small[SUM_ROW]
    return (
        layer_out,
        grad_in,
        qkv_part[:, :width],
        bias_row[:width],
        qkv_part[:, PAD : PAD + width],
        qkv_part[:, 2 * PAD : 2 * PAD + width],
        bias_row[2 * PAD : 2 * PAD + width],
        up_part[:, hidden : hidden + width].T,
        small[5],
        small[3],
        small[4],
        up_part[:, :hidden],
        jnp.take(small[6 : 6 + teams], me, axis=0),
        down_part.T,
        small[2],
        small[0],
        small[1],
    )


def solution(mesh):
    in_specs = (
        P(("dp", "tensor"), None),
        P(("dp", "tensor"), None),
        P("dp", "tensor"),
        P("tensor"),
        P("dp", "tensor"),
        P("dp", "tensor"),
        P("tensor"),
        P("tensor", "dp"),
        P(),
        P(),
        P(),
        P("dp", "tensor"),
        P(),
        P("tensor", "dp"),
        P(),
        P(),
        P(),
        P("dp"),
        P("dp", None),
        P("dp", None, None),
    )
    out_specs = (
        P(("dp", "tensor"), None),
        P(("dp", "tensor"), None),
        P("dp", "tensor"),
        P("tensor"),
        P("dp", "tensor"),
        P("dp", "tensor"),
        P("tensor"),
        P("tensor", "dp"),
        P(),
        P(),
        P(),
        P("dp", "tensor"),
        P("tensor"),
        P("tensor", "dp"),
        P(),
        P(),
        P(),
    )
    return jax.shard_map(
        per_device, mesh=mesh, in_specs=in_specs, out_specs=out_specs, check_vma=False
    )
```

```python
from functools import partial

import jax
import jax.numpy as jnp
from jax import lax
from jax.experimental import pallas as pl
from jax.experimental.pallas import tpu as pltpu
from jax.sharding import PartitionSpec as P

D = 768
HD = 64
FF = 3072
BLK = 64
GLOB = 2
RAND = 3
LMAX = 2048
NB = 32
KEYS = (3 + GLOB + RAND) * BLK
PAD = 256
LANES = 128
SUM_ROW = 10
SUM_ROWS = 16
BELOW = SUM_ROWS * (D // PAD)
GATE = 5

masked_score = -1e30
EPSILON = 1e-12
f32 = jnp.float32
bf16 = jnp.bfloat16


def swap(array, bit):
    size = lax.axis_size("tensor")
    return lax.ppermute(array, "tensor", [(t, t ^ bit) for t in range(size)])


def dp_swap(array, bit):
    size = lax.axis_size("dp")
    return lax.ppermute(array, "dp", [(t, t ^ bit) for t in range(size)])


def swap_both(array):
    size = lax.axis_size("dp") * 4
    axes = ("dp", "tensor")
    return lax.ppermute(array, axes, [(t, t ^ 6) for t in range(size)])


def ring_order(size):
    return list(range(0, size, 2)) + list(range(size - 1, 0, -2))


def ring_member(steps):
    size = lax.axis_size("dp")
    me = lax.axis_index("dp")
    place = jnp.where(me % 2 == 0, me // 2, size - 1 - me // 2)
    place = (place + steps + size) % size
    return jnp.where(place < size // 2, 2 * place, 2 * (size - 1 - place) + 1)


def ring_send(array, step):
    size = lax.axis_size("dp")
    order = ring_order(size)
    return lax.ppermute(
        array, "dp", [(order[i], order[(i + step) % size]) for i in range(size)]
    )


RING_STEPS = (0, -1, 1, -2, 2, -3, 3, -4)


def ring_pieces(shard):
    pieces = [shard]
    ahead, behind = shard, shard
    for step in range(1, 5):
        ahead = ring_send(ahead, 1)
        pieces.append(ahead)
        if step < 4:
            behind = ring_send(behind, -1)
            pieces.append(behind)
    return pieces


def far_exchange(blocks):
    groups = [[2 * f + n for f in range(4)] for n in range(2)]
    return lax.all_to_all(blocks, "dp", 0, 0, axis_index_groups=groups, tiled=True)


def dp_scatter_sum(sums):
    size = lax.axis_size("dp")
    if size != 8:
        return lax.psum_scatter(sums, "dp", scatter_dimension=0, tiled=True).astype(f32)
    blocks = lax.all_to_all(sums.reshape(size, -1, sums.shape[1]), "dp", 0, 0, tiled=True)
    return jnp.sum(blocks.astype(f32), axis=0)


def sum_over(vector, dp_only=False):
    if not dp_only:
        bit = 1
        while bit < lax.axis_size("tensor"):
            vector = vector + swap(vector, bit)
            bit *= 2
    bit = 1
    while bit < lax.axis_size("dp"):
        vector = vector + dp_swap(vector, bit)
        bit *= 2
    return vector


def block_tables(lengths, global_raw, random_raw, own_blocks, pieces):
    count = own_blocks * pieces

    def kernel(length_ref, global_ref, random_ref, table, bias):
        me = lax.axis_index("tensor")
        lane = lax.broadcasted_iota(jnp.int32, (1, KEYS), 1)
        slot = lane // BLK
        within = lane % BLK
        wide = lax.broadcasted_iota(jnp.int32, (own_blocks, LANES), 1)
        row = lax.broadcasted_iota(jnp.int32, (own_blocks, 1), 0)
        for s in range(pieces):
            first = (s ^ me) * own_blocks
            seq = first // NB
            start = first - seq * NB
            length = length_ref[seq]
            live = (length + BLK - 1) // BLK
            raw = random_ref[seq, pl.ds(pl.multiple_of(start, 8), own_blocks), :]
            rest = raw - live * jnp.floor(raw.astype(f32) / live.astype(f32)).astype(jnp.int32)
            rest = jnp.where(rest < 0, rest + live, rest)
            rest = jnp.where(rest >= live, rest - live, rest)
            block = row + start
            ids = [jnp.maximum(block - 1, 0), block, jnp.minimum(block + 1, NB - 1)]
            ids += [jnp.full((own_blocks, 1), lax.rem(global_ref[seq, j], live)) for j in range(GLOB)]
            ids += [rest[:, r : r + 1] for r in range(RAND)]
            spread_ids = jnp.zeros((own_blocks, KEYS), jnp.int32)
            packed = jnp.zeros((own_blocks, LANES), jnp.int32)
            for j, own in enumerate(ids):
                spread_ids = jnp.where(slot == j, own, spread_ids)
                there = own + seq * NB
                there = ((there // own_blocks) ^ me) * own_blocks + there % own_blocks
                packed = jnp.where(wide == j, there, packed)
            table[s * own_blocks : (s + 1) * own_blocks, :] = packed
            lost = (spread_ids * BLK + within) >= length
            lost = lost | ((slot == 0) & (block == 0)) | ((slot == 2) & (block == NB - 1))
            bias[s * own_blocks : (s + 1) * own_blocks, :] = jnp.where(lost, masked_score, 0.0).astype(f32)

    smem = pl.BlockSpec(memory_space=pltpu.SMEM)
    vmem = pl.BlockSpec(memory_space=pltpu.VMEM)
    return pl.pallas_call(
        kernel,
        out_shape=[
            jax.ShapeDtypeStruct((count, LANES), jnp.int32),
            jax.ShapeDtypeStruct((count, KEYS), f32),
        ],
        in_specs=[smem, smem, vmem],
        out_specs=[vmem, vmem],
        cost_estimate=cost(count * KEYS * 16, count * KEYS * 4),
        name="block_tables",
    )(lengths, global_raw, random_raw)


def head_masks(heads, scale, dtype):
    lane = lax.broadcasted_iota(jnp.int32, (1, PAD), 1)
    return [
        jnp.where((lane >= h * HD) & (lane < (h + 1) * HD), scale, 0.0).astype(dtype)
        for h in range(heads)
    ]


def stacked_heads(rows, masks):
    return jnp.concatenate([rows * mask for mask in masks], axis=0)


def unstacked_heads(stacked, masks):
    rows = stacked.shape[0] // len(masks)
    total = stacked[:rows] * masks[0]
    for h in range(1, len(masks)):
        total = total + stacked[h * rows : (h + 1) * rows] * masks[h]
    return total


def key_blocks(ref, table, block, column):
    return jnp.concatenate(
        [
            ref[pl.ds(pl.multiple_of(table[block, j] * BLK, BLK), BLK), column : column + PAD]
            for j in range(KEYS // BLK)
        ],
        axis=0,
    )


def contract(a, b, dims):
    return lax.dot_general(a, b, ((dims[:1], dims[1:]), ((), ())), preferred_element_type=f32)


def attend_kernel(heads, chosen, pieces, own_blocks, table, *refs):
    parts = refs[:pieces]
    bias = refs[pieces]
    out = refs[pieces + 1]
    totals = refs[pieces + 2 : pieces + 2 + len(chosen)]
    rows, sems = refs[pieces + 2 + len(chosen) :]
    own_rows = own_blocks * BLK
    copies = [
        pltpu.make_async_copy(
            parts[s], rows.at[pl.ds(s * own_rows, own_rows)], sems.at[s]
        )
        for s in range(pieces)
    ]
    for copy in copies:
        copy.start()
    for copy in copies:
        copy.wait()
    query_masks = head_masks(heads, HD**-0.5, bf16)
    out_masks = head_masks(heads, 1.0, f32)
    lane = lax.broadcasted_iota(jnp.int32, (BLK, LANES), 1)

    def step(i, carry):
        for at, s in enumerate(chosen):
            block = s * own_blocks + i
            start = pl.multiple_of(i * BLK, BLK)
            queries = stacked_heads(
                rows[pl.ds(pl.multiple_of(block * BLK, BLK), BLK), 0:PAD], query_masks
            )
            keys = key_blocks(rows, table, block, PAD)
            values = key_blocks(rows, table, block, 2 * PAD)
            scores = contract(queries, keys, (1, 1)) + bias[pl.ds(block, 1), :]
            top = jnp.max(scores, axis=-1, keepdims=True)
            weights = jnp.exp(scores - top)
            total = jnp.sum(weights, axis=-1, keepdims=True)
            mixed = contract(weights.astype(bf16), values, (1, 0)) / total
            out[at, pl.ds(start, BLK), :] = unstacked_heads(mixed, out_masks).astype(bf16)
            log_total = top + jnp.log(total)
            kept = jnp.zeros((BLK, LANES), f32)
            for h in range(heads):
                kept = jnp.where(lane == h, log_total[h * BLK : (h + 1) * BLK], kept)
            totals[at][pl.ds(start, BLK), :] = kept
        return carry

    lax.fori_loop(0, own_blocks, step, 0)


def attend_forward(parts, table, bias, heads, chosen):
    own_rows = parts[0].shape[0]
    pieces = len(parts)
    own_blocks = own_rows // BLK
    n = len(chosen)
    vmem = pl.BlockSpec(memory_space=pltpu.VMEM)
    work = n * own_rows * KEYS * heads
    results = pl.pallas_call(
        partial(attend_kernel, heads, chosen, pieces, own_blocks),
        out_shape=[jax.ShapeDtypeStruct((n, own_rows, PAD), bf16)]
        + [jax.ShapeDtypeStruct((own_rows, LANES), f32)] * n,
        in_specs=[pl.BlockSpec(memory_space=pltpu.SMEM)]
        + [pl.BlockSpec(memory_space=pl.ANY)] * pieces
        + [vmem],
        out_specs=[vmem] * (1 + n),
        scratch_shapes=[
            pltpu.VMEM((pieces * own_rows, 3 * PAD), bf16),
            pltpu.SemaphoreType.DMA((pieces,)),
        ],
        cost_estimate=cost(48 * work * HD, 16 << 20, 4 * work, 1),
        name="attend_forward",
    )(table, *parts, bias)
    return results[0], results[1:]


def attend_back_kernel(heads, chosen, pieces, own_blocks, waited, carried, table, *refs):
    refs = list(refs)

    def take(count):
        taken = refs[:count]
        del refs[:count]
        return taken

    parts = take(pieces)
    ups = take(len(chosen))
    totals = take(len(chosen))
    (bias,) = take(1)
    take(waited)
    if carried:
        key_before, value_before = take(2)
        query_before = take(pieces - len(chosen))
        (small_ref,) = take(1)
        outs = take(pieces)
        (tail,) = take(1)
        key_sum, value_sum, key_kept, value_kept, row_sums = take(5)
    else:
        outs = take(len(chosen))
        key_sum, value_sum = take(2)
    rows, up_rows, sems = refs
    own_rows = own_blocks * BLK
    copies = [
        pltpu.make_async_copy(parts[s], rows.at[pl.ds(s * own_rows, own_rows)], sems.at[s])
        for s in range(pieces)
    ] + [
        pltpu.make_async_copy(ups[at], up_rows.at[at], sems.at[pieces + at])
        for at in range(len(chosen))
    ]
    late = []
    if carried:
        late = [
            pltpu.make_async_copy(key_before, key_kept, sems.at[pieces + len(chosen)]),
            pltpu.make_async_copy(value_before, value_kept, sems.at[pieces + len(chosen) + 1]),
        ]
    for copy in copies + late:
        copy.start()
    key_sum[...] = jnp.zeros_like(key_sum)
    value_sum[...] = jnp.zeros_like(value_sum)
    for copy in copies:
        copy.wait()
    query_masks = head_masks(heads, HD**-0.5, bf16)
    up_masks = head_masks(heads, 1.0, bf16)
    out_masks = head_masks(heads, HD**-0.5, f32)

    side = 2 if len(chosen) == 1 else 1

    def step(step_at, carry):
        for at, s in enumerate(chosen * side):
            i = step_at * side + at // len(chosen)
            at = at % len(chosen)
            block = s * own_blocks + i
            start = pl.multiple_of(i * BLK, BLK)
            here = pl.ds(pl.multiple_of(block * BLK, BLK), BLK)
            queries = stacked_heads(rows[here, 0:PAD], query_masks)
            upstream = stacked_heads(up_rows[at, pl.ds(start, BLK), :], up_masks)
            keys = key_blocks(rows, table, block, PAD)
            values = key_blocks(rows, table, block, 2 * PAD)
            kept = totals[at][pl.ds(start, BLK), :]
            log_total = jnp.concatenate([kept[:, h : h + 1] for h in range(heads)], axis=0)
            scores = contract(queries, keys, (1, 1)) + bias[pl.ds(block, 1), :]
            weights = jnp.exp(scores - log_total)
            grad_weights = contract(upstream, values, (1, 1))
            inner = jnp.sum(weights * grad_weights, axis=-1, keepdims=True)
            grad_scores = (weights * (grad_weights - inner)).astype(bf16)
            grad_query = contract(grad_scores, keys, (1, 0))
            to = outs[s] if carried else outs[at]
            to[pl.ds(start, BLK), 0:PAD] = unstacked_heads(grad_query, out_masks).astype(bf16)
            key_part = contract(grad_scores, queries, (0, 0))
            value_part = contract(weights.astype(bf16), upstream, (0, 0))
            for j in range(KEYS // BLK):
                there = pl.ds(pl.multiple_of(table[block, j] * BLK, BLK), BLK)
                key_sum[there, :] += key_part[j * BLK : (j + 1) * BLK]
                value_sum[there, :] += value_part[j * BLK : (j + 1) * BLK]
        return carry

    lax.fori_loop(0, own_blocks // side, step, 0)
    if not carried:
        return
    for copy in late:
        copy.wait()
    before = [s for s in range(pieces) if s not in chosen]
    for at, s in enumerate(before):
        outs[s][:, 0:PAD] = query_before[at][...]
    row_sums[...] = jnp.zeros_like(row_sums)
    for s in range(pieces):

        def finish(i, carry, s=s):
            at = pl.ds(pl.multiple_of(i * BLK, BLK), BLK)
            span = pl.ds(pl.multiple_of(s * own_rows + i * BLK, BLK), BLK)
            outs[s][at, PAD : 2 * PAD] = (key_sum[span, :] + key_kept[span, :]).astype(bf16)
            outs[s][at, 2 * PAD : 3 * PAD] = (value_sum[span, :] + value_kept[span, :]).astype(bf16)
            whole = outs[s][at, :].astype(f32)
            row_sums[...] += jnp.sum(whole.reshape(BLK // 8, 8, 3 * PAD), axis=0)
            return carry

        lax.fori_loop(0, own_blocks, finish, 0)
    slot = lax.broadcasted_iota(jnp.int32, tail.shape, 0)
    whole = jnp.sum(row_sums[...], axis=0, keepdims=True)
    small = small_ref[...]
    for at in range(len(chosen)):
        parts = [
            up_rows[at, own_rows + k * SUM_ROWS : own_rows + (k + 1) * SUM_ROWS, :]
            for k in range(BELOW // SUM_ROWS)
        ]
        small = small + jnp.concatenate(parts, axis=1).astype(f32)
    tail[...] = jnp.where(slot == SUM_ROW, whole, small).astype(bf16)


def attend_backward(parts, ups, totals, table, bias, heads, chosen, small=None, waited=(), before=None):
    own_rows = parts[0].shape[0]
    pieces = len(parts)
    n = len(chosen)
    own_blocks = own_rows // BLK
    vmem = pl.BlockSpec(memory_space=pltpu.VMEM)
    anyspace = pl.BlockSpec(memory_space=pl.ANY)
    work = n * own_rows * KEYS * heads
    sum_shape = (pieces * own_rows, PAD)
    if before is None:
        outs = [((own_rows, PAD), bf16)] * n + [(sum_shape, f32)] * 2
        extra, extra_specs, scratch = [], [], []
    else:
        outs = [((own_rows, 3 * PAD), bf16)] * pieces + [((16, 3 * PAD), bf16)]
        extra = [*before, small]
        extra_specs = [anyspace] * 2 + [vmem] * (len(before) - 1)
        scratch = [pltpu.VMEM(sum_shape, f32)] * 4 + [pltpu.VMEM((8, 3 * PAD), f32)]
    return pl.pallas_call(
        partial(
            attend_back_kernel, heads, chosen, pieces, own_blocks, len(waited), before is not None
        ),
        out_shape=[jax.ShapeDtypeStruct(*out) for out in outs],
        in_specs=[pl.BlockSpec(memory_space=pltpu.SMEM)]
        + [anyspace] * (pieces + n)
        + [vmem] * (n + 1)
        + [anyspace] * len(waited)
        + extra_specs,
        out_specs=[vmem] * len(outs),
        scratch_shapes=scratch
        + [
            pltpu.VMEM((pieces * own_rows, 3 * PAD), bf16),
            pltpu.VMEM((n, own_rows + BELOW, PAD), bf16),
            pltpu.SemaphoreType.DMA((pieces + n + 2,)),
        ],
        cost_estimate=cost(30 * work * HD, 12 << 20, work),
        name="attend_backward",
    )(table, *parts, *ups, *totals, bias, *waited, *extra)


VMEM_SPEC = pl.BlockSpec(memory_space=pltpu.VMEM)
ANY_SPEC = pl.BlockSpec(memory_space=pl.ANY)
SMEM_SPEC = pl.BlockSpec(memory_space=pltpu.SMEM)
COST_CUT = 64
GELU_A = 0.7978845608028654
GELU_B = 0.044715


def cost(flops, size, transcendentals=0, cut=None):
    cut = cut or COST_CUT
    return pl.CostEstimate(
        flops=flops // cut, bytes_accessed=size // cut, transcendentals=transcendentals // cut
    )


def struct(shape, dtype):
    return jax.ShapeDtypeStruct(shape, dtype)


def row_stats(values):
    centred = values - jnp.mean(values, axis=-1, keepdims=True)
    inv_std = lax.rsqrt(jnp.mean(centred * centred, axis=-1, keepdims=True) + EPSILON)
    return centred * inv_std, inv_std


def norm_backward(upstream, scaled, inv_std, gain):
    weighted = upstream * gain
    inner = jnp.mean(weighted * scaled, axis=-1, keepdims=True)
    return inv_std * (weighted - jnp.mean(weighted, axis=-1, keepdims=True) - scaled * inner)


def column_sum(array):
    return jnp.sum(array.reshape(array.shape[0] // 8, 8, array.shape[1]), axis=0)


def rows_kernel(places, sources, length, *refs):
    teams = len(places)
    refs = list(refs)

    def take(count):
        taken = refs[:count]
        del refs[:count]
        return taken

    mixed = take(teams)
    x_in, g_in = take(2)
    weights = take(sources)
    vectors, b_up = take(2)
    b_out, g1, c1, b_down, g2, c2 = [vectors.at[k : k + 1, :] for k in range(6)]
    layer_out, near_out, far_out, turned_out = take(4)
    back_out = take(teams)
    after_out, small = take(2)
    (
        o_buf,
        x_buf,
        g_buf,
        out_w,
        up_w,
        down_w,
        scaled_buf,
        inv_buf,
        wide_buf,
        low_buf,
        act_buf,
        slope_buf,
        last_buf,
        turned_buf,
        sums,
        up_sums,
        in_sems,
        w_sems,
        out_sems,
    ) = refs
    rows = x_in.shape[0]
    hidden = up_w.shape[2]
    tile, cut = 64, 256
    me = lax.axis_index("tensor")
    ring = sources > 1

    first = []
    for s in range(teams):
        source = mixed[s] if places[s] is None else mixed[s].at[places[s]]
        first.append(
            pltpu.make_async_copy(source, o_buf.at[s, pl.ds(0, x_in.shape[0]), :], in_sems.at[s])
        )
    first.append(pltpu.make_async_copy(x_in, x_buf, in_sems.at[teams]))
    upstream_copy = pltpu.make_async_copy(g_in, g_buf, in_sems.at[teams + 1])
    fetched = ([], [], [])

    def fetch(kind, source, to):
        sem = w_sems.at[kind, len(fetched[kind])]
        fetched[kind].append(pltpu.make_async_copy(source, to, sem))

    wholes = (out_w, up_w, down_w)
    if ring:
        part = weights[0].shape[0]
        spans = ((2 * hidden, PAD), (0, hidden), (2 * hidden + 2 * PAD, hidden))
        for at, piece in enumerate(weights):
            row = pl.multiple_of(ring_member(RING_STEPS[at % 8]) * part, 16)
            for kind, (start, size) in enumerate(spans):
                for pair in range(2):
                    fetch(
                        kind,
                        piece.at[:, pl.ds(start + pair * size, size)],
                        wholes[kind].at[2 * pair + at // 8, pl.ds(row, part), :],
                    )
    else:
        spans = ((hidden, PAD), (0, hidden), (hidden + PAD, hidden))
        for kind, (start, size) in enumerate(spans):
            for s in range(teams):
                fetch(kind, weights[0].at[me ^ s, :, pl.ds(start, size)], wholes[kind].at[s])
    for copy in first + fetched[0] + fetched[1] + fetched[2] + [upstream_copy]:
        copy.start()
    sums[...] = jnp.zeros_like(sums)
    up_sums[...] = jnp.zeros_like(up_sums)
    leaving = []

    def leave(ref, to):
        copy = pltpu.make_async_copy(ref, to, out_sems.at[len(leaving)])
        copy.start()
        leaving.append(copy)

    def leave_turned(k, source, to):
        for n in range(D // LANES):
            span = slice(n * LANES, (n + 1) * LANES)
            turned_buf[k, span, :] = source[:, span].T
        bits, far, part, _ = to.shape
        here = lax.axis_index("dp")
        for b in range(bits):
            for z in range(far):
                row = (here ^ (2 * z + b)) * part if ring else 0
                leave(turned_buf.at[k, pl.ds(pl.multiple_of(row, 16), part), :], to.at[b, z])

    def tiles(body):
        def step(i, carry):
            body(i, pl.ds(pl.multiple_of(i * tile, tile), tile))
            return carry

        lax.fori_loop(0, rows // tile, step, 0)

    for copy in first + fetched[0]:
        copy.wait()
    for n in range(D // cut):
        cols = slice(n * cut, (n + 1) * cut)
        total = contract(o_buf[0, :rows, :], out_w[0, cols, :], (1, 1))
        for s in range(1, teams):
            total = total + contract(o_buf[s, :rows, :], out_w[s, cols, :], (1, 1))
        wide_buf[:, cols] = total

    def first_norm(i, at):
        after = x_buf[at, :].astype(f32) + wide_buf[at, :] + b_out[...]
        scaled, inv_std = row_stats(after)
        scaled_buf[at, :] = scaled
        inv_buf[at, :] = jnp.broadcast_to(inv_std, (tile, LANES))
        low_buf[at, :] = (scaled * g1[...] + c1[...]).astype(bf16)

    tiles(first_norm)
    leave_turned(0, low_buf, turned_out.at[0])
    for copy in fetched[1]:
        copy.wait()

    def up_step(s, carry):
        bias = b_up[pl.ds(s ^ me, 1), :]
        for c in range(hidden // cut):
            cols = slice(c * cut, (c + 1) * cut)
            u = contract(low_buf[...], up_w[s, :, cols], (1, 0)) + bias[:, cols]
            square = u * u
            t = jnp.tanh(u * (GELU_A + GELU_A * GELU_B * square))
            half = 0.5 + 0.5 * t
            act_buf[s, :, cols] = (u * half).astype(bf16)
            slope_buf[s, :, cols] = (
                half + (0.5 * u) * (1.0 - t * t) * (GELU_A + 3.0 * GELU_A * GELU_B * square)
            ).astype(bf16)
        return carry

    lax.fori_loop(0, teams, up_step, 0)
    for s in range(teams):
        leave(act_buf.at[s], (far_out if s % 2 else near_out).at[s // 2])
    for copy in fetched[2]:
        copy.wait()
    upstream_copy.wait()
    for n in range(D // cut):
        cols = slice(n * cut, (n + 1) * cut)
        total = contract(act_buf[0], down_w[0, cols, :], (1, 1))
        for s in range(1, teams):
            total = total + contract(act_buf[s], down_w[s, cols, :], (1, 1))
        wide_buf[:, cols] = total
    start = me * rows
    seq = start // LMAX
    live = length[seq] - (start - seq * LMAX)

    def second_norm(i, at):
        z = (scaled_buf[at, :] * g1[...] + c1[...]) + wide_buf[at, :] + b_down[...]
        scaled, inv_std = row_stats(z)
        x_buf[at, :] = (scaled * g2[...] + c2[...]).astype(bf16)
        row = lax.broadcasted_iota(jnp.int32, (tile, D), 0) + i * tile
        upstream = jnp.where(row < live, g_buf[at, :].astype(f32), 0.0)
        grad = norm_backward(upstream, scaled, inv_std, g2[...]).astype(bf16)
        g_buf[at, :] = grad
        sums[0:8, :] += column_sum(upstream * scaled)
        sums[8:16, :] += column_sum(upstream)
        sums[16:24, :] += column_sum(grad.astype(f32))

    tiles(second_norm)
    leave(x_buf, layer_out)
    leave_turned(1, g_buf, turned_out.at[1])

    def down_back(s, carry):
        for c in range(hidden // cut):
            cols = slice(c * cut, (c + 1) * cut)
            g = contract(g_buf[...], down_w[s, :, cols], (1, 0))
            g = (g * slope_buf[s, :, cols].astype(f32)).astype(bf16)
            slope_buf[s, :, cols] = g
            up_sums[pl.ds(pl.multiple_of(s * 8, 8), 8), cols] = column_sum(g.astype(f32))
        return carry

    lax.fori_loop(0, teams, down_back, 0)
    for s in range(teams):
        leave(slope_buf.at[s], (far_out if s % 2 else near_out).at[2 + s // 2])
    for n in range(D // cut):
        cols = slice(n * cut, (n + 1) * cut)
        total = contract(slope_buf[0], up_w[0, cols, :], (1, 1))
        for s in range(1, teams):
            total = total + contract(slope_buf[s], up_w[s, cols, :], (1, 1))
        wide_buf[:, cols] = total

    def first_back(i, at):
        upstream = g_buf[at, :].astype(f32) + wide_buf[at, :]
        scaled = scaled_buf[at, :]
        grad = norm_backward(upstream, scaled, inv_buf[at, :][:, :1], g1[...]).astype(bf16)
        last_buf[at, :] = grad
        sums[24:32, :] += column_sum(upstream * scaled)
        sums[32:40, :] += column_sum(upstream)
        sums[40:48, :] += column_sum(grad.astype(f32))

    tiles(first_back)
    leave(last_buf, after_out)
    leave_turned(2, last_buf, turned_out.at[2])
    small[...] = jnp.zeros_like(small)
    for k in range(6):
        small[k : k + 1, :] = jnp.sum(sums[8 * k : 8 * k + 8, :], axis=0, keepdims=True)
    for s in range(teams):
        small[pl.ds(6 + (s ^ me), 1), :] = jnp.sum(
            up_sums[8 * s : 8 * s + 8, :], axis=0, keepdims=True
        )
    for s in (2, 3, 1, 0):
        o_buf[s, :rows, :] = contract(last_buf[...], out_w[s], (1, 0)).astype(bf16)
        for k in range(D // PAD):
            o_buf[s, rows + k * SUM_ROWS : rows + (k + 1) * SUM_ROWS, :] = small[
                :, k * PAD : (k + 1) * PAD
            ].astype(bf16)
        leave(o_buf.at[s], back_out[s])
    for copy in leaving:
        copy.wait()


def layer_rows(mixed, hidden_in, grad_out, weights, vectors, lengths):
    teams = len(mixed)
    rows = hidden_in.shape[0]
    rows_of, b_up = vectors
    hidden = b_up.shape[1]
    half = teams // 2
    low = struct((rows, D), bf16)
    pair = struct((2 * half, rows, hidden), bf16)
    ring = len(weights) > 1
    turned = struct((3, 2, 4, D // 8, rows) if ring else (3, 1, 1, D, rows), bf16)
    return pl.pallas_call(
        partial(rows_kernel, [at for _, at in mixed], len(weights)),
        out_shape=[low, pair, pair, turned]
        + [struct((rows + BELOW, PAD), bf16)] * teams
        + [low, struct((16, D), f32)],
        in_specs=[SMEM_SPEC]
        + [ANY_SPEC] * (teams + 2 + len(weights))
        + [VMEM_SPEC] * 2,
        out_specs=[ANY_SPEC] * (5 + teams) + [VMEM_SPEC],
        scratch_shapes=[
            pltpu.VMEM((teams, rows + BELOW, PAD), bf16),
            pltpu.VMEM((rows, D), bf16),
            pltpu.VMEM((rows, D), bf16),
            pltpu.VMEM((teams, D, PAD), bf16),
            pltpu.VMEM((teams, D, hidden), bf16),
            pltpu.VMEM((teams, D, hidden), bf16),
            pltpu.VMEM((rows, D), f32),
            pltpu.VMEM((rows, LANES), f32),
            pltpu.VMEM((rows, D), f32),
            pltpu.VMEM((rows, D), bf16),
            pltpu.VMEM((teams, rows, hidden), bf16),
            pltpu.VMEM((teams, rows, hidden), bf16),
            pltpu.VMEM((rows, D), bf16),
            pltpu.VMEM((3, D, rows), bf16),
            pltpu.VMEM((48, D), f32),
            pltpu.VMEM((8 * teams, hidden), f32),
            pltpu.SemaphoreType.DMA((teams + 2,)),
            pltpu.SemaphoreType.DMA((3, 32)),
            pltpu.SemaphoreType.DMA((2 + 3 * teams + 24,)),
        ],
        cost_estimate=cost(8 * rows * D * (teams * hidden) + 4 * rows * D * teams * PAD, 24 << 20),
        compiler_params=pltpu.CompilerParams(vmem_limit_bytes=60 << 20),
        name="layer_rows",
    )(
        lengths,
        *[array for array, _ in mixed],
        hidden_in,
        grad_out,
        *weights,
        rows_of,
        b_up,
    )


def row_dot(groups, count, cut_by=None, waited=(), tail=None):
    sets = len(groups[0][0])
    bits, far, part, rows = groups[0][0][0][0].shape[1:]
    cut = 256
    lows = [0]
    for _, rights in groups:
        lows.append(lows[-1] + rights[0][0][0].shape[2] // cut)
    high = bits * far * part
    below = 0 if tail is None else tail.shape[0]
    cuts = {"bits": 2, "quads": 4}.get(cut_by, 1)

    def kernel(*refs):
        refs = list(refs)
        ins = [[refs.pop(0) for _ in range(sets)] for _ in groups]
        others = [[[refs.pop(0) for _ in range(count)] for _ in range(sets)] for _ in groups]
        if below:
            tail_ref = refs.pop(0)
        outs = refs[len(waited) :]
        j = pl.program_id(0)
        for g in range(len(groups)):

            @pl.when((j >= lows[g]) & (j < lows[g + 1]))
            def _(g=g):
                for i in range(count):
                    total = contract(ins[g][0][...].reshape(high, rows), others[g][0][i][...], (1, 0))
                    for k in range(1, sets):
                        total = total + contract(
                            ins[g][k][...].reshape(high, rows), others[g][k][i][...], (1, 0)
                        )
                    total = total.astype(bf16).reshape(bits, far, part, cut)
                    if cut_by == "far":
                        mine = lax.axis_index("dp") // 2
                        for z in range(far):
                            outs[0][z ^ mine, i] = total[:, z]
                        continue
                    for b in range(bits):
                        if cut_by == "bits":
                            to = outs[b].at[i, 0]
                        elif cut_by == "quads":
                            to = outs[2 * b + i].at[0, 0]
                        else:
                            to = outs[0].at[i, b]
                        if below:
                            to[:, :part, :] = total[b]
                            to[:, part:, :] = jnp.broadcast_to(
                                tail_ref[...][None], (far, below, cut)
                            )
                        else:
                            to[...] = total[b]

    def column(g, at):
        return lambda j: (at, 0, jnp.clip(j - lows[g], 0, lows[g + 1] - lows[g] - 1))

    specs, arrays = [], []
    for lefts, _ in groups:
        for array, at in lefts:
            specs.append(
                pl.BlockSpec((None, bits, far, part, rows), lambda j, at=at: (at, 0, 0, 0, 0))
            )
            arrays.append(array)
    for g, (_, rights) in enumerate(groups):
        for pairs in rights:
            for array, at in pairs:
                specs.append(pl.BlockSpec((None, rows, cut), column(g, at)))
                arrays.append(array)
    if below:
        specs.append(pl.BlockSpec((below, cut), lambda j: (0, j)))
        arrays.append(tail)
    width = lows[-1] * cut
    lead = (1 if cut_by == "quads" else count, 1 if cut_by in ("bits", "quads") else bits)
    return pl.pallas_call(
        kernel,
        grid=(lows[-1],),
        out_shape=[
            struct((far, *lead, part, width) if cut_by == "far" else (*lead, far, part + below, width), bf16)
        ]
        * cuts,
        in_specs=specs + [ANY_SPEC] * len(waited),
        out_specs=[
            pl.BlockSpec(
                (far, *lead, part, cut) if cut_by == "far" else (*lead, far, part + below, cut),
                lambda j: (0, 0, 0, 0, j),
            )
        ]
        * cuts,
        cost_estimate=cost(2 * sets * rows * high * count * width, 8 << 20),
        name="row_dot",
    )(*arrays, *waited)


def plus(a, b, waited=(), cuts=1, dtype=bf16):
    lead = a.shape[0] // cuts

    def kernel(a_ref, b_ref, *refs):
        for k in range(cuts):
            span = slice(k * lead, (k + 1) * lead)
            refs[len(waited) + k][...] = (
                a_ref[span].astype(f32) + b_ref[span].astype(f32)
            ).astype(dtype)

    return pl.pallas_call(
        kernel,
        out_shape=[struct((lead, *a.shape[1:]), dtype)] * cuts,
        in_specs=[VMEM_SPEC] * 2 + [ANY_SPEC] * len(waited),
        out_specs=[VMEM_SPEC] * cuts,
        cost_estimate=cost(a.size, 6 * a.size),
        name="plus",
    )(a, b, *waited)


def held(array, waited):
    def kernel(a_ref, *refs):
        refs[-1][...] = a_ref[...]

    return pl.pallas_call(
        kernel,
        out_shape=struct(array.shape, array.dtype),
        in_specs=[VMEM_SPEC] + [ANY_SPEC] * len(waited),
        out_specs=VMEM_SPEC,
        cost_estimate=cost(array.size, 8 * array.size),
        name="held",
    )(array, *waited)


def fold(blocks, waited=()):
    def kernel(ref, *refs):
        for k in range(2):
            total = ref[0, k].astype(f32)
            for z in range(1, 4):
                total = total + ref[z, k].astype(f32)
            refs[len(waited) + k][...] = total.astype(bf16)

    return pl.pallas_call(
        kernel,
        out_shape=[struct(blocks.shape[2:], bf16)] * 2,
        in_specs=[VMEM_SPEC] + [ANY_SPEC] * len(waited),
        out_specs=[VMEM_SPEC] * 2,
        cost_estimate=cost(blocks.size, 3 * blocks.size),
        name="fold",
    )(blocks, *waited)


def joined_sums(lists, waited=(), apart=False):
    rows, width = lists[0].shape[1:]
    count = len(lists)

    def kernel(*refs):
        mine = lax.axis_index("dp") // 2
        for z in range(4):
            total = refs[0][z].astype(f32)
            for k in range(1, count):
                total = total + refs[k][z].astype(f32)
            if apart:
                refs[count + len(waited) + z][...] = total.astype(bf16)
            else:
                refs[-1][z ^ mine] = total.astype(bf16)

    return pl.pallas_call(
        kernel,
        out_shape=[struct((rows, width), bf16)] * 4 if apart else struct((4, rows, width), bf16),
        in_specs=[VMEM_SPEC] * count + [ANY_SPEC] * len(waited),
        out_specs=[VMEM_SPEC] * 4 if apart else VMEM_SPEC,
        cost_estimate=cost(rows * width * 4 * count, rows * width * 8 * count),
        name="joined_sums",
    )(*lists, *waited)


def spread(grads, weight, added=None, after=None, waited=()):
    rows = grads[0].shape[0]

    def kernel(first, second, w, *refs):
        if added is None:
            out = refs[-1]
            out[0] = contract(first[...], w[...], (1, 1)).astype(bf16)
            out[1] = contract(second[...], w[...], (1, 1)).astype(bf16)
            return
        plus_ref, after_ref = refs[:2]
        away, here = refs[-2:]
        away[...] = (contract(first[...], w[...], (1, 1)) + plus_ref[0].astype(f32)).astype(bf16)
        here[...] = contract(second[...], w[...], (1, 1)) + (
            plus_ref[1].astype(f32) + after_ref[...].astype(f32)
        )

    if added is None:
        outs, more = struct((2, rows, D), bf16), []
    else:
        outs, more = [struct((rows, D), bf16), struct((rows, D), f32)], [added, after]
    return pl.pallas_call(
        kernel,
        out_shape=outs,
        in_specs=[VMEM_SPEC] * (3 + len(more)) + [ANY_SPEC] * len(waited),
        out_specs=VMEM_SPEC if added is None else [VMEM_SPEC] * 2,
        cost_estimate=cost(4 * rows * D * weight.shape[1], 5 << 20),
        name="spread",
    )(*grads, weight, *more, *waited)


def pack_queries(w_query, w_key, w_value):
    rows, width = w_query.shape

    def kernel(q, k, v, qkv):
        qkv[...] = jnp.zeros_like(qkv)
        for at, ref in enumerate((q, k, v)):
            qkv[:, at * PAD : at * PAD + width] = ref[...]

    return pl.pallas_call(
        kernel,
        out_shape=struct((rows, 3 * PAD), bf16),
        in_specs=[VMEM_SPEC] * 3,
        out_specs=VMEM_SPEC,
        cost_estimate=cost(rows * PAD, rows * PAD * 8),
        name="pack_queries",
    )(w_query, w_key, w_value)


def pack_weights(w_up, w_out, w_down, waited):
    rows, hidden = w_up.shape
    width = w_out.shape[0]

    def kernel(up, out, down, _, own):
        own[:, :hidden] = up[...]
        own[:, hidden : hidden + PAD] = jnp.zeros((rows, PAD), bf16)
        own[:, hidden : hidden + width] = out[...].T
        own[:, hidden + PAD :] = down[...].T

    return pl.pallas_call(
        kernel,
        out_shape=struct((rows, 2 * hidden + PAD), bf16),
        in_specs=[VMEM_SPEC] * 3 + [ANY_SPEC],
        out_specs=VMEM_SPEC,
        cost_estimate=cost(rows * hidden, 2 << 20),
        name="pack_weights",
    )(w_up, w_out, w_down, waited)


def pair_weights(own, beyond, hidden, waited):
    rows, width = own.shape
    starts = (0, hidden, hidden + PAD, width)

    def kernel(a, b, *refs):
        out = refs[-1]
        for at, end in zip(starts, starts[1:]):
            out[:, 2 * at : at + end] = a[:, at:end]
            out[:, at + end : 2 * end] = b[:, at:end]

    return pl.pallas_call(
        kernel,
        out_shape=struct((rows, 2 * width), bf16),
        in_specs=[VMEM_SPEC] * 2 + [ANY_SPEC] * len(waited),
        out_specs=VMEM_SPEC,
        cost_estimate=cost(rows * width, 4 * rows * width),
        name="pair_weights",
    )(own, beyond, *waited)


def project_in(xs, weights, bias):
    rows = xs[0].shape[0]
    pieces = len(xs)
    sources = len(weights)
    ordered = sources > 1
    bits, far = (2, 4) if ordered else (1, 1)
    part = D // (bits * far)
    wide = weights[0].shape[1]

    def kernel(*refs):
        refs = list(refs)
        ins = [refs.pop(0) for _ in range(pieces)]
        shards = [refs.pop(0) for _ in range(sources)]
        b = refs.pop(0)
        outs = [refs.pop(0) for _ in range(pieces)]
        turned_outs = [refs.pop(0) for _ in range(pieces)]
        whole_out, x_buf, w, out_buf, turned, sems, w_sems, out_sems = refs
        here = lax.axis_index("dp") if ordered else 0
        copies = [
            pltpu.make_async_copy(ins[s], x_buf.at[s], sems.at[s]) for s in range(pieces)
        ]
        fetched = []
        for at in range(sources):
            row = ring_member(RING_STEPS[at]) * part if ordered else 0
            fetched.append(
                pltpu.make_async_copy(
                    shards[at],
                    w.at[pl.ds(pl.multiple_of(row, 16), shards[at].shape[0]), :],
                    w_sems.at[at],
                )
            )
        for copy in fetched + copies:
            copy.start()
        for copy in fetched:
            copy.wait()
        leaving = []

        def leave(ref, to):
            copy = pltpu.make_async_copy(ref, to, out_sems.at[len(leaving)])
            copy.start()
            leaving.append(copy)

        leave(w, whole_out)
        for s in range(pieces):
            copies[s].wait()
            for c in range(0, wide, PAD):
                cols = slice(c, c + PAD)
                out_buf[s, :, cols] = (
                    contract(x_buf[s], w[:, cols], (1, 0)) + b[:, cols]
                ).astype(bf16)
            leave(out_buf.at[s], outs[s])
            for n in range(D // LANES):
                span = slice(n * LANES, (n + 1) * LANES)
                turned[s, span, :] = x_buf[s, :, span].T
            for k in range(bits):
                for z in range(far):
                    row = (here ^ (2 * z + k)) * part if ordered else 0
                    leave(
                        turned.at[s, pl.ds(pl.multiple_of(row, 16), part), :],
                        turned_outs[s].at[k, z],
                    )
        for copy in leaving:
            copy.wait()

    results = pl.pallas_call(
        kernel,
        out_shape=[struct((rows, wide), bf16)] * pieces
        + [struct((bits, far, part, rows), bf16)] * pieces
        + [struct((D, wide), bf16)],
        in_specs=[ANY_SPEC] * (pieces + sources) + [VMEM_SPEC],
        out_specs=[ANY_SPEC] * (2 * pieces + 1),
        scratch_shapes=[
            pltpu.VMEM((pieces, rows, D), bf16),
            pltpu.VMEM((D, wide), bf16),
            pltpu.VMEM((pieces, rows, wide), bf16),
            pltpu.VMEM((pieces, D, rows), bf16),
            pltpu.SemaphoreType.DMA((pieces,)),
            pltpu.SemaphoreType.DMA((sources,)),
            pltpu.SemaphoreType.DMA((1 + pieces * (1 + bits * far),)),
        ],
        cost_estimate=cost(4 * pieces * rows * D * wide, 24 << 20, 0, 1),
        name="project_in",
    )(*xs, *weights, bias)
    return results[:pieces], results[pieces : 2 * pieces], results[2 * pieces]


def padded(array):
    return jnp.pad(array, ((0, 0), (0, PAD - array.shape[1])))


def dot(a, b, dims=(1, 0)):
    return contract(a, b, dims)


def per_device(
    hidden_in,
    grad_out,
    w_query,
    b_query,
    w_key,
    w_value,
    b_value,
    w_out,
    b_out,
    gain_one,
    shift_one,
    w_up,
    b_up,
    w_down,
    b_down,
    gain_two,
    shift_two,
    lengths,
    global_raw,
    random_raw,
):
    own_rows = hidden_in.shape[0]
    me = lax.axis_index("tensor")
    teams = lax.axis_size("tensor")
    members = lax.axis_size("dp")
    width = w_query.shape[1]
    heads = width // HD
    hidden = w_up.shape[1]

    table, bias = block_tables(lengths, global_raw, random_raw, own_rows // BLK, teams)

    qkv_b = jnp.concatenate(
        [jnp.pad(b_query, (0, PAD - width)), jnp.zeros((PAD,), f32), jnp.pad(b_value, (0, PAD - width))]
    )
    halved = members == 8
    if halved:
        queries = pack_queries(w_query, w_key, w_value)
        own = pack_weights(w_up, w_out, w_down, queries)
        qkv_pieces = ring_pieces(queries)
        beyond_own = swap(own, 2)
        shard = pair_weights(own, beyond_own, hidden, qkv_pieces[GATE:])
    else:
        qkv_shard = jnp.concatenate([padded(w_query), padded(w_key), padded(w_value)], axis=1)
        qkv_pieces = [lax.all_gather(qkv_shard, "dp", axis=0, tiled=True)]
        shard = jnp.concatenate([w_up, padded(w_out.T), w_down.T], axis=1)
        weights = lax.all_gather(shard, ("dp", "tensor"), axis=0, tiled=False)
        weights = jnp.swapaxes(weights.reshape(members, teams, *shard.shape), 0, 1)
        weights = [weights.reshape(teams, D, shard.shape[1])]

    x2 = swap(held(hidden_in, (beyond_own,)) if halved else hidden_in, 2)
    x1 = swap(hidden_in, 1)
    x3 = swap(x2, 1)
    qkv, x_turned, qkv_w = project_in([hidden_in, x1, x2, x3], qkv_pieces, qkv_b[None])
    far_mixed, (t2, t3) = attend_forward(qkv, table, bias, heads, (2, 3))
    far_mixed = swap(far_mixed, 2)
    near_mixed, (t0, t1) = attend_forward(qkv, table, bias, heads, (0, 1))
    r1 = swap(near_mixed[1], 1)
    r3 = swap(far_mixed[1], 1)
    if halved:

        weights = ring_pieces(shard)
        weights = weights + [swap(piece, 1) for piece in weights]

    results = layer_rows(
        [(near_mixed, 0), (r1, None), (far_mixed, 0), (r3, None)],
        hidden_in,
        grad_out,
        weights,
        (
            jnp.stack([b_out, gain_one, shift_one, b_down, gain_two, shift_two]),
            b_up.reshape(teams, hidden),
        ),
        lengths,
    )
    layer_out, near_rows, far_rows, turned = results[:4]
    backs = results[4 : 4 + teams]
    after_low, small = results[4 + teams :]
    ups = [backs[0]] + [swap(backs[s], s) for s in range(1, teams)]
    totals = [t0, t1, t2, t3]
    before = attend_backward(qkv, ups[:1], totals[:1], table, bias, heads, (0,))

    next_rows, next_turned = swap(far_rows, 1), swap(turned, 1)
    down_group = (
        [(turned, 1), (next_turned, 1)],
        [[(near_rows, 0), (near_rows, 1)], [(next_rows, 0), (next_rows, 1)]],
    )
    up_group = (
        [(turned, 0), (next_turned, 0)],
        [[(near_rows, 2), (near_rows, 3)], [(next_rows, 2), (next_rows, 3)]],
    )
    out_group = (
        [(turned, 2), (next_turned, 2)],
        [[(near_mixed, 0), (far_mixed, 0)], [(near_mixed, 1), (far_mixed, 1)]],
    )
    if halved:
        (down_gone,) = row_dot([down_group], 2, "far", (before[0], *ups[1:]))
        down_blocks = far_exchange(down_gone)
        up_quads = row_dot([up_group, out_group], 2, "quads", (down_gone,))
        up_gone = up_quads[3]
        up_away = [swap(up_quads[1], 2), dp_swap(up_quads[2], 1), swap_both(up_gone)]
        waited = (up_gone,)
    else:
        down_sums = row_dot([down_group], 2)[0].reshape(2, D, -1)
        up_sums = row_dot([up_group, out_group], 2)[0].reshape(2, D, -1)
        waited = ()
    results = attend_backward(
        qkv,
        ups[1:],
        totals[1:],
        table,
        bias,
        heads,
        (1, 2, 3),
        small,
        waited,
        (before[1], before[2], before[0]),
    )
    grads, tail = results[:4], results[4]
    qkv_group = ([(x[None], 0) for x in x_turned], [[(g[None], 0)] for g in grads])
    if halved:
        kept, gone = row_dot([qkv_group], 1, "bits", (), tail)
        away = dp_swap(gone, 1)
        parts = spread([grads[3], grads[1]], qkv_w, waited=(gone,))
        spread_away = swap(parts, 1)
        up_blocks = joined_sums([a[0, 0] for a in (up_quads[0], *up_away)], (parts,))
        up_arrived = far_exchange(up_blocks)
        beyond, here = spread([grads[2], grads[0]], qkv_w, spread_away, after_low, (up_blocks,))
        beyond_away = swap(beyond, 2)
        down_here, down_next = fold(down_blocks, (beyond,))
        down_away = swap(down_next, 2)
        blocks = joined_sums([kept[0, 0], away[0, 0]], (down_next,))
        arrived = far_exchange(blocks)
        qkv_part = jnp.sum(arrived.astype(f32), axis=0)
        down_here, down_next = plus(down_here, down_away, (blocks,), 2)
        down_away = dp_swap(down_next, 1)
        down_part = down_here[0].astype(f32) + down_away[0].astype(f32)
        up_part = jnp.sum(up_arrived.astype(f32), axis=0)
        qkv_part, small = qkv_part[:-16], qkv_part[-16:]
    else:
        blocks = row_dot([qkv_group], 1)[0].reshape(D, -1)
        qkv_part = dp_scatter_sum(blocks)
        small = lax.psum(tail.astype(f32), "dp")
        spread_away = swap(spread([grads[3], grads[1]], qkv_w), 1)
        beyond, here = spread([grads[2], grads[0]], qkv_w, spread_away, after_low)
        beyond_away = swap(beyond, 2)
        down_part = dp_scatter_sum(down_sums[0] + swap(down_sums[1], 2))
        up_part = dp_scatter_sum(up_sums[0] + swap(up_sums[1], 2))
    grad_in = here + beyond_away.astype(f32)

    bias_row = small[SUM_ROW]
    return (
        layer_out,
        grad_in,
        qkv_part[:, :width],
        bias_row[:width],
        qkv_part[:, PAD : PAD + width],
        qkv_part[:, 2 * PAD : 2 * PAD + width],
        bias_row[2 * PAD : 2 * PAD + width],
        up_part[:, hidden : hidden + width].T,
        small[5],
        small[3],
        small[4],
        up_part[:, :hidden],
        jnp.take(small[6 : 6 + teams], me, axis=0),
        down_part.T,
        small[2],
        small[0],
        small[1],
    )


def solution(mesh):
    in_specs = (
        P(("dp", "tensor"), None),
        P(("dp", "tensor"), None),
        P("dp", "tensor"),
        P("tensor"),
        P("dp", "tensor"),
        P("dp", "tensor"),
        P("tensor"),
        P("tensor", "dp"),
        P(),
        P(),
        P(),
        P("dp", "tensor"),
        P(),
        P("tensor", "dp"),
        P(),
        P(),
        P(),
        P("dp"),
        P("dp", None),
        P("dp", None, None),
    )
    out_specs = (
        P(("dp", "tensor"), None),
        P(("dp", "tensor"), None),
        P("dp", "tensor"),
        P("tensor"),
        P("dp", "tensor"),
        P("dp", "tensor"),
        P("tensor"),
        P("tensor", "dp"),
        P(),
        P(),
        P(),
        P("dp", "tensor"),
        P("tensor"),
        P("tensor", "dp"),
        P(),
        P(),
        P(),
    )
    return jax.shard_map(
        per_device, mesh=mesh, in_specs=in_specs, out_specs=out_specs, check_vma=False
    )
```

```python
from functools import partial

import jax
import jax.numpy as jnp
from jax import lax
from jax.experimental import pallas as pl
from jax.experimental.pallas import tpu as pltpu
from jax.sharding import PartitionSpec as P

D = 768
HD = 64
FF = 3072
BLK = 64
GLOB = 2
RAND = 3
LMAX = 2048
NB = 32
KEYS = (3 + GLOB + RAND) * BLK
PAD = 256
LANES = 128
SUM_ROW = 10
ORDER = (0, 1, 2, 3)
SUM_ROWS = 16
BELOW = SUM_ROWS * (D // PAD)
GATE = 5

masked_score = -1e30
EPSILON = 1e-12
f32 = jnp.float32
bf16 = jnp.bfloat16


def swap(array, bit):
    size = lax.axis_size("tensor")
    return lax.ppermute(array, "tensor", [(t, t ^ bit) for t in range(size)])


def dp_swap(array, bit):
    size = lax.axis_size("dp")
    return lax.ppermute(array, "dp", [(t, t ^ bit) for t in range(size)])


def swap_both(array):
    size = lax.axis_size("dp") * 4
    axes = ("dp", "tensor")
    return lax.ppermute(array, axes, [(t, t ^ 6) for t in range(size)])


def ring_order(size):
    return list(range(0, size, 2)) + list(range(size - 1, 0, -2))


def ring_member(steps):
    size = lax.axis_size("dp")
    me = lax.axis_index("dp")
    place = jnp.where(me % 2 == 0, me // 2, size - 1 - me // 2)
    place = (place + steps + size) % size
    return jnp.where(place < size // 2, 2 * place, 2 * (size - 1 - place) + 1)


def ring_send(array, step):
    size = lax.axis_size("dp")
    order = ring_order(size)
    return lax.ppermute(
        array, "dp", [(order[i], order[(i + step) % size]) for i in range(size)]
    )


RING_STEPS = (0, -1, 1, -2, 2, -3, 3, -4)


def ring_pieces(shard):
    pieces = [shard]
    ahead, behind = shard, shard
    for step in range(1, 5):
        ahead = ring_send(ahead, 1)
        pieces.append(ahead)
        if step < 4:
            behind = ring_send(behind, -1)
            pieces.append(behind)
    return pieces


def far_exchange(blocks):
    groups = [[2 * f + n for f in range(4)] for n in range(2)]
    return lax.all_to_all(blocks, "dp", 0, 0, axis_index_groups=groups, tiled=True)


def dp_scatter_sum(sums):
    size = lax.axis_size("dp")
    if size != 8:
        return lax.psum_scatter(sums, "dp", scatter_dimension=0, tiled=True).astype(f32)
    blocks = lax.all_to_all(sums.reshape(size, -1, sums.shape[1]), "dp", 0, 0, tiled=True)
    return jnp.sum(blocks.astype(f32), axis=0)


def sum_over(vector, dp_only=False):
    if not dp_only:
        bit = 1
        while bit < lax.axis_size("tensor"):
            vector = vector + swap(vector, bit)
            bit *= 2
    bit = 1
    while bit < lax.axis_size("dp"):
        vector = vector + dp_swap(vector, bit)
        bit *= 2
    return vector


def block_tables(lengths, global_raw, random_raw, own_blocks, pieces):
    count = own_blocks * pieces

    def kernel(length_ref, global_ref, random_ref, table, bias):
        me = lax.axis_index("tensor")
        lane = lax.broadcasted_iota(jnp.int32, (1, KEYS), 1)
        slot = lane // BLK
        within = lane % BLK
        wide = lax.broadcasted_iota(jnp.int32, (own_blocks, LANES), 1)
        row = lax.broadcasted_iota(jnp.int32, (own_blocks, 1), 0)
        for s in range(pieces):
            first = (s ^ me) * own_blocks
            seq = first // NB
            start = first - seq * NB
            length = length_ref[seq]
            live = (length + BLK - 1) // BLK
            raw = random_ref[seq, pl.ds(pl.multiple_of(start, 8), own_blocks), :]
            rest = raw - live * jnp.floor(raw.astype(f32) / live.astype(f32)).astype(jnp.int32)
            rest = jnp.where(rest < 0, rest + live, rest)
            rest = jnp.where(rest >= live, rest - live, rest)
            block = row + start
            ids = [jnp.maximum(block - 1, 0), block, jnp.minimum(block + 1, NB - 1)]
            ids += [jnp.full((own_blocks, 1), lax.rem(global_ref[seq, j], live)) for j in range(GLOB)]
            ids += [rest[:, r : r + 1] for r in range(RAND)]
            spread_ids = jnp.zeros((own_blocks, KEYS), jnp.int32)
            packed = jnp.zeros((own_blocks, LANES), jnp.int32)
            for j, own in enumerate(ids):
                spread_ids = jnp.where(slot == j, own, spread_ids)
                there = own + seq * NB
                there = ((there // own_blocks) ^ me) * own_blocks + there % own_blocks
                packed = jnp.where(wide == j, there, packed)
            table[s * own_blocks : (s + 1) * own_blocks, :] = packed
            lost = (spread_ids * BLK + within) >= length
            lost = lost | ((slot == 0) & (block == 0)) | ((slot == 2) & (block == NB - 1))
            bias[s * own_blocks : (s + 1) * own_blocks, :] = jnp.where(lost, masked_score, 0.0).astype(f32)

    smem = pl.BlockSpec(memory_space=pltpu.SMEM)
    vmem = pl.BlockSpec(memory_space=pltpu.VMEM)
    return pl.pallas_call(
        kernel,
        out_shape=[
            jax.ShapeDtypeStruct((count, LANES), jnp.int32),
            jax.ShapeDtypeStruct((count, KEYS), f32),
        ],
        in_specs=[smem, smem, vmem],
        out_specs=[vmem, vmem],
        cost_estimate=cost(count * KEYS * 16, count * KEYS * 4),
        name="block_tables",
    )(lengths, global_raw, random_raw)


def head_masks(heads, scale, dtype):
    lane = lax.broadcasted_iota(jnp.int32, (1, PAD), 1)
    return [
        jnp.where((lane >= h * HD) & (lane < (h + 1) * HD), scale, 0.0).astype(dtype)
        for h in range(heads)
    ]


def stacked_heads(rows, masks):
    return jnp.concatenate([rows * mask for mask in masks], axis=0)


def unstacked_heads(stacked, masks):
    rows = stacked.shape[0] // len(masks)
    total = stacked[:rows] * masks[0]
    for h in range(1, len(masks)):
        total = total + stacked[h * rows : (h + 1) * rows] * masks[h]
    return total


def key_blocks(ref, table, block, column):
    return jnp.concatenate(
        [
            ref[pl.ds(pl.multiple_of(table[block, j] * BLK, BLK), BLK), column : column + PAD]
            for j in range(KEYS // BLK)
        ],
        axis=0,
    )


def contract(a, b, dims):
    return lax.dot_general(a, b, ((dims[:1], dims[1:]), ((), ())), preferred_element_type=f32)


def attend_kernel(heads, chosen, pieces, own_blocks, table, *refs):
    parts = refs[:pieces]
    bias = refs[pieces]
    out = refs[pieces + 1]
    totals = refs[pieces + 2 : pieces + 2 + len(chosen)]
    rows, sems = refs[pieces + 2 + len(chosen) :]
    own_rows = own_blocks * BLK
    copies = [
        pltpu.make_async_copy(
            parts[s], rows.at[pl.ds(s * own_rows, own_rows)], sems.at[s]
        )
        for s in range(pieces)
    ]
    for copy in copies:
        copy.start()
    for copy in copies:
        copy.wait()
    query_masks = head_masks(heads, HD**-0.5, bf16)
    out_masks = head_masks(heads, 1.0, f32)
    lane = lax.broadcasted_iota(jnp.int32, (BLK, LANES), 1)

    side = 2
    count = len(chosen) * side

    def step(step_at, carry):
        blocks, held = [], [{} for _ in range(count)]
        for at in range(count):
            i = step_at * side + at // len(chosen)
            piece = at % len(chosen)
            blocks.append((piece, i, chosen[piece] * own_blocks + i))

        def scored(at):
            block = blocks[at][2]
            here = pl.ds(pl.multiple_of(block * BLK, BLK), BLK)
            queries = stacked_heads(rows[here, 0:PAD], query_masks)
            keys = key_blocks(rows, table, block, PAD)
            held[at]["scores"] = contract(queries, keys, (1, 1))

        def weighed(at):
            has = held[at]
            masked = bias[pl.ds(blocks[at][2], 1), :]
            low, has["total"], has["log_total"] = [], [], []
            for h in range(heads):
                scores = has["scores"][h * BLK : (h + 1) * BLK] + masked
                top = jnp.max(scores, axis=-1, keepdims=True)
                weights = jnp.exp(scores - top)
                total = jnp.sum(weights, axis=-1, keepdims=True)
                low.append(weights.astype(bf16))
                has["total"].append(total)
                has["log_total"].append(top + jnp.log(total))
            has["weights"] = jnp.concatenate(low, axis=0)

        def mixed(at):
            piece, i, block = blocks[at]
            has = held[at]
            values = key_blocks(rows, table, block, 2 * PAD)
            outs = contract(has["weights"], values, (1, 0))
            start = pl.ds(pl.multiple_of(i * BLK, BLK), BLK)
            kept = jnp.zeros((BLK, LANES), f32)
            total = jnp.zeros((BLK, PAD), f32)
            for h in range(heads):
                total = total + outs[h * BLK : (h + 1) * BLK] * (out_masks[h] / has["total"][h])
                kept = jnp.where(lane == h, has["log_total"][h], kept)
            out[piece, start, :] = total.astype(bf16)
            totals[piece][start, :] = kept

        stages = (scored, weighed, mixed)
        for turn in range(count + len(stages) - 1):
            for k in range(len(stages)):
                if 0 <= turn - k < count:
                    stages[k](turn - k)
        return carry

    lax.fori_loop(0, own_blocks // side, step, 0)


def attend_forward(parts, table, bias, heads, chosen):
    own_rows = parts[0].shape[0]
    pieces = len(parts)
    own_blocks = own_rows // BLK
    n = len(chosen)
    vmem = pl.BlockSpec(memory_space=pltpu.VMEM)
    work = n * own_rows * KEYS * heads
    results = pl.pallas_call(
        partial(attend_kernel, heads, chosen, pieces, own_blocks),
        out_shape=[jax.ShapeDtypeStruct((n, own_rows, PAD), bf16)]
        + [jax.ShapeDtypeStruct((own_rows, LANES), f32)] * n,
        in_specs=[pl.BlockSpec(memory_space=pltpu.SMEM)]
        + [pl.BlockSpec(memory_space=pl.ANY)] * pieces
        + [vmem],
        out_specs=[vmem] * (1 + n),
        scratch_shapes=[
            pltpu.VMEM((pieces * own_rows, 3 * PAD), bf16),
            pltpu.SemaphoreType.DMA((pieces,)),
        ],
        cost_estimate=cost(48 * work * HD, 16 << 20, 4 * work, 1),
        name="attend_forward",
    )(table, *parts, bias)
    return results[0], results[1:]


def attend_back_kernel(heads, chosen, pieces, own_blocks, waited, carried, table, *refs):
    refs = list(refs)

    def take(count):
        taken = refs[:count]
        del refs[:count]
        return taken

    parts = take(pieces)
    ups = take(len(chosen))
    totals = take(len(chosen))
    (bias,) = take(1)
    take(waited)
    if carried:
        key_before, value_before = take(2)
        query_before = take(pieces - len(chosen))
        (small_ref,) = take(1)
        outs = take(pieces)
        (tail,) = take(1)
        key_sum, value_sum, key_kept, value_kept, row_sums = take(5)
    else:
        outs = take(len(chosen))
        key_sum, value_sum = take(2)
    rows, up_rows, sems = refs
    own_rows = own_blocks * BLK
    copies = [
        pltpu.make_async_copy(parts[s], rows.at[pl.ds(s * own_rows, own_rows)], sems.at[s])
        for s in range(pieces)
    ] + [
        pltpu.make_async_copy(ups[at], up_rows.at[at], sems.at[pieces + at])
        for at in range(len(chosen))
    ]
    late = []
    if carried:
        late = [
            pltpu.make_async_copy(key_before, key_kept, sems.at[pieces + len(chosen)]),
            pltpu.make_async_copy(value_before, value_kept, sems.at[pieces + len(chosen) + 1]),
        ]
    for copy in copies + late:
        copy.start()
    key_sum[...] = jnp.zeros_like(key_sum)
    value_sum[...] = jnp.zeros_like(value_sum)
    for copy in copies:
        copy.wait()
    query_masks = head_masks(heads, HD**-0.5, bf16)
    up_masks = head_masks(heads, 1.0, bf16)
    out_masks = head_masks(heads, HD**-0.5, f32)

    side = 2 if len(chosen) == 1 else 1

    count = len(chosen) * side

    def step(step_at, carry):
        blocks, held = [], [{} for _ in range(count)]
        for at in range(count):
            i = step_at * side + at // len(chosen)
            piece = at % len(chosen)
            blocks.append((piece, i, chosen[piece] * own_blocks + i))

        def scored(at):
            piece, i, block = blocks[at]
            start = pl.multiple_of(i * BLK, BLK)
            here = pl.ds(pl.multiple_of(block * BLK, BLK), BLK)
            has = held[at]
            has["queries"] = stacked_heads(rows[here, 0:PAD], query_masks)
            has["upstream"] = stacked_heads(up_rows[piece, pl.ds(start, BLK), :], up_masks)
            has["keys"] = key_blocks(rows, table, block, PAD)
            values = key_blocks(rows, table, block, 2 * PAD)
            has["scores"] = contract(has["queries"], has["keys"], (1, 1))
            has["grad_weights"] = contract(has["upstream"], values, (1, 1))

        def weighed(at):
            piece, i, block = blocks[at]
            has = held[at]
            kept = totals[piece][pl.ds(pl.multiple_of(i * BLK, BLK), BLK), :]
            masked = bias[pl.ds(block, 1), :]
            low, grad = [], []
            for h in range(heads):
                span = slice(h * BLK, (h + 1) * BLK)
                weights = jnp.exp(has["scores"][span] + (masked - kept[:, h : h + 1]))
                grad_weights = has["grad_weights"][span]
                inner = jnp.sum(weights * grad_weights, axis=-1, keepdims=True)
                low.append(weights.astype(bf16))
                grad.append((weights * (grad_weights - inner)).astype(bf16))
            has["weights"] = jnp.concatenate(low, axis=0)
            has["grad_scores"] = jnp.concatenate(grad, axis=0)

        def spread_back(at):
            piece, i, block = blocks[at]
            has = held[at]
            to = outs[chosen[piece]] if carried else outs[piece]
            grad_query = contract(has["grad_scores"], has["keys"], (1, 0))
            to[pl.ds(pl.multiple_of(i * BLK, BLK), BLK), 0:PAD] = unstacked_heads(
                grad_query, out_masks
            ).astype(bf16)
            has["key_part"] = contract(has["grad_scores"], has["queries"], (0, 0))
            has["value_part"] = contract(has["weights"], has["upstream"], (0, 0))

        def summed(at):
            block, has = blocks[at][2], held[at]
            for j in range(KEYS // BLK):
                there = pl.ds(pl.multiple_of(table[block, j] * BLK, BLK), BLK)
                key_sum[there, :] += has["key_part"][j * BLK : (j + 1) * BLK]
                value_sum[there, :] += has["value_part"][j * BLK : (j + 1) * BLK]

        stages = (scored, weighed, spread_back, summed)
        for turn in range(count + len(stages) - 1):
            for k in ORDER:
                at = turn - k
                if 0 <= at < count:
                    stages[k](at)
        return carry

    lax.fori_loop(0, own_blocks // side, step, 0)
    if not carried:
        return
    for copy in late:
        copy.wait()
    before = [s for s in range(pieces) if s not in chosen]
    for at, s in enumerate(before):
        outs[s][:, 0:PAD] = query_before[at][...]
    row_sums[...] = jnp.zeros_like(row_sums)
    for s in range(pieces):

        def finish(i, carry, s=s):
            at = pl.ds(pl.multiple_of(i * BLK, BLK), BLK)
            span = pl.ds(pl.multiple_of(s * own_rows + i * BLK, BLK), BLK)
            outs[s][at, PAD : 2 * PAD] = (key_sum[span, :] + key_kept[span, :]).astype(bf16)
            outs[s][at, 2 * PAD : 3 * PAD] = (value_sum[span, :] + value_kept[span, :]).astype(bf16)
            whole = outs[s][at, :].astype(f32)
            row_sums[...] += jnp.sum(whole.reshape(BLK // 8, 8, 3 * PAD), axis=0)
            return carry

        lax.fori_loop(0, own_blocks, finish, 0)
    slot = lax.broadcasted_iota(jnp.int32, tail.shape, 0)
    whole = jnp.sum(row_sums[...], axis=0, keepdims=True)
    small = small_ref[...]
    for at in range(len(chosen)):
        parts = [
            up_rows[at, own_rows + k * SUM_ROWS : own_rows + (k + 1) * SUM_ROWS, :]
            for k in range(BELOW // SUM_ROWS)
        ]
        small = small + jnp.concatenate(parts, axis=1).astype(f32)
    tail[...] = jnp.where(slot == SUM_ROW, whole, small).astype(bf16)


def attend_backward(parts, ups, totals, table, bias, heads, chosen, small=None, waited=(), before=None):
    own_rows = parts[0].shape[0]
    pieces = len(parts)
    n = len(chosen)
    own_blocks = own_rows // BLK
    vmem = pl.BlockSpec(memory_space=pltpu.VMEM)
    anyspace = pl.BlockSpec(memory_space=pl.ANY)
    work = n * own_rows * KEYS * heads
    sum_shape = (pieces * own_rows, PAD)
    if before is None:
        outs = [((own_rows, PAD), bf16)] * n + [(sum_shape, f32)] * 2
        extra, extra_specs, scratch = [], [], []
    else:
        outs = [((own_rows, 3 * PAD), bf16)] * pieces + [((16, 3 * PAD), bf16)]
        extra = [*before, small]
        extra_specs = [anyspace] * 2 + [vmem] * (len(before) - 1)
        scratch = [pltpu.VMEM(sum_shape, f32)] * 4 + [pltpu.VMEM((8, 3 * PAD), f32)]
    return pl.pallas_call(
        partial(
            attend_back_kernel, heads, chosen, pieces, own_blocks, len(waited), before is not None
        ),
        out_shape=[jax.ShapeDtypeStruct(*out) for out in outs],
        in_specs=[pl.BlockSpec(memory_space=pltpu.SMEM)]
        + [anyspace] * (pieces + n)
        + [vmem] * (n + 1)
        + [anyspace] * len(waited)
        + extra_specs,
        out_specs=[vmem] * len(outs),
        scratch_shapes=scratch
        + [
            pltpu.VMEM((pieces * own_rows, 3 * PAD), bf16),
            pltpu.VMEM((n, own_rows + BELOW, PAD), bf16),
            pltpu.SemaphoreType.DMA((pieces + n + 2,)),
        ],
        cost_estimate=cost(30 * work * HD, 12 << 20, work),
        name="attend_backward",
    )(table, *parts, *ups, *totals, bias, *waited, *extra)


VMEM_SPEC = pl.BlockSpec(memory_space=pltpu.VMEM)
ANY_SPEC = pl.BlockSpec(memory_space=pl.ANY)
SMEM_SPEC = pl.BlockSpec(memory_space=pltpu.SMEM)
COST_CUT = 64
GELU_A = 0.7978845608028654
GELU_B = 0.044715


def cost(flops, size, transcendentals=0, cut=None):
    cut = cut or COST_CUT
    return pl.CostEstimate(
        flops=flops // cut, bytes_accessed=size // cut, transcendentals=transcendentals // cut
    )


def struct(shape, dtype):
    return jax.ShapeDtypeStruct(shape, dtype)


def row_stats(values):
    centred = values - jnp.mean(values, axis=-1, keepdims=True)
    inv_std = lax.rsqrt(jnp.mean(centred * centred, axis=-1, keepdims=True) + EPSILON)
    return centred * inv_std, inv_std


def norm_backward(upstream, scaled, inv_std, gain):
    weighted = upstream * gain
    inner = jnp.mean(weighted * scaled, axis=-1, keepdims=True)
    return inv_std * (weighted - jnp.mean(weighted, axis=-1, keepdims=True) - scaled * inner)


def column_sum(array):
    return jnp.sum(array.reshape(array.shape[0] // 8, 8, array.shape[1]), axis=0)


def rows_kernel(places, sources, length, *refs):
    teams = len(places)
    refs = list(refs)

    def take(count):
        taken = refs[:count]
        del refs[:count]
        return taken

    mixed = take(teams)
    x_in, g_in = take(2)
    weights = take(sources)
    vectors, b_up = take(2)
    b_out, g1, c1, b_down, g2, c2 = [vectors.at[k : k + 1, :] for k in range(6)]
    layer_out, near_out, far_out, turned_out = take(4)
    back_out = take(teams)
    after_out, small = take(2)
    (
        o_buf,
        x_buf,
        g_buf,
        out_w,
        up_w,
        down_w,
        scaled_buf,
        inv_buf,
        wide_buf,
        low_buf,
        act_buf,
        slope_buf,
        last_buf,
        turned_buf,
        sums,
        up_sums,
        in_sems,
        w_sems,
        out_sems,
    ) = refs
    rows = x_in.shape[0]
    hidden = up_w.shape[2]
    tile, cut = 64, 256
    me = lax.axis_index("tensor")
    ring = sources > 1

    first = []
    for s in range(teams):
        source = mixed[s] if places[s] is None else mixed[s].at[places[s]]
        first.append(
            pltpu.make_async_copy(source, o_buf.at[s, pl.ds(0, x_in.shape[0]), :], in_sems.at[s])
        )
    first.append(pltpu.make_async_copy(x_in, x_buf, in_sems.at[teams]))
    upstream_copy = pltpu.make_async_copy(g_in, g_buf, in_sems.at[teams + 1])
    fetched = ([], [], [])

    def fetch(kind, source, to):
        sem = w_sems.at[kind, len(fetched[kind])]
        fetched[kind].append(pltpu.make_async_copy(source, to, sem))

    wholes = (out_w, up_w, down_w)
    if ring:
        part = weights[0].shape[0]
        spans = ((2 * hidden, PAD), (0, hidden), (2 * hidden + 2 * PAD, hidden))
        for at, piece in enumerate(weights):
            row = pl.multiple_of(ring_member(RING_STEPS[at % 8]) * part, 16)
            for kind, (start, size) in enumerate(spans):
                for pair in range(2):
                    fetch(
                        kind,
                        piece.at[:, pl.ds(start + pair * size, size)],
                        wholes[kind].at[2 * pair + at // 8, pl.ds(row, part), :],
                    )
    else:
        spans = ((hidden, PAD), (0, hidden), (hidden + PAD, hidden))
        for kind, (start, size) in enumerate(spans):
            for s in range(teams):
                fetch(kind, weights[0].at[me ^ s, :, pl.ds(start, size)], wholes[kind].at[s])
    for copy in first + fetched[0] + fetched[1] + fetched[2] + [upstream_copy]:
        copy.start()
    sums[...] = jnp.zeros_like(sums)
    up_sums[...] = jnp.zeros_like(up_sums)
    leaving = []

    def leave(ref, to):
        copy = pltpu.make_async_copy(ref, to, out_sems.at[len(leaving)])
        copy.start()
        leaving.append(copy)

    def leave_turned(k, source, to):
        for n in range(D // LANES):
            span = slice(n * LANES, (n + 1) * LANES)
            turned_buf[k, span, :] = source[:, span].T
        bits, far, part, _ = to.shape
        here = lax.axis_index("dp")
        for b in range(bits):
            for z in range(far):
                row = (here ^ (2 * z + b)) * part if ring else 0
                leave(turned_buf.at[k, pl.ds(pl.multiple_of(row, 16), part), :], to.at[b, z])

    def tiles(body):
        def step(i, carry):
            body(i, pl.ds(pl.multiple_of(i * tile, tile), tile))
            return carry

        lax.fori_loop(0, rows // tile, step, 0)

    for copy in first + fetched[0]:
        copy.wait()
    for n in range(D // cut):
        cols = slice(n * cut, (n + 1) * cut)
        total = contract(o_buf[0, :rows, :], out_w[0, cols, :], (1, 1))
        for s in range(1, teams):
            total = total + contract(o_buf[s, :rows, :], out_w[s, cols, :], (1, 1))
        wide_buf[:, cols] = total

    def first_norm(i, at):
        after = x_buf[at, :].astype(f32) + wide_buf[at, :] + b_out[...]
        scaled, inv_std = row_stats(after)
        scaled_buf[at, :] = scaled
        inv_buf[at, :] = jnp.broadcast_to(inv_std, (tile, LANES))
        low_buf[at, :] = (scaled * g1[...] + c1[...]).astype(bf16)

    tiles(first_norm)
    leave_turned(0, low_buf, turned_out.at[0])
    for copy in fetched[1]:
        copy.wait()

    def up_step(s, carry):
        bias = b_up[pl.ds(s ^ me, 1), :]
        for c in range(hidden // cut):
            cols = slice(c * cut, (c + 1) * cut)
            u = contract(low_buf[...], up_w[s, :, cols], (1, 0)) + bias[:, cols]
            cubic = (GELU_A * GELU_B) * (u * u)
            t = jnp.tanh(u * (GELU_A + cubic))
            half = 0.5 + 0.5 * t
            act = u * half
            act_buf[s, :, cols] = act.astype(bf16)
            slope_buf[s, :, cols] = (
                half + act * ((1.0 - t) * (GELU_A + 3.0 * cubic))
            ).astype(bf16)
        return carry

    lax.fori_loop(0, teams, up_step, 0)
    for s in range(teams):
        leave(act_buf.at[s], (far_out if s % 2 else near_out).at[s // 2])
    for copy in fetched[2]:
        copy.wait()
    upstream_copy.wait()
    for n in range(D // cut):
        cols = slice(n * cut, (n + 1) * cut)
        total = contract(act_buf[0], down_w[0, cols, :], (1, 1))
        for s in range(1, teams):
            total = total + contract(act_buf[s], down_w[s, cols, :], (1, 1))
        wide_buf[:, cols] = total
    start = me * rows
    seq = start // LMAX
    live = length[seq] - (start - seq * LMAX)

    def second_norm(i, at):
        z = (scaled_buf[at, :] * g1[...] + c1[...]) + wide_buf[at, :] + b_down[...]
        scaled, inv_std = row_stats(z)
        x_buf[at, :] = (scaled * g2[...] + c2[...]).astype(bf16)
        row = lax.broadcasted_iota(jnp.int32, (tile, D), 0) + i * tile
        upstream = jnp.where(row < live, g_buf[at, :].astype(f32), 0.0)
        grad = norm_backward(upstream, scaled, inv_std, g2[...]).astype(bf16)
        g_buf[at, :] = grad
        sums[0:8, :] += column_sum(upstream * scaled)
        sums[8:16, :] += column_sum(upstream)
        sums[16:24, :] += column_sum(grad.astype(f32))

    tiles(second_norm)
    leave(x_buf, layer_out)
    leave_turned(1, g_buf, turned_out.at[1])

    def down_back(s, carry):
        for c in range(hidden // cut):
            cols = slice(c * cut, (c + 1) * cut)
            g = contract(g_buf[...], down_w[s, :, cols], (1, 0))
            g = (g * slope_buf[s, :, cols].astype(f32)).astype(bf16)
            slope_buf[s, :, cols] = g
            up_sums[pl.ds(pl.multiple_of(s * 8, 8), 8), cols] = column_sum(g.astype(f32))
        return carry

    lax.fori_loop(0, teams, down_back, 0)
    for s in range(teams):
        leave(slope_buf.at[s], (far_out if s % 2 else near_out).at[2 + s // 2])
    for n in range(D // cut):
        cols = slice(n * cut, (n + 1) * cut)
        total = contract(slope_buf[0], up_w[0, cols, :], (1, 1))
        for s in range(1, teams):
            total = total + contract(slope_buf[s], up_w[s, cols, :], (1, 1))
        wide_buf[:, cols] = total

    def first_back(i, at):
        upstream = g_buf[at, :].astype(f32) + wide_buf[at, :]
        scaled = scaled_buf[at, :]
        grad = norm_backward(upstream, scaled, inv_buf[at, :][:, :1], g1[...]).astype(bf16)
        last_buf[at, :] = grad
        sums[24:32, :] += column_sum(upstream * scaled)
        sums[32:40, :] += column_sum(upstream)
        sums[40:48, :] += column_sum(grad.astype(f32))

    tiles(first_back)
    leave(last_buf, after_out)
    leave_turned(2, last_buf, turned_out.at[2])
    small[...] = jnp.zeros_like(small)
    for k in range(6):
        small[k : k + 1, :] = jnp.sum(sums[8 * k : 8 * k + 8, :], axis=0, keepdims=True)
    for s in range(teams):
        small[pl.ds(6 + (s ^ me), 1), :] = jnp.sum(
            up_sums[8 * s : 8 * s + 8, :], axis=0, keepdims=True
        )
    for s in (2, 3, 1, 0):
        o_buf[s, :rows, :] = contract(last_buf[...], out_w[s], (1, 0)).astype(bf16)
        for k in range(D // PAD):
            o_buf[s, rows + k * SUM_ROWS : rows + (k + 1) * SUM_ROWS, :] = small[
                :, k * PAD : (k + 1) * PAD
            ].astype(bf16)
        leave(o_buf.at[s], back_out[s])
    for copy in leaving:
        copy.wait()


def layer_rows(mixed, hidden_in, grad_out, weights, vectors, lengths):
    teams = len(mixed)
    rows = hidden_in.shape[0]
    rows_of, b_up = vectors
    hidden = b_up.shape[1]
    half = teams // 2
    low = struct((rows, D), bf16)
    pair = struct((2 * half, rows, hidden), bf16)
    ring = len(weights) > 1
    turned = struct((3, 2, 4, D // 8, rows) if ring else (3, 1, 1, D, rows), bf16)
    return pl.pallas_call(
        partial(rows_kernel, [at for _, at in mixed], len(weights)),
        out_shape=[low, pair, pair, turned]
        + [struct((rows + BELOW, PAD), bf16)] * teams
        + [low, struct((16, D), f32)],
        in_specs=[SMEM_SPEC]
        + [ANY_SPEC] * (teams + 2 + len(weights))
        + [VMEM_SPEC] * 2,
        out_specs=[ANY_SPEC] * (5 + teams) + [VMEM_SPEC],
        scratch_shapes=[
            pltpu.VMEM((teams, rows + BELOW, PAD), bf16),
            pltpu.VMEM((rows, D), bf16),
            pltpu.VMEM((rows, D), bf16),
            pltpu.VMEM((teams, D, PAD), bf16),
            pltpu.VMEM((teams, D, hidden), bf16),
            pltpu.VMEM((teams, D, hidden), bf16),
            pltpu.VMEM((rows, D), f32),
            pltpu.VMEM((rows, LANES), f32),
            pltpu.VMEM((rows, D), f32),
            pltpu.VMEM((rows, D), bf16),
            pltpu.VMEM((teams, rows, hidden), bf16),
            pltpu.VMEM((teams, rows, hidden), bf16),
            pltpu.VMEM((rows, D), bf16),
            pltpu.VMEM((3, D, rows), bf16),
            pltpu.VMEM((48, D), f32),
            pltpu.VMEM((8 * teams, hidden), f32),
            pltpu.SemaphoreType.DMA((teams + 2,)),
            pltpu.SemaphoreType.DMA((3, 32)),
            pltpu.SemaphoreType.DMA((2 + 3 * teams + 24,)),
        ],
        cost_estimate=cost(8 * rows * D * (teams * hidden) + 4 * rows * D * teams * PAD, 24 << 20),
        compiler_params=pltpu.CompilerParams(vmem_limit_bytes=60 << 20),
        name="layer_rows",
    )(
        lengths,
        *[array for array, _ in mixed],
        hidden_in,
        grad_out,
        *weights,
        rows_of,
        b_up,
    )


def row_dot(groups, count, cut_by=None, waited=(), tail=None):
    sets = len(groups[0][0])
    bits, far, part, rows = groups[0][0][0][0].shape[1:]
    cut = 256
    lows = [0]
    for _, rights in groups:
        lows.append(lows[-1] + rights[0][0][0].shape[2] // cut)
    high = bits * far * part
    below = 0 if tail is None else tail.shape[0]
    cuts = {"bits": 2, "quads": 4}.get(cut_by, 1)

    def kernel(*refs):
        refs = list(refs)
        ins = [[refs.pop(0) for _ in range(sets)] for _ in groups]
        others = [[[refs.pop(0) for _ in range(count)] for _ in range(sets)] for _ in groups]
        if below:
            tail_ref = refs.pop(0)
        outs = refs[len(waited) :]
        j = pl.program_id(0)
        for g in range(len(groups)):

            @pl.when((j >= lows[g]) & (j < lows[g + 1]))
            def _(g=g):
                for i in range(count):
                    total = contract(ins[g][0][...].reshape(high, rows), others[g][0][i][...], (1, 0))
                    for k in range(1, sets):
                        total = total + contract(
                            ins[g][k][...].reshape(high, rows), others[g][k][i][...], (1, 0)
                        )
                    total = total.astype(bf16).reshape(bits, far, part, cut)
                    if cut_by == "far":
                        mine = lax.axis_index("dp") // 2
                        for z in range(far):
                            outs[0][z ^ mine, i] = total[:, z]
                        continue
                    for b in range(bits):
                        if cut_by == "bits":
                            to = outs[b].at[i, 0]
                        elif cut_by == "quads":
                            to = outs[2 * b + i].at[0, 0]
                        else:
                            to = outs[0].at[i, b]
                        if below:
                            to[:, :part, :] = total[b]
                            to[:, part:, :] = jnp.broadcast_to(
                                tail_ref[...][None], (far, below, cut)
                            )
                        else:
                            to[...] = total[b]

    def column(g, at):
        return lambda j: (at, 0, jnp.clip(j - lows[g], 0, lows[g + 1] - lows[g] - 1))

    specs, arrays = [], []
    for lefts, _ in groups:
        for array, at in lefts:
            specs.append(
                pl.BlockSpec((None, bits, far, part, rows), lambda j, at=at: (at, 0, 0, 0, 0))
            )
            arrays.append(array)
    for g, (_, rights) in enumerate(groups):
        for pairs in rights:
            for array, at in pairs:
                specs.append(pl.BlockSpec((None, rows, cut), column(g, at)))
                arrays.append(array)
    if below:
        specs.append(pl.BlockSpec((below, cut), lambda j: (0, j)))
        arrays.append(tail)
    width = lows[-1] * cut
    lead = (1 if cut_by == "quads" else count, 1 if cut_by in ("bits", "quads") else bits)
    return pl.pallas_call(
        kernel,
        grid=(lows[-1],),
        out_shape=[
            struct((far, *lead, part, width) if cut_by == "far" else (*lead, far, part + below, width), bf16)
        ]
        * cuts,
        in_specs=specs + [ANY_SPEC] * len(waited),
        out_specs=[
            pl.BlockSpec(
                (far, *lead, part, cut) if cut_by == "far" else (*lead, far, part + below, cut),
                lambda j: (0, 0, 0, 0, j),
            )
        ]
        * cuts,
        cost_estimate=cost(2 * sets * rows * high * count * width, 8 << 20),
        name="row_dot",
    )(*arrays, *waited)


def plus(a, b, waited=(), cuts=1, dtype=bf16):
    lead = a.shape[0] // cuts

    def kernel(a_ref, b_ref, *refs):
        for k in range(cuts):
            span = slice(k * lead, (k + 1) * lead)
            refs[len(waited) + k][...] = (
                a_ref[span].astype(f32) + b_ref[span].astype(f32)
            ).astype(dtype)

    return pl.pallas_call(
        kernel,
        out_shape=[struct((lead, *a.shape[1:]), dtype)] * cuts,
        in_specs=[VMEM_SPEC] * 2 + [ANY_SPEC] * len(waited),
        out_specs=[VMEM_SPEC] * cuts,
        cost_estimate=cost(a.size, 6 * a.size),
        name="plus",
    )(a, b, *waited)


def held(array, waited):
    def kernel(a_ref, *refs):
        refs[-1][...] = a_ref[...]

    return pl.pallas_call(
        kernel,
        out_shape=struct(array.shape, array.dtype),
        in_specs=[VMEM_SPEC] + [ANY_SPEC] * len(waited),
        out_specs=VMEM_SPEC,
        cost_estimate=cost(array.size, 8 * array.size),
        name="held",
    )(array, *waited)


def fold(blocks, waited=()):
    def kernel(ref, *refs):
        for k in range(2):
            total = ref[0, k].astype(f32)
            for z in range(1, 4):
                total = total + ref[z, k].astype(f32)
            refs[len(waited) + k][...] = total.astype(bf16)

    return pl.pallas_call(
        kernel,
        out_shape=[struct(blocks.shape[2:], bf16)] * 2,
        in_specs=[VMEM_SPEC] + [ANY_SPEC] * len(waited),
        out_specs=[VMEM_SPEC] * 2,
        cost_estimate=cost(blocks.size, 3 * blocks.size),
        name="fold",
    )(blocks, *waited)


def joined_sums(lists, waited=(), apart=False):
    rows, width = lists[0].shape[1:]
    count = len(lists)

    def kernel(*refs):
        mine = lax.axis_index("dp") // 2
        for z in range(4):
            total = refs[0][z].astype(f32)
            for k in range(1, count):
                total = total + refs[k][z].astype(f32)
            if apart:
                refs[count + len(waited) + z][...] = total.astype(bf16)
            else:
                refs[-1][z ^ mine] = total.astype(bf16)

    return pl.pallas_call(
        kernel,
        out_shape=[struct((rows, width), bf16)] * 4 if apart else struct((4, rows, width), bf16),
        in_specs=[VMEM_SPEC] * count + [ANY_SPEC] * len(waited),
        out_specs=[VMEM_SPEC] * 4 if apart else VMEM_SPEC,
        cost_estimate=cost(rows * width * 4 * count, rows * width * 8 * count),
        name="joined_sums",
    )(*lists, *waited)


def spread(grads, weight, added=None, after=None, waited=()):
    rows = grads[0].shape[0]

    def kernel(first, second, w, *refs):
        if added is None:
            out = refs[-1]
            out[0] = contract(first[...], w[...], (1, 1)).astype(bf16)
            out[1] = contract(second[...], w[...], (1, 1)).astype(bf16)
            return
        plus_ref, after_ref = refs[:2]
        away, here = refs[-2:]
        away[...] = (contract(first[...], w[...], (1, 1)) + plus_ref[0].astype(f32)).astype(bf16)
        here[...] = contract(second[...], w[...], (1, 1)) + (
            plus_ref[1].astype(f32) + after_ref[...].astype(f32)
        )

    if added is None:
        outs, more = struct((2, rows, D), bf16), []
    else:
        outs, more = [struct((rows, D), bf16), struct((rows, D), f32)], [added, after]
    return pl.pallas_call(
        kernel,
        out_shape=outs,
        in_specs=[VMEM_SPEC] * (3 + len(more)) + [ANY_SPEC] * len(waited),
        out_specs=VMEM_SPEC if added is None else [VMEM_SPEC] * 2,
        cost_estimate=cost(4 * rows * D * weight.shape[1], 5 << 20),
        name="spread",
    )(*grads, weight, *more, *waited)


def pack_queries(w_query, w_key, w_value):
    rows, width = w_query.shape

    def kernel(q, k, v, qkv):
        qkv[...] = jnp.zeros_like(qkv)
        for at, ref in enumerate((q, k, v)):
            qkv[:, at * PAD : at * PAD + width] = ref[...]

    return pl.pallas_call(
        kernel,
        out_shape=struct((rows, 3 * PAD), bf16),
        in_specs=[VMEM_SPEC] * 3,
        out_specs=VMEM_SPEC,
        cost_estimate=cost(rows * PAD, rows * PAD * 8),
        name="pack_queries",
    )(w_query, w_key, w_value)


def pack_weights(w_up, w_out, w_down, waited):
    rows, hidden = w_up.shape
    width = w_out.shape[0]

    def kernel(up, out, down, _, own):
        own[:, :hidden] = up[...]
        own[:, hidden : hidden + PAD] = jnp.zeros((rows, PAD), bf16)
        own[:, hidden : hidden + width] = out[...].T
        own[:, hidden + PAD :] = down[...].T

    return pl.pallas_call(
        kernel,
        out_shape=struct((rows, 2 * hidden + PAD), bf16),
        in_specs=[VMEM_SPEC] * 3 + [ANY_SPEC],
        out_specs=VMEM_SPEC,
        cost_estimate=cost(rows * hidden, 2 << 20),
        name="pack_weights",
    )(w_up, w_out, w_down, waited)


def pair_weights(own, beyond, hidden, waited):
    rows, width = own.shape
    starts = (0, hidden, hidden + PAD, width)

    def kernel(a, b, *refs):
        out = refs[-1]
        for at, end in zip(starts, starts[1:]):
            out[:, 2 * at : at + end] = a[:, at:end]
            out[:, at + end : 2 * end] = b[:, at:end]

    return pl.pallas_call(
        kernel,
        out_shape=struct((rows, 2 * width), bf16),
        in_specs=[VMEM_SPEC] * 2 + [ANY_SPEC] * len(waited),
        out_specs=VMEM_SPEC,
        cost_estimate=cost(rows * width, 4 * rows * width),
        name="pair_weights",
    )(own, beyond, *waited)


def project_in(xs, weights, bias):
    rows = xs[0].shape[0]
    pieces = len(xs)
    sources = len(weights)
    ordered = sources > 1
    bits, far = (2, 4) if ordered else (1, 1)
    part = D // (bits * far)
    wide = weights[0].shape[1]

    def kernel(*refs):
        refs = list(refs)
        ins = [refs.pop(0) for _ in range(pieces)]
        shards = [refs.pop(0) for _ in range(sources)]
        b = refs.pop(0)
        outs = [refs.pop(0) for _ in range(pieces)]
        turned_outs = [refs.pop(0) for _ in range(pieces)]
        whole_out, x_buf, w, out_buf, turned, sems, w_sems, out_sems = refs
        here = lax.axis_index("dp") if ordered else 0
        copies = [
            pltpu.make_async_copy(ins[s], x_buf.at[s], sems.at[s]) for s in range(pieces)
        ]
        fetched = []
        for at in range(sources):
            row = ring_member(RING_STEPS[at]) * part if ordered else 0
            fetched.append(
                pltpu.make_async_copy(
                    shards[at],
                    w.at[pl.ds(pl.multiple_of(row, 16), shards[at].shape[0]), :],
                    w_sems.at[at],
                )
            )
        for copy in fetched + copies:
            copy.start()
        for copy in fetched:
            copy.wait()
        leaving = []

        def leave(ref, to):
            copy = pltpu.make_async_copy(ref, to, out_sems.at[len(leaving)])
            copy.start()
            leaving.append(copy)

        leave(w, whole_out)
        for s in range(pieces):
            copies[s].wait()
            for c in range(0, wide, PAD):
                cols = slice(c, c + PAD)
                out_buf[s, :, cols] = (
                    contract(x_buf[s], w[:, cols], (1, 0)) + b[:, cols]
                ).astype(bf16)
            leave(out_buf.at[s], outs[s])
            for n in range(D // LANES):
                span = slice(n * LANES, (n + 1) * LANES)
                turned[s, span, :] = x_buf[s, :, span].T
            for k in range(bits):
                for z in range(far):
                    row = (here ^ (2 * z + k)) * part if ordered else 0
                    leave(
                        turned.at[s, pl.ds(pl.multiple_of(row, 16), part), :],
                        turned_outs[s].at[k, z],
                    )
        for copy in leaving:
            copy.wait()

    results = pl.pallas_call(
        kernel,
        out_shape=[struct((rows, wide), bf16)] * pieces
        + [struct((bits, far, part, rows), bf16)] * pieces
        + [struct((D, wide), bf16)],
        in_specs=[ANY_SPEC] * (pieces + sources) + [VMEM_SPEC],
        out_specs=[ANY_SPEC] * (2 * pieces + 1),
        scratch_shapes=[
            pltpu.VMEM((pieces, rows, D), bf16),
            pltpu.VMEM((D, wide), bf16),
            pltpu.VMEM((pieces, rows, wide), bf16),
            pltpu.VMEM((pieces, D, rows), bf16),
            pltpu.SemaphoreType.DMA((pieces,)),
            pltpu.SemaphoreType.DMA((sources,)),
            pltpu.SemaphoreType.DMA((1 + pieces * (1 + bits * far),)),
        ],
        cost_estimate=cost(4 * pieces * rows * D * wide, 24 << 20, 0, 1),
        name="project_in",
    )(*xs, *weights, bias)
    return results[:pieces], results[pieces : 2 * pieces], results[2 * pieces]


def padded(array):
    return jnp.pad(array, ((0, 0), (0, PAD - array.shape[1])))


def dot(a, b, dims=(1, 0)):
    return contract(a, b, dims)


def per_device(
    hidden_in,
    grad_out,
    w_query,
    b_query,
    w_key,
    w_value,
    b_value,
    w_out,
    b_out,
    gain_one,
    shift_one,
    w_up,
    b_up,
    w_down,
    b_down,
    gain_two,
    shift_two,
    lengths,
    global_raw,
    random_raw,
):
    own_rows = hidden_in.shape[0]
    me = lax.axis_index("tensor")
    teams = lax.axis_size("tensor")
    members = lax.axis_size("dp")
    width = w_query.shape[1]
    heads = width // HD
    hidden = w_up.shape[1]

    table, bias = block_tables(lengths, global_raw, random_raw, own_rows // BLK, teams)

    qkv_b = jnp.concatenate(
        [jnp.pad(b_query, (0, PAD - width)), jnp.zeros((PAD,), f32), jnp.pad(b_value, (0, PAD - width))]
    )
    halved = members == 8
    if halved:
        queries = pack_queries(w_query, w_key, w_value)
        own = pack_weights(w_up, w_out, w_down, queries)
        qkv_pieces = ring_pieces(queries)
        beyond_own = swap(own, 2)
        shard = pair_weights(own, beyond_own, hidden, qkv_pieces[GATE:])
    else:
        qkv_shard = jnp.concatenate([padded(w_query), padded(w_key), padded(w_value)], axis=1)
        qkv_pieces = [lax.all_gather(qkv_shard, "dp", axis=0, tiled=True)]
        shard = jnp.concatenate([w_up, padded(w_out.T), w_down.T], axis=1)
        weights = lax.all_gather(shard, ("dp", "tensor"), axis=0, tiled=False)
        weights = jnp.swapaxes(weights.reshape(members, teams, *shard.shape), 0, 1)
        weights = [weights.reshape(teams, D, shard.shape[1])]

    x2 = swap(held(hidden_in, (beyond_own,)) if halved else hidden_in, 2)
    x1 = swap(hidden_in, 1)
    x3 = swap(x2, 1)
    qkv, x_turned, qkv_w = project_in([hidden_in, x1, x2, x3], qkv_pieces, qkv_b[None])
    far_mixed, (t2, t3) = attend_forward(qkv, table, bias, heads, (2, 3))
    far_mixed = swap(far_mixed, 2)
    near_mixed, (t0, t1) = attend_forward(qkv, table, bias, heads, (0, 1))
    r1 = swap(near_mixed[1], 1)
    r3 = swap(far_mixed[1], 1)
    if halved:

        weights = ring_pieces(shard)
        weights = weights + [swap(piece, 1) for piece in weights]

    results = layer_rows(
        [(near_mixed, 0), (r1, None), (far_mixed, 0), (r3, None)],
        hidden_in,
        grad_out,
        weights,
        (
            jnp.stack([b_out, gain_one, shift_one, b_down, gain_two, shift_two]),
            b_up.reshape(teams, hidden),
        ),
        lengths,
    )
    layer_out, near_rows, far_rows, turned = results[:4]
    backs = results[4 : 4 + teams]
    after_low, small = results[4 + teams :]
    ups = [backs[0]] + [swap(backs[s], s) for s in range(1, teams)]
    totals = [t0, t1, t2, t3]
    before = attend_backward(qkv, ups[:1], totals[:1], table, bias, heads, (0,))

    next_rows, next_turned = swap(far_rows, 1), swap(turned, 1)
    down_group = (
        [(turned, 1), (next_turned, 1)],
        [[(near_rows, 0), (near_rows, 1)], [(next_rows, 0), (next_rows, 1)]],
    )
    up_group = (
        [(turned, 0), (next_turned, 0)],
        [[(near_rows, 2), (near_rows, 3)], [(next_rows, 2), (next_rows, 3)]],
    )
    out_group = (
        [(turned, 2), (next_turned, 2)],
        [[(near_mixed, 0), (far_mixed, 0)], [(near_mixed, 1), (far_mixed, 1)]],
    )
    if halved:
        (down_gone,) = row_dot([down_group], 2, "far", (before[0], *ups[1:]))
        down_blocks = far_exchange(down_gone)
        up_quads = row_dot([up_group, out_group], 2, "quads", (down_gone,))
        up_gone = up_quads[3]
        up_away = [swap(up_quads[1], 2), dp_swap(up_quads[2], 1), swap_both(up_gone)]
        waited = (up_gone,)
    else:
        down_sums = row_dot([down_group], 2)[0].reshape(2, D, -1)
        up_sums = row_dot([up_group, out_group], 2)[0].reshape(2, D, -1)
        waited = ()
    results = attend_backward(
        qkv,
        ups[1:],
        totals[1:],
        table,
        bias,
        heads,
        (1, 2, 3),
        small,
        waited,
        (before[1], before[2], before[0]),
    )
    grads, tail = results[:4], results[4]
    qkv_group = ([(x[None], 0) for x in x_turned], [[(g[None], 0)] for g in grads])
    if halved:
        kept, gone = row_dot([qkv_group], 1, "bits", (), tail)
        away = dp_swap(gone, 1)
        parts = spread([grads[3], grads[1]], qkv_w, waited=(gone,))
        spread_away = swap(parts, 1)
        up_blocks = joined_sums([a[0, 0] for a in (up_quads[0], *up_away)], (parts,))
        up_arrived = far_exchange(up_blocks)
        beyond, here = spread([grads[2], grads[0]], qkv_w, spread_away, after_low, (up_blocks,))
        beyond_away = swap(beyond, 2)
        down_here, down_next = fold(down_blocks, (beyond,))
        down_away = swap(down_next, 2)
        blocks = joined_sums([kept[0, 0], away[0, 0]], (down_next,))
        arrived = far_exchange(blocks)
        qkv_part = jnp.sum(arrived.astype(f32), axis=0)
        down_here, down_next = plus(down_here, down_away, (blocks,), 2)
        down_away = dp_swap(down_next, 1)
        down_part = down_here[0].astype(f32) + down_away[0].astype(f32)
        up_part = jnp.sum(up_arrived.astype(f32), axis=0)
        qkv_part, small = qkv_part[:-16], qkv_part[-16:]
    else:
        blocks = row_dot([qkv_group], 1)[0].reshape(D, -1)
        qkv_part = dp_scatter_sum(blocks)
        small = lax.psum(tail.astype(f32), "dp")
        spread_away = swap(spread([grads[3], grads[1]], qkv_w), 1)
        beyond, here = spread([grads[2], grads[0]], qkv_w, spread_away, after_low)
        beyond_away = swap(beyond, 2)
        down_part = dp_scatter_sum(down_sums[0] + swap(down_sums[1], 2))
        up_part = dp_scatter_sum(up_sums[0] + swap(up_sums[1], 2))
    grad_in = here + beyond_away.astype(f32)

    bias_row = small[SUM_ROW]
    return (
        layer_out,
        grad_in,
        qkv_part[:, :width],
        bias_row[:width],
        qkv_part[:, PAD : PAD + width],
        qkv_part[:, 2 * PAD : 2 * PAD + width],
        bias_row[2 * PAD : 2 * PAD + width],
        up_part[:, hidden : hidden + width].T,
        small[5],
        small[3],
        small[4],
        up_part[:, :hidden],
        jnp.take(small[6 : 6 + teams], me, axis=0),
        down_part.T,
        small[2],
        small[0],
        small[1],
    )


def solution(mesh):
    in_specs = (
        P(("dp", "tensor"), None),
        P(("dp", "tensor"), None),
        P("dp", "tensor"),
        P("tensor"),
        P("dp", "tensor"),
        P("dp", "tensor"),
        P("tensor"),
        P("tensor", "dp"),
        P(),
        P(),
        P(),
        P("dp", "tensor"),
        P(),
        P("tensor", "dp"),
        P(),
        P(),
        P(),
        P("dp"),
        P("dp", None),
        P("dp", None, None),
    )
    out_specs = (
        P(("dp", "tensor"), None),
        P(("dp", "tensor"), None),
        P("dp", "tensor"),
        P("tensor"),
        P("dp", "tensor"),
        P("dp", "tensor"),
        P("tensor"),
        P("tensor", "dp"),
        P(),
        P(),
        P(),
        P("dp", "tensor"),
        P("tensor"),
        P("tensor", "dp"),
        P(),
        P(),
        P(),
    )
    return jax.shard_map(
        per_device, mesh=mesh, in_specs=in_specs, out_specs=out_specs, check_vma=False
    )
```

```python
from functools import partial

import jax
import jax.numpy as jnp
from jax import lax
from jax.experimental import pallas as pl
from jax.experimental.pallas import tpu as pltpu
from jax.sharding import PartitionSpec as P

D = 768
HD = 64
FF = 3072
BLK = 64
GLOB = 2
RAND = 3
LMAX = 2048
NB = 32
KEYS = (3 + GLOB + RAND) * BLK
PAD = 256
LANES = 128
SUM_ROW = 10
ORDER = (0, 1, 2, 3)
SUM_ROWS = 16
BELOW = SUM_ROWS * (D // LANES)
GATE = 5

masked_score = -1e30
EPSILON = 1e-12
f32 = jnp.float32
bf16 = jnp.bfloat16


def swap(array, bit):
    size = lax.axis_size("tensor")
    return lax.ppermute(array, "tensor", [(t, t ^ bit) for t in range(size)])


def dp_swap(array, bit):
    size = lax.axis_size("dp")
    return lax.ppermute(array, "dp", [(t, t ^ bit) for t in range(size)])


def swap_both(array):
    size = lax.axis_size("dp") * 4
    axes = ("dp", "tensor")
    return lax.ppermute(array, axes, [(t, t ^ 6) for t in range(size)])


def ring_order(size):
    return list(range(0, size, 2)) + list(range(size - 1, 0, -2))


def ring_member(steps):
    size = lax.axis_size("dp")
    me = lax.axis_index("dp")
    place = jnp.where(me % 2 == 0, me // 2, size - 1 - me // 2)
    place = (place + steps + size) % size
    return jnp.where(place < size // 2, 2 * place, 2 * (size - 1 - place) + 1)


def ring_send(array, step):
    size = lax.axis_size("dp")
    order = ring_order(size)
    return lax.ppermute(
        array, "dp", [(order[i], order[(i + step) % size]) for i in range(size)]
    )


RING_STEPS = (0, -1, 1, -2, 2, -3, 3, -4)


def ring_pieces(shard):
    pieces = [shard]
    ahead, behind = shard, shard
    for step in range(1, 5):
        ahead = ring_send(ahead, 1)
        pieces.append(ahead)
        if step < 4:
            behind = ring_send(behind, -1)
            pieces.append(behind)
    return pieces


def far_exchange(blocks):
    groups = [[2 * f + n for f in range(4)] for n in range(2)]
    return lax.all_to_all(blocks, "dp", 0, 0, axis_index_groups=groups, tiled=True)


def dp_scatter_sum(sums):
    size = lax.axis_size("dp")
    if size != 8:
        return lax.psum_scatter(sums, "dp", scatter_dimension=0, tiled=True).astype(f32)
    blocks = lax.all_to_all(sums.reshape(size, -1, sums.shape[1]), "dp", 0, 0, tiled=True)
    return jnp.sum(blocks.astype(f32), axis=0)


def sum_over(vector, dp_only=False):
    if not dp_only:
        bit = 1
        while bit < lax.axis_size("tensor"):
            vector = vector + swap(vector, bit)
            bit *= 2
    bit = 1
    while bit < lax.axis_size("dp"):
        vector = vector + dp_swap(vector, bit)
        bit *= 2
    return vector


def block_tables(lengths, global_raw, random_raw, own_blocks, pieces):
    count = own_blocks * pieces

    def kernel(length_ref, global_ref, random_ref, table, bias):
        me = lax.axis_index("tensor")
        lane = lax.broadcasted_iota(jnp.int32, (1, KEYS), 1)
        slot = lane // BLK
        within = lane % BLK
        wide = lax.broadcasted_iota(jnp.int32, (own_blocks, LANES), 1)
        row = lax.broadcasted_iota(jnp.int32, (own_blocks, 1), 0)
        for s in range(pieces):
            first = (s ^ me) * own_blocks
            seq = first // NB
            start = first - seq * NB
            length = length_ref[seq]
            live = (length + BLK - 1) // BLK
            raw = random_ref[seq, pl.ds(pl.multiple_of(start, 8), own_blocks), :]
            rest = raw - live * jnp.floor(raw.astype(f32) / live.astype(f32)).astype(jnp.int32)
            rest = jnp.where(rest < 0, rest + live, rest)
            rest = jnp.where(rest >= live, rest - live, rest)
            block = row + start
            ids = [jnp.maximum(block - 1, 0), block, jnp.minimum(block + 1, NB - 1)]
            ids += [jnp.full((own_blocks, 1), lax.rem(global_ref[seq, j], live)) for j in range(GLOB)]
            ids += [rest[:, r : r + 1] for r in range(RAND)]
            spread_ids = jnp.zeros((own_blocks, KEYS), jnp.int32)
            packed = jnp.zeros((own_blocks, LANES), jnp.int32)
            for j, own in enumerate(ids):
                spread_ids = jnp.where(slot == j, own, spread_ids)
                there = own + seq * NB
                there = ((there // own_blocks) ^ me) * own_blocks + there % own_blocks
                packed = jnp.where(wide == j, there, packed)
            table[s * own_blocks : (s + 1) * own_blocks, :] = packed
            lost = (spread_ids * BLK + within) >= length
            lost = lost | ((slot == 0) & (block == 0)) | ((slot == 2) & (block == NB - 1))
            bias[s * own_blocks : (s + 1) * own_blocks, :] = jnp.where(lost, masked_score, 0.0).astype(f32)

    smem = pl.BlockSpec(memory_space=pltpu.SMEM)
    vmem = pl.BlockSpec(memory_space=pltpu.VMEM)
    return pl.pallas_call(
        kernel,
        out_shape=[
            jax.ShapeDtypeStruct((count, LANES), jnp.int32),
            jax.ShapeDtypeStruct((count, KEYS), f32),
        ],
        in_specs=[smem, smem, vmem],
        out_specs=[vmem, vmem],
        cost_estimate=cost(count * KEYS * 16, count * KEYS * 4),
        name="block_tables",
    )(lengths, global_raw, random_raw)


def head_masks(heads, scale, dtype):
    lane = lax.broadcasted_iota(jnp.int32, (1, PAD), 1)
    return [
        jnp.where((lane >= h * HD) & (lane < (h + 1) * HD), scale, 0.0).astype(dtype)
        for h in range(heads)
    ]


def stacked_heads(rows, masks):
    return jnp.concatenate([rows * mask for mask in masks], axis=0)


def unstacked_heads(stacked, masks):
    rows = stacked.shape[0] // len(masks)
    total = stacked[:rows] * masks[0]
    for h in range(1, len(masks)):
        total = total + stacked[h * rows : (h + 1) * rows] * masks[h]
    return total


def key_blocks(ref, table, block, column):
    return jnp.concatenate(
        [
            ref[pl.ds(pl.multiple_of(table[block, j] * BLK, BLK), BLK), column : column + PAD]
            for j in range(KEYS // BLK)
        ],
        axis=0,
    )


def contract(a, b, dims):
    return lax.dot_general(a, b, ((dims[:1], dims[1:]), ((), ())), preferred_element_type=f32)


def attend_kernel(heads, chosen, pieces, own_blocks, table, *refs):
    parts = refs[:pieces]
    bias = refs[pieces]
    out = refs[pieces + 1]
    totals = refs[pieces + 2 : pieces + 2 + len(chosen)]
    rows, sems = refs[pieces + 2 + len(chosen) :]
    own_rows = own_blocks * BLK
    copies = [
        pltpu.make_async_copy(
            parts[s], rows.at[pl.ds(s * own_rows, own_rows)], sems.at[s]
        )
        for s in range(pieces)
    ]
    for copy in copies:
        copy.start()
    for copy in copies:
        copy.wait()
    query_masks = head_masks(heads, HD**-0.5, bf16)
    out_masks = head_masks(heads, 1.0, f32)
    lane = lax.broadcasted_iota(jnp.int32, (BLK, LANES), 1)

    side = 2
    count = len(chosen) * side

    def step(step_at, carry):
        blocks, held = [], [{} for _ in range(count)]
        for at in range(count):
            i = step_at * side + at // len(chosen)
            piece = at % len(chosen)
            blocks.append((piece, i, chosen[piece] * own_blocks + i))

        def scored(at):
            block = blocks[at][2]
            here = pl.ds(pl.multiple_of(block * BLK, BLK), BLK)
            queries = stacked_heads(rows[here, 0:PAD], query_masks)
            keys = key_blocks(rows, table, block, PAD)
            held[at]["scores"] = contract(queries, keys, (1, 1))

        def weighed(at):
            has = held[at]
            masked = bias[pl.ds(blocks[at][2], 1), :]
            low, has["total"], has["log_total"] = [], [], []
            for h in range(heads):
                scores = has["scores"][h * BLK : (h + 1) * BLK] + masked
                top = jnp.max(scores, axis=-1, keepdims=True)
                weights = jnp.exp(scores - top)
                total = jnp.sum(weights, axis=-1, keepdims=True)
                low.append(weights.astype(bf16))
                has["total"].append(total)
                has["log_total"].append(top + jnp.log(total))
            has["weights"] = jnp.concatenate(low, axis=0)

        def mixed(at):
            piece, i, block = blocks[at]
            has = held[at]
            values = key_blocks(rows, table, block, 2 * PAD)
            outs = contract(has["weights"], values, (1, 0))
            start = pl.ds(pl.multiple_of(i * BLK, BLK), BLK)
            kept = jnp.zeros((BLK, LANES), f32)
            total = jnp.zeros((BLK, PAD), f32)
            for h in range(heads):
                total = total + outs[h * BLK : (h + 1) * BLK] * (out_masks[h] / has["total"][h])
                kept = jnp.where(lane == h, has["log_total"][h], kept)
            out[piece, start, :] = total.astype(bf16)
            totals[piece][start, :] = kept

        stages = (scored, weighed, mixed)
        for turn in range(count + len(stages) - 1):
            for k in range(len(stages)):
                if 0 <= turn - k < count:
                    stages[k](turn - k)
        return carry

    lax.fori_loop(0, own_blocks // side, step, 0)


def attend_forward(parts, table, bias, heads, chosen):
    own_rows = parts[0].shape[0]
    pieces = len(parts)
    own_blocks = own_rows // BLK
    n = len(chosen)
    vmem = pl.BlockSpec(memory_space=pltpu.VMEM)
    work = n * own_rows * KEYS * heads
    results = pl.pallas_call(
        partial(attend_kernel, heads, chosen, pieces, own_blocks),
        out_shape=[jax.ShapeDtypeStruct((n, own_rows, PAD), bf16)]
        + [jax.ShapeDtypeStruct((own_rows, LANES), f32)] * n,
        in_specs=[pl.BlockSpec(memory_space=pltpu.SMEM)]
        + [pl.BlockSpec(memory_space=pl.ANY)] * pieces
        + [vmem],
        out_specs=[vmem] * (1 + n),
        scratch_shapes=[
            pltpu.VMEM((pieces * own_rows, 3 * PAD), bf16),
            pltpu.SemaphoreType.DMA((pieces,)),
        ],
        cost_estimate=cost(48 * work * HD, 16 << 20, 4 * work, 1),
        name="attend_forward",
    )(table, *parts, bias)
    return results[0], results[1:]


def attend_back_kernel(heads, chosen, pieces, own_blocks, waited, carried, table, *refs):
    refs = list(refs)

    def take(count):
        taken = refs[:count]
        del refs[:count]
        return taken

    parts = take(pieces)
    ups = take(len(chosen))
    totals = take(len(chosen))
    (bias,) = take(1)
    take(waited)
    if carried:
        key_before, value_before = take(2)
        query_before = take(pieces - len(chosen))
        (small_ref,) = take(1)
        outs = take(pieces)
        (tail,) = take(1)
        key_sum, value_sum, key_kept, value_kept, row_sums = take(5)
    else:
        outs = take(len(chosen))
        key_sum, value_sum = take(2)
    rows, up_rows, up_packed, sems = refs
    own_rows = own_blocks * BLK
    copies = [
        pltpu.make_async_copy(parts[s], rows.at[pl.ds(s * own_rows, own_rows)], sems.at[s])
        for s in range(pieces)
    ] + [
        pltpu.make_async_copy(ups[at], up_packed.at[at], sems.at[pieces + at])
        for at in range(len(chosen))
    ]
    late = []
    if carried:
        late = [
            pltpu.make_async_copy(key_before, key_kept, sems.at[pieces + len(chosen)]),
            pltpu.make_async_copy(value_before, value_kept, sems.at[pieces + len(chosen) + 1]),
        ]
    for copy in copies + late:
        copy.start()
    key_sum[...] = jnp.zeros_like(key_sum)
    value_sum[...] = jnp.zeros_like(value_sum)
    for copy in copies:
        copy.wait()
    query_masks = head_masks(heads, HD**-0.5, bf16)
    up_masks = head_masks(heads, 1.0, bf16)
    out_masks = head_masks(heads, HD**-0.5, f32)
    half = own_rows // 2
    for at in range(len(chosen)):
        up_rows[at, :, :LANES] = up_packed[at, :own_rows, :]
        last = up_packed[at, own_rows : own_rows + half, :]
        up_rows[at, :half, LANES:] = last
        up_rows[at, half:, LANES:] = pltpu.roll(last.astype(f32), HD, 1).astype(bf16)

    side = 2 if len(chosen) == 1 else 1

    count = len(chosen) * side

    def step(step_at, carry):
        blocks, held = [], [{} for _ in range(count)]
        for at in range(count):
            i = step_at * side + at // len(chosen)
            piece = at % len(chosen)
            blocks.append((piece, i, chosen[piece] * own_blocks + i))

        def scored(at):
            piece, i, block = blocks[at]
            start = pl.multiple_of(i * BLK, BLK)
            here = pl.ds(pl.multiple_of(block * BLK, BLK), BLK)
            has = held[at]
            has["queries"] = stacked_heads(rows[here, 0:PAD], query_masks)
            has["upstream"] = stacked_heads(up_rows[piece, pl.ds(start, BLK), :], up_masks)
            has["keys"] = key_blocks(rows, table, block, PAD)
            values = key_blocks(rows, table, block, 2 * PAD)
            has["scores"] = contract(has["queries"], has["keys"], (1, 1))
            has["grad_weights"] = contract(has["upstream"], values, (1, 1))

        def weighed(at):
            piece, i, block = blocks[at]
            has = held[at]
            kept = totals[piece][pl.ds(pl.multiple_of(i * BLK, BLK), BLK), :]
            masked = bias[pl.ds(block, 1), :]
            low, grad = [], []
            for h in range(heads):
                span = slice(h * BLK, (h + 1) * BLK)
                weights = jnp.exp(has["scores"][span] + (masked - kept[:, h : h + 1]))
                grad_weights = has["grad_weights"][span]
                inner = jnp.sum(weights * grad_weights, axis=-1, keepdims=True)
                low.append(weights.astype(bf16))
                grad.append((weights * (grad_weights - inner)).astype(bf16))
            has["weights"] = jnp.concatenate(low, axis=0)
            has["grad_scores"] = jnp.concatenate(grad, axis=0)

        def spread_back(at):
            piece, i, block = blocks[at]
            has = held[at]
            to = outs[chosen[piece]] if carried else outs[piece]
            grad_query = contract(has["grad_scores"], has["keys"], (1, 0))
            to[pl.ds(pl.multiple_of(i * BLK, BLK), BLK), 0:PAD] = unstacked_heads(
                grad_query, out_masks
            ).astype(bf16)
            has["key_part"] = contract(has["grad_scores"], has["queries"], (0, 0))
            has["value_part"] = contract(has["weights"], has["upstream"], (0, 0))

        def summed(at):
            block, has = blocks[at][2], held[at]
            for j in range(KEYS // BLK):
                there = pl.ds(pl.multiple_of(table[block, j] * BLK, BLK), BLK)
                key_sum[there, :] += has["key_part"][j * BLK : (j + 1) * BLK]
                value_sum[there, :] += has["value_part"][j * BLK : (j + 1) * BLK]

        stages = (scored, weighed, spread_back, summed)
        for turn in range(count + len(stages) - 1):
            for k in ORDER:
                at = turn - k
                if 0 <= at < count:
                    stages[k](at)
        return carry

    lax.fori_loop(0, own_blocks // side, step, 0)
    if not carried:
        return
    for copy in late:
        copy.wait()
    before = [s for s in range(pieces) if s not in chosen]
    for at, s in enumerate(before):
        outs[s][:, 0:PAD] = query_before[at][...]
    row_sums[...] = jnp.zeros_like(row_sums)
    for s in range(pieces):

        def finish(i, carry, s=s):
            at = pl.ds(pl.multiple_of(i * BLK, BLK), BLK)
            span = pl.ds(pl.multiple_of(s * own_rows + i * BLK, BLK), BLK)
            outs[s][at, PAD : 2 * PAD] = (key_sum[span, :] + key_kept[span, :]).astype(bf16)
            outs[s][at, 2 * PAD : 3 * PAD] = (value_sum[span, :] + value_kept[span, :]).astype(bf16)
            whole = outs[s][at, :].astype(f32)
            row_sums[...] += jnp.sum(whole.reshape(BLK // 8, 8, 3 * PAD), axis=0)
            return carry

        lax.fori_loop(0, own_blocks, finish, 0)
    slot = lax.broadcasted_iota(jnp.int32, tail.shape, 0)
    whole = jnp.sum(row_sums[...], axis=0, keepdims=True)
    small = small_ref[...]
    for at in range(len(chosen)):
        parts = [
            up_packed[at, own_rows + half + k * SUM_ROWS : own_rows + half + (k + 1) * SUM_ROWS, :]
            for k in range(BELOW // SUM_ROWS)
        ]
        small = small + jnp.concatenate(parts, axis=1).astype(f32)
    tail[...] = jnp.where(slot == SUM_ROW, whole, small).astype(bf16)


def attend_backward(parts, ups, totals, table, bias, heads, chosen, small=None, waited=(), before=None):
    own_rows = parts[0].shape[0]
    pieces = len(parts)
    n = len(chosen)
    own_blocks = own_rows // BLK
    vmem = pl.BlockSpec(memory_space=pltpu.VMEM)
    anyspace = pl.BlockSpec(memory_space=pl.ANY)
    work = n * own_rows * KEYS * heads
    sum_shape = (pieces * own_rows, PAD)
    if before is None:
        outs = [((own_rows, PAD), bf16)] * n + [(sum_shape, f32)] * 2
        extra, extra_specs, scratch = [], [], []
    else:
        outs = [((own_rows, 3 * PAD), bf16)] * pieces + [((16, 3 * PAD), bf16)]
        extra = [*before, small]
        extra_specs = [anyspace] * 2 + [vmem] * (len(before) - 1)
        scratch = [pltpu.VMEM(sum_shape, f32)] * 4 + [pltpu.VMEM((8, 3 * PAD), f32)]
    return pl.pallas_call(
        partial(
            attend_back_kernel, heads, chosen, pieces, own_blocks, len(waited), before is not None
        ),
        out_shape=[jax.ShapeDtypeStruct(*out) for out in outs],
        in_specs=[pl.BlockSpec(memory_space=pltpu.SMEM)]
        + [anyspace] * (pieces + n)
        + [vmem] * (n + 1)
        + [anyspace] * len(waited)
        + extra_specs,
        out_specs=[vmem] * len(outs),
        scratch_shapes=scratch
        + [
            pltpu.VMEM((pieces * own_rows, 3 * PAD), bf16),
            pltpu.VMEM((n, own_rows, PAD), bf16),
            pltpu.VMEM((n, own_rows + own_rows // 2 + BELOW, LANES), bf16),
            pltpu.SemaphoreType.DMA((pieces + n + 2,)),
        ],
        cost_estimate=cost(30 * work * HD, 12 << 20, work),
        name="attend_backward",
    )(table, *parts, *ups, *totals, bias, *waited, *extra)


VMEM_SPEC = pl.BlockSpec(memory_space=pltpu.VMEM)
ANY_SPEC = pl.BlockSpec(memory_space=pl.ANY)
SMEM_SPEC = pl.BlockSpec(memory_space=pltpu.SMEM)
COST_CUT = 64
GELU_A = 0.7978845608028654
GELU_B = 0.044715


def cost(flops, size, transcendentals=0, cut=None):
    cut = cut or COST_CUT
    return pl.CostEstimate(
        flops=flops // cut, bytes_accessed=size // cut, transcendentals=transcendentals // cut
    )


def struct(shape, dtype):
    return jax.ShapeDtypeStruct(shape, dtype)


def row_stats(values):
    centred = values - jnp.mean(values, axis=-1, keepdims=True)
    inv_std = lax.rsqrt(jnp.mean(centred * centred, axis=-1, keepdims=True) + EPSILON)
    return centred * inv_std, inv_std


def norm_backward(upstream, scaled, inv_std, gain):
    weighted = upstream * gain
    inner = jnp.mean(weighted * scaled, axis=-1, keepdims=True)
    return inv_std * (weighted - jnp.mean(weighted, axis=-1, keepdims=True) - scaled * inner)


def column_sum(array):
    return jnp.sum(array.reshape(array.shape[0] // 8, 8, array.shape[1]), axis=0)


def rows_kernel(places, sources, length, *refs):
    teams = len(places)
    refs = list(refs)

    def take(count):
        taken = refs[:count]
        del refs[:count]
        return taken

    mixed = take(teams)
    x_in, g_in = take(2)
    weights = take(sources)
    vectors, b_up = take(2)
    b_out, g1, c1, b_down, g2, c2 = [vectors.at[k : k + 1, :] for k in range(6)]
    layer_out, near_out, far_out, turned_out = take(4)
    back_out = take(teams)
    after_out, small = take(2)
    (
        o_buf,
        x_buf,
        g_buf,
        out_w,
        up_w,
        down_w,
        scaled_buf,
        inv_buf,
        wide_buf,
        low_buf,
        act_buf,
        slope_buf,
        last_buf,
        turned_buf,
        send_buf,
        sums,
        up_sums,
        in_sems,
        w_sems,
        out_sems,
    ) = refs
    rows = x_in.shape[0]
    hidden = up_w.shape[2]
    tile, cut = 64, 256
    me = lax.axis_index("tensor")
    ring = sources > 1

    first = []
    for s in range(teams):
        source = mixed[s] if places[s] is None else mixed[s].at[places[s]]
        first.append(
            pltpu.make_async_copy(source, o_buf.at[s], in_sems.at[s])
        )
    first.append(pltpu.make_async_copy(x_in, x_buf, in_sems.at[teams]))
    upstream_copy = pltpu.make_async_copy(g_in, g_buf, in_sems.at[teams + 1])
    fetched = ([], [], [])

    def fetch(kind, source, to):
        sem = w_sems.at[kind, len(fetched[kind])]
        fetched[kind].append(pltpu.make_async_copy(source, to, sem))

    wholes = (out_w, up_w, down_w)
    if ring:
        part = weights[0].shape[0]
        spans = ((2 * hidden, PAD), (0, hidden), (2 * hidden + 2 * PAD, hidden))
        for at, piece in enumerate(weights):
            row = pl.multiple_of(ring_member(RING_STEPS[at % 8]) * part, 16)
            for kind, (start, size) in enumerate(spans):
                for pair in range(2):
                    fetch(
                        kind,
                        piece.at[:, pl.ds(start + pair * size, size)],
                        wholes[kind].at[2 * pair + at // 8, pl.ds(row, part), :],
                    )
    else:
        spans = ((hidden, PAD), (0, hidden), (hidden + PAD, hidden))
        for kind, (start, size) in enumerate(spans):
            for s in range(teams):
                fetch(kind, weights[0].at[me ^ s, :, pl.ds(start, size)], wholes[kind].at[s])
    for copy in first + fetched[0] + fetched[1] + fetched[2] + [upstream_copy]:
        copy.start()
    sums[...] = jnp.zeros_like(sums)
    up_sums[...] = jnp.zeros_like(up_sums)
    leaving = []

    def leave(ref, to):
        copy = pltpu.make_async_copy(ref, to, out_sems.at[len(leaving)])
        copy.start()
        leaving.append(copy)

    def leave_turned(k, source, to):
        for n in range(D // LANES):
            span = slice(n * LANES, (n + 1) * LANES)
            turned_buf[k, span, :] = source[:, span].T
        bits, far, part, _ = to.shape
        here = lax.axis_index("dp")
        for b in range(bits):
            for z in range(far):
                row = (here ^ (2 * z + b)) * part if ring else 0
                leave(turned_buf.at[k, pl.ds(pl.multiple_of(row, 16), part), :], to.at[b, z])

    def tiles(body):
        def step(i, carry):
            body(i, pl.ds(pl.multiple_of(i * tile, tile), tile))
            return carry

        lax.fori_loop(0, rows // tile, step, 0)

    for copy in first + fetched[0]:
        copy.wait()
    for n in range(D // cut):
        cols = slice(n * cut, (n + 1) * cut)
        total = contract(o_buf[0, :rows, :], out_w[0, cols, :], (1, 1))
        for s in range(1, teams):
            total = total + contract(o_buf[s, :rows, :], out_w[s, cols, :], (1, 1))
        wide_buf[:, cols] = total

    def first_norm(i, at):
        after = x_buf[at, :].astype(f32) + wide_buf[at, :] + b_out[...]
        scaled, inv_std = row_stats(after)
        scaled_buf[at, :] = scaled
        inv_buf[at, :] = jnp.broadcast_to(inv_std, (tile, LANES))
        low_buf[at, :] = (scaled * g1[...] + c1[...]).astype(bf16)

    tiles(first_norm)
    leave_turned(0, low_buf, turned_out.at[0])
    for copy in fetched[1]:
        copy.wait()

    def up_step(s, carry):
        bias = b_up[pl.ds(s ^ me, 1), :]
        for c in range(hidden // cut):
            cols = slice(c * cut, (c + 1) * cut)
            u = contract(low_buf[...], up_w[s, :, cols], (1, 0)) + bias[:, cols]
            cubic = (GELU_A * GELU_B) * (u * u)
            t = jnp.tanh(u * (GELU_A + cubic))
            half = 0.5 + 0.5 * t
            act = u * half
            act_buf[s, :, cols] = act.astype(bf16)
            slope_buf[s, :, cols] = (
                half + act * ((1.0 - t) * (GELU_A + 3.0 * cubic))
            ).astype(bf16)
        return carry

    lax.fori_loop(0, teams, up_step, 0)
    for s in range(teams):
        leave(act_buf.at[s], (far_out if s % 2 else near_out).at[s // 2])
    for copy in fetched[2]:
        copy.wait()
    upstream_copy.wait()
    for n in range(D // cut):
        cols = slice(n * cut, (n + 1) * cut)
        total = contract(act_buf[0], down_w[0, cols, :], (1, 1))
        for s in range(1, teams):
            total = total + contract(act_buf[s], down_w[s, cols, :], (1, 1))
        wide_buf[:, cols] = total
    start = me * rows
    seq = start // LMAX
    live = length[seq] - (start - seq * LMAX)

    def second_norm(i, at):
        z = (scaled_buf[at, :] * g1[...] + c1[...]) + wide_buf[at, :] + b_down[...]
        scaled, inv_std = row_stats(z)
        x_buf[at, :] = (scaled * g2[...] + c2[...]).astype(bf16)
        row = lax.broadcasted_iota(jnp.int32, (tile, D), 0) + i * tile
        upstream = jnp.where(row < live, g_buf[at, :].astype(f32), 0.0)
        grad = norm_backward(upstream, scaled, inv_std, g2[...]).astype(bf16)
        g_buf[at, :] = grad
        sums[0:8, :] += column_sum(upstream * scaled)
        sums[8:16, :] += column_sum(upstream)
        sums[16:24, :] += column_sum(grad.astype(f32))

    tiles(second_norm)
    leave(x_buf, layer_out)
    leave_turned(1, g_buf, turned_out.at[1])

    def down_back(s, carry):
        for c in range(hidden // cut):
            cols = slice(c * cut, (c + 1) * cut)
            g = contract(g_buf[...], down_w[s, :, cols], (1, 0))
            g = (g * slope_buf[s, :, cols].astype(f32)).astype(bf16)
            slope_buf[s, :, cols] = g
            up_sums[pl.ds(pl.multiple_of(s * 8, 8), 8), cols] = column_sum(g.astype(f32))
        return carry

    lax.fori_loop(0, teams, down_back, 0)
    for s in range(teams):
        leave(slope_buf.at[s], (far_out if s % 2 else near_out).at[2 + s // 2])
    for n in range(D // cut):
        cols = slice(n * cut, (n + 1) * cut)
        total = contract(slope_buf[0], up_w[0, cols, :], (1, 1))
        for s in range(1, teams):
            total = total + contract(slope_buf[s], up_w[s, cols, :], (1, 1))
        wide_buf[:, cols] = total

    def first_back(i, at):
        upstream = g_buf[at, :].astype(f32) + wide_buf[at, :]
        scaled = scaled_buf[at, :]
        grad = norm_backward(upstream, scaled, inv_buf[at, :][:, :1], g1[...]).astype(bf16)
        last_buf[at, :] = grad
        sums[24:32, :] += column_sum(upstream * scaled)
        sums[32:40, :] += column_sum(upstream)
        sums[40:48, :] += column_sum(grad.astype(f32))

    tiles(first_back)
    leave(last_buf, after_out)
    leave_turned(2, last_buf, turned_out.at[2])
    small[...] = jnp.zeros_like(small)
    for k in range(6):
        small[k : k + 1, :] = jnp.sum(sums[8 * k : 8 * k + 8, :], axis=0, keepdims=True)
    for s in range(teams):
        small[pl.ds(6 + (s ^ me), 1), :] = jnp.sum(
            up_sums[8 * s : 8 * s + 8, :], axis=0, keepdims=True
        )
    for s in (2, 3, 1, 0):
        back = contract(last_buf[...], out_w[s], (1, 0))
        half = rows // 2
        send_buf[s, :rows, :] = back[:, :LANES].astype(bf16)
        send_buf[s, rows : rows + half, :] = (
            back[:half, LANES:] + pltpu.roll(back[half:, LANES:], HD, 1)
        ).astype(bf16)
        for k in range(D // LANES):
            at = rows + half + k * SUM_ROWS
            send_buf[s, at : at + SUM_ROWS, :] = small[:, k * LANES : (k + 1) * LANES].astype(bf16)
        leave(send_buf.at[s], back_out[s])
    for copy in leaving:
        copy.wait()


def layer_rows(mixed, hidden_in, grad_out, weights, vectors, lengths):
    teams = len(mixed)
    rows = hidden_in.shape[0]
    rows_of, b_up = vectors
    hidden = b_up.shape[1]
    half = teams // 2
    low = struct((rows, D), bf16)
    pair = struct((2 * half, rows, hidden), bf16)
    ring = len(weights) > 1
    turned = struct((3, 2, 4, D // 8, rows) if ring else (3, 1, 1, D, rows), bf16)
    return pl.pallas_call(
        partial(rows_kernel, [at for _, at in mixed], len(weights)),
        out_shape=[low, pair, pair, turned]
        + [struct((rows + rows // 2 + BELOW, LANES), bf16)] * teams
        + [low, struct((16, D), f32)],
        in_specs=[SMEM_SPEC]
        + [ANY_SPEC] * (teams + 2 + len(weights))
        + [VMEM_SPEC] * 2,
        out_specs=[ANY_SPEC] * (5 + teams) + [VMEM_SPEC],
        scratch_shapes=[
            pltpu.VMEM((teams, rows, PAD), bf16),
            pltpu.VMEM((rows, D), bf16),
            pltpu.VMEM((rows, D), bf16),
            pltpu.VMEM((teams, D, PAD), bf16),
            pltpu.VMEM((teams, D, hidden), bf16),
            pltpu.VMEM((teams, D, hidden), bf16),
            pltpu.VMEM((rows, D), f32),
            pltpu.VMEM((rows, LANES), f32),
            pltpu.VMEM((rows, D), f32),
            pltpu.VMEM((rows, D), bf16),
            pltpu.VMEM((teams, rows, hidden), bf16),
            pltpu.VMEM((teams, rows, hidden), bf16),
            pltpu.VMEM((rows, D), bf16),
            pltpu.VMEM((3, D, rows), bf16),
            pltpu.VMEM((teams, rows + rows // 2 + BELOW, LANES), bf16),
            pltpu.VMEM((48, D), f32),
            pltpu.VMEM((8 * teams, hidden), f32),
            pltpu.SemaphoreType.DMA((teams + 2,)),
            pltpu.SemaphoreType.DMA((3, 32)),
            pltpu.SemaphoreType.DMA((2 + 3 * teams + 24,)),
        ],
        cost_estimate=cost(8 * rows * D * (teams * hidden) + 4 * rows * D * teams * PAD, 24 << 20),
        compiler_params=pltpu.CompilerParams(vmem_limit_bytes=60 << 20),
        name="layer_rows",
    )(
        lengths,
        *[array for array, _ in mixed],
        hidden_in,
        grad_out,
        *weights,
        rows_of,
        b_up,
    )


def row_dot(groups, count, cut_by=None, waited=(), tail=None):
    sets = len(groups[0][0])
    bits, far, part, rows = groups[0][0][0][0].shape[1:]
    cut = 256
    lows = [0]
    for _, rights in groups:
        lows.append(lows[-1] + rights[0][0][0].shape[2] // cut)
    high = bits * far * part
    below = 0 if tail is None else tail.shape[0]
    cuts = {"bits": 2, "quads": 4}.get(cut_by, 1)

    def kernel(*refs):
        refs = list(refs)
        ins = [[refs.pop(0) for _ in range(sets)] for _ in groups]
        others = [[[refs.pop(0) for _ in range(count)] for _ in range(sets)] for _ in groups]
        if below:
            tail_ref = refs.pop(0)
        outs = refs[len(waited) :]
        j = pl.program_id(0)
        for g in range(len(groups)):

            @pl.when((j >= lows[g]) & (j < lows[g + 1]))
            def _(g=g):
                for i in range(count):
                    total = contract(ins[g][0][...].reshape(high, rows), others[g][0][i][...], (1, 0))
                    for k in range(1, sets):
                        total = total + contract(
                            ins[g][k][...].reshape(high, rows), others[g][k][i][...], (1, 0)
                        )
                    total = total.astype(bf16).reshape(bits, far, part, cut)
                    if cut_by == "far":
                        mine = lax.axis_index("dp") // 2
                        for z in range(far):
                            outs[0][z ^ mine, i] = total[:, z]
                        continue
                    for b in range(bits):
                        if cut_by == "bits":
                            to = outs[b].at[i, 0]
                        elif cut_by == "quads":
                            to = outs[2 * b + i].at[0, 0]
                        else:
                            to = outs[0].at[i, b]
                        if below:
                            to[:, :part, :] = total[b]
                            to[:, part:, :] = jnp.broadcast_to(
                                tail_ref[...][None], (far, below, cut)
                            )
                        else:
                            to[...] = total[b]

    def column(g, at):
        return lambda j: (at, 0, jnp.clip(j - lows[g], 0, lows[g + 1] - lows[g] - 1))

    specs, arrays = [], []
    for lefts, _ in groups:
        for array, at in lefts:
            specs.append(
                pl.BlockSpec((None, bits, far, part, rows), lambda j, at=at: (at, 0, 0, 0, 0))
            )
            arrays.append(array)
    for g, (_, rights) in enumerate(groups):
        for pairs in rights:
            for array, at in pairs:
                specs.append(pl.BlockSpec((None, rows, cut), column(g, at)))
                arrays.append(array)
    if below:
        specs.append(pl.BlockSpec((below, cut), lambda j: (0, j)))
        arrays.append(tail)
    width = lows[-1] * cut
    lead = (1 if cut_by == "quads" else count, 1 if cut_by in ("bits", "quads") else bits)
    return pl.pallas_call(
        kernel,
        grid=(lows[-1],),
        out_shape=[
            struct((far, *lead, part, width) if cut_by == "far" else (*lead, far, part + below, width), bf16)
        ]
        * cuts,
        in_specs=specs + [ANY_SPEC] * len(waited),
        out_specs=[
            pl.BlockSpec(
                (far, *lead, part, cut) if cut_by == "far" else (*lead, far, part + below, cut),
                lambda j: (0, 0, 0, 0, j),
            )
        ]
        * cuts,
        cost_estimate=cost(2 * sets * rows * high * count * width, 8 << 20),
        name="row_dot",
    )(*arrays, *waited)


def plus(a, b, waited=(), cuts=1, dtype=bf16):
    lead = a.shape[0] // cuts

    def kernel(a_ref, b_ref, *refs):
        for k in range(cuts):
            span = slice(k * lead, (k + 1) * lead)
            refs[len(waited) + k][...] = (
                a_ref[span].astype(f32) + b_ref[span].astype(f32)
            ).astype(dtype)

    return pl.pallas_call(
        kernel,
        out_shape=[struct((lead, *a.shape[1:]), dtype)] * cuts,
        in_specs=[VMEM_SPEC] * 2 + [ANY_SPEC] * len(waited),
        out_specs=[VMEM_SPEC] * cuts,
        cost_estimate=cost(a.size, 6 * a.size),
        name="plus",
    )(a, b, *waited)


def held(array, waited):
    def kernel(a_ref, *refs):
        refs[-1][...] = a_ref[...]

    return pl.pallas_call(
        kernel,
        out_shape=struct(array.shape, array.dtype),
        in_specs=[VMEM_SPEC] + [ANY_SPEC] * len(waited),
        out_specs=VMEM_SPEC,
        cost_estimate=cost(array.size, 8 * array.size),
        name="held",
    )(array, *waited)


def fold(blocks, waited=()):
    def kernel(ref, *refs):
        for k in range(2):
            total = ref[0, k].astype(f32)
            for z in range(1, 4):
                total = total + ref[z, k].astype(f32)
            refs[len(waited) + k][...] = total.astype(bf16)

    return pl.pallas_call(
        kernel,
        out_shape=[struct(blocks.shape[2:], bf16)] * 2,
        in_specs=[VMEM_SPEC] + [ANY_SPEC] * len(waited),
        out_specs=[VMEM_SPEC] * 2,
        cost_estimate=cost(blocks.size, 3 * blocks.size),
        name="fold",
    )(blocks, *waited)


def joined_sums(lists, waited=(), apart=False):
    rows, width = lists[0].shape[1:]
    count = len(lists)

    def kernel(*refs):
        mine = lax.axis_index("dp") // 2
        for z in range(4):
            total = refs[0][z].astype(f32)
            for k in range(1, count):
                total = total + refs[k][z].astype(f32)
            if apart:
                refs[count + len(waited) + z][...] = total.astype(bf16)
            else:
                refs[-1][z ^ mine] = total.astype(bf16)

    return pl.pallas_call(
        kernel,
        out_shape=[struct((rows, width), bf16)] * 4 if apart else struct((4, rows, width), bf16),
        in_specs=[VMEM_SPEC] * count + [ANY_SPEC] * len(waited),
        out_specs=[VMEM_SPEC] * 4 if apart else VMEM_SPEC,
        cost_estimate=cost(rows * width * 4 * count, rows * width * 8 * count),
        name="joined_sums",
    )(*lists, *waited)


def spread(grads, weight, added=None, after=None, waited=()):
    rows = grads[0].shape[0]

    def kernel(first, second, w, *refs):
        if added is None:
            out = refs[-1]
            out[0] = contract(first[...], w[...], (1, 1)).astype(bf16)
            out[1] = contract(second[...], w[...], (1, 1)).astype(bf16)
            return
        plus_ref, after_ref = refs[:2]
        away, here = refs[-2:]
        away[...] = (contract(first[...], w[...], (1, 1)) + plus_ref[0].astype(f32)).astype(bf16)
        here[...] = contract(second[...], w[...], (1, 1)) + (
            plus_ref[1].astype(f32) + after_ref[...].astype(f32)
        )

    if added is None:
        outs, more = struct((2, rows, D), bf16), []
    else:
        outs, more = [struct((rows, D), bf16), struct((rows, D), f32)], [added, after]
    return pl.pallas_call(
        kernel,
        out_shape=outs,
        in_specs=[VMEM_SPEC] * (3 + len(more)) + [ANY_SPEC] * len(waited),
        out_specs=VMEM_SPEC if added is None else [VMEM_SPEC] * 2,
        cost_estimate=cost(4 * rows * D * weight.shape[1], 5 << 20),
        name="spread",
    )(*grads, weight, *more, *waited)


def pack_queries(w_query, w_key, w_value):
    rows, width = w_query.shape

    def kernel(q, k, v, qkv):
        qkv[...] = jnp.zeros_like(qkv)
        for at, ref in enumerate((q, k, v)):
            qkv[:, at * PAD : at * PAD + width] = ref[...]

    return pl.pallas_call(
        kernel,
        out_shape=struct((rows, 3 * PAD), bf16),
        in_specs=[VMEM_SPEC] * 3,
        out_specs=VMEM_SPEC,
        cost_estimate=cost(rows * PAD, rows * PAD * 8),
        name="pack_queries",
    )(w_query, w_key, w_value)


def pack_weights(w_up, w_out, w_down, waited):
    rows, hidden = w_up.shape
    width = w_out.shape[0]

    def kernel(up, out, down, _, own):
        own[:, :hidden] = up[...]
        own[:, hidden : hidden + PAD] = jnp.zeros((rows, PAD), bf16)
        own[:, hidden : hidden + width] = out[...].T
        own[:, hidden + PAD :] = down[...].T

    return pl.pallas_call(
        kernel,
        out_shape=struct((rows, 2 * hidden + PAD), bf16),
        in_specs=[VMEM_SPEC] * 3 + [ANY_SPEC],
        out_specs=VMEM_SPEC,
        cost_estimate=cost(rows * hidden, 2 << 20),
        name="pack_weights",
    )(w_up, w_out, w_down, waited)


def pair_weights(own, beyond, hidden, waited):
    rows, width = own.shape
    starts = (0, hidden, hidden + PAD, width)

    def kernel(a, b, *refs):
        out = refs[-1]
        for at, end in zip(starts, starts[1:]):
            out[:, 2 * at : at + end] = a[:, at:end]
            out[:, at + end : 2 * end] = b[:, at:end]

    return pl.pallas_call(
        kernel,
        out_shape=struct((rows, 2 * width), bf16),
        in_specs=[VMEM_SPEC] * 2 + [ANY_SPEC] * len(waited),
        out_specs=VMEM_SPEC,
        cost_estimate=cost(rows * width, 4 * rows * width),
        name="pair_weights",
    )(own, beyond, *waited)


def project_in(xs, weights, bias):
    rows = xs[0].shape[0]
    pieces = len(xs)
    sources = len(weights)
    ordered = sources > 1
    bits, far = (2, 4) if ordered else (1, 1)
    part = D // (bits * far)
    wide = weights[0].shape[1]

    def kernel(*refs):
        refs = list(refs)
        ins = [refs.pop(0) for _ in range(pieces)]
        shards = [refs.pop(0) for _ in range(sources)]
        b = refs.pop(0)
        outs = [refs.pop(0) for _ in range(pieces)]
        turned_outs = [refs.pop(0) for _ in range(pieces)]
        whole_out, x_buf, w, out_buf, turned, sems, w_sems, out_sems = refs
        here = lax.axis_index("dp") if ordered else 0
        copies = [
            pltpu.make_async_copy(ins[s], x_buf.at[s], sems.at[s]) for s in range(pieces)
        ]
        fetched = []
        for at in range(sources):
            row = ring_member(RING_STEPS[at]) * part if ordered else 0
            fetched.append(
                pltpu.make_async_copy(
                    shards[at],
                    w.at[pl.ds(pl.multiple_of(row, 16), shards[at].shape[0]), :],
                    w_sems.at[at],
                )
            )
        for copy in fetched + copies:
            copy.start()
        for copy in fetched:
            copy.wait()
        leaving = []

        def leave(ref, to):
            copy = pltpu.make_async_copy(ref, to, out_sems.at[len(leaving)])
            copy.start()
            leaving.append(copy)

        leave(w, whole_out)
        for s in range(pieces):
            copies[s].wait()
            for c in range(0, wide, PAD):
                cols = slice(c, c + PAD)
                out_buf[s, :, cols] = (
                    contract(x_buf[s], w[:, cols], (1, 0)) + b[:, cols]
                ).astype(bf16)
            leave(out_buf.at[s], outs[s])
            for n in range(D // LANES):
                span = slice(n * LANES, (n + 1) * LANES)
                turned[s, span, :] = x_buf[s, :, span].T
            for k in range(bits):
                for z in range(far):
                    row = (here ^ (2 * z + k)) * part if ordered else 0
                    leave(
                        turned.at[s, pl.ds(pl.multiple_of(row, 16), part), :],
                        turned_outs[s].at[k, z],
                    )
        for copy in leaving:
            copy.wait()

    results = pl.pallas_call(
        kernel,
        out_shape=[struct((rows, wide), bf16)] * pieces
        + [struct((bits, far, part, rows), bf16)] * pieces
        + [struct((D, wide), bf16)],
        in_specs=[ANY_SPEC] * (pieces + sources) + [VMEM_SPEC],
        out_specs=[ANY_SPEC] * (2 * pieces + 1),
        scratch_shapes=[
            pltpu.VMEM((pieces, rows, D), bf16),
            pltpu.VMEM((D, wide), bf16),
            pltpu.VMEM((pieces, rows, wide), bf16),
            pltpu.VMEM((pieces, D, rows), bf16),
            pltpu.SemaphoreType.DMA((pieces,)),
            pltpu.SemaphoreType.DMA((sources,)),
            pltpu.SemaphoreType.DMA((1 + pieces * (1 + bits * far),)),
        ],
        cost_estimate=cost(4 * pieces * rows * D * wide, 24 << 20, 0, 1),
        name="project_in",
    )(*xs, *weights, bias)
    return results[:pieces], results[pieces : 2 * pieces], results[2 * pieces]


def padded(array):
    return jnp.pad(array, ((0, 0), (0, PAD - array.shape[1])))


def dot(a, b, dims=(1, 0)):
    return contract(a, b, dims)


def per_device(
    hidden_in,
    grad_out,
    w_query,
    b_query,
    w_key,
    w_value,
    b_value,
    w_out,
    b_out,
    gain_one,
    shift_one,
    w_up,
    b_up,
    w_down,
    b_down,
    gain_two,
    shift_two,
    lengths,
    global_raw,
    random_raw,
):
    own_rows = hidden_in.shape[0]
    me = lax.axis_index("tensor")
    teams = lax.axis_size("tensor")
    members = lax.axis_size("dp")
    width = w_query.shape[1]
    heads = width // HD
    hidden = w_up.shape[1]

    table, bias = block_tables(lengths, global_raw, random_raw, own_rows // BLK, teams)

    qkv_b = jnp.concatenate(
        [jnp.pad(b_query, (0, PAD - width)), jnp.zeros((PAD,), f32), jnp.pad(b_value, (0, PAD - width))]
    )
    halved = members == 8
    if halved:
        queries = pack_queries(w_query, w_key, w_value)
        own = pack_weights(w_up, w_out, w_down, queries)
        qkv_pieces = ring_pieces(queries)
        beyond_own = swap(own, 2)
        shard = pair_weights(own, beyond_own, hidden, qkv_pieces[GATE:])
    else:
        qkv_shard = jnp.concatenate([padded(w_query), padded(w_key), padded(w_value)], axis=1)
        qkv_pieces = [lax.all_gather(qkv_shard, "dp", axis=0, tiled=True)]
        shard = jnp.concatenate([w_up, padded(w_out.T), w_down.T], axis=1)
        weights = lax.all_gather(shard, ("dp", "tensor"), axis=0, tiled=False)
        weights = jnp.swapaxes(weights.reshape(members, teams, *shard.shape), 0, 1)
        weights = [weights.reshape(teams, D, shard.shape[1])]

    x2 = swap(held(hidden_in, (beyond_own,)) if halved else hidden_in, 2)
    x1 = swap(hidden_in, 1)
    x3 = swap(x2, 1)
    qkv, x_turned, qkv_w = project_in([hidden_in, x1, x2, x3], qkv_pieces, qkv_b[None])
    far_mixed, (t2, t3) = attend_forward(qkv, table, bias, heads, (2, 3))
    far_mixed = swap(far_mixed, 2)
    near_mixed, (t0, t1) = attend_forward(qkv, table, bias, heads, (0, 1))
    r1 = swap(near_mixed[1], 1)
    r3 = swap(far_mixed[1], 1)
    if halved:

        weights = ring_pieces(shard)
        weights = weights + [swap(piece, 1) for piece in weights]

    results = layer_rows(
        [(near_mixed, 0), (r1, None), (far_mixed, 0), (r3, None)],
        hidden_in,
        grad_out,
        weights,
        (
            jnp.stack([b_out, gain_one, shift_one, b_down, gain_two, shift_two]),
            b_up.reshape(teams, hidden),
        ),
        lengths,
    )
    layer_out, near_rows, far_rows, turned = results[:4]
    backs = results[4 : 4 + teams]
    after_low, small = results[4 + teams :]
    ups = [backs[0]] + [swap(backs[s], s) for s in range(1, teams)]
    totals = [t0, t1, t2, t3]
    before = attend_backward(qkv, ups[:1], totals[:1], table, bias, heads, (0,))

    next_rows, next_turned = swap(far_rows, 1), swap(turned, 1)
    down_group = (
        [(turned, 1), (next_turned, 1)],
        [[(near_rows, 0), (near_rows, 1)], [(next_rows, 0), (next_rows, 1)]],
    )
    up_group = (
        [(turned, 0), (next_turned, 0)],
        [[(near_rows, 2), (near_rows, 3)], [(next_rows, 2), (next_rows, 3)]],
    )
    out_group = (
        [(turned, 2), (next_turned, 2)],
        [[(near_mixed, 0), (far_mixed, 0)], [(near_mixed, 1), (far_mixed, 1)]],
    )
    if halved:
        (down_gone,) = row_dot([down_group], 2, "far", (before[0], *ups[1:]))
        down_blocks = far_exchange(down_gone)
        up_quads = row_dot([up_group, out_group], 2, "quads", (down_gone,))
        up_gone = up_quads[3]
        up_away = [swap(up_quads[1], 2), dp_swap(up_quads[2], 1), swap_both(up_gone)]
        waited = (up_gone,)
    else:
        down_sums = row_dot([down_group], 2)[0].reshape(2, D, -1)
        up_sums = row_dot([up_group, out_group], 2)[0].reshape(2, D, -1)
        waited = ()
    results = attend_backward(
        qkv,
        ups[1:],
        totals[1:],
        table,
        bias,
        heads,
        (1, 2, 3),
        small,
        waited,
        (before[1], before[2], before[0]),
    )
    grads, tail = results[:4], results[4]
    qkv_group = ([(x[None], 0) for x in x_turned], [[(g[None], 0)] for g in grads])
    if halved:
        kept, gone = row_dot([qkv_group], 1, "bits", (), tail)
        away = dp_swap(gone, 1)
        parts = spread([grads[3], grads[1]], qkv_w, waited=(gone,))
        spread_away = swap(parts, 1)
        up_blocks = joined_sums([a[0, 0] for a in (up_quads[0], *up_away)], (parts,))
        up_arrived = far_exchange(up_blocks)
        beyond, here = spread([grads[2], grads[0]], qkv_w, spread_away, after_low, (up_blocks,))
        beyond_away = swap(beyond, 2)
        down_here, down_next = fold(down_blocks, (beyond,))
        down_away = swap(down_next, 2)
        blocks = joined_sums([kept[0, 0], away[0, 0]], (down_next,))
        arrived = far_exchange(blocks)
        qkv_part = jnp.sum(arrived.astype(f32), axis=0)
        down_here, down_next = plus(down_here, down_away, (blocks,), 2)
        down_away = dp_swap(down_next, 1)
        down_part = down_here[0].astype(f32) + down_away[0].astype(f32)
        up_part = jnp.sum(up_arrived.astype(f32), axis=0)
        qkv_part, small = qkv_part[:-16], qkv_part[-16:]
    else:
        blocks = row_dot([qkv_group], 1)[0].reshape(D, -1)
        qkv_part = dp_scatter_sum(blocks)
        small = lax.psum(tail.astype(f32), "dp")
        spread_away = swap(spread([grads[3], grads[1]], qkv_w), 1)
        beyond, here = spread([grads[2], grads[0]], qkv_w, spread_away, after_low)
        beyond_away = swap(beyond, 2)
        down_part = dp_scatter_sum(down_sums[0] + swap(down_sums[1], 2))
        up_part = dp_scatter_sum(up_sums[0] + swap(up_sums[1], 2))
    grad_in = here + beyond_away.astype(f32)

    bias_row = small[SUM_ROW]
    return (
        layer_out,
        grad_in,
        qkv_part[:, :width],
        bias_row[:width],
        qkv_part[:, PAD : PAD + width],
        qkv_part[:, 2 * PAD : 2 * PAD + width],
        bias_row[2 * PAD : 2 * PAD + width],
        up_part[:, hidden : hidden + width].T,
        small[5],
        small[3],
        small[4],
        up_part[:, :hidden],
        jnp.take(small[6 : 6 + teams], me, axis=0),
        down_part.T,
        small[2],
        small[0],
        small[1],
    )


def solution(mesh):
    in_specs = (
        P(("dp", "tensor"), None),
        P(("dp", "tensor"), None),
        P("dp", "tensor"),
        P("tensor"),
        P("dp", "tensor"),
        P("dp", "tensor"),
        P("tensor"),
        P("tensor", "dp"),
        P(),
        P(),
        P(),
        P("dp", "tensor"),
        P(),
        P("tensor", "dp"),
        P(),
        P(),
        P(),
        P("dp"),
        P("dp", None),
        P("dp", None, None),
    )
    out_specs = (
        P(("dp", "tensor"), None),
        P(("dp", "tensor"), None),
        P("dp", "tensor"),
        P("tensor"),
        P("dp", "tensor"),
        P("dp", "tensor"),
        P("tensor"),
        P("tensor", "dp"),
        P(),
        P(),
        P(),
        P("dp", "tensor"),
        P("tensor"),
        P("tensor", "dp"),
        P(),
        P(),
        P(),
    )
    return jax.shard_map(
        per_device, mesh=mesh, in_specs=in_specs, out_specs=out_specs, check_vma=False
    )
```

```python
from functools import partial

import jax
import jax.numpy as jnp
from jax import lax
from jax.experimental import pallas as pl
from jax.experimental.pallas import tpu as pltpu
from jax.sharding import PartitionSpec as P

D = 768
HD = 64
FF = 3072
BLK = 64
GLOB = 2
RAND = 3
LMAX = 2048
NB = 32
KEYS = (3 + GLOB + RAND) * BLK
PAD = 256
LANES = 128
SUM_ROW = 10
ORDER = (0, 1, 2, 3)
SUM_ROWS = 16
BELOW = SUM_ROWS * (D // LANES)
GATE = 5

masked_score = -1e30
EPSILON = 1e-12
f32 = jnp.float32
bf16 = jnp.bfloat16


def swap(array, bit):
    size = lax.axis_size("tensor")
    return lax.ppermute(array, "tensor", [(t, t ^ bit) for t in range(size)])


def dp_swap(array, bit):
    size = lax.axis_size("dp")
    return lax.ppermute(array, "dp", [(t, t ^ bit) for t in range(size)])


def swap_both(array):
    size = lax.axis_size("dp") * 4
    axes = ("dp", "tensor")
    return lax.ppermute(array, axes, [(t, t ^ 6) for t in range(size)])


def ring_order(size):
    return list(range(0, size, 2)) + list(range(size - 1, 0, -2))


def ring_member(steps):
    size = lax.axis_size("dp")
    me = lax.axis_index("dp")
    place = jnp.where(me % 2 == 0, me // 2, size - 1 - me // 2)
    place = (place + steps + size) % size
    return jnp.where(place < size // 2, 2 * place, 2 * (size - 1 - place) + 1)


def ring_send(array, step):
    size = lax.axis_size("dp")
    order = ring_order(size)
    return lax.ppermute(
        array, "dp", [(order[i], order[(i + step) % size]) for i in range(size)]
    )


RING_STEPS = (0, -1, 1, -2, 2, -3, 3, -4)


def ring_pieces(shard):
    pieces = [shard]
    ahead, behind = shard, shard
    for step in range(1, 5):
        ahead = ring_send(ahead, 1)
        pieces.append(ahead)
        if step < 4:
            behind = ring_send(behind, -1)
            pieces.append(behind)
    return pieces


def far_exchange(blocks):
    groups = [[2 * f + n for f in range(4)] for n in range(2)]
    return lax.all_to_all(blocks, "dp", 0, 0, axis_index_groups=groups, tiled=True)


def dp_scatter_sum(sums):
    size = lax.axis_size("dp")
    if size != 8:
        return lax.psum_scatter(sums, "dp", scatter_dimension=0, tiled=True).astype(f32)
    blocks = lax.all_to_all(sums.reshape(size, -1, sums.shape[1]), "dp", 0, 0, tiled=True)
    return jnp.sum(blocks.astype(f32), axis=0)


def sum_over(vector, dp_only=False):
    if not dp_only:
        bit = 1
        while bit < lax.axis_size("tensor"):
            vector = vector + swap(vector, bit)
            bit *= 2
    bit = 1
    while bit < lax.axis_size("dp"):
        vector = vector + dp_swap(vector, bit)
        bit *= 2
    return vector


def block_tables(lengths, global_raw, random_raw, own_blocks, pieces):
    count = own_blocks * pieces

    def kernel(length_ref, global_ref, random_ref, table, bias):
        me = lax.axis_index("tensor")
        lane = lax.broadcasted_iota(jnp.int32, (1, KEYS), 1)
        slot = lane // BLK
        within = lane % BLK
        wide = lax.broadcasted_iota(jnp.int32, (own_blocks, LANES), 1)
        row = lax.broadcasted_iota(jnp.int32, (own_blocks, 1), 0)
        for s in range(pieces):
            first = (s ^ me) * own_blocks
            seq = first // NB
            start = first - seq * NB
            length = length_ref[seq]
            live = (length + BLK - 1) // BLK
            raw = random_ref[seq, pl.ds(pl.multiple_of(start, 8), own_blocks), :]
            rest = raw - live * jnp.floor(raw.astype(f32) / live.astype(f32)).astype(jnp.int32)
            rest = jnp.where(rest < 0, rest + live, rest)
            rest = jnp.where(rest >= live, rest - live, rest)
            block = row + start
            ids = [jnp.maximum(block - 1, 0), block, jnp.minimum(block + 1, NB - 1)]
            ids += [jnp.full((own_blocks, 1), lax.rem(global_ref[seq, j], live)) for j in range(GLOB)]
            ids += [rest[:, r : r + 1] for r in range(RAND)]
            spread_ids = jnp.zeros((own_blocks, KEYS), jnp.int32)
            packed = jnp.zeros((own_blocks, LANES), jnp.int32)
            for j, own in enumerate(ids):
                spread_ids = jnp.where(slot == j, own, spread_ids)
                there = own + seq * NB
                there = ((there // own_blocks) ^ me) * own_blocks + there % own_blocks
                packed = jnp.where(wide == j, there, packed)
            table[s * own_blocks : (s + 1) * own_blocks, :] = packed
            lost = (spread_ids * BLK + within) >= length
            lost = lost | ((slot == 0) & (block == 0)) | ((slot == 2) & (block == NB - 1))
            bias[s * own_blocks : (s + 1) * own_blocks, :] = jnp.where(lost, masked_score, 0.0).astype(f32)

    smem = pl.BlockSpec(memory_space=pltpu.SMEM)
    vmem = pl.BlockSpec(memory_space=pltpu.VMEM)
    return pl.pallas_call(
        kernel,
        out_shape=[
            jax.ShapeDtypeStruct((count, LANES), jnp.int32),
            jax.ShapeDtypeStruct((count, KEYS), f32),
        ],
        in_specs=[smem, smem, vmem],
        out_specs=[vmem, vmem],
        cost_estimate=cost(count * KEYS * 16, count * KEYS * 4),
        name="block_tables",
    )(lengths, global_raw, random_raw)


def head_masks(heads, scale, dtype):
    lane = lax.broadcasted_iota(jnp.int32, (1, PAD), 1)
    return [
        jnp.where((lane >= h * HD) & (lane < (h + 1) * HD), scale, 0.0).astype(dtype)
        for h in range(heads)
    ]


def stacked_heads(rows, masks):
    return jnp.concatenate([rows * mask for mask in masks], axis=0)


def unstacked_heads(stacked, masks):
    rows = stacked.shape[0] // len(masks)
    total = stacked[:rows] * masks[0]
    for h in range(1, len(masks)):
        total = total + stacked[h * rows : (h + 1) * rows] * masks[h]
    return total


def key_blocks(ref, table, block, column):
    return jnp.concatenate(
        [
            ref[pl.ds(pl.multiple_of(table[block, j] * BLK, BLK), BLK), column : column + PAD]
            for j in range(KEYS // BLK)
        ],
        axis=0,
    )


def contract(a, b, dims):
    return lax.dot_general(a, b, ((dims[:1], dims[1:]), ((), ())), preferred_element_type=f32)


def attend_kernel(heads, chosen, pieces, own_blocks, table, *refs):
    parts = refs[:pieces]
    bias = refs[pieces]
    out = refs[pieces + 1]
    totals = refs[pieces + 2 : pieces + 2 + len(chosen)]
    rows, sems = refs[pieces + 2 + len(chosen) :]
    own_rows = own_blocks * BLK
    copies = [
        pltpu.make_async_copy(
            parts[s], rows.at[pl.ds(s * own_rows, own_rows)], sems.at[s]
        )
        for s in range(pieces)
    ]
    for copy in copies:
        copy.start()
    for copy in copies:
        copy.wait()
    query_masks = head_masks(heads, HD**-0.5, bf16)
    out_masks = head_masks(heads, 1.0, f32)
    lane = lax.broadcasted_iota(jnp.int32, (BLK, LANES), 1)

    side = 2
    count = len(chosen) * side

    def step(step_at, carry):
        blocks, held = [], [{} for _ in range(count)]
        for at in range(count):
            i = step_at * side + at // len(chosen)
            piece = at % len(chosen)
            blocks.append((piece, i, chosen[piece] * own_blocks + i))

        def scored(at):
            block = blocks[at][2]
            here = pl.ds(pl.multiple_of(block * BLK, BLK), BLK)
            queries = stacked_heads(rows[here, 0:PAD], query_masks)
            keys = key_blocks(rows, table, block, PAD)
            held[at]["scores"] = contract(queries, keys, (1, 1))

        def weighed(at):
            has = held[at]
            masked = bias[pl.ds(blocks[at][2], 1), :]
            low, has["total"], has["log_total"] = [], [], []
            for h in range(heads):
                scores = has["scores"][h * BLK : (h + 1) * BLK] + masked
                top = jnp.max(scores, axis=-1, keepdims=True)
                weights = jnp.exp(scores - top)
                total = jnp.sum(weights, axis=-1, keepdims=True)
                low.append(weights.astype(bf16))
                has["total"].append(total)
                has["log_total"].append(top + jnp.log(total))
            has["weights"] = jnp.concatenate(low, axis=0)

        def mixed(at):
            piece, i, block = blocks[at]
            has = held[at]
            values = key_blocks(rows, table, block, 2 * PAD)
            outs = contract(has["weights"], values, (1, 0))
            start = pl.ds(pl.multiple_of(i * BLK, BLK), BLK)
            kept = jnp.zeros((BLK, LANES), f32)
            total = jnp.zeros((BLK, PAD), f32)
            for h in range(heads):
                total = total + outs[h * BLK : (h + 1) * BLK] * (out_masks[h] / has["total"][h])
                kept = jnp.where(lane == h, has["log_total"][h], kept)
            out[piece, start, :] = total.astype(bf16)
            totals[piece][start, :] = kept

        stages = (scored, weighed, mixed)
        for turn in range(count + len(stages) - 1):
            for k in range(len(stages)):
                if 0 <= turn - k < count:
                    stages[k](turn - k)
        return carry

    lax.fori_loop(0, own_blocks // side, step, 0)


def attend_forward(parts, table, bias, heads, chosen):
    own_rows = parts[0].shape[0]
    pieces = len(parts)
    own_blocks = own_rows // BLK
    n = len(chosen)
    vmem = pl.BlockSpec(memory_space=pltpu.VMEM)
    work = n * own_rows * KEYS * heads
    results = pl.pallas_call(
        partial(attend_kernel, heads, chosen, pieces, own_blocks),
        out_shape=[jax.ShapeDtypeStruct((n, own_rows, PAD), bf16)]
        + [jax.ShapeDtypeStruct((own_rows, LANES), f32)] * n,
        in_specs=[pl.BlockSpec(memory_space=pltpu.SMEM)]
        + [pl.BlockSpec(memory_space=pl.ANY)] * pieces
        + [vmem],
        out_specs=[vmem] * (1 + n),
        scratch_shapes=[
            pltpu.VMEM((pieces * own_rows, 3 * PAD), bf16),
            pltpu.SemaphoreType.DMA((pieces,)),
        ],
        cost_estimate=cost(48 * work * HD, 16 << 20, 4 * work, 1),
        name="attend_forward",
    )(table, *parts, bias)
    return results[0], results[1:]


def attend_back_kernel(heads, chosen, pieces, own_blocks, waited, carried, table, *refs):
    refs = list(refs)

    def take(count):
        taken = refs[:count]
        del refs[:count]
        return taken

    parts = take(pieces)
    ups = take(len(chosen))
    totals = take(len(chosen))
    (bias,) = take(1)
    take(waited)
    if carried:
        key_before, value_before = take(2)
        query_before = take(pieces - len(chosen))
        (small_ref,) = take(1)
        outs = take(pieces)
        (tail,) = take(1)
        key_sum, value_sum, key_kept, value_kept, row_sums = take(5)
    else:
        outs = take(len(chosen))
        key_sum, value_sum = take(2)
    rows, up_rows, up_packed, sems = refs
    own_rows = own_blocks * BLK
    copies = [
        pltpu.make_async_copy(parts[s], rows.at[pl.ds(s * own_rows, own_rows)], sems.at[s])
        for s in range(pieces)
    ] + [
        pltpu.make_async_copy(ups[at], up_packed.at[at], sems.at[pieces + at])
        for at in range(len(chosen))
    ]
    late = []
    if carried:
        late = [
            pltpu.make_async_copy(key_before, key_kept, sems.at[pieces + len(chosen)]),
            pltpu.make_async_copy(value_before, value_kept, sems.at[pieces + len(chosen) + 1]),
        ]
    for copy in copies + late:
        copy.start()
    key_sum[...] = jnp.zeros_like(key_sum)
    value_sum[...] = jnp.zeros_like(value_sum)
    for copy in copies:
        copy.wait()
    query_masks = head_masks(heads, HD**-0.5, bf16)
    up_masks = head_masks(heads, 1.0, bf16)
    out_masks = head_masks(heads, HD**-0.5, f32)
    half = own_rows // 2
    for at in range(len(chosen)):
        up_rows[at, :, :LANES] = up_packed[at, :own_rows, :]
        last = up_packed[at, own_rows : own_rows + half, :]
        up_rows[at, :half, LANES:] = last
        up_rows[at, half:, LANES:] = pltpu.roll(last.astype(f32), HD, 1).astype(bf16)

    side = 2 if len(chosen) == 1 else 1

    count = len(chosen) * side

    def step(step_at, carry):
        blocks, held = [], [{} for _ in range(count)]
        for at in range(count):
            i = step_at * side + at // len(chosen)
            piece = at % len(chosen)
            blocks.append((piece, i, chosen[piece] * own_blocks + i))

        def scored(at):
            piece, i, block = blocks[at]
            start = pl.multiple_of(i * BLK, BLK)
            here = pl.ds(pl.multiple_of(block * BLK, BLK), BLK)
            has = held[at]
            has["queries"] = stacked_heads(rows[here, 0:PAD], query_masks)
            has["upstream"] = stacked_heads(up_rows[piece, pl.ds(start, BLK), :], up_masks)
            has["keys"] = key_blocks(rows, table, block, PAD)
            values = key_blocks(rows, table, block, 2 * PAD)
            has["scores"] = contract(has["queries"], has["keys"], (1, 1))
            has["grad_weights"] = contract(has["upstream"], values, (1, 1))

        def weighed(at):
            piece, i, block = blocks[at]
            has = held[at]
            kept = totals[piece][pl.ds(pl.multiple_of(i * BLK, BLK), BLK), :]
            masked = bias[pl.ds(block, 1), :]
            low, grad = [], []
            for h in range(heads):
                span = slice(h * BLK, (h + 1) * BLK)
                weights = jnp.exp(has["scores"][span] + (masked - kept[:, h : h + 1]))
                grad_weights = has["grad_weights"][span]
                inner = jnp.sum(weights * grad_weights, axis=-1, keepdims=True)
                low.append(weights.astype(bf16))
                grad.append((weights * (grad_weights - inner)).astype(bf16))
            has["weights"] = jnp.concatenate(low, axis=0)
            has["grad_scores"] = jnp.concatenate(grad, axis=0)

        def spread_back(at):
            piece, i, block = blocks[at]
            has = held[at]
            to = outs[chosen[piece]] if carried else outs[piece]
            grad_query = contract(has["grad_scores"], has["keys"], (1, 0))
            to[pl.ds(pl.multiple_of(i * BLK, BLK), BLK), 0:PAD] = unstacked_heads(
                grad_query, out_masks
            ).astype(bf16)
            has["key_part"] = contract(has["grad_scores"], has["queries"], (0, 0))
            has["value_part"] = contract(has["weights"], has["upstream"], (0, 0))

        def summed(at):
            block, has = blocks[at][2], held[at]
            for j in range(KEYS // BLK):
                there = pl.ds(pl.multiple_of(table[block, j] * BLK, BLK), BLK)
                key_sum[there, :] += has["key_part"][j * BLK : (j + 1) * BLK]
                value_sum[there, :] += has["value_part"][j * BLK : (j + 1) * BLK]

        stages = (scored, weighed, spread_back, summed)
        for turn in range(count + len(stages) - 1):
            for k in ORDER:
                at = turn - k
                if 0 <= at < count:
                    stages[k](at)
        return carry

    lax.fori_loop(0, own_blocks // side, step, 0)
    if not carried:
        return
    for copy in late:
        copy.wait()
    before = [s for s in range(pieces) if s not in chosen]
    for at, s in enumerate(before):
        outs[s][:, 0:PAD] = query_before[at][...]
    row_sums[...] = jnp.zeros_like(row_sums)
    for s in range(pieces):

        def finish(i, carry, s=s):
            at = pl.ds(pl.multiple_of(i * BLK, BLK), BLK)
            span = pl.ds(pl.multiple_of(s * own_rows + i * BLK, BLK), BLK)
            outs[s][at, PAD : 2 * PAD] = (key_sum[span, :] + key_kept[span, :]).astype(bf16)
            outs[s][at, 2 * PAD : 3 * PAD] = (value_sum[span, :] + value_kept[span, :]).astype(bf16)
            whole = outs[s][at, :].astype(f32)
            row_sums[...] += jnp.sum(whole.reshape(BLK // 8, 8, 3 * PAD), axis=0)
            return carry

        lax.fori_loop(0, own_blocks, finish, 0)
    slot = lax.broadcasted_iota(jnp.int32, tail.shape, 0)
    whole = jnp.sum(row_sums[...], axis=0, keepdims=True)
    small = small_ref[...]
    for at in range(len(chosen)):
        parts = [
            up_packed[at, own_rows + half + k * SUM_ROWS : own_rows + half + (k + 1) * SUM_ROWS, :]
            for k in range(BELOW // SUM_ROWS)
        ]
        small = small + jnp.concatenate(parts, axis=1).astype(f32)
    tail[...] = jnp.where(slot == SUM_ROW, whole, small).astype(bf16)


def attend_backward(parts, ups, totals, table, bias, heads, chosen, small=None, waited=(), before=None):
    own_rows = parts[0].shape[0]
    pieces = len(parts)
    n = len(chosen)
    own_blocks = own_rows // BLK
    vmem = pl.BlockSpec(memory_space=pltpu.VMEM)
    anyspace = pl.BlockSpec(memory_space=pl.ANY)
    work = n * own_rows * KEYS * heads
    sum_shape = (pieces * own_rows, PAD)
    if before is None:
        outs = [((own_rows, PAD), bf16)] * n + [(sum_shape, f32)] * 2
        extra, extra_specs, scratch = [], [], []
    else:
        outs = [((own_rows, 3 * PAD), bf16)] * pieces + [((16, 3 * PAD), bf16)]
        extra = [*before, small]
        extra_specs = [anyspace] * 2 + [vmem] * (len(before) - 1)
        scratch = [pltpu.VMEM(sum_shape, f32)] * 4 + [pltpu.VMEM((8, 3 * PAD), f32)]
    return pl.pallas_call(
        partial(
            attend_back_kernel, heads, chosen, pieces, own_blocks, len(waited), before is not None
        ),
        out_shape=[jax.ShapeDtypeStruct(*out) for out in outs],
        in_specs=[pl.BlockSpec(memory_space=pltpu.SMEM)]
        + [anyspace] * (pieces + n)
        + [vmem] * (n + 1)
        + [anyspace] * len(waited)
        + extra_specs,
        out_specs=[vmem] * len(outs),
        scratch_shapes=scratch
        + [
            pltpu.VMEM((pieces * own_rows, 3 * PAD), bf16),
            pltpu.VMEM((n, own_rows, PAD), bf16),
            pltpu.VMEM((n, own_rows + own_rows // 2 + BELOW, LANES), bf16),
            pltpu.SemaphoreType.DMA((pieces + n + 2,)),
        ],
        cost_estimate=cost(30 * work * HD, 12 << 20, work),
        name="attend_backward",
    )(table, *parts, *ups, *totals, bias, *waited, *extra)


VMEM_SPEC = pl.BlockSpec(memory_space=pltpu.VMEM)
ANY_SPEC = pl.BlockSpec(memory_space=pl.ANY)
SMEM_SPEC = pl.BlockSpec(memory_space=pltpu.SMEM)
COST_CUT = 64
GELU_A = 0.7978845608028654
GELU_B = 0.044715


def cost(flops, size, transcendentals=0, cut=None):
    cut = cut or COST_CUT
    return pl.CostEstimate(
        flops=flops // cut, bytes_accessed=size // cut, transcendentals=transcendentals // cut
    )


def struct(shape, dtype):
    return jax.ShapeDtypeStruct(shape, dtype)


def row_stats(values):
    centred = values - jnp.mean(values, axis=-1, keepdims=True)
    inv_std = lax.rsqrt(jnp.mean(centred * centred, axis=-1, keepdims=True) + EPSILON)
    return centred * inv_std, inv_std


def norm_backward(upstream, scaled, inv_std, gain):
    weighted = upstream * gain
    inner = jnp.mean(weighted * scaled, axis=-1, keepdims=True)
    return inv_std * (weighted - jnp.mean(weighted, axis=-1, keepdims=True) - scaled * inner)


def column_sum(array):
    return jnp.sum(array.reshape(array.shape[0] // 8, 8, array.shape[1]), axis=0)


def rows_kernel(places, sources, length, *refs):
    teams = len(places)
    refs = list(refs)

    def take(count):
        taken = refs[:count]
        del refs[:count]
        return taken

    mixed = take(teams)
    x_in, g_in = take(2)
    weights = take(sources)
    vectors, b_up = take(2)
    b_out, g1, c1, b_down, g2, c2 = [vectors.at[k : k + 1, :] for k in range(6)]
    layer_out, near_out, far_out, turned_out = take(4)
    back_out = take(teams)
    after_out, small = take(2)
    (
        o_buf,
        x_buf,
        g_buf,
        out_w,
        up_w,
        down_w,
        scaled_buf,
        inv_buf,
        wide_buf,
        low_buf,
        act_buf,
        slope_buf,
        last_buf,
        turned_buf,
        send_buf,
        sums,
        up_sums,
        in_sems,
        w_sems,
        out_sems,
    ) = refs
    rows = x_in.shape[0]
    hidden = up_w.shape[2]
    tile, cut = 64, 256
    me = lax.axis_index("tensor")
    ring = sources > 1

    first = []
    for s in range(teams):
        source = mixed[s] if places[s] is None else mixed[s].at[places[s]]
        first.append(
            pltpu.make_async_copy(source, o_buf.at[s], in_sems.at[s])
        )
    first.append(pltpu.make_async_copy(x_in, x_buf, in_sems.at[teams]))
    upstream_copy = pltpu.make_async_copy(g_in, g_buf, in_sems.at[teams + 1])
    fetched = ([], [], [])

    def fetch(kind, source, to):
        sem = w_sems.at[kind, len(fetched[kind])]
        fetched[kind].append(pltpu.make_async_copy(source, to, sem))

    wholes = (out_w, up_w, down_w)
    if ring:
        part = weights[0].shape[0]
        spans = ((2 * hidden, PAD), (0, hidden), (2 * hidden + 2 * PAD, hidden))
        for at, piece in enumerate(weights):
            row = pl.multiple_of(ring_member(RING_STEPS[at % 8]) * part, 16)
            for kind, (start, size) in enumerate(spans):
                for pair in range(2):
                    fetch(
                        kind,
                        piece.at[:, pl.ds(start + pair * size, size)],
                        wholes[kind].at[2 * pair + at // 8, pl.ds(row, part), :],
                    )
    else:
        spans = ((hidden, PAD), (0, hidden), (hidden + PAD, hidden))
        for kind, (start, size) in enumerate(spans):
            for s in range(teams):
                fetch(kind, weights[0].at[me ^ s, :, pl.ds(start, size)], wholes[kind].at[s])
    for copy in first + fetched[0] + fetched[1] + fetched[2] + [upstream_copy]:
        copy.start()
    sums[...] = jnp.zeros_like(sums)
    up_sums[...] = jnp.zeros_like(up_sums)
    leaving = []

    def leave(ref, to):
        copy = pltpu.make_async_copy(ref, to, out_sems.at[len(leaving)])
        copy.start()
        leaving.append(copy)

    def leave_turned(k, source, to):
        for n in range(D // LANES):
            span = slice(n * LANES, (n + 1) * LANES)
            turned_buf[k, span, :] = source[:, span].T
        bits, far, part, _ = to.shape
        here = lax.axis_index("dp")
        for b in range(bits):
            for z in range(far):
                row = (here ^ (2 * z + b)) * part if ring else 0
                leave(turned_buf.at[k, pl.ds(pl.multiple_of(row, 16), part), :], to.at[b, z])

    def tiles(body):
        def step(i, carry):
            body(i, pl.ds(pl.multiple_of(i * tile, tile), tile))
            return carry

        lax.fori_loop(0, rows // tile, step, 0)

    for copy in first + fetched[0]:
        copy.wait()
    for n in range(D // cut):
        cols = slice(n * cut, (n + 1) * cut)
        total = contract(o_buf[0, :rows, :], out_w[0, cols, :], (1, 1))
        for s in range(1, teams):
            total = total + contract(o_buf[s, :rows, :], out_w[s, cols, :], (1, 1))
        wide_buf[:, cols] = total

    def first_norm(i, at):
        after = x_buf[at, :].astype(f32) + wide_buf[at, :] + b_out[...]
        scaled, inv_std = row_stats(after)
        scaled_buf[at, :] = scaled
        inv_buf[at, :] = jnp.broadcast_to(inv_std, (tile, LANES))
        low_buf[at, :] = (scaled * g1[...] + c1[...]).astype(bf16)

    tiles(first_norm)
    leave_turned(0, low_buf, turned_out.at[0])
    for copy in fetched[1]:
        copy.wait()

    def up_step(s, carry):
        bias = b_up[pl.ds(s ^ me, 1), :]
        for c in range(hidden // cut):
            cols = slice(c * cut, (c + 1) * cut)
            u = contract(low_buf[...], up_w[s, :, cols], (1, 0)) + bias[:, cols]
            cubic = (GELU_A * GELU_B) * (u * u)
            t = jnp.tanh(u * (GELU_A + cubic))
            half = 0.5 + 0.5 * t
            act = u * half
            act_buf[s, :, cols] = act.astype(bf16)
            slope_buf[s, :, cols] = (
                half + act * ((1.0 - t) * (GELU_A + 3.0 * cubic))
            ).astype(bf16)
        return carry

    lax.fori_loop(0, teams, up_step, 0)
    for s in range(teams):
        leave(act_buf.at[s], (far_out if s % 2 else near_out).at[s // 2])
    for copy in fetched[2]:
        copy.wait()
    upstream_copy.wait()
    for n in range(D // cut):
        cols = slice(n * cut, (n + 1) * cut)
        total = contract(act_buf[0], down_w[0, cols, :], (1, 1))
        for s in range(1, teams):
            total = total + contract(act_buf[s], down_w[s, cols, :], (1, 1))
        wide_buf[:, cols] = total
    start = me * rows
    seq = start // LMAX
    live = length[seq] - (start - seq * LMAX)

    def second_norm(i, at):
        z = (scaled_buf[at, :] * g1[...] + c1[...]) + wide_buf[at, :] + b_down[...]
        scaled, inv_std = row_stats(z)
        x_buf[at, :] = (scaled * g2[...] + c2[...]).astype(bf16)
        row = lax.broadcasted_iota(jnp.int32, (tile, D), 0) + i * tile
        upstream = jnp.where(row < live, g_buf[at, :].astype(f32), 0.0)
        grad = norm_backward(upstream, scaled, inv_std, g2[...]).astype(bf16)
        g_buf[at, :] = grad
        sums[0:8, :] += column_sum(upstream * scaled)
        sums[8:16, :] += column_sum(upstream)
        sums[16:24, :] += column_sum(grad.astype(f32))

    tiles(second_norm)
    leave(x_buf, layer_out)
    leave_turned(1, g_buf, turned_out.at[1])

    def down_back(s, carry):
        for c in range(hidden // cut):
            cols = slice(c * cut, (c + 1) * cut)
            g = contract(g_buf[...], down_w[s, :, cols], (1, 0))
            g = (g * slope_buf[s, :, cols].astype(f32)).astype(bf16)
            slope_buf[s, :, cols] = g
            up_sums[pl.ds(pl.multiple_of(s * 8, 8), 8), cols] = column_sum(g.astype(f32))
        return carry

    lax.fori_loop(0, teams, down_back, 0)
    for s in range(teams):
        leave(slope_buf.at[s], (far_out if s % 2 else near_out).at[2 + s // 2])
    for n in range(D // cut):
        cols = slice(n * cut, (n + 1) * cut)
        total = contract(slope_buf[0], up_w[0, cols, :], (1, 1))
        for s in range(1, teams):
            total = total + contract(slope_buf[s], up_w[s, cols, :], (1, 1))
        wide_buf[:, cols] = total

    def first_back(i, at):
        upstream = g_buf[at, :].astype(f32) + wide_buf[at, :]
        scaled = scaled_buf[at, :]
        grad = norm_backward(upstream, scaled, inv_buf[at, :][:, :1], g1[...]).astype(bf16)
        last_buf[at, :] = grad
        sums[24:32, :] += column_sum(upstream * scaled)
        sums[32:40, :] += column_sum(upstream)
        sums[40:48, :] += column_sum(grad.astype(f32))

    tiles(first_back)
    leave(last_buf, after_out)
    leave_turned(2, last_buf, turned_out.at[2])
    small[...] = jnp.zeros_like(small)
    for k in range(6):
        small[k : k + 1, :] = jnp.sum(sums[8 * k : 8 * k + 8, :], axis=0, keepdims=True)
    for s in range(teams):
        small[pl.ds(6 + (s ^ me), 1), :] = jnp.sum(
            up_sums[8 * s : 8 * s + 8, :], axis=0, keepdims=True
        )
    for s in (2, 3, 1, 0):
        back = contract(last_buf[...], out_w[s], (1, 0))
        half = rows // 2
        send_buf[s, :rows, :] = back[:, :LANES].astype(bf16)
        send_buf[s, rows : rows + half, :] = (
            back[:half, LANES:] + pltpu.roll(back[half:, LANES:], HD, 1)
        ).astype(bf16)
        for k in range(D // LANES):
            at = rows + half + k * SUM_ROWS
            send_buf[s, at : at + SUM_ROWS, :] = small[:, k * LANES : (k + 1) * LANES].astype(bf16)
        leave(send_buf.at[s], back_out[s])
    for copy in leaving:
        copy.wait()


def layer_rows(mixed, hidden_in, grad_out, weights, vectors, lengths):
    teams = len(mixed)
    rows = hidden_in.shape[0]
    rows_of, b_up = vectors
    hidden = b_up.shape[1]
    half = teams // 2
    low = struct((rows, D), bf16)
    pair = struct((2 * half, rows, hidden), bf16)
    ring = len(weights) > 1
    turned = struct((3, 2, 4, D // 8, rows) if ring else (3, 1, 1, D, rows), bf16)
    return pl.pallas_call(
        partial(rows_kernel, [at for _, at in mixed], len(weights)),
        out_shape=[low, pair, pair, turned]
        + [struct((rows + rows // 2 + BELOW, LANES), bf16)] * teams
        + [low, struct((16, D), f32)],
        in_specs=[SMEM_SPEC]
        + [ANY_SPEC] * (teams + 2 + len(weights))
        + [VMEM_SPEC] * 2,
        out_specs=[ANY_SPEC] * (5 + teams) + [VMEM_SPEC],
        scratch_shapes=[
            pltpu.VMEM((teams, rows, PAD), bf16),
            pltpu.VMEM((rows, D), bf16),
            pltpu.VMEM((rows, D), bf16),
            pltpu.VMEM((teams, D, PAD), bf16),
            pltpu.VMEM((teams, D, hidden), bf16),
            pltpu.VMEM((teams, D, hidden), bf16),
            pltpu.VMEM((rows, D), f32),
            pltpu.VMEM((rows, LANES), f32),
            pltpu.VMEM((rows, D), f32),
            pltpu.VMEM((rows, D), bf16),
            pltpu.VMEM((teams, rows, hidden), bf16),
            pltpu.VMEM((teams, rows, hidden), bf16),
            pltpu.VMEM((rows, D), bf16),
            pltpu.VMEM((3, D, rows), bf16),
            pltpu.VMEM((teams, rows + rows // 2 + BELOW, LANES), bf16),
            pltpu.VMEM((48, D), f32),
            pltpu.VMEM((8 * teams, hidden), f32),
            pltpu.SemaphoreType.DMA((teams + 2,)),
            pltpu.SemaphoreType.DMA((3, 32)),
            pltpu.SemaphoreType.DMA((2 + 3 * teams + 24,)),
        ],
        cost_estimate=cost(8 * rows * D * (teams * hidden) + 4 * rows * D * teams * PAD, 24 << 20),
        compiler_params=pltpu.CompilerParams(vmem_limit_bytes=60 << 20),
        name="layer_rows",
    )(
        lengths,
        *[array for array, _ in mixed],
        hidden_in,
        grad_out,
        *weights,
        rows_of,
        b_up,
    )


def row_dot(groups, count, cut_by=None, waited=(), tail=None):
    sets = len(groups[0][0])
    bits, far, part, rows = groups[0][0][0][0].shape[1:]
    cut = 256
    lows = [0]
    for _, rights in groups:
        lows.append(lows[-1] + rights[0][0][0].shape[2] // cut)
    high = bits * far * part
    below = 0 if tail is None else tail.shape[0]
    cuts = {"bits": 2, "quads": 4}.get(cut_by, 1)

    def kernel(*refs):
        refs = list(refs)
        ins = [[refs.pop(0) for _ in range(sets)] for _ in groups]
        others = [[[refs.pop(0) for _ in range(count)] for _ in range(sets)] for _ in groups]
        if below:
            tail_ref = refs.pop(0)
        outs = refs[len(waited) :]
        j = pl.program_id(0)
        for g in range(len(groups)):

            @pl.when((j >= lows[g]) & (j < lows[g + 1]))
            def _(g=g):
                for i in range(count):
                    total = contract(ins[g][0][...].reshape(high, rows), others[g][0][i][...], (1, 0))
                    for k in range(1, sets):
                        total = total + contract(
                            ins[g][k][...].reshape(high, rows), others[g][k][i][...], (1, 0)
                        )
                    total = total.astype(bf16).reshape(bits, far, part, cut)
                    if cut_by == "far":
                        mine = lax.axis_index("dp") // 2
                        for z in range(far):
                            outs[0][z ^ mine, i] = total[:, z]
                        continue
                    for b in range(bits):
                        if cut_by == "bits":
                            to = outs[b].at[i, 0]
                        elif cut_by == "quads":
                            to = outs[2 * b + i].at[0, 0]
                        else:
                            to = outs[0].at[i, b]
                        if below:
                            to[:, :part, :] = total[b]
                            to[:, part:, :] = jnp.broadcast_to(
                                tail_ref[...][None], (far, below, cut)
                            )
                        else:
                            to[...] = total[b]

    def column(g, at):
        return lambda j: (at, 0, jnp.clip(j - lows[g], 0, lows[g + 1] - lows[g] - 1))

    specs, arrays = [], []
    for lefts, _ in groups:
        for array, at in lefts:
            specs.append(
                pl.BlockSpec((None, bits, far, part, rows), lambda j, at=at: (at, 0, 0, 0, 0))
            )
            arrays.append(array)
    for g, (_, rights) in enumerate(groups):
        for pairs in rights:
            for array, at in pairs:
                specs.append(pl.BlockSpec((None, rows, cut), column(g, at)))
                arrays.append(array)
    if below:
        specs.append(pl.BlockSpec((below, cut), lambda j: (0, j)))
        arrays.append(tail)
    width = lows[-1] * cut
    lead = (1 if cut_by == "quads" else count, 1 if cut_by in ("bits", "quads") else bits)
    return pl.pallas_call(
        kernel,
        grid=(lows[-1],),
        out_shape=[
            struct((far, *lead, part, width) if cut_by == "far" else (*lead, far, part + below, width), bf16)
        ]
        * cuts,
        in_specs=specs + [ANY_SPEC] * len(waited),
        out_specs=[
            pl.BlockSpec(
                (far, *lead, part, cut) if cut_by == "far" else (*lead, far, part + below, cut),
                lambda j: (0, 0, 0, 0, j),
            )
        ]
        * cuts,
        cost_estimate=cost(2 * sets * rows * high * count * width, 8 << 20),
        name="row_dot",
    )(*arrays, *waited)


def plus(a, b, waited=(), cuts=1, dtype=bf16):
    lead = a.shape[0] // cuts

    def kernel(a_ref, b_ref, *refs):
        for k in range(cuts):
            span = slice(k * lead, (k + 1) * lead)
            refs[len(waited) + k][...] = (
                a_ref[span].astype(f32) + b_ref[span].astype(f32)
            ).astype(dtype)

    return pl.pallas_call(
        kernel,
        out_shape=[struct((lead, *a.shape[1:]), dtype)] * cuts,
        in_specs=[VMEM_SPEC] * 2 + [ANY_SPEC] * len(waited),
        out_specs=[VMEM_SPEC] * cuts,
        cost_estimate=cost(a.size, 6 * a.size),
        name="plus",
    )(a, b, *waited)


def held(array, waited):
    def kernel(a_ref, *refs):
        refs[-1][...] = a_ref[...]

    return pl.pallas_call(
        kernel,
        out_shape=struct(array.shape, array.dtype),
        in_specs=[VMEM_SPEC] + [ANY_SPEC] * len(waited),
        out_specs=VMEM_SPEC,
        cost_estimate=cost(array.size, 8 * array.size),
        name="held",
    )(array, *waited)


def fold(blocks, waited=()):
    def kernel(ref, *refs):
        for k in range(2):
            total = ref[0, k].astype(f32)
            for z in range(1, 4):
                total = total + ref[z, k].astype(f32)
            refs[len(waited) + k][...] = total.astype(bf16)

    return pl.pallas_call(
        kernel,
        out_shape=[struct(blocks.shape[2:], bf16)] * 2,
        in_specs=[VMEM_SPEC] + [ANY_SPEC] * len(waited),
        out_specs=[VMEM_SPEC] * 2,
        cost_estimate=cost(blocks.size, 3 * blocks.size),
        name="fold",
    )(blocks, *waited)


def joined_sums(lists, waited=(), apart=False):
    rows, width = lists[0].shape[1:]
    count = len(lists)

    def kernel(*refs):
        mine = lax.axis_index("dp") // 2
        for z in range(4):
            total = refs[0][z].astype(f32)
            for k in range(1, count):
                total = total + refs[k][z].astype(f32)
            if apart:
                refs[count + len(waited) + z][...] = total.astype(bf16)
            else:
                refs[-1][z ^ mine] = total.astype(bf16)

    return pl.pallas_call(
        kernel,
        out_shape=[struct((rows, width), bf16)] * 4 if apart else struct((4, rows, width), bf16),
        in_specs=[VMEM_SPEC] * count + [ANY_SPEC] * len(waited),
        out_specs=[VMEM_SPEC] * 4 if apart else VMEM_SPEC,
        cost_estimate=cost(rows * width * 4 * count, rows * width * 8 * count),
        name="joined_sums",
    )(*lists, *waited)


def spread(grads, weight, added=None, after=None, waited=()):
    rows = grads[0].shape[0]

    def kernel(first, second, w, *refs):
        if added is None:
            out = refs[-1]
            out[0] = contract(first[...], w[...], (1, 1)).astype(bf16)
            out[1] = contract(second[...], w[...], (1, 1)).astype(bf16)
            return
        plus_ref, after_ref = refs[:2]
        away, here = refs[-2:]
        away[...] = (contract(first[...], w[...], (1, 1)) + plus_ref[0].astype(f32)).astype(bf16)
        here[...] = contract(second[...], w[...], (1, 1)) + (
            plus_ref[1].astype(f32) + after_ref[...].astype(f32)
        )

    if added is None:
        outs, more = struct((2, rows, D), bf16), []
    else:
        outs, more = [struct((rows, D), bf16), struct((rows, D), f32)], [added, after]
    return pl.pallas_call(
        kernel,
        out_shape=outs,
        in_specs=[VMEM_SPEC] * (3 + len(more)) + [ANY_SPEC] * len(waited),
        out_specs=VMEM_SPEC if added is None else [VMEM_SPEC] * 2,
        cost_estimate=cost(4 * rows * D * weight.shape[1], 5 << 20),
        name="spread",
    )(*grads, weight, *more, *waited)


def pack_queries(w_query, w_key, w_value):
    rows, width = w_query.shape

    def kernel(q, k, v, qkv):
        qkv[...] = jnp.zeros_like(qkv)
        for at, ref in enumerate((q, k, v)):
            qkv[:, at * PAD : at * PAD + width] = ref[...]

    return pl.pallas_call(
        kernel,
        out_shape=struct((rows, 3 * PAD), bf16),
        in_specs=[VMEM_SPEC] * 3,
        out_specs=VMEM_SPEC,
        cost_estimate=cost(rows * PAD, rows * PAD * 8),
        name="pack_queries",
    )(w_query, w_key, w_value)


def pack_weights(w_up, w_out, w_down, waited):
    rows, hidden = w_up.shape
    width = w_out.shape[0]

    def kernel(up, out, down, _, own):
        own[:, :hidden] = up[...]
        own[:, hidden : hidden + PAD] = jnp.zeros((rows, PAD), bf16)
        own[:, hidden : hidden + width] = out[...].T
        own[:, hidden + PAD :] = down[...].T

    return pl.pallas_call(
        kernel,
        out_shape=struct((rows, 2 * hidden + PAD), bf16),
        in_specs=[VMEM_SPEC] * 3 + [ANY_SPEC],
        out_specs=VMEM_SPEC,
        cost_estimate=cost(rows * hidden, 2 << 20),
        name="pack_weights",
    )(w_up, w_out, w_down, waited)


def pair_weights(own, beyond, hidden, waited):
    rows, width = own.shape
    starts = (0, hidden, hidden + PAD, width)

    def kernel(a, b, *refs):
        out = refs[-1]
        for at, end in zip(starts, starts[1:]):
            out[:, 2 * at : at + end] = a[:, at:end]
            out[:, at + end : 2 * end] = b[:, at:end]

    return pl.pallas_call(
        kernel,
        out_shape=struct((rows, 2 * width), bf16),
        in_specs=[VMEM_SPEC] * 2 + [ANY_SPEC] * len(waited),
        out_specs=VMEM_SPEC,
        cost_estimate=cost(rows * width, 4 * rows * width),
        name="pair_weights",
    )(own, beyond, *waited)


def project_in(xs, weights, bias):
    rows = xs[0].shape[0]
    pieces = len(xs)
    sources = len(weights)
    ordered = sources > 1
    bits, far = (2, 4) if ordered else (1, 1)
    part = D // (bits * far)
    wide = weights[0].shape[1]

    def kernel(*refs):
        refs = list(refs)
        ins = [refs.pop(0) for _ in range(pieces)]
        shards = [refs.pop(0) for _ in range(sources)]
        b = refs.pop(0)
        outs = [refs.pop(0) for _ in range(pieces)]
        turned_outs = [refs.pop(0) for _ in range(pieces)]
        whole_out, x_buf, w, out_buf, turned, sems, w_sems, out_sems = refs
        here = lax.axis_index("dp") if ordered else 0
        copies = [
            pltpu.make_async_copy(ins[s], x_buf.at[s], sems.at[s]) for s in range(pieces)
        ]
        fetched = []
        for at in range(sources):
            row = ring_member(RING_STEPS[at]) * part if ordered else 0
            fetched.append(
                pltpu.make_async_copy(
                    shards[at],
                    w.at[pl.ds(pl.multiple_of(row, 16), shards[at].shape[0]), :],
                    w_sems.at[at],
                )
            )
        for copy in fetched + copies:
            copy.start()
        for copy in fetched:
            copy.wait()
        leaving = []

        def leave(ref, to):
            copy = pltpu.make_async_copy(ref, to, out_sems.at[len(leaving)])
            copy.start()
            leaving.append(copy)

        leave(w, whole_out)
        for s in range(pieces):
            copies[s].wait()
            for c in range(0, wide, PAD):
                cols = slice(c, c + PAD)
                out_buf[s, :, cols] = (
                    contract(x_buf[s], w[:, cols], (1, 0)) + b[:, cols]
                ).astype(bf16)
            leave(out_buf.at[s], outs[s])
            for n in range(D // LANES):
                span = slice(n * LANES, (n + 1) * LANES)
                turned[s, span, :] = x_buf[s, :, span].T
            for k in range(bits):
                for z in range(far):
                    row = (here ^ (2 * z + k)) * part if ordered else 0
                    leave(
                        turned.at[s, pl.ds(pl.multiple_of(row, 16), part), :],
                        turned_outs[s].at[k, z],
                    )
        for copy in leaving:
            copy.wait()

    results = pl.pallas_call(
        kernel,
        out_shape=[struct((rows, wide), bf16)] * pieces
        + [struct((bits, far, part, rows), bf16)] * pieces
        + [struct((D, wide), bf16)],
        in_specs=[ANY_SPEC] * (pieces + sources) + [VMEM_SPEC],
        out_specs=[ANY_SPEC] * (2 * pieces + 1),
        scratch_shapes=[
            pltpu.VMEM((pieces, rows, D), bf16),
            pltpu.VMEM((D, wide), bf16),
            pltpu.VMEM((pieces, rows, wide), bf16),
            pltpu.VMEM((pieces, D, rows), bf16),
            pltpu.SemaphoreType.DMA((pieces,)),
            pltpu.SemaphoreType.DMA((sources,)),
            pltpu.SemaphoreType.DMA((1 + pieces * (1 + bits * far),)),
        ],
        cost_estimate=cost(4 * pieces * rows * D * wide, 24 << 20, 0, 1),
        name="project_in",
    )(*xs, *weights, bias)
    return results[:pieces], results[pieces : 2 * pieces], results[2 * pieces]


def padded(array):
    return jnp.pad(array, ((0, 0), (0, PAD - array.shape[1])))


def dot(a, b, dims=(1, 0)):
    return contract(a, b, dims)


def per_device(
    hidden_in,
    grad_out,
    w_query,
    b_query,
    w_key,
    w_value,
    b_value,
    w_out,
    b_out,
    gain_one,
    shift_one,
    w_up,
    b_up,
    w_down,
    b_down,
    gain_two,
    shift_two,
    lengths,
    global_raw,
    random_raw,
):
    own_rows = hidden_in.shape[0]
    me = lax.axis_index("tensor")
    teams = lax.axis_size("tensor")
    members = lax.axis_size("dp")
    width = w_query.shape[1]
    heads = width // HD
    hidden = w_up.shape[1]

    table, bias = block_tables(lengths, global_raw, random_raw, own_rows // BLK, teams)

    qkv_b = jnp.concatenate(
        [jnp.pad(b_query, (0, PAD - width)), jnp.zeros((PAD,), f32), jnp.pad(b_value, (0, PAD - width))]
    )
    halved = members == 8
    if halved:
        queries = pack_queries(w_query, w_key, w_value)
        own = pack_weights(w_up, w_out, w_down, queries)
        qkv_pieces = ring_pieces(queries)
        beyond_own = swap(own, 2)
        shard = pair_weights(own, beyond_own, hidden, qkv_pieces[GATE:])
    else:
        qkv_shard = jnp.concatenate([padded(w_query), padded(w_key), padded(w_value)], axis=1)
        qkv_pieces = [lax.all_gather(qkv_shard, "dp", axis=0, tiled=True)]
        shard = jnp.concatenate([w_up, padded(w_out.T), w_down.T], axis=1)
        weights = lax.all_gather(shard, ("dp", "tensor"), axis=0, tiled=False)
        weights = jnp.swapaxes(weights.reshape(members, teams, *shard.shape), 0, 1)
        weights = [weights.reshape(teams, D, shard.shape[1])]

    x2 = swap(held(hidden_in, (beyond_own,)) if halved else hidden_in, 2)
    x1 = swap(hidden_in, 1)
    x3 = swap(x2, 1)
    qkv, x_turned, qkv_w = project_in([hidden_in, x1, x2, x3], qkv_pieces, qkv_b[None])
    far_mixed, (t2, t3) = attend_forward(qkv, table, bias, heads, (2, 3))
    far_mixed = swap(far_mixed, 2)
    near_mixed, (t0, t1) = attend_forward(qkv, table, bias, heads, (0, 1))
    r1 = swap(near_mixed[1], 1)
    r3 = swap(far_mixed[1], 1)
    if halved:

        weights = ring_pieces(shard)
        weights = weights + [swap(piece, 1) for piece in weights]

    results = layer_rows(
        [(near_mixed, 0), (r1, None), (far_mixed, 0), (r3, None)],
        hidden_in,
        grad_out,
        weights,
        (
            jnp.stack([b_out, gain_one, shift_one, b_down, gain_two, shift_two]),
            b_up.reshape(teams, hidden),
        ),
        lengths,
    )
    layer_out, near_rows, far_rows, turned = results[:4]
    backs = results[4 : 4 + teams]
    after_low, small = results[4 + teams :]
    ups = [backs[0]] + [swap(backs[s], s) for s in range(1, teams)]
    totals = [t0, t1, t2, t3]
    before = attend_backward(qkv, ups[:1], totals[:1], table, bias, heads, (0,))

    next_rows, next_turned = swap(far_rows, 1), swap(turned, 1)
    down_group = (
        [(turned, 1), (next_turned, 1)],
        [[(near_rows, 0), (near_rows, 1)], [(next_rows, 0), (next_rows, 1)]],
    )
    up_group = (
        [(turned, 0), (next_turned, 0)],
        [[(near_rows, 2), (near_rows, 3)], [(next_rows, 2), (next_rows, 3)]],
    )
    out_group = (
        [(turned, 2), (next_turned, 2)],
        [[(near_mixed, 0), (far_mixed, 0)], [(near_mixed, 1), (far_mixed, 1)]],
    )
    if halved:
        (down_gone,) = row_dot([down_group], 2, "far", (before[0], *ups[1:]))
        down_blocks = far_exchange(down_gone)
        up_quads = row_dot([up_group, out_group], 2, "quads", (down_gone,))
        up_gone = up_quads[3]
        up_away = [swap(up_quads[1], 2), dp_swap(up_quads[2], 1), swap_both(up_gone)]
        waited = (up_gone,)
    else:
        down_sums = row_dot([down_group], 2)[0].reshape(2, D, -1)
        up_sums = row_dot([up_group, out_group], 2)[0].reshape(2, D, -1)
        waited = ()
    results = attend_backward(
        qkv,
        ups[1:],
        totals[1:],
        table,
        bias,
        heads,
        (1, 2, 3),
        small,
        waited,
        (before[1], before[2], before[0]),
    )
    grads, tail = results[:4], results[4]
    qkv_group = ([(x[None], 0) for x in x_turned], [[(g[None], 0)] for g in grads])
    if halved:
        kept, gone = row_dot([qkv_group], 1, "bits", (), tail)
        away = dp_swap(gone, 1)
        parts = spread([grads[3], grads[1]], qkv_w, waited=(gone, *up_away))
        spread_away = swap(parts, 1)
        up_blocks = joined_sums([a[0, 0] for a in (up_quads[0], *up_away)], (parts,), True)
        up_part = up_blocks[0].astype(f32)
        for z in range(1, 4):
            up_part = up_part + dp_swap(up_blocks[z], 2 * z).astype(f32)
        beyond, here = spread([grads[2], grads[0]], qkv_w, spread_away, after_low, (up_blocks[0],))
        beyond_away = swap(beyond, 2)
        down_here, down_next = fold(down_blocks, (beyond,))
        down_away = swap(down_next, 2)
        blocks = joined_sums([kept[0, 0], away[0, 0]], (down_next,))
        arrived = far_exchange(blocks)
        qkv_part = jnp.sum(arrived.astype(f32), axis=0)
        down_here, down_next = plus(down_here, down_away, (blocks,), 2)
        down_away = dp_swap(down_next, 1)
        down_part = down_here[0].astype(f32) + down_away[0].astype(f32)
        qkv_part, small = qkv_part[:-16], qkv_part[-16:]
    else:
        blocks = row_dot([qkv_group], 1)[0].reshape(D, -1)
        qkv_part = dp_scatter_sum(blocks)
        small = lax.psum(tail.astype(f32), "dp")
        spread_away = swap(spread([grads[3], grads[1]], qkv_w), 1)
        beyond, here = spread([grads[2], grads[0]], qkv_w, spread_away, after_low)
        beyond_away = swap(beyond, 2)
        down_part = dp_scatter_sum(down_sums[0] + swap(down_sums[1], 2))
        up_part = dp_scatter_sum(up_sums[0] + swap(up_sums[1], 2))
    grad_in = here + beyond_away.astype(f32)

    bias_row = small[SUM_ROW]
    return (
        layer_out,
        grad_in,
        qkv_part[:, :width],
        bias_row[:width],
        qkv_part[:, PAD : PAD + width],
        qkv_part[:, 2 * PAD : 2 * PAD + width],
        bias_row[2 * PAD : 2 * PAD + width],
        up_part[:, hidden : hidden + width].T,
        small[5],
        small[3],
        small[4],
        up_part[:, :hidden],
        jnp.take(small[6 : 6 + teams], me, axis=0),
        down_part.T,
        small[2],
        small[0],
        small[1],
    )


def solution(mesh):
    in_specs = (
        P(("dp", "tensor"), None),
        P(("dp", "tensor"), None),
        P("dp", "tensor"),
        P("tensor"),
        P("dp", "tensor"),
        P("dp", "tensor"),
        P("tensor"),
        P("tensor", "dp"),
        P(),
        P(),
        P(),
        P("dp", "tensor"),
        P(),
        P("tensor", "dp"),
        P(),
        P(),
        P(),
        P("dp"),
        P("dp", None),
        P("dp", None, None),
    )
    out_specs = (
        P(("dp", "tensor"), None),
        P(("dp", "tensor"), None),
        P("dp", "tensor"),
        P("tensor"),
        P("dp", "tensor"),
        P("dp", "tensor"),
        P("tensor"),
        P("tensor", "dp"),
        P(),
        P(),
        P(),
        P("dp", "tensor"),
        P("tensor"),
        P("tensor", "dp"),
        P(),
        P(),
        P(),
    )
    return jax.shard_map(
        per_device, mesh=mesh, in_specs=in_specs, out_specs=out_specs, check_vma=False
    )
```

```python
from functools import partial

import jax
import jax.numpy as jnp
from jax import lax
from jax.experimental import pallas as pl
from jax.experimental.pallas import tpu as pltpu
from jax.sharding import PartitionSpec as P

D = 768
HD = 64
FF = 3072
BLK = 64
GLOB = 2
RAND = 3
LMAX = 2048
NB = 32
KEYS = (3 + GLOB + RAND) * BLK
PAD = 256
LANES = 128
SUM_ROW = 10
ORDER = (0, 1, 2, 3)
SUM_ROWS = 16
BELOW = SUM_ROWS * (D // LANES)
GATE = 5

masked_score = -1e30
EPSILON = 1e-12
f32 = jnp.float32
bf16 = jnp.bfloat16


def swap(array, bit):
    size = lax.axis_size("tensor")
    return lax.ppermute(array, "tensor", [(t, t ^ bit) for t in range(size)])


def dp_swap(array, bit):
    size = lax.axis_size("dp")
    return lax.ppermute(array, "dp", [(t, t ^ bit) for t in range(size)])


def swap_both(array):
    size = lax.axis_size("dp") * 4
    axes = ("dp", "tensor")
    return lax.ppermute(array, axes, [(t, t ^ 6) for t in range(size)])


def ring_order(size):
    return list(range(0, size, 2)) + list(range(size - 1, 0, -2))


def ring_member(steps):
    size = lax.axis_size("dp")
    me = lax.axis_index("dp")
    place = jnp.where(me % 2 == 0, me // 2, size - 1 - me // 2)
    place = (place + steps + size) % size
    return jnp.where(place < size // 2, 2 * place, 2 * (size - 1 - place) + 1)


def ring_send(array, step):
    size = lax.axis_size("dp")
    order = ring_order(size)
    return lax.ppermute(
        array, "dp", [(order[i], order[(i + step) % size]) for i in range(size)]
    )


RING_STEPS = (0, -1, 1, -2, 2, -3, 3, -4)


def ring_pieces(shard):
    pieces = [shard]
    ahead, behind = shard, shard
    for step in range(1, 5):
        ahead = ring_send(ahead, 1)
        pieces.append(ahead)
        if step < 4:
            behind = ring_send(behind, -1)
            pieces.append(behind)
    return pieces


def far_exchange(blocks):
    groups = [[2 * f + n for f in range(4)] for n in range(2)]
    return lax.all_to_all(blocks, "dp", 0, 0, axis_index_groups=groups, tiled=True)


def dp_scatter_sum(sums):
    size = lax.axis_size("dp")
    if size != 8:
        return lax.psum_scatter(sums, "dp", scatter_dimension=0, tiled=True).astype(f32)
    blocks = lax.all_to_all(sums.reshape(size, -1, sums.shape[1]), "dp", 0, 0, tiled=True)
    return jnp.sum(blocks.astype(f32), axis=0)


def sum_over(vector, dp_only=False):
    if not dp_only:
        bit = 1
        while bit < lax.axis_size("tensor"):
            vector = vector + swap(vector, bit)
            bit *= 2
    bit = 1
    while bit < lax.axis_size("dp"):
        vector = vector + dp_swap(vector, bit)
        bit *= 2
    return vector


def block_tables(lengths, global_raw, random_raw, own_blocks, pieces):
    count = own_blocks * pieces

    def kernel(length_ref, global_ref, random_ref, table, bias):
        me = lax.axis_index("tensor")
        lane = lax.broadcasted_iota(jnp.int32, (1, KEYS), 1)
        slot = lane // BLK
        within = lane % BLK
        wide = lax.broadcasted_iota(jnp.int32, (own_blocks, LANES), 1)
        row = lax.broadcasted_iota(jnp.int32, (own_blocks, 1), 0)
        for s in range(pieces):
            first = (s ^ me) * own_blocks
            seq = first // NB
            start = first - seq * NB
            length = length_ref[seq]
            live = (length + BLK - 1) // BLK
            raw = random_ref[seq, pl.ds(pl.multiple_of(start, 8), own_blocks), :]
            rest = raw - live * jnp.floor(raw.astype(f32) / live.astype(f32)).astype(jnp.int32)
            rest = jnp.where(rest < 0, rest + live, rest)
            rest = jnp.where(rest >= live, rest - live, rest)
            block = row + start
            ids = [jnp.maximum(block - 1, 0), block, jnp.minimum(block + 1, NB - 1)]
            ids += [jnp.full((own_blocks, 1), lax.rem(global_ref[seq, j], live)) for j in range(GLOB)]
            ids += [rest[:, r : r + 1] for r in range(RAND)]
            spread_ids = jnp.zeros((own_blocks, KEYS), jnp.int32)
            packed = jnp.zeros((own_blocks, LANES), jnp.int32)
            for j, own in enumerate(ids):
                spread_ids = jnp.where(slot == j, own, spread_ids)
                there = own + seq * NB
                there = ((there // own_blocks) ^ me) * own_blocks + there % own_blocks
                packed = jnp.where(wide == j, there, packed)
            table[s * own_blocks : (s + 1) * own_blocks, :] = packed
            lost = (spread_ids * BLK + within) >= length
            lost = lost | ((slot == 0) & (block == 0)) | ((slot == 2) & (block == NB - 1))
            bias[s * own_blocks : (s + 1) * own_blocks, :] = jnp.where(lost, masked_score, 0.0).astype(f32)

    smem = pl.BlockSpec(memory_space=pltpu.SMEM)
    vmem = pl.BlockSpec(memory_space=pltpu.VMEM)
    return pl.pallas_call(
        kernel,
        out_shape=[
            jax.ShapeDtypeStruct((count, LANES), jnp.int32),
            jax.ShapeDtypeStruct((count, KEYS), f32),
        ],
        in_specs=[smem, smem, vmem],
        out_specs=[vmem, vmem],
        cost_estimate=cost(count * KEYS * 16, count * KEYS * 4),
        name="block_tables",
    )(lengths, global_raw, random_raw)


def head_masks(heads, scale, dtype):
    lane = lax.broadcasted_iota(jnp.int32, (1, PAD), 1)
    return [
        jnp.where((lane >= h * HD) & (lane < (h + 1) * HD), scale, 0.0).astype(dtype)
        for h in range(heads)
    ]


def stacked_heads(rows, masks):
    return jnp.concatenate([rows * mask for mask in masks], axis=0)


def unstacked_heads(stacked, masks):
    rows = stacked.shape[0] // len(masks)
    total = stacked[:rows] * masks[0]
    for h in range(1, len(masks)):
        total = total + stacked[h * rows : (h + 1) * rows] * masks[h]
    return total


def key_blocks(ref, table, block, column):
    return jnp.concatenate(
        [
            ref[pl.ds(pl.multiple_of(table[block, j] * BLK, BLK), BLK), column : column + PAD]
            for j in range(KEYS // BLK)
        ],
        axis=0,
    )


def contract(a, b, dims):
    return lax.dot_general(a, b, ((dims[:1], dims[1:]), ((), ())), preferred_element_type=f32)


def attend_kernel(heads, chosen, pieces, own_blocks, table, *refs):
    parts = refs[:pieces]
    bias = refs[pieces]
    out = refs[pieces + 1]
    totals = refs[pieces + 2 : pieces + 2 + len(chosen)]
    rows, sems = refs[pieces + 2 + len(chosen) :]
    own_rows = own_blocks * BLK
    copies = [
        pltpu.make_async_copy(
            parts[s], rows.at[pl.ds(s * own_rows, own_rows)], sems.at[s]
        )
        for s in range(pieces)
    ]
    for copy in copies:
        copy.start()
    for copy in copies:
        copy.wait()
    query_masks = head_masks(heads, HD**-0.5, bf16)
    out_masks = head_masks(heads, 1.0, f32)
    lane = lax.broadcasted_iota(jnp.int32, (BLK, LANES), 1)

    side = 2
    count = len(chosen) * side

    def step(step_at, carry):
        blocks, held = [], [{} for _ in range(count)]
        for at in range(count):
            i = step_at * side + at // len(chosen)
            piece = at % len(chosen)
            blocks.append((piece, i, chosen[piece] * own_blocks + i))

        def scored(at):
            block = blocks[at][2]
            here = pl.ds(pl.multiple_of(block * BLK, BLK), BLK)
            queries = stacked_heads(rows[here, 0:PAD], query_masks)
            keys = key_blocks(rows, table, block, PAD)
            held[at]["scores"] = contract(queries, keys, (1, 1))

        def weighed(at):
            has = held[at]
            masked = bias[pl.ds(blocks[at][2], 1), :]
            low, has["total"], has["log_total"] = [], [], []
            for h in range(heads):
                scores = has["scores"][h * BLK : (h + 1) * BLK] + masked
                top = jnp.max(scores, axis=-1, keepdims=True)
                weights = jnp.exp(scores - top)
                total = jnp.sum(weights, axis=-1, keepdims=True)
                low.append(weights.astype(bf16))
                has["total"].append(total)
                has["log_total"].append(top + jnp.log(total))
            has["weights"] = jnp.concatenate(low, axis=0)

        def mixed(at):
            piece, i, block = blocks[at]
            has = held[at]
            values = key_blocks(rows, table, block, 2 * PAD)
            outs = contract(has["weights"], values, (1, 0))
            start = pl.ds(pl.multiple_of(i * BLK, BLK), BLK)
            kept = jnp.zeros((BLK, LANES), f32)
            total = jnp.zeros((BLK, PAD), f32)
            for h in range(heads):
                total = total + outs[h * BLK : (h + 1) * BLK] * (out_masks[h] / has["total"][h])
                kept = jnp.where(lane == h, has["log_total"][h], kept)
            out[piece, start, :] = total.astype(bf16)
            totals[piece][start, :] = kept

        stages = (scored, weighed, mixed)
        for turn in range(count + len(stages) - 1):
            for k in range(len(stages)):
                if 0 <= turn - k < count:
                    stages[k](turn - k)
        return carry

    lax.fori_loop(0, own_blocks // side, step, 0)


def attend_forward(parts, table, bias, heads, chosen):
    own_rows = parts[0].shape[0]
    pieces = len(parts)
    own_blocks = own_rows // BLK
    n = len(chosen)
    vmem = pl.BlockSpec(memory_space=pltpu.VMEM)
    work = n * own_rows * KEYS * heads
    results = pl.pallas_call(
        partial(attend_kernel, heads, chosen, pieces, own_blocks),
        out_shape=[jax.ShapeDtypeStruct((n, own_rows, PAD), bf16)]
        + [jax.ShapeDtypeStruct((own_rows, LANES), f32)] * n,
        in_specs=[pl.BlockSpec(memory_space=pltpu.SMEM)]
        + [pl.BlockSpec(memory_space=pl.ANY)] * pieces
        + [vmem],
        out_specs=[vmem] * (1 + n),
        scratch_shapes=[
            pltpu.VMEM((pieces * own_rows, 3 * PAD), bf16),
            pltpu.SemaphoreType.DMA((pieces,)),
        ],
        cost_estimate=cost(48 * work * HD, 16 << 20, 4 * work, 1),
        name="attend_forward",
    )(table, *parts, bias)
    return results[0], results[1:]


def attend_back_kernel(heads, chosen, pieces, own_blocks, waited, carried, table, *refs):
    refs = list(refs)

    def take(count):
        taken = refs[:count]
        del refs[:count]
        return taken

    parts = take(pieces)
    ups = take(len(chosen))
    totals = take(len(chosen))
    (bias,) = take(1)
    take(waited)
    if carried:
        key_before, value_before = take(2)
        query_before = take(pieces - len(chosen))
        (small_ref,) = take(1)
        outs = take(pieces)
        (tail,) = take(1)
        key_sum, value_sum, key_kept, value_kept, row_sums = take(5)
    else:
        outs = take(len(chosen))
        key_sum, value_sum = take(2)
    rows, up_rows, up_packed, sems = refs
    own_rows = own_blocks * BLK
    copies = [
        pltpu.make_async_copy(parts[s], rows.at[pl.ds(s * own_rows, own_rows)], sems.at[s])
        for s in range(pieces)
    ] + [
        pltpu.make_async_copy(ups[at], up_packed.at[at], sems.at[pieces + at])
        for at in range(len(chosen))
    ]
    late = []
    if carried:
        late = [
            pltpu.make_async_copy(key_before, key_kept, sems.at[pieces + len(chosen)]),
            pltpu.make_async_copy(value_before, value_kept, sems.at[pieces + len(chosen) + 1]),
        ]
    for copy in copies + late:
        copy.start()
    key_sum[...] = jnp.zeros_like(key_sum)
    value_sum[...] = jnp.zeros_like(value_sum)
    for copy in copies:
        copy.wait()
    query_masks = head_masks(heads, HD**-0.5, bf16)
    up_masks = head_masks(heads, 1.0, bf16)
    out_masks = head_masks(heads, HD**-0.5, f32)
    half = own_rows // 2
    for at in range(len(chosen)):
        up_rows[at, :, :LANES] = up_packed[at, :own_rows, :]
        last = up_packed[at, own_rows : own_rows + half, :]
        up_rows[at, :half, LANES:] = last
        up_rows[at, half:, LANES:] = pltpu.roll(last.astype(f32), HD, 1).astype(bf16)

    side = 2 if len(chosen) == 1 else 1

    count = len(chosen) * side

    def step(step_at, carry):
        blocks, held = [], [{} for _ in range(count)]
        for at in range(count):
            i = step_at * side + at // len(chosen)
            piece = at % len(chosen)
            blocks.append((piece, i, chosen[piece] * own_blocks + i))

        def scored(at):
            piece, i, block = blocks[at]
            start = pl.multiple_of(i * BLK, BLK)
            here = pl.ds(pl.multiple_of(block * BLK, BLK), BLK)
            has = held[at]
            has["queries"] = stacked_heads(rows[here, 0:PAD], query_masks)
            has["upstream"] = stacked_heads(up_rows[piece, pl.ds(start, BLK), :], up_masks)
            has["keys"] = key_blocks(rows, table, block, PAD)
            values = key_blocks(rows, table, block, 2 * PAD)
            has["scores"] = contract(has["queries"], has["keys"], (1, 1))
            has["grad_weights"] = contract(has["upstream"], values, (1, 1))

        def weighed(at):
            piece, i, block = blocks[at]
            has = held[at]
            kept = totals[piece][pl.ds(pl.multiple_of(i * BLK, BLK), BLK), :]
            masked = bias[pl.ds(block, 1), :]
            low, grad = [], []
            for h in range(heads):
                span = slice(h * BLK, (h + 1) * BLK)
                weights = jnp.exp(has["scores"][span] + (masked - kept[:, h : h + 1]))
                grad_weights = has["grad_weights"][span]
                inner = jnp.sum(weights * grad_weights, axis=-1, keepdims=True)
                low.append(weights.astype(bf16))
                grad.append((weights * (grad_weights - inner)).astype(bf16))
            has["weights"] = jnp.concatenate(low, axis=0)
            has["grad_scores"] = jnp.concatenate(grad, axis=0)

        def spread_back(at):
            piece, i, block = blocks[at]
            has = held[at]
            to = outs[chosen[piece]] if carried else outs[piece]
            grad_query = contract(has["grad_scores"], has["keys"], (1, 0))
            to[pl.ds(pl.multiple_of(i * BLK, BLK), BLK), 0:PAD] = unstacked_heads(
                grad_query, out_masks
            ).astype(bf16)
            has["key_part"] = contract(has["grad_scores"], has["queries"], (0, 0))
            has["value_part"] = contract(has["weights"], has["upstream"], (0, 0))

        def summed(at):
            block, has = blocks[at][2], held[at]
            for j in range(KEYS // BLK):
                there = pl.ds(pl.multiple_of(table[block, j] * BLK, BLK), BLK)
                key_sum[there, :] += has["key_part"][j * BLK : (j + 1) * BLK]
                value_sum[there, :] += has["value_part"][j * BLK : (j + 1) * BLK]

        stages = (scored, weighed, spread_back, summed)
        for turn in range(count + len(stages) - 1):
            for k in ORDER:
                at = turn - k
                if 0 <= at < count:
                    stages[k](at)
        return carry

    lax.fori_loop(0, own_blocks // side, step, 0)
    if not carried:
        return
    for copy in late:
        copy.wait()
    before = [s for s in range(pieces) if s not in chosen]
    for at, s in enumerate(before):
        outs[s][:, 0:PAD] = query_before[at][...]
    row_sums[...] = jnp.zeros_like(row_sums)
    for s in range(pieces):

        def finish(i, carry, s=s):
            at = pl.ds(pl.multiple_of(i * BLK, BLK), BLK)
            span = pl.ds(pl.multiple_of(s * own_rows + i * BLK, BLK), BLK)
            outs[s][at, PAD : 2 * PAD] = (key_sum[span, :] + key_kept[span, :]).astype(bf16)
            outs[s][at, 2 * PAD : 3 * PAD] = (value_sum[span, :] + value_kept[span, :]).astype(bf16)
            whole = outs[s][at, :].astype(f32)
            row_sums[...] += jnp.sum(whole.reshape(BLK // 8, 8, 3 * PAD), axis=0)
            return carry

        lax.fori_loop(0, own_blocks, finish, 0)
    slot = lax.broadcasted_iota(jnp.int32, tail.shape, 0)
    whole = jnp.sum(row_sums[...], axis=0, keepdims=True)
    small = small_ref[...]
    for at in range(len(chosen)):
        parts = [
            up_packed[at, own_rows + half + k * SUM_ROWS : own_rows + half + (k + 1) * SUM_ROWS, :]
            for k in range(BELOW // SUM_ROWS)
        ]
        small = small + jnp.concatenate(parts, axis=1).astype(f32)
    tail[...] = jnp.where(slot == SUM_ROW, whole, small).astype(bf16)


def attend_backward(parts, ups, totals, table, bias, heads, chosen, small=None, waited=(), before=None):
    own_rows = parts[0].shape[0]
    pieces = len(parts)
    n = len(chosen)
    own_blocks = own_rows // BLK
    vmem = pl.BlockSpec(memory_space=pltpu.VMEM)
    anyspace = pl.BlockSpec(memory_space=pl.ANY)
    work = n * own_rows * KEYS * heads
    sum_shape = (pieces * own_rows, PAD)
    if before is None:
        outs = [((own_rows, PAD), bf16)] * n + [(sum_shape, f32)] * 2
        extra, extra_specs, scratch = [], [], []
    else:
        outs = [((own_rows, 3 * PAD), bf16)] * pieces + [((16, 3 * PAD), bf16)]
        extra = [*before, small]
        extra_specs = [anyspace] * 2 + [vmem] * (len(before) - 1)
        scratch = [pltpu.VMEM(sum_shape, f32)] * 4 + [pltpu.VMEM((8, 3 * PAD), f32)]
    return pl.pallas_call(
        partial(
            attend_back_kernel, heads, chosen, pieces, own_blocks, len(waited), before is not None
        ),
        out_shape=[jax.ShapeDtypeStruct(*out) for out in outs],
        in_specs=[pl.BlockSpec(memory_space=pltpu.SMEM)]
        + [anyspace] * (pieces + n)
        + [vmem] * (n + 1)
        + [anyspace] * len(waited)
        + extra_specs,
        out_specs=[vmem] * len(outs),
        scratch_shapes=scratch
        + [
            pltpu.VMEM((pieces * own_rows, 3 * PAD), bf16),
            pltpu.VMEM((n, own_rows, PAD), bf16),
            pltpu.VMEM((n, own_rows + own_rows // 2 + BELOW, LANES), bf16),
            pltpu.SemaphoreType.DMA((pieces + n + 2,)),
        ],
        cost_estimate=cost(30 * work * HD, 12 << 20, work),
        name="attend_backward",
    )(table, *parts, *ups, *totals, bias, *waited, *extra)


VMEM_SPEC = pl.BlockSpec(memory_space=pltpu.VMEM)
ANY_SPEC = pl.BlockSpec(memory_space=pl.ANY)
SMEM_SPEC = pl.BlockSpec(memory_space=pltpu.SMEM)
COST_CUT = 64
GELU_A = 0.7978845608028654
GELU_B = 0.044715


def cost(flops, size, transcendentals=0, cut=None):
    cut = cut or COST_CUT
    return pl.CostEstimate(
        flops=flops // cut, bytes_accessed=size // cut, transcendentals=transcendentals // cut
    )


def struct(shape, dtype):
    return jax.ShapeDtypeStruct(shape, dtype)


def row_stats(values):
    centred = values - jnp.mean(values, axis=-1, keepdims=True)
    inv_std = lax.rsqrt(jnp.mean(centred * centred, axis=-1, keepdims=True) + EPSILON)
    return centred * inv_std, inv_std


def norm_backward(upstream, scaled, inv_std, gain):
    weighted = upstream * gain
    inner = jnp.mean(weighted * scaled, axis=-1, keepdims=True)
    return inv_std * (weighted - jnp.mean(weighted, axis=-1, keepdims=True) - scaled * inner)


def column_sum(array):
    return jnp.sum(array.reshape(array.shape[0] // 8, 8, array.shape[1]), axis=0)


def rows_kernel(places, sources, length, *refs):
    teams = len(places)
    refs = list(refs)

    def take(count):
        taken = refs[:count]
        del refs[:count]
        return taken

    mixed = take(teams)
    x_in, g_in = take(2)
    weights = take(sources)
    vectors, b_up = take(2)
    b_out, g1, c1, b_down, g2, c2 = [vectors.at[k : k + 1, :] for k in range(6)]
    layer_out, near_out, far_out, turned_out = take(4)
    back_out = take(teams)
    after_out, small = take(2)
    (
        o_buf,
        x_buf,
        g_buf,
        out_w,
        up_w,
        down_w,
        scaled_buf,
        inv_buf,
        wide_buf,
        low_buf,
        act_buf,
        slope_buf,
        last_buf,
        turned_buf,
        send_buf,
        sums,
        up_sums,
        in_sems,
        w_sems,
        out_sems,
    ) = refs
    rows = x_in.shape[0]
    hidden = up_w.shape[2]
    tile, cut = 64, 256
    me = lax.axis_index("tensor")
    ring = sources > 1

    first = []
    for s in range(teams):
        source = mixed[s] if places[s] is None else mixed[s].at[places[s]]
        first.append(
            pltpu.make_async_copy(source, o_buf.at[s], in_sems.at[s])
        )
    first.append(pltpu.make_async_copy(x_in, x_buf, in_sems.at[teams]))
    upstream_copy = pltpu.make_async_copy(g_in, g_buf, in_sems.at[teams + 1])
    fetched = ([], [], [])

    def fetch(kind, source, to):
        sem = w_sems.at[kind, len(fetched[kind])]
        fetched[kind].append(pltpu.make_async_copy(source, to, sem))

    wholes = (out_w, up_w, down_w)
    if ring:
        part = weights[0].shape[0]
        spans = ((2 * hidden, PAD), (0, hidden), (2 * hidden + 2 * PAD, hidden))
        for at, piece in enumerate(weights):
            row = pl.multiple_of(ring_member(RING_STEPS[at % 8]) * part, 16)
            for kind, (start, size) in enumerate(spans):
                for pair in range(2):
                    fetch(
                        kind,
                        piece.at[:, pl.ds(start + pair * size, size)],
                        wholes[kind].at[2 * pair + at // 8, pl.ds(row, part), :],
                    )
    else:
        spans = ((hidden, PAD), (0, hidden), (hidden + PAD, hidden))
        for kind, (start, size) in enumerate(spans):
            for s in range(teams):
                fetch(kind, weights[0].at[me ^ s, :, pl.ds(start, size)], wholes[kind].at[s])
    for copy in first + fetched[0] + fetched[1] + fetched[2] + [upstream_copy]:
        copy.start()
    sums[...] = jnp.zeros_like(sums)
    up_sums[...] = jnp.zeros_like(up_sums)
    leaving = []

    def leave(ref, to):
        copy = pltpu.make_async_copy(ref, to, out_sems.at[len(leaving)])
        copy.start()
        leaving.append(copy)

    def leave_turned(k, source, to):
        for n in range(D // LANES):
            span = slice(n * LANES, (n + 1) * LANES)
            turned_buf[k, span, :] = source[:, span].T
        bits, far, part, _ = to.shape
        here = lax.axis_index("dp")
        for b in range(bits):
            for z in range(far):
                row = (here ^ (2 * z + b)) * part if ring else 0
                leave(turned_buf.at[k, pl.ds(pl.multiple_of(row, 16), part), :], to.at[b, z])

    def tiles(body):
        def step(i, carry):
            body(i, pl.ds(pl.multiple_of(i * tile, tile), tile))
            return carry

        lax.fori_loop(0, rows // tile, step, 0)

    for copy in first + fetched[0]:
        copy.wait()
    for n in range(D // cut):
        cols = slice(n * cut, (n + 1) * cut)
        total = contract(o_buf[0, :rows, :], out_w[0, cols, :], (1, 1))
        for s in range(1, teams):
            total = total + contract(o_buf[s, :rows, :], out_w[s, cols, :], (1, 1))
        wide_buf[:, cols] = total

    def first_norm(i, at):
        after = x_buf[at, :].astype(f32) + wide_buf[at, :] + b_out[...]
        scaled, inv_std = row_stats(after)
        scaled_buf[at, :] = scaled
        inv_buf[at, :] = jnp.broadcast_to(inv_std, (tile, LANES))
        low_buf[at, :] = (scaled * g1[...] + c1[...]).astype(bf16)

    tiles(first_norm)
    leave_turned(0, low_buf, turned_out.at[0])
    for copy in fetched[1]:
        copy.wait()

    def up_step(s, carry):
        bias = b_up[pl.ds(s ^ me, 1), :]
        for c in range(hidden // cut):
            cols = slice(c * cut, (c + 1) * cut)
            u = contract(low_buf[...], up_w[s, :, cols], (1, 0)) + bias[:, cols]
            cubic = (GELU_A * GELU_B) * (u * u)
            t = jnp.tanh(u * (GELU_A + cubic))
            half = 0.5 + 0.5 * t
            act = u * half
            act_buf[s, :, cols] = act.astype(bf16)
            slope_buf[s, :, cols] = (
                half + act * ((1.0 - t) * (GELU_A + 3.0 * cubic))
            ).astype(bf16)
        return carry

    lax.fori_loop(0, teams, up_step, 0)
    for s in range(teams):
        leave(act_buf.at[s], (far_out if s % 2 else near_out).at[s // 2])
    for copy in fetched[2]:
        copy.wait()
    upstream_copy.wait()
    for n in range(D // cut):
        cols = slice(n * cut, (n + 1) * cut)
        total = contract(act_buf[0], down_w[0, cols, :], (1, 1))
        for s in range(1, teams):
            total = total + contract(act_buf[s], down_w[s, cols, :], (1, 1))
        wide_buf[:, cols] = total
    start = me * rows
    seq = start // LMAX
    live = length[seq] - (start - seq * LMAX)

    def second_norm(i, at):
        z = (scaled_buf[at, :] * g1[...] + c1[...]) + wide_buf[at, :] + b_down[...]
        scaled, inv_std = row_stats(z)
        x_buf[at, :] = (scaled * g2[...] + c2[...]).astype(bf16)
        row = lax.broadcasted_iota(jnp.int32, (tile, D), 0) + i * tile
        upstream = jnp.where(row < live, g_buf[at, :].astype(f32), 0.0)
        grad = norm_backward(upstream, scaled, inv_std, g2[...]).astype(bf16)
        g_buf[at, :] = grad
        sums[0:8, :] += column_sum(upstream * scaled)
        sums[8:16, :] += column_sum(upstream)
        sums[16:24, :] += column_sum(grad.astype(f32))

    tiles(second_norm)
    leave(x_buf, layer_out)
    leave_turned(1, g_buf, turned_out.at[1])

    def down_back(s, carry):
        for c in range(hidden // cut):
            cols = slice(c * cut, (c + 1) * cut)
            g = contract(g_buf[...], down_w[s, :, cols], (1, 0))
            g = (g * slope_buf[s, :, cols].astype(f32)).astype(bf16)
            slope_buf[s, :, cols] = g
            up_sums[pl.ds(pl.multiple_of(s * 8, 8), 8), cols] = column_sum(g.astype(f32))
        return carry

    lax.fori_loop(0, teams, down_back, 0)
    for s in range(teams):
        leave(slope_buf.at[s], (far_out if s % 2 else near_out).at[2 + s // 2])
    for n in range(D // cut):
        cols = slice(n * cut, (n + 1) * cut)
        total = contract(slope_buf[0], up_w[0, cols, :], (1, 1))
        for s in range(1, teams):
            total = total + contract(slope_buf[s], up_w[s, cols, :], (1, 1))
        wide_buf[:, cols] = total

    def first_back(i, at):
        upstream = g_buf[at, :].astype(f32) + wide_buf[at, :]
        scaled = scaled_buf[at, :]
        grad = norm_backward(upstream, scaled, inv_buf[at, :][:, :1], g1[...]).astype(bf16)
        last_buf[at, :] = grad
        sums[24:32, :] += column_sum(upstream * scaled)
        sums[32:40, :] += column_sum(upstream)
        sums[40:48, :] += column_sum(grad.astype(f32))

    tiles(first_back)
    leave(last_buf, after_out)
    leave_turned(2, last_buf, turned_out.at[2])
    small[...] = jnp.zeros_like(small)
    for k in range(6):
        small[k : k + 1, :] = jnp.sum(sums[8 * k : 8 * k + 8, :], axis=0, keepdims=True)
    for s in range(teams):
        small[pl.ds(6 + (s ^ me), 1), :] = jnp.sum(
            up_sums[8 * s : 8 * s + 8, :], axis=0, keepdims=True
        )
    for s in (2, 3, 1, 0):
        back = contract(last_buf[...], out_w[s], (1, 0))
        half = rows // 2
        send_buf[s, :rows, :] = back[:, :LANES].astype(bf16)
        send_buf[s, rows : rows + half, :] = (
            back[:half, LANES:] + pltpu.roll(back[half:, LANES:], HD, 1)
        ).astype(bf16)
        for k in range(D // LANES):
            at = rows + half + k * SUM_ROWS
            send_buf[s, at : at + SUM_ROWS, :] = small[:, k * LANES : (k + 1) * LANES].astype(bf16)
        leave(send_buf.at[s], back_out[s])
    for copy in leaving:
        copy.wait()


def layer_rows(mixed, hidden_in, grad_out, weights, vectors, lengths):
    teams = len(mixed)
    rows = hidden_in.shape[0]
    rows_of, b_up = vectors
    hidden = b_up.shape[1]
    half = teams // 2
    low = struct((rows, D), bf16)
    pair = struct((2 * half, rows, hidden), bf16)
    ring = len(weights) > 1
    turned = struct((3, 2, 4, D // 8, rows) if ring else (3, 1, 1, D, rows), bf16)
    return pl.pallas_call(
        partial(rows_kernel, [at for _, at in mixed], len(weights)),
        out_shape=[low, pair, pair, turned]
        + [struct((rows + rows // 2 + BELOW, LANES), bf16)] * teams
        + [low, struct((16, D), f32)],
        in_specs=[SMEM_SPEC]
        + [ANY_SPEC] * (teams + 2 + len(weights))
        + [VMEM_SPEC] * 2,
        out_specs=[ANY_SPEC] * (5 + teams) + [VMEM_SPEC],
        scratch_shapes=[
            pltpu.VMEM((teams, rows, PAD), bf16),
            pltpu.VMEM((rows, D), bf16),
            pltpu.VMEM((rows, D), bf16),
            pltpu.VMEM((teams, D, PAD), bf16),
            pltpu.VMEM((teams, D, hidden), bf16),
            pltpu.VMEM((teams, D, hidden), bf16),
            pltpu.VMEM((rows, D), f32),
            pltpu.VMEM((rows, LANES), f32),
            pltpu.VMEM((rows, D), f32),
            pltpu.VMEM((rows, D), bf16),
            pltpu.VMEM((teams, rows, hidden), bf16),
            pltpu.VMEM((teams, rows, hidden), bf16),
            pltpu.VMEM((rows, D), bf16),
            pltpu.VMEM((3, D, rows), bf16),
            pltpu.VMEM((teams, rows + rows // 2 + BELOW, LANES), bf16),
            pltpu.VMEM((48, D), f32),
            pltpu.VMEM((8 * teams, hidden), f32),
            pltpu.SemaphoreType.DMA((teams + 2,)),
            pltpu.SemaphoreType.DMA((3, 32)),
            pltpu.SemaphoreType.DMA((2 + 3 * teams + 24,)),
        ],
        cost_estimate=cost(8 * rows * D * (teams * hidden) + 4 * rows * D * teams * PAD, 24 << 20),
        compiler_params=pltpu.CompilerParams(vmem_limit_bytes=60 << 20),
        name="layer_rows",
    )(
        lengths,
        *[array for array, _ in mixed],
        hidden_in,
        grad_out,
        *weights,
        rows_of,
        b_up,
    )


def row_dot(groups, count, cut_by=None, waited=(), tail=None):
    sets = len(groups[0][0])
    bits, far, part, rows = groups[0][0][0][0].shape[1:]
    cut = 256
    lows = [0]
    for _, rights in groups:
        lows.append(lows[-1] + rights[0][0][0].shape[2] // cut)
    high = bits * far * part
    below = 0 if tail is None else tail.shape[0]
    cuts = {"bits": 2, "quads": 4}.get(cut_by, 1)

    def kernel(*refs):
        refs = list(refs)
        ins = [[refs.pop(0) for _ in range(sets)] for _ in groups]
        others = [[[refs.pop(0) for _ in range(count)] for _ in range(sets)] for _ in groups]
        if below:
            tail_ref = refs.pop(0)
        outs = refs[len(waited) :]
        j = pl.program_id(0)
        for g in range(len(groups)):

            @pl.when((j >= lows[g]) & (j < lows[g + 1]))
            def _(g=g):
                for i in range(count):
                    total = contract(ins[g][0][...].reshape(high, rows), others[g][0][i][...], (1, 0))
                    for k in range(1, sets):
                        total = total + contract(
                            ins[g][k][...].reshape(high, rows), others[g][k][i][...], (1, 0)
                        )
                    total = total.astype(bf16).reshape(bits, far, part, cut)
                    if cut_by == "far":
                        mine = lax.axis_index("dp") // 2
                        for z in range(far):
                            outs[0][z ^ mine, i] = total[:, z]
                        continue
                    for b in range(bits):
                        if cut_by == "bits":
                            to = outs[b].at[i, 0]
                        elif cut_by == "quads":
                            to = outs[2 * b + i].at[0, 0]
                        else:
                            to = outs[0].at[i, b]
                        if below:
                            to[:, :part, :] = total[b]
                            to[:, part:, :] = jnp.broadcast_to(
                                tail_ref[...][None], (far, below, cut)
                            )
                        else:
                            to[...] = total[b]

    def column(g, at):
        return lambda j: (at, 0, jnp.clip(j - lows[g], 0, lows[g + 1] - lows[g] - 1))

    specs, arrays = [], []
    for lefts, _ in groups:
        for array, at in lefts:
            specs.append(
                pl.BlockSpec((None, bits, far, part, rows), lambda j, at=at: (at, 0, 0, 0, 0))
            )
            arrays.append(array)
    for g, (_, rights) in enumerate(groups):
        for pairs in rights:
            for array, at in pairs:
                specs.append(pl.BlockSpec((None, rows, cut), column(g, at)))
                arrays.append(array)
    if below:
        specs.append(pl.BlockSpec((below, cut), lambda j: (0, j)))
        arrays.append(tail)
    width = lows[-1] * cut
    lead = (1 if cut_by == "quads" else count, 1 if cut_by in ("bits", "quads") else bits)
    return pl.pallas_call(
        kernel,
        grid=(lows[-1],),
        out_shape=[
            struct((far, *lead, part, width) if cut_by == "far" else (*lead, far, part + below, width), bf16)
        ]
        * cuts,
        in_specs=specs + [ANY_SPEC] * len(waited),
        out_specs=[
            pl.BlockSpec(
                (far, *lead, part, cut) if cut_by == "far" else (*lead, far, part + below, cut),
                lambda j: (0, 0, 0, 0, j),
            )
        ]
        * cuts,
        cost_estimate=cost(2 * sets * rows * high * count * width, 8 << 20),
        name="row_dot",
    )(*arrays, *waited)


def plus(a, b, waited=(), cuts=1, dtype=bf16):
    lead = a.shape[0] // cuts

    def kernel(a_ref, b_ref, *refs):
        for k in range(cuts):
            span = slice(k * lead, (k + 1) * lead)
            refs[len(waited) + k][...] = (
                a_ref[span].astype(f32) + b_ref[span].astype(f32)
            ).astype(dtype)

    return pl.pallas_call(
        kernel,
        out_shape=[struct((lead, *a.shape[1:]), dtype)] * cuts,
        in_specs=[VMEM_SPEC] * 2 + [ANY_SPEC] * len(waited),
        out_specs=[VMEM_SPEC] * cuts,
        cost_estimate=cost(a.size, 6 * a.size),
        name="plus",
    )(a, b, *waited)


def held(array, waited):
    def kernel(a_ref, *refs):
        refs[-1][...] = a_ref[...]

    return pl.pallas_call(
        kernel,
        out_shape=struct(array.shape, array.dtype),
        in_specs=[VMEM_SPEC] + [ANY_SPEC] * len(waited),
        out_specs=VMEM_SPEC,
        cost_estimate=cost(array.size, 8 * array.size),
        name="held",
    )(array, *waited)


def fold(blocks, waited=()):
    def kernel(ref, *refs):
        for k in range(2):
            total = ref[0, k].astype(f32)
            for z in range(1, 4):
                total = total + ref[z, k].astype(f32)
            refs[len(waited) + k][...] = total.astype(bf16)

    return pl.pallas_call(
        kernel,
        out_shape=[struct(blocks.shape[2:], bf16)] * 2,
        in_specs=[VMEM_SPEC] + [ANY_SPEC] * len(waited),
        out_specs=[VMEM_SPEC] * 2,
        cost_estimate=cost(blocks.size, 3 * blocks.size),
        name="fold",
    )(blocks, *waited)


def joined_sums(lists, waited=(), apart=False):
    rows, width = lists[0].shape[1:]
    count = len(lists)

    def kernel(*refs):
        mine = lax.axis_index("dp") // 2
        for z in range(4):
            total = refs[0][z].astype(f32)
            for k in range(1, count):
                total = total + refs[k][z].astype(f32)
            if apart:
                refs[count + len(waited) + z][...] = total.astype(bf16)
            else:
                refs[-1][z ^ mine] = total.astype(bf16)

    return pl.pallas_call(
        kernel,
        out_shape=[struct((rows, width), bf16)] * 4 if apart else struct((4, rows, width), bf16),
        in_specs=[VMEM_SPEC] * count + [ANY_SPEC] * len(waited),
        out_specs=[VMEM_SPEC] * 4 if apart else VMEM_SPEC,
        cost_estimate=cost(rows * width * 4 * count, rows * width * 8 * count),
        name="joined_sums",
    )(*lists, *waited)


def spread(grads, weight, added=None, after=None, waited=()):
    rows = grads[0].shape[0]

    def kernel(first, second, w, *refs):
        if added is None:
            out = refs[-1]
            out[0] = contract(first[...], w[...], (1, 1)).astype(bf16)
            out[1] = contract(second[...], w[...], (1, 1)).astype(bf16)
            return
        plus_ref, after_ref = refs[:2]
        away, here = refs[-2:]
        away[...] = (contract(first[...], w[...], (1, 1)) + plus_ref[0].astype(f32)).astype(bf16)
        here[...] = contract(second[...], w[...], (1, 1)) + (
            plus_ref[1].astype(f32) + after_ref[...].astype(f32)
        )

    if added is None:
        outs, more = struct((2, rows, D), bf16), []
    else:
        outs, more = [struct((rows, D), bf16), struct((rows, D), f32)], [added, after]
    return pl.pallas_call(
        kernel,
        out_shape=outs,
        in_specs=[VMEM_SPEC] * (3 + len(more)) + [ANY_SPEC] * len(waited),
        out_specs=VMEM_SPEC if added is None else [VMEM_SPEC] * 2,
        cost_estimate=cost(4 * rows * D * weight.shape[1], 5 << 20),
        name="spread",
    )(*grads, weight, *more, *waited)


def pack_queries(w_query, w_key, w_value):
    rows, width = w_query.shape

    def kernel(q, k, v, qkv):
        qkv[...] = jnp.zeros_like(qkv)
        for at, ref in enumerate((q, k, v)):
            qkv[:, at * PAD : at * PAD + width] = ref[...]

    return pl.pallas_call(
        kernel,
        out_shape=struct((rows, 3 * PAD), bf16),
        in_specs=[VMEM_SPEC] * 3,
        out_specs=VMEM_SPEC,
        cost_estimate=cost(rows * PAD, rows * PAD * 8),
        name="pack_queries",
    )(w_query, w_key, w_value)


def pack_weights(w_up, w_out, w_down, waited):
    rows, hidden = w_up.shape
    width = w_out.shape[0]

    def kernel(up, out, down, _, own):
        own[:, :hidden] = up[...]
        own[:, hidden : hidden + PAD] = jnp.zeros((rows, PAD), bf16)
        own[:, hidden : hidden + width] = out[...].T
        own[:, hidden + PAD :] = down[...].T

    return pl.pallas_call(
        kernel,
        out_shape=struct((rows, 2 * hidden + PAD), bf16),
        in_specs=[VMEM_SPEC] * 3 + [ANY_SPEC],
        out_specs=VMEM_SPEC,
        cost_estimate=cost(rows * hidden, 2 << 20),
        name="pack_weights",
    )(w_up, w_out, w_down, waited)


def pair_weights(own, beyond, hidden, waited):
    rows, width = own.shape
    starts = (0, hidden, hidden + PAD, width)

    def kernel(a, b, *refs):
        out = refs[-1]
        for at, end in zip(starts, starts[1:]):
            out[:, 2 * at : at + end] = a[:, at:end]
            out[:, at + end : 2 * end] = b[:, at:end]

    return pl.pallas_call(
        kernel,
        out_shape=struct((rows, 2 * width), bf16),
        in_specs=[VMEM_SPEC] * 2 + [ANY_SPEC] * len(waited),
        out_specs=VMEM_SPEC,
        cost_estimate=cost(rows * width, 4 * rows * width),
        name="pair_weights",
    )(own, beyond, *waited)


def project_in(xs, weights, bias):
    rows = xs[0].shape[0]
    pieces = len(xs)
    sources = len(weights)
    ordered = sources > 1
    bits, far = (2, 4) if ordered else (1, 1)
    part = D // (bits * far)
    wide = weights[0].shape[1]

    def kernel(*refs):
        refs = list(refs)
        ins = [refs.pop(0) for _ in range(pieces)]
        shards = [refs.pop(0) for _ in range(sources)]
        b = refs.pop(0)
        outs = [refs.pop(0) for _ in range(pieces)]
        turned_outs = [refs.pop(0) for _ in range(pieces)]
        whole_out, x_buf, w, out_buf, turned, sems, w_sems, out_sems = refs
        here = lax.axis_index("dp") if ordered else 0
        copies = [
            pltpu.make_async_copy(ins[s], x_buf.at[s], sems.at[s]) for s in range(pieces)
        ]
        fetched = []
        for at in range(sources):
            row = ring_member(RING_STEPS[at]) * part if ordered else 0
            fetched.append(
                pltpu.make_async_copy(
                    shards[at],
                    w.at[pl.ds(pl.multiple_of(row, 16), shards[at].shape[0]), :],
                    w_sems.at[at],
                )
            )
        for copy in fetched + copies:
            copy.start()
        for copy in fetched:
            copy.wait()
        leaving = []

        def leave(ref, to):
            copy = pltpu.make_async_copy(ref, to, out_sems.at[len(leaving)])
            copy.start()
            leaving.append(copy)

        leave(w, whole_out)
        for s in range(pieces):
            copies[s].wait()
            for c in range(0, wide, PAD):
                cols = slice(c, c + PAD)
                out_buf[s, :, cols] = (
                    contract(x_buf[s], w[:, cols], (1, 0)) + b[:, cols]
                ).astype(bf16)
            leave(out_buf.at[s], outs[s])
            for n in range(D // LANES):
                span = slice(n * LANES, (n + 1) * LANES)
                turned[s, span, :] = x_buf[s, :, span].T
            for k in range(bits):
                for z in range(far):
                    row = (here ^ (2 * z + k)) * part if ordered else 0
                    leave(
                        turned.at[s, pl.ds(pl.multiple_of(row, 16), part), :],
                        turned_outs[s].at[k, z],
                    )
        for copy in leaving:
            copy.wait()

    results = pl.pallas_call(
        kernel,
        out_shape=[struct((rows, wide), bf16)] * pieces
        + [struct((bits, far, part, rows), bf16)] * pieces
        + [struct((D, wide), bf16)],
        in_specs=[ANY_SPEC] * (pieces + sources) + [VMEM_SPEC],
        out_specs=[ANY_SPEC] * (2 * pieces + 1),
        scratch_shapes=[
            pltpu.VMEM((pieces, rows, D), bf16),
            pltpu.VMEM((D, wide), bf16),
            pltpu.VMEM((pieces, rows, wide), bf16),
            pltpu.VMEM((pieces, D, rows), bf16),
            pltpu.SemaphoreType.DMA((pieces,)),
            pltpu.SemaphoreType.DMA((sources,)),
            pltpu.SemaphoreType.DMA((1 + pieces * (1 + bits * far),)),
        ],
        cost_estimate=cost(4 * pieces * rows * D * wide, 24 << 20, 0, 1),
        name="project_in",
    )(*xs, *weights, bias)
    return results[:pieces], results[pieces : 2 * pieces], results[2 * pieces]


def padded(array):
    return jnp.pad(array, ((0, 0), (0, PAD - array.shape[1])))


def dot(a, b, dims=(1, 0)):
    return contract(a, b, dims)


def per_device(
    hidden_in,
    grad_out,
    w_query,
    b_query,
    w_key,
    w_value,
    b_value,
    w_out,
    b_out,
    gain_one,
    shift_one,
    w_up,
    b_up,
    w_down,
    b_down,
    gain_two,
    shift_two,
    lengths,
    global_raw,
    random_raw,
):
    own_rows = hidden_in.shape[0]
    me = lax.axis_index("tensor")
    teams = lax.axis_size("tensor")
    members = lax.axis_size("dp")
    width = w_query.shape[1]
    heads = width // HD
    hidden = w_up.shape[1]

    table, bias = block_tables(lengths, global_raw, random_raw, own_rows // BLK, teams)

    qkv_b = jnp.concatenate(
        [jnp.pad(b_query, (0, PAD - width)), jnp.zeros((PAD,), f32), jnp.pad(b_value, (0, PAD - width))]
    )
    halved = members == 8
    if halved:
        queries = pack_queries(w_query, w_key, w_value)
        qkv_pieces = ring_pieces(queries)
        own = pack_weights(w_up, w_out, w_down, qkv_pieces[2])
        beyond_own = swap(own, 2)
        shard = pair_weights(own, beyond_own, hidden, qkv_pieces[GATE:])
    else:
        qkv_shard = jnp.concatenate([padded(w_query), padded(w_key), padded(w_value)], axis=1)
        qkv_pieces = [lax.all_gather(qkv_shard, "dp", axis=0, tiled=True)]
        shard = jnp.concatenate([w_up, padded(w_out.T), w_down.T], axis=1)
        weights = lax.all_gather(shard, ("dp", "tensor"), axis=0, tiled=False)
        weights = jnp.swapaxes(weights.reshape(members, teams, *shard.shape), 0, 1)
        weights = [weights.reshape(teams, D, shard.shape[1])]

    x2 = swap(held(hidden_in, (beyond_own,)) if halved else hidden_in, 2)
    x1 = swap(hidden_in, 1)
    x3 = swap(x2, 1)
    qkv, x_turned, qkv_w = project_in([hidden_in, x1, x2, x3], qkv_pieces, qkv_b[None])
    far_mixed, (t2, t3) = attend_forward(qkv, table, bias, heads, (2, 3))
    far_mixed = swap(far_mixed, 2)
    near_mixed, (t0, t1) = attend_forward(qkv, table, bias, heads, (0, 1))
    r1 = swap(near_mixed[1], 1)
    r3 = swap(far_mixed[1], 1)
    if halved:

        weights = ring_pieces(shard)
        weights = weights + [swap(piece, 1) for piece in weights]

    results = layer_rows(
        [(near_mixed, 0), (r1, None), (far_mixed, 0), (r3, None)],
        hidden_in,
        grad_out,
        weights,
        (
            jnp.stack([b_out, gain_one, shift_one, b_down, gain_two, shift_two]),
            b_up.reshape(teams, hidden),
        ),
        lengths,
    )
    layer_out, near_rows, far_rows, turned = results[:4]
    backs = results[4 : 4 + teams]
    after_low, small = results[4 + teams :]
    ups = [backs[0]] + [swap(backs[s], s) for s in range(1, teams)]
    totals = [t0, t1, t2, t3]
    before = attend_backward(qkv, ups[:1], totals[:1], table, bias, heads, (0,))

    next_rows, next_turned = swap(far_rows, 1), swap(turned, 1)
    down_group = (
        [(turned, 1), (next_turned, 1)],
        [[(near_rows, 0), (near_rows, 1)], [(next_rows, 0), (next_rows, 1)]],
    )
    up_group = (
        [(turned, 0), (next_turned, 0)],
        [[(near_rows, 2), (near_rows, 3)], [(next_rows, 2), (next_rows, 3)]],
    )
    out_group = (
        [(turned, 2), (next_turned, 2)],
        [[(near_mixed, 0), (far_mixed, 0)], [(near_mixed, 1), (far_mixed, 1)]],
    )
    if halved:
        (down_gone,) = row_dot([down_group], 2, "far", (before[0], *ups[1:]))
        down_blocks = far_exchange(down_gone)
        up_quads = row_dot([up_group, out_group], 2, "quads", (down_gone,))
        up_gone = up_quads[3]
        up_away = [swap(up_quads[1], 2), dp_swap(up_quads[2], 1), swap_both(up_gone)]
        waited = (up_gone,)
    else:
        down_sums = row_dot([down_group], 2)[0].reshape(2, D, -1)
        up_sums = row_dot([up_group, out_group], 2)[0].reshape(2, D, -1)
        waited = ()
    results = attend_backward(
        qkv,
        ups[1:],
        totals[1:],
        table,
        bias,
        heads,
        (1, 2, 3),
        small,
        waited,
        (before[1], before[2], before[0]),
    )
    grads, tail = results[:4], results[4]
    qkv_group = ([(x[None], 0) for x in x_turned], [[(g[None], 0)] for g in grads])
    if halved:
        kept, gone = row_dot([qkv_group], 1, "bits", (), tail)
        away = dp_swap(gone, 1)
        parts = spread([grads[3], grads[1]], qkv_w, waited=(gone, *up_away))
        spread_away = swap(parts, 1)
        up_blocks = joined_sums([a[0, 0] for a in (up_quads[0], *up_away)], (parts,), True)
        up_part = up_blocks[0].astype(f32)
        for z in range(1, 4):
            up_part = up_part + dp_swap(up_blocks[z], 2 * z).astype(f32)
        beyond, here = spread([grads[2], grads[0]], qkv_w, spread_away, after_low, (up_blocks[0],))
        beyond_away = swap(beyond, 2)
        down_here, down_next = fold(down_blocks, (beyond,))
        down_away = swap(down_next, 2)
        blocks = joined_sums([kept[0, 0], away[0, 0]], (down_next,))
        arrived = far_exchange(blocks)
        qkv_part = jnp.sum(arrived.astype(f32), axis=0)
        down_here, down_next = plus(down_here, down_away, (blocks,), 2)
        down_away = dp_swap(down_next, 1)
        down_part = down_here[0].astype(f32) + down_away[0].astype(f32)
        qkv_part, small = qkv_part[:-16], qkv_part[-16:]
    else:
        blocks = row_dot([qkv_group], 1)[0].reshape(D, -1)
        qkv_part = dp_scatter_sum(blocks)
        small = lax.psum(tail.astype(f32), "dp")
        spread_away = swap(spread([grads[3], grads[1]], qkv_w), 1)
        beyond, here = spread([grads[2], grads[0]], qkv_w, spread_away, after_low)
        beyond_away = swap(beyond, 2)
        down_part = dp_scatter_sum(down_sums[0] + swap(down_sums[1], 2))
        up_part = dp_scatter_sum(up_sums[0] + swap(up_sums[1], 2))
    grad_in = here + beyond_away.astype(f32)

    bias_row = small[SUM_ROW]
    return (
        layer_out,
        grad_in,
        qkv_part[:, :width],
        bias_row[:width],
        qkv_part[:, PAD : PAD + width],
        qkv_part[:, 2 * PAD : 2 * PAD + width],
        bias_row[2 * PAD : 2 * PAD + width],
        up_part[:, hidden : hidden + width].T,
        small[5],
        small[3],
        small[4],
        up_part[:, :hidden],
        jnp.take(small[6 : 6 + teams], me, axis=0),
        down_part.T,
        small[2],
        small[0],
        small[1],
    )


def solution(mesh):
    in_specs = (
        P(("dp", "tensor"), None),
        P(("dp", "tensor"), None),
        P("dp", "tensor"),
        P("tensor"),
        P("dp", "tensor"),
        P("dp", "tensor"),
        P("tensor"),
        P("tensor", "dp"),
        P(),
        P(),
        P(),
        P("dp", "tensor"),
        P(),
        P("tensor", "dp"),
        P(),
        P(),
        P(),
        P("dp"),
        P("dp", None),
        P("dp", None, None),
    )
    out_specs = (
        P(("dp", "tensor"), None),
        P(("dp", "tensor"), None),
        P("dp", "tensor"),
        P("tensor"),
        P("dp", "tensor"),
        P("dp", "tensor"),
        P("tensor"),
        P("tensor", "dp"),
        P(),
        P(),
        P(),
        P("dp", "tensor"),
        P("tensor"),
        P("tensor", "dp"),
        P(),
        P(),
        P(),
    )
    return jax.shard_map(
        per_device, mesh=mesh, in_specs=in_specs, out_specs=out_specs, check_vma=False
    )
```

```python
from functools import partial

import jax
import jax.numpy as jnp
from jax import lax
from jax.experimental import pallas as pl
from jax.experimental.pallas import tpu as pltpu
from jax.sharding import PartitionSpec as P

D = 768
HD = 64
FF = 3072
BLK = 64
GLOB = 2
RAND = 3
LMAX = 2048
NB = 32
KEYS = (3 + GLOB + RAND) * BLK
PAD = 256
LANES = 128
SUM_ROW = 10
ORDER = (0, 1, 2, 3)
SUM_ROWS = 16
BELOW = SUM_ROWS * (D // LANES)
GATE = 5

masked_score = -1e30
EPSILON = 1e-12
f32 = jnp.float32
bf16 = jnp.bfloat16


def swap(array, bit):
    size = lax.axis_size("tensor")
    return lax.ppermute(array, "tensor", [(t, t ^ bit) for t in range(size)])


def dp_swap(array, bit):
    size = lax.axis_size("dp")
    return lax.ppermute(array, "dp", [(t, t ^ bit) for t in range(size)])


def swap_both(array):
    size = lax.axis_size("dp") * 4
    axes = ("dp", "tensor")
    return lax.ppermute(array, axes, [(t, t ^ 6) for t in range(size)])


def ring_order(size):
    return list(range(0, size, 2)) + list(range(size - 1, 0, -2))


def ring_member(steps):
    size = lax.axis_size("dp")
    me = lax.axis_index("dp")
    place = jnp.where(me % 2 == 0, me // 2, size - 1 - me // 2)
    place = (place + steps + size) % size
    return jnp.where(place < size // 2, 2 * place, 2 * (size - 1 - place) + 1)


def ring_send(array, step):
    size = lax.axis_size("dp")
    order = ring_order(size)
    return lax.ppermute(
        array, "dp", [(order[i], order[(i + step) % size]) for i in range(size)]
    )


RING_STEPS = (0, -1, 1, -2, 2, -3, 3, -4)


def ring_pieces(shard):
    pieces = [shard]
    ahead, behind = shard, shard
    for step in range(1, 5):
        ahead = ring_send(ahead, 1)
        pieces.append(ahead)
        if step < 4:
            behind = ring_send(behind, -1)
            pieces.append(behind)
    return pieces


def far_exchange(blocks):
    groups = [[2 * f + n for f in range(4)] for n in range(2)]
    return lax.all_to_all(blocks, "dp", 0, 0, axis_index_groups=groups, tiled=True)


def dp_scatter_sum(sums):
    size = lax.axis_size("dp")
    if size != 8:
        return lax.psum_scatter(sums, "dp", scatter_dimension=0, tiled=True).astype(f32)
    blocks = lax.all_to_all(sums.reshape(size, -1, sums.shape[1]), "dp", 0, 0, tiled=True)
    return jnp.sum(blocks.astype(f32), axis=0)


def sum_over(vector, dp_only=False):
    if not dp_only:
        bit = 1
        while bit < lax.axis_size("tensor"):
            vector = vector + swap(vector, bit)
            bit *= 2
    bit = 1
    while bit < lax.axis_size("dp"):
        vector = vector + dp_swap(vector, bit)
        bit *= 2
    return vector


def block_tables(lengths, global_raw, random_raw, own_blocks, pieces):
    count = own_blocks * pieces

    def kernel(length_ref, global_ref, random_ref, table, bias):
        me = lax.axis_index("tensor")
        lane = lax.broadcasted_iota(jnp.int32, (1, KEYS), 1)
        slot = lane // BLK
        within = lane % BLK
        wide = lax.broadcasted_iota(jnp.int32, (own_blocks, LANES), 1)
        row = lax.broadcasted_iota(jnp.int32, (own_blocks, 1), 0)
        for s in range(pieces):
            first = (s ^ me) * own_blocks
            seq = first // NB
            start = first - seq * NB
            length = length_ref[seq]
            live = (length + BLK - 1) // BLK
            raw = random_ref[seq, pl.ds(pl.multiple_of(start, 8), own_blocks), :]
            rest = raw - live * jnp.floor(raw.astype(f32) / live.astype(f32)).astype(jnp.int32)
            rest = jnp.where(rest < 0, rest + live, rest)
            rest = jnp.where(rest >= live, rest - live, rest)
            block = row + start
            ids = [jnp.maximum(block - 1, 0), block, jnp.minimum(block + 1, NB - 1)]
            ids += [jnp.full((own_blocks, 1), lax.rem(global_ref[seq, j], live)) for j in range(GLOB)]
            ids += [rest[:, r : r + 1] for r in range(RAND)]
            spread_ids = jnp.zeros((own_blocks, KEYS), jnp.int32)
            packed = jnp.zeros((own_blocks, LANES), jnp.int32)
            for j, own in enumerate(ids):
                spread_ids = jnp.where(slot == j, own, spread_ids)
                there = own + seq * NB
                there = ((there // own_blocks) ^ me) * own_blocks + there % own_blocks
                packed = jnp.where(wide == j, there, packed)
            table[s * own_blocks : (s + 1) * own_blocks, :] = packed
            lost = (spread_ids * BLK + within) >= length
            lost = lost | ((slot == 0) & (block == 0)) | ((slot == 2) & (block == NB - 1))
            bias[s * own_blocks : (s + 1) * own_blocks, :] = jnp.where(lost, masked_score, 0.0).astype(f32)

    smem = pl.BlockSpec(memory_space=pltpu.SMEM)
    vmem = pl.BlockSpec(memory_space=pltpu.VMEM)
    return pl.pallas_call(
        kernel,
        out_shape=[
            jax.ShapeDtypeStruct((count, LANES), jnp.int32),
            jax.ShapeDtypeStruct((count, KEYS), f32),
        ],
        in_specs=[smem, smem, vmem],
        out_specs=[vmem, vmem],
        cost_estimate=cost(count * KEYS * 16, count * KEYS * 4),
        name="block_tables",
    )(lengths, global_raw, random_raw)


def head_masks(heads, scale, dtype):
    lane = lax.broadcasted_iota(jnp.int32, (1, PAD), 1)
    return [
        jnp.where((lane >= h * HD) & (lane < (h + 1) * HD), scale, 0.0).astype(dtype)
        for h in range(heads)
    ]


def stacked_heads(rows, masks):
    return jnp.concatenate([rows * mask for mask in masks], axis=0)


def unstacked_heads(stacked, masks):
    rows = stacked.shape[0] // len(masks)
    total = stacked[:rows] * masks[0]
    for h in range(1, len(masks)):
        total = total + stacked[h * rows : (h + 1) * rows] * masks[h]
    return total


def key_blocks(ref, table, block, column):
    return jnp.concatenate(
        [
            ref[pl.ds(pl.multiple_of(table[block, j] * BLK, BLK), BLK), column : column + PAD]
            for j in range(KEYS // BLK)
        ],
        axis=0,
    )


def contract(a, b, dims):
    return lax.dot_general(a, b, ((dims[:1], dims[1:]), ((), ())), preferred_element_type=f32)


def attend_kernel(heads, chosen, pieces, own_blocks, table, *refs):
    parts = refs[:pieces]
    bias = refs[pieces]
    out = refs[pieces + 1]
    totals = refs[pieces + 2 : pieces + 2 + len(chosen)]
    rows, sems = refs[pieces + 2 + len(chosen) :]
    own_rows = own_blocks * BLK
    copies = [
        pltpu.make_async_copy(
            parts[s], rows.at[pl.ds(s * own_rows, own_rows)], sems.at[s]
        )
        for s in range(pieces)
    ]
    for copy in copies:
        copy.start()
    for copy in copies:
        copy.wait()
    query_masks = head_masks(heads, HD**-0.5, bf16)
    out_masks = head_masks(heads, 1.0, f32)
    lane = lax.broadcasted_iota(jnp.int32, (BLK, LANES), 1)

    side = 2
    count = len(chosen) * side

    def step(step_at, carry):
        blocks, held = [], [{} for _ in range(count)]
        for at in range(count):
            i = step_at * side + at // len(chosen)
            piece = at % len(chosen)
            blocks.append((piece, i, chosen[piece] * own_blocks + i))

        def scored(at):
            block = blocks[at][2]
            here = pl.ds(pl.multiple_of(block * BLK, BLK), BLK)
            queries = stacked_heads(rows[here, 0:PAD], query_masks)
            keys = key_blocks(rows, table, block, PAD)
            held[at]["scores"] = contract(queries, keys, (1, 1))

        def weighed(at):
            has = held[at]
            masked = bias[pl.ds(blocks[at][2], 1), :]
            low, has["total"], has["log_total"] = [], [], []
            for h in range(heads):
                scores = has["scores"][h * BLK : (h + 1) * BLK] + masked
                top = jnp.max(scores, axis=-1, keepdims=True)
                weights = jnp.exp(scores - top)
                total = jnp.sum(weights, axis=-1, keepdims=True)
                low.append(weights.astype(bf16))
                has["total"].append(total)
                has["log_total"].append(top + jnp.log(total))
            has["weights"] = jnp.concatenate(low, axis=0)

        def mixed(at):
            piece, i, block = blocks[at]
            has = held[at]
            values = key_blocks(rows, table, block, 2 * PAD)
            outs = contract(has["weights"], values, (1, 0))
            start = pl.ds(pl.multiple_of(i * BLK, BLK), BLK)
            kept = jnp.zeros((BLK, LANES), f32)
            total = jnp.zeros((BLK, PAD), f32)
            for h in range(heads):
                total = total + outs[h * BLK : (h + 1) * BLK] * (out_masks[h] / has["total"][h])
                kept = jnp.where(lane == h, has["log_total"][h], kept)
            out[piece, start, :] = total.astype(bf16)
            totals[piece][start, :] = kept

        stages = (scored, weighed, mixed)
        for turn in range(count + len(stages) - 1):
            for k in range(len(stages)):
                if 0 <= turn - k < count:
                    stages[k](turn - k)
        return carry

    lax.fori_loop(0, own_blocks // side, step, 0)


def attend_forward(parts, table, bias, heads, chosen):
    own_rows = parts[0].shape[0]
    pieces = len(parts)
    own_blocks = own_rows // BLK
    n = len(chosen)
    vmem = pl.BlockSpec(memory_space=pltpu.VMEM)
    work = n * own_rows * KEYS * heads
    results = pl.pallas_call(
        partial(attend_kernel, heads, chosen, pieces, own_blocks),
        out_shape=[jax.ShapeDtypeStruct((n, own_rows, PAD), bf16)]
        + [jax.ShapeDtypeStruct((own_rows, LANES), f32)] * n,
        in_specs=[pl.BlockSpec(memory_space=pltpu.SMEM)]
        + [pl.BlockSpec(memory_space=pl.ANY)] * pieces
        + [vmem],
        out_specs=[vmem] * (1 + n),
        scratch_shapes=[
            pltpu.VMEM((pieces * own_rows, 3 * PAD), bf16),
            pltpu.SemaphoreType.DMA((pieces,)),
        ],
        cost_estimate=cost(48 * work * HD, 16 << 20, 4 * work, 1),
        name="attend_forward",
    )(table, *parts, bias)
    return results[0], results[1:]


def attend_back_kernel(heads, chosen, pieces, own_blocks, waited, carried, table, *refs):
    refs = list(refs)

    def take(count):
        taken = refs[:count]
        del refs[:count]
        return taken

    parts = take(pieces)
    ups = take(len(chosen))
    totals = take(len(chosen))
    (bias,) = take(1)
    take(waited)
    if carried:
        key_before, value_before = take(2)
        query_before = take(pieces - len(chosen))
        (small_ref,) = take(1)
        outs = take(pieces)
        (tail,) = take(1)
        key_sum, value_sum, key_kept, value_kept, row_sums = take(5)
    else:
        outs = take(len(chosen))
        key_sum, value_sum = take(2)
    rows, up_rows, up_packed, sems = refs
    own_rows = own_blocks * BLK
    copies = [
        pltpu.make_async_copy(parts[s], rows.at[pl.ds(s * own_rows, own_rows)], sems.at[s])
        for s in range(pieces)
    ] + [
        pltpu.make_async_copy(ups[at], up_packed.at[at], sems.at[pieces + at])
        for at in range(len(chosen))
    ]
    late = []
    if carried:
        late = [
            pltpu.make_async_copy(key_before, key_kept, sems.at[pieces + len(chosen)]),
            pltpu.make_async_copy(value_before, value_kept, sems.at[pieces + len(chosen) + 1]),
        ]
    for copy in copies + late:
        copy.start()
    key_sum[...] = jnp.zeros_like(key_sum)
    value_sum[...] = jnp.zeros_like(value_sum)
    for copy in copies:
        copy.wait()
    query_masks = head_masks(heads, HD**-0.5, bf16)
    up_masks = head_masks(heads, 1.0, bf16)
    out_masks = head_masks(heads, HD**-0.5, f32)
    half = own_rows // 2
    for at in range(len(chosen)):
        up_rows[at, :, :LANES] = up_packed[at, :own_rows, :]
        last = up_packed[at, own_rows : own_rows + half, :]
        up_rows[at, :half, LANES:] = last
        up_rows[at, half:, LANES:] = pltpu.roll(last.astype(f32), HD, 1).astype(bf16)

    side = 2 if len(chosen) == 1 else 1

    count = len(chosen) * side

    def step(step_at, carry):
        blocks, held = [], [{} for _ in range(count)]
        for at in range(count):
            i = step_at * side + at // len(chosen)
            piece = at % len(chosen)
            blocks.append((piece, i, chosen[piece] * own_blocks + i))

        def scored(at):
            piece, i, block = blocks[at]
            start = pl.multiple_of(i * BLK, BLK)
            here = pl.ds(pl.multiple_of(block * BLK, BLK), BLK)
            has = held[at]
            has["queries"] = stacked_heads(rows[here, 0:PAD], query_masks)
            has["upstream"] = stacked_heads(up_rows[piece, pl.ds(start, BLK), :], up_masks)
            has["keys"] = key_blocks(rows, table, block, PAD)
            values = key_blocks(rows, table, block, 2 * PAD)
            has["scores"] = contract(has["queries"], has["keys"], (1, 1))
            has["grad_weights"] = contract(has["upstream"], values, (1, 1))

        def weighed(at):
            piece, i, block = blocks[at]
            has = held[at]
            kept = totals[piece][pl.ds(pl.multiple_of(i * BLK, BLK), BLK), :]
            masked = bias[pl.ds(block, 1), :]
            low, grad = [], []
            for h in range(heads):
                span = slice(h * BLK, (h + 1) * BLK)
                weights = jnp.exp(has["scores"][span] + (masked - kept[:, h : h + 1]))
                grad_weights = has["grad_weights"][span]
                inner = jnp.sum(weights * grad_weights, axis=-1, keepdims=True)
                low.append(weights.astype(bf16))
                grad.append((weights * (grad_weights - inner)).astype(bf16))
            has["weights"] = jnp.concatenate(low, axis=0)
            has["grad_scores"] = jnp.concatenate(grad, axis=0)

        def spread_back(at):
            piece, i, block = blocks[at]
            has = held[at]
            to = outs[chosen[piece]] if carried else outs[piece]
            grad_query = contract(has["grad_scores"], has["keys"], (1, 0))
            to[pl.ds(pl.multiple_of(i * BLK, BLK), BLK), 0:PAD] = unstacked_heads(
                grad_query, out_masks
            ).astype(bf16)
            has["key_part"] = contract(has["grad_scores"], has["queries"], (0, 0))
            has["value_part"] = contract(has["weights"], has["upstream"], (0, 0))

        def summed(at):
            block, has = blocks[at][2], held[at]
            for j in range(KEYS // BLK):
                there = pl.ds(pl.multiple_of(table[block, j] * BLK, BLK), BLK)
                key_sum[there, :] += has["key_part"][j * BLK : (j + 1) * BLK]
                value_sum[there, :] += has["value_part"][j * BLK : (j + 1) * BLK]

        stages = (scored, weighed, spread_back, summed)
        for turn in range(count + len(stages) - 1):
            for k in ORDER:
                at = turn - k
                if 0 <= at < count:
                    stages[k](at)
        return carry

    lax.fori_loop(0, own_blocks // side, step, 0)
    if not carried:
        return
    for copy in late:
        copy.wait()
    before = [s for s in range(pieces) if s not in chosen]
    for at, s in enumerate(before):
        outs[s][:, 0:PAD] = query_before[at][...]
    row_sums[...] = jnp.zeros_like(row_sums)
    for s in range(pieces):

        def finish(i, carry, s=s):
            at = pl.ds(pl.multiple_of(i * BLK, BLK), BLK)
            span = pl.ds(pl.multiple_of(s * own_rows + i * BLK, BLK), BLK)
            outs[s][at, PAD : 2 * PAD] = (key_sum[span, :] + key_kept[span, :]).astype(bf16)
            outs[s][at, 2 * PAD : 3 * PAD] = (value_sum[span, :] + value_kept[span, :]).astype(bf16)
            whole = outs[s][at, :].astype(f32)
            row_sums[...] += jnp.sum(whole.reshape(BLK // 8, 8, 3 * PAD), axis=0)
            return carry

        lax.fori_loop(0, own_blocks, finish, 0)
    slot = lax.broadcasted_iota(jnp.int32, tail.shape, 0)
    whole = jnp.sum(row_sums[...], axis=0, keepdims=True)
    small = small_ref[...]
    for at in range(len(chosen)):
        parts = [
            up_packed[at, own_rows + half + k * SUM_ROWS : own_rows + half + (k + 1) * SUM_ROWS, :]
            for k in range(BELOW // SUM_ROWS)
        ]
        small = small + jnp.concatenate(parts, axis=1).astype(f32)
    tail[...] = jnp.where(slot == SUM_ROW, whole, small).astype(bf16)


def attend_backward(parts, ups, totals, table, bias, heads, chosen, small=None, waited=(), before=None):
    own_rows = parts[0].shape[0]
    pieces = len(parts)
    n = len(chosen)
    own_blocks = own_rows // BLK
    vmem = pl.BlockSpec(memory_space=pltpu.VMEM)
    anyspace = pl.BlockSpec(memory_space=pl.ANY)
    work = n * own_rows * KEYS * heads
    sum_shape = (pieces * own_rows, PAD)
    if before is None:
        outs = [((own_rows, PAD), bf16)] * n + [(sum_shape, f32)] * 2
        extra, extra_specs, scratch = [], [], []
    else:
        outs = [((own_rows, 3 * PAD), bf16)] * pieces + [((16, 3 * PAD), bf16)]
        extra = [*before, small]
        extra_specs = [anyspace] * 2 + [vmem] * (len(before) - 1)
        scratch = [pltpu.VMEM(sum_shape, f32)] * 4 + [pltpu.VMEM((8, 3 * PAD), f32)]
    return pl.pallas_call(
        partial(
            attend_back_kernel, heads, chosen, pieces, own_blocks, len(waited), before is not None
        ),
        out_shape=[jax.ShapeDtypeStruct(*out) for out in outs],
        in_specs=[pl.BlockSpec(memory_space=pltpu.SMEM)]
        + [anyspace] * (pieces + n)
        + [vmem] * (n + 1)
        + [anyspace] * len(waited)
        + extra_specs,
        out_specs=[vmem] * len(outs),
        scratch_shapes=scratch
        + [
            pltpu.VMEM((pieces * own_rows, 3 * PAD), bf16),
            pltpu.VMEM((n, own_rows, PAD), bf16),
            pltpu.VMEM((n, own_rows + own_rows // 2 + BELOW, LANES), bf16),
            pltpu.SemaphoreType.DMA((pieces + n + 2,)),
        ],
        cost_estimate=cost(30 * work * HD, 12 << 20, work),
        name="attend_backward",
    )(table, *parts, *ups, *totals, bias, *waited, *extra)


VMEM_SPEC = pl.BlockSpec(memory_space=pltpu.VMEM)
ANY_SPEC = pl.BlockSpec(memory_space=pl.ANY)
SMEM_SPEC = pl.BlockSpec(memory_space=pltpu.SMEM)
COST_CUT = 64
GELU_A = 0.7978845608028654
GELU_B = 0.044715


def cost(flops, size, transcendentals=0, cut=None):
    cut = cut or COST_CUT
    return pl.CostEstimate(
        flops=flops // cut, bytes_accessed=size // cut, transcendentals=transcendentals // cut
    )


def struct(shape, dtype):
    return jax.ShapeDtypeStruct(shape, dtype)


def row_stats(values):
    centred = values - jnp.mean(values, axis=-1, keepdims=True)
    inv_std = lax.rsqrt(jnp.mean(centred * centred, axis=-1, keepdims=True) + EPSILON)
    return centred * inv_std, inv_std


def norm_backward(upstream, scaled, inv_std, gain):
    weighted = upstream * gain
    inner = jnp.mean(weighted * scaled, axis=-1, keepdims=True)
    return inv_std * (weighted - jnp.mean(weighted, axis=-1, keepdims=True) - scaled * inner)


def column_sum(array):
    return jnp.sum(array.reshape(array.shape[0] // 8, 8, array.shape[1]), axis=0)


def rows_kernel(places, sources, length, *refs):
    teams = len(places)
    refs = list(refs)

    def take(count):
        taken = refs[:count]
        del refs[:count]
        return taken

    mixed = take(teams)
    x_in, g_in = take(2)
    weights = take(sources)
    vectors, b_up = take(2)
    b_out, g1, c1, b_down, g2, c2 = [vectors.at[k : k + 1, :] for k in range(6)]
    layer_out, near_out, far_out, turned_out = take(4)
    back_out = take(teams)
    after_out, small = take(2)
    (
        o_buf,
        x_buf,
        g_buf,
        out_w,
        up_w,
        down_w,
        scaled_buf,
        inv_buf,
        wide_buf,
        low_buf,
        act_buf,
        slope_buf,
        last_buf,
        turned_buf,
        send_buf,
        sums,
        up_sums,
        in_sems,
        w_sems,
        out_sems,
    ) = refs
    rows = x_in.shape[0]
    hidden = up_w.shape[2]
    tile, cut = 64, 256
    me = lax.axis_index("tensor")
    ring = sources > 1

    first = []
    for s in range(teams):
        source = mixed[s] if places[s] is None else mixed[s].at[places[s]]
        first.append(
            pltpu.make_async_copy(source, o_buf.at[s], in_sems.at[s])
        )
    first.append(pltpu.make_async_copy(x_in, x_buf, in_sems.at[teams]))
    upstream_copy = pltpu.make_async_copy(g_in, g_buf, in_sems.at[teams + 1])
    fetched = ([], [], [])

    def fetch(kind, source, to):
        sem = w_sems.at[kind, len(fetched[kind])]
        fetched[kind].append(pltpu.make_async_copy(source, to, sem))

    wholes = (out_w, up_w, down_w)
    if ring:
        part = weights[0].shape[0]
        spans = ((2 * hidden, PAD), (0, hidden), (2 * hidden + 2 * PAD, hidden))
        for at, piece in enumerate(weights):
            row = pl.multiple_of(ring_member(RING_STEPS[at % 8]) * part, 16)
            for kind, (start, size) in enumerate(spans):
                for pair in range(2):
                    fetch(
                        kind,
                        piece.at[:, pl.ds(start + pair * size, size)],
                        wholes[kind].at[2 * pair + at // 8, pl.ds(row, part), :],
                    )
    else:
        spans = ((hidden, PAD), (0, hidden), (hidden + PAD, hidden))
        for kind, (start, size) in enumerate(spans):
            for s in range(teams):
                fetch(kind, weights[0].at[me ^ s, :, pl.ds(start, size)], wholes[kind].at[s])
    for copy in first + fetched[0] + fetched[1] + fetched[2] + [upstream_copy]:
        copy.start()
    sums[...] = jnp.zeros_like(sums)
    up_sums[...] = jnp.zeros_like(up_sums)
    leaving = []

    def leave(ref, to):
        copy = pltpu.make_async_copy(ref, to, out_sems.at[len(leaving)])
        copy.start()
        leaving.append(copy)

    def leave_turned(k, source, to):
        for n in range(D // LANES):
            span = slice(n * LANES, (n + 1) * LANES)
            turned_buf[k, span, :] = source[:, span].T
        bits, far, part, _ = to.shape
        here = lax.axis_index("dp")
        for b in range(bits):
            for z in range(far):
                row = (here ^ (2 * z + b)) * part if ring else 0
                leave(turned_buf.at[k, pl.ds(pl.multiple_of(row, 16), part), :], to.at[b, z])

    def tiles(body):
        def step(i, carry):
            body(i, pl.ds(pl.multiple_of(i * tile, tile), tile))
            return carry

        lax.fori_loop(0, rows // tile, step, 0)

    for copy in first + fetched[0]:
        copy.wait()
    for n in range(D // cut):
        cols = slice(n * cut, (n + 1) * cut)
        total = contract(o_buf[0, :rows, :], out_w[0, cols, :], (1, 1))
        for s in range(1, teams):
            total = total + contract(o_buf[s, :rows, :], out_w[s, cols, :], (1, 1))
        wide_buf[:, cols] = total

    def first_norm(i, at):
        after = x_buf[at, :].astype(f32) + wide_buf[at, :] + b_out[...]
        scaled, inv_std = row_stats(after)
        scaled_buf[at, :] = scaled
        inv_buf[at, :] = jnp.broadcast_to(inv_std, (tile, LANES))
        low_buf[at, :] = (scaled * g1[...] + c1[...]).astype(bf16)

    tiles(first_norm)
    leave_turned(0, low_buf, turned_out.at[0])
    for copy in fetched[1]:
        copy.wait()

    def up_step(s, carry):
        bias = b_up[pl.ds(s ^ me, 1), :]
        for c in range(hidden // cut):
            cols = slice(c * cut, (c + 1) * cut)
            u = contract(low_buf[...], up_w[s, :, cols], (1, 0)) + bias[:, cols]
            cubic = (GELU_A * GELU_B) * (u * u)
            t = jnp.tanh(u * (GELU_A + cubic))
            half = 0.5 + 0.5 * t
            act = u * half
            act_buf[s, :, cols] = act.astype(bf16)
            slope_buf[s, :, cols] = (
                half + act * ((1.0 - t) * (GELU_A + 3.0 * cubic))
            ).astype(bf16)
        return carry

    lax.fori_loop(0, teams, up_step, 0)
    for s in range(teams):
        leave(act_buf.at[s], (far_out if s % 2 else near_out).at[s // 2])
    for copy in fetched[2]:
        copy.wait()
    upstream_copy.wait()
    for n in range(D // cut):
        cols = slice(n * cut, (n + 1) * cut)
        total = contract(act_buf[0], down_w[0, cols, :], (1, 1))
        for s in range(1, teams):
            total = total + contract(act_buf[s], down_w[s, cols, :], (1, 1))
        wide_buf[:, cols] = total
    start = me * rows
    seq = start // LMAX
    live = length[seq] - (start - seq * LMAX)

    def second_norm(i, at):
        z = (scaled_buf[at, :] * g1[...] + c1[...]) + wide_buf[at, :] + b_down[...]
        scaled, inv_std = row_stats(z)
        x_buf[at, :] = (scaled * g2[...] + c2[...]).astype(bf16)
        row = lax.broadcasted_iota(jnp.int32, (tile, 1), 0) + i * tile
        upstream = jnp.where(row < live, g_buf[at, :].astype(f32), 0.0)
        grad = norm_backward(upstream, scaled, inv_std, g2[...]).astype(bf16)
        g_buf[at, :] = grad
        sums[0:8, :] += column_sum(upstream * scaled)
        sums[8:16, :] += column_sum(upstream)
        sums[16:24, :] += column_sum(grad.astype(f32))

    tiles(second_norm)
    leave(x_buf, layer_out)
    leave_turned(1, g_buf, turned_out.at[1])

    def down_back(s, carry):
        for c in range(hidden // cut):
            cols = slice(c * cut, (c + 1) * cut)
            g = contract(g_buf[...], down_w[s, :, cols], (1, 0))
            g = (g * slope_buf[s, :, cols].astype(f32)).astype(bf16)
            slope_buf[s, :, cols] = g
            up_sums[pl.ds(pl.multiple_of(s * 8, 8), 8), cols] = column_sum(g.astype(f32))
        return carry

    lax.fori_loop(0, teams, down_back, 0)
    for s in range(teams):
        leave(slope_buf.at[s], (far_out if s % 2 else near_out).at[2 + s // 2])
    for n in range(D // cut):
        cols = slice(n * cut, (n + 1) * cut)
        total = contract(slope_buf[0], up_w[0, cols, :], (1, 1))
        for s in range(1, teams):
            total = total + contract(slope_buf[s], up_w[s, cols, :], (1, 1))
        wide_buf[:, cols] = total

    def first_back(i, at):
        upstream = g_buf[at, :].astype(f32) + wide_buf[at, :]
        scaled = scaled_buf[at, :]
        grad = norm_backward(upstream, scaled, inv_buf[at, :][:, :1], g1[...]).astype(bf16)
        last_buf[at, :] = grad
        sums[24:32, :] += column_sum(upstream * scaled)
        sums[32:40, :] += column_sum(upstream)
        sums[40:48, :] += column_sum(grad.astype(f32))

    tiles(first_back)
    leave(last_buf, after_out)
    leave_turned(2, last_buf, turned_out.at[2])
    small[...] = jnp.zeros_like(small)
    for k in range(6):
        small[k : k + 1, :] = jnp.sum(sums[8 * k : 8 * k + 8, :], axis=0, keepdims=True)
    for s in range(teams):
        small[pl.ds(6 + (s ^ me), 1), :] = jnp.sum(
            up_sums[8 * s : 8 * s + 8, :], axis=0, keepdims=True
        )
    for s in (2, 3, 1, 0):
        back = contract(last_buf[...], out_w[s], (1, 0))
        half = rows // 2
        send_buf[s, :rows, :] = back[:, :LANES].astype(bf16)
        send_buf[s, rows : rows + half, :] = (
            back[:half, LANES:] + pltpu.roll(back[half:, LANES:], HD, 1)
        ).astype(bf16)
        for k in range(D // LANES):
            at = rows + half + k * SUM_ROWS
            send_buf[s, at : at + SUM_ROWS, :] = small[:, k * LANES : (k + 1) * LANES].astype(bf16)
        leave(send_buf.at[s], back_out[s])
    for copy in leaving:
        copy.wait()


def layer_rows(mixed, hidden_in, grad_out, weights, vectors, lengths):
    teams = len(mixed)
    rows = hidden_in.shape[0]
    rows_of, b_up = vectors
    hidden = b_up.shape[1]
    half = teams // 2
    low = struct((rows, D), bf16)
    pair = struct((2 * half, rows, hidden), bf16)
    ring = len(weights) > 1
    turned = struct((3, 2, 4, D // 8, rows) if ring else (3, 1, 1, D, rows), bf16)
    return pl.pallas_call(
        partial(rows_kernel, [at for _, at in mixed], len(weights)),
        out_shape=[low, pair, pair, turned]
        + [struct((rows + rows // 2 + BELOW, LANES), bf16)] * teams
        + [low, struct((16, D), f32)],
        in_specs=[SMEM_SPEC]
        + [ANY_SPEC] * (teams + 2 + len(weights))
        + [VMEM_SPEC] * 2,
        out_specs=[ANY_SPEC] * (5 + teams) + [VMEM_SPEC],
        scratch_shapes=[
            pltpu.VMEM((teams, rows, PAD), bf16),
            pltpu.VMEM((rows, D), bf16),
            pltpu.VMEM((rows, D), bf16),
            pltpu.VMEM((teams, D, PAD), bf16),
            pltpu.VMEM((teams, D, hidden), bf16),
            pltpu.VMEM((teams, D, hidden), bf16),
            pltpu.VMEM((rows, D), f32),
            pltpu.VMEM((rows, LANES), f32),
            pltpu.VMEM((rows, D), f32),
            pltpu.VMEM((rows, D), bf16),
            pltpu.VMEM((teams, rows, hidden), bf16),
            pltpu.VMEM((teams, rows, hidden), bf16),
            pltpu.VMEM((rows, D), bf16),
            pltpu.VMEM((3, D, rows), bf16),
            pltpu.VMEM((teams, rows + rows // 2 + BELOW, LANES), bf16),
            pltpu.VMEM((48, D), f32),
            pltpu.VMEM((8 * teams, hidden), f32),
            pltpu.SemaphoreType.DMA((teams + 2,)),
            pltpu.SemaphoreType.DMA((3, 32)),
            pltpu.SemaphoreType.DMA((2 + 3 * teams + 24,)),
        ],
        cost_estimate=cost(8 * rows * D * (teams * hidden) + 4 * rows * D * teams * PAD, 24 << 20),
        compiler_params=pltpu.CompilerParams(vmem_limit_bytes=60 << 20),
        name="layer_rows",
    )(
        lengths,
        *[array for array, _ in mixed],
        hidden_in,
        grad_out,
        *weights,
        rows_of,
        b_up,
    )


def row_dot(groups, count, cut_by=None, waited=(), tail=None):
    sets = len(groups[0][0])
    bits, far, part, rows = groups[0][0][0][0].shape[1:]
    cut = 256
    lows = [0]
    for _, rights in groups:
        lows.append(lows[-1] + rights[0][0][0].shape[2] // cut)
    high = bits * far * part
    below = 0 if tail is None else tail.shape[0]
    cuts = {"bits": 2, "quads": 4}.get(cut_by, 1)

    def kernel(*refs):
        refs = list(refs)
        ins = [[refs.pop(0) for _ in range(sets)] for _ in groups]
        others = [[[refs.pop(0) for _ in range(count)] for _ in range(sets)] for _ in groups]
        if below:
            tail_ref = refs.pop(0)
        outs = refs[len(waited) :]
        j = pl.program_id(0)
        for g in range(len(groups)):

            @pl.when((j >= lows[g]) & (j < lows[g + 1]))
            def _(g=g):
                for i in range(count):
                    total = contract(ins[g][0][...].reshape(high, rows), others[g][0][i][...], (1, 0))
                    for k in range(1, sets):
                        total = total + contract(
                            ins[g][k][...].reshape(high, rows), others[g][k][i][...], (1, 0)
                        )
                    total = total.astype(bf16).reshape(bits, far, part, cut)
                    if cut_by == "far":
                        mine = lax.axis_index("dp") // 2
                        for z in range(far):
                            outs[0][z ^ mine, i] = total[:, z]
                        continue
                    for b in range(bits):
                        if cut_by == "bits":
                            to = outs[b].at[i, 0]
                        elif cut_by == "quads":
                            to = outs[2 * b + i].at[0, 0]
                        else:
                            to = outs[0].at[i, b]
                        if below:
                            to[:, :part, :] = total[b]
                            to[:, part:, :] = jnp.broadcast_to(
                                tail_ref[...][None], (far, below, cut)
                            )
                        else:
                            to[...] = total[b]

    def column(g, at):
        return lambda j: (at, 0, jnp.clip(j - lows[g], 0, lows[g + 1] - lows[g] - 1))

    specs, arrays = [], []
    for lefts, _ in groups:
        for array, at in lefts:
            specs.append(
                pl.BlockSpec((None, bits, far, part, rows), lambda j, at=at: (at, 0, 0, 0, 0))
            )
            arrays.append(array)
    for g, (_, rights) in enumerate(groups):
        for pairs in rights:
            for array, at in pairs:
                specs.append(pl.BlockSpec((None, rows, cut), column(g, at)))
                arrays.append(array)
    if below:
        specs.append(pl.BlockSpec((below, cut), lambda j: (0, j)))
        arrays.append(tail)
    width = lows[-1] * cut
    lead = (1 if cut_by == "quads" else count, 1 if cut_by in ("bits", "quads") else bits)
    return pl.pallas_call(
        kernel,
        grid=(lows[-1],),
        out_shape=[
            struct((far, *lead, part, width) if cut_by == "far" else (*lead, far, part + below, width), bf16)
        ]
        * cuts,
        in_specs=specs + [ANY_SPEC] * len(waited),
        out_specs=[
            pl.BlockSpec(
                (far, *lead, part, cut) if cut_by == "far" else (*lead, far, part + below, cut),
                lambda j: (0, 0, 0, 0, j),
            )
        ]
        * cuts,
        cost_estimate=cost(2 * sets * rows * high * count * width, 8 << 20),
        name="row_dot",
    )(*arrays, *waited)


def plus(a, b, waited=(), cuts=1, dtype=bf16):
    lead = a.shape[0] // cuts

    def kernel(a_ref, b_ref, *refs):
        for k in range(cuts):
            span = slice(k * lead, (k + 1) * lead)
            refs[len(waited) + k][...] = (
                a_ref[span].astype(f32) + b_ref[span].astype(f32)
            ).astype(dtype)

    return pl.pallas_call(
        kernel,
        out_shape=[struct((lead, *a.shape[1:]), dtype)] * cuts,
        in_specs=[VMEM_SPEC] * 2 + [ANY_SPEC] * len(waited),
        out_specs=[VMEM_SPEC] * cuts,
        cost_estimate=cost(a.size, 6 * a.size),
        name="plus",
    )(a, b, *waited)


def held(array, waited):
    def kernel(a_ref, *refs):
        refs[-1][...] = a_ref[...]

    return pl.pallas_call(
        kernel,
        out_shape=struct(array.shape, array.dtype),
        in_specs=[VMEM_SPEC] + [ANY_SPEC] * len(waited),
        out_specs=VMEM_SPEC,
        cost_estimate=cost(array.size, 8 * array.size),
        name="held",
    )(array, *waited)


def fold(blocks, waited=()):
    def kernel(ref, *refs):
        for k in range(2):
            total = ref[0, k].astype(f32)
            for z in range(1, 4):
                total = total + ref[z, k].astype(f32)
            refs[len(waited) + k][...] = total.astype(bf16)

    return pl.pallas_call(
        kernel,
        out_shape=[struct(blocks.shape[2:], bf16)] * 2,
        in_specs=[VMEM_SPEC] + [ANY_SPEC] * len(waited),
        out_specs=[VMEM_SPEC] * 2,
        cost_estimate=cost(blocks.size, 3 * blocks.size),
        name="fold",
    )(blocks, *waited)


def joined_sums(lists, waited=(), apart=False):
    rows, width = lists[0].shape[1:]
    count = len(lists)

    def kernel(*refs):
        mine = lax.axis_index("dp") // 2
        for z in range(4):
            total = refs[0][z].astype(f32)
            for k in range(1, count):
                total = total + refs[k][z].astype(f32)
            if apart:
                refs[count + len(waited) + z][...] = total.astype(bf16)
            else:
                refs[-1][z ^ mine] = total.astype(bf16)

    return pl.pallas_call(
        kernel,
        out_shape=[struct((rows, width), bf16)] * 4 if apart else struct((4, rows, width), bf16),
        in_specs=[VMEM_SPEC] * count + [ANY_SPEC] * len(waited),
        out_specs=[VMEM_SPEC] * 4 if apart else VMEM_SPEC,
        cost_estimate=cost(rows * width * 4 * count, rows * width * 8 * count),
        name="joined_sums",
    )(*lists, *waited)


def spread(grads, weight, added=None, after=None, waited=()):
    rows = grads[0].shape[0]

    def kernel(first, second, w, *refs):
        if added is None:
            out = refs[-1]
            out[0] = contract(first[...], w[...], (1, 1)).astype(bf16)
            out[1] = contract(second[...], w[...], (1, 1)).astype(bf16)
            return
        plus_ref, after_ref = refs[:2]
        away, here = refs[-2:]
        away[...] = (contract(first[...], w[...], (1, 1)) + plus_ref[0].astype(f32)).astype(bf16)
        here[...] = contract(second[...], w[...], (1, 1)) + (
            plus_ref[1].astype(f32) + after_ref[...].astype(f32)
        )

    if added is None:
        outs, more = struct((2, rows, D), bf16), []
    else:
        outs, more = [struct((rows, D), bf16), struct((rows, D), f32)], [added, after]
    return pl.pallas_call(
        kernel,
        out_shape=outs,
        in_specs=[VMEM_SPEC] * (3 + len(more)) + [ANY_SPEC] * len(waited),
        out_specs=VMEM_SPEC if added is None else [VMEM_SPEC] * 2,
        cost_estimate=cost(4 * rows * D * weight.shape[1], 5 << 20),
        name="spread",
    )(*grads, weight, *more, *waited)


def pack_queries(w_query, w_key, w_value):
    rows, width = w_query.shape

    def kernel(q, k, v, qkv):
        qkv[...] = jnp.zeros_like(qkv)
        for at, ref in enumerate((q, k, v)):
            qkv[:, at * PAD : at * PAD + width] = ref[...]

    return pl.pallas_call(
        kernel,
        out_shape=struct((rows, 3 * PAD), bf16),
        in_specs=[VMEM_SPEC] * 3,
        out_specs=VMEM_SPEC,
        cost_estimate=cost(rows * PAD, rows * PAD * 8),
        name="pack_queries",
    )(w_query, w_key, w_value)


def pack_weights(w_up, w_out, w_down, waited):
    rows, hidden = w_up.shape
    width = w_out.shape[0]

    def kernel(up, out, down, _, own):
        own[:, :hidden] = up[...]
        own[:, hidden : hidden + PAD] = jnp.zeros((rows, PAD), bf16)
        own[:, hidden : hidden + width] = out[...].T
        own[:, hidden + PAD :] = down[...].T

    return pl.pallas_call(
        kernel,
        out_shape=struct((rows, 2 * hidden + PAD), bf16),
        in_specs=[VMEM_SPEC] * 3 + [ANY_SPEC],
        out_specs=VMEM_SPEC,
        cost_estimate=cost(rows * hidden, 2 << 20),
        name="pack_weights",
    )(w_up, w_out, w_down, waited)


def pair_weights(own, beyond, hidden, waited):
    rows, width = own.shape
    starts = (0, hidden, hidden + PAD, width)

    def kernel(a, b, *refs):
        out = refs[-1]
        for at, end in zip(starts, starts[1:]):
            out[:, 2 * at : at + end] = a[:, at:end]
            out[:, at + end : 2 * end] = b[:, at:end]

    return pl.pallas_call(
        kernel,
        out_shape=struct((rows, 2 * width), bf16),
        in_specs=[VMEM_SPEC] * 2 + [ANY_SPEC] * len(waited),
        out_specs=VMEM_SPEC,
        cost_estimate=cost(rows * width, 4 * rows * width),
        name="pair_weights",
    )(own, beyond, *waited)


def project_in(xs, weights, bias):
    rows = xs[0].shape[0]
    pieces = len(xs)
    sources = len(weights)
    ordered = sources > 1
    bits, far = (2, 4) if ordered else (1, 1)
    part = D // (bits * far)
    wide = weights[0].shape[1]

    def kernel(*refs):
        refs = list(refs)
        ins = [refs.pop(0) for _ in range(pieces)]
        shards = [refs.pop(0) for _ in range(sources)]
        b = refs.pop(0)
        outs = [refs.pop(0) for _ in range(pieces)]
        turned_outs = [refs.pop(0) for _ in range(pieces)]
        whole_out, x_buf, w, out_buf, turned, sems, w_sems, out_sems = refs
        here = lax.axis_index("dp") if ordered else 0
        copies = [
            pltpu.make_async_copy(ins[s], x_buf.at[s], sems.at[s]) for s in range(pieces)
        ]
        fetched = []
        for at in range(sources):
            row = ring_member(RING_STEPS[at]) * part if ordered else 0
            fetched.append(
                pltpu.make_async_copy(
                    shards[at],
                    w.at[pl.ds(pl.multiple_of(row, 16), shards[at].shape[0]), :],
                    w_sems.at[at],
                )
            )
        for copy in fetched + copies:
            copy.start()
        for copy in fetched:
            copy.wait()
        leaving = []

        def leave(ref, to):
            copy = pltpu.make_async_copy(ref, to, out_sems.at[len(leaving)])
            copy.start()
            leaving.append(copy)

        leave(w, whole_out)
        for s in range(pieces):
            copies[s].wait()
            for c in range(0, wide, PAD):
                cols = slice(c, c + PAD)
                out_buf[s, :, cols] = (
                    contract(x_buf[s], w[:, cols], (1, 0)) + b[:, cols]
                ).astype(bf16)
            leave(out_buf.at[s], outs[s])
            for n in range(D // LANES):
                span = slice(n * LANES, (n + 1) * LANES)
                turned[s, span, :] = x_buf[s, :, span].T
            for k in range(bits):
                for z in range(far):
                    row = (here ^ (2 * z + k)) * part if ordered else 0
                    leave(
                        turned.at[s, pl.ds(pl.multiple_of(row, 16), part), :],
                        turned_outs[s].at[k, z],
                    )
        for copy in leaving:
            copy.wait()

    results = pl.pallas_call(
        kernel,
        out_shape=[struct((rows, wide), bf16)] * pieces
        + [struct((bits, far, part, rows), bf16)] * pieces
        + [struct((D, wide), bf16)],
        in_specs=[ANY_SPEC] * (pieces + sources) + [VMEM_SPEC],
        out_specs=[ANY_SPEC] * (2 * pieces + 1),
        scratch_shapes=[
            pltpu.VMEM((pieces, rows, D), bf16),
            pltpu.VMEM((D, wide), bf16),
            pltpu.VMEM((pieces, rows, wide), bf16),
            pltpu.VMEM((pieces, D, rows), bf16),
            pltpu.SemaphoreType.DMA((pieces,)),
            pltpu.SemaphoreType.DMA((sources,)),
            pltpu.SemaphoreType.DMA((1 + pieces * (1 + bits * far),)),
        ],
        cost_estimate=cost(4 * pieces * rows * D * wide, 24 << 20, 0, 1),
        name="project_in",
    )(*xs, *weights, bias)
    return results[:pieces], results[pieces : 2 * pieces], results[2 * pieces]


def padded(array):
    return jnp.pad(array, ((0, 0), (0, PAD - array.shape[1])))


def dot(a, b, dims=(1, 0)):
    return contract(a, b, dims)


def per_device(
    hidden_in,
    grad_out,
    w_query,
    b_query,
    w_key,
    w_value,
    b_value,
    w_out,
    b_out,
    gain_one,
    shift_one,
    w_up,
    b_up,
    w_down,
    b_down,
    gain_two,
    shift_two,
    lengths,
    global_raw,
    random_raw,
):
    own_rows = hidden_in.shape[0]
    me = lax.axis_index("tensor")
    teams = lax.axis_size("tensor")
    members = lax.axis_size("dp")
    width = w_query.shape[1]
    heads = width // HD
    hidden = w_up.shape[1]

    table, bias = block_tables(lengths, global_raw, random_raw, own_rows // BLK, teams)

    qkv_b = jnp.concatenate(
        [jnp.pad(b_query, (0, PAD - width)), jnp.zeros((PAD,), f32), jnp.pad(b_value, (0, PAD - width))]
    )
    halved = members == 8
    if halved:
        queries = pack_queries(w_query, w_key, w_value)
        own = pack_weights(w_up, w_out, w_down, queries)
        qkv_pieces = ring_pieces(queries)
        beyond_own = swap(own, 2)
        shard = pair_weights(own, beyond_own, hidden, qkv_pieces[GATE:])
    else:
        qkv_shard = jnp.concatenate([padded(w_query), padded(w_key), padded(w_value)], axis=1)
        qkv_pieces = [lax.all_gather(qkv_shard, "dp", axis=0, tiled=True)]
        shard = jnp.concatenate([w_up, padded(w_out.T), w_down.T], axis=1)
        weights = lax.all_gather(shard, ("dp", "tensor"), axis=0, tiled=False)
        weights = jnp.swapaxes(weights.reshape(members, teams, *shard.shape), 0, 1)
        weights = [weights.reshape(teams, D, shard.shape[1])]

    x2 = swap(held(hidden_in, (beyond_own,)) if halved else hidden_in, 2)
    x1 = swap(hidden_in, 1)
    x3 = swap(x2, 1)
    qkv, x_turned, qkv_w = project_in([hidden_in, x1, x2, x3], qkv_pieces, qkv_b[None])
    far_mixed, (t2, t3) = attend_forward(qkv, table, bias, heads, (2, 3))
    far_mixed = swap(far_mixed, 2)
    near_mixed, (t0, t1) = attend_forward(qkv, table, bias, heads, (0, 1))
    r1 = swap(near_mixed[1], 1)
    r3 = swap(far_mixed[1], 1)
    if halved:

        weights = ring_pieces(shard)
        weights = weights + [swap(piece, 1) for piece in weights]

    results = layer_rows(
        [(near_mixed, 0), (r1, None), (far_mixed, 0), (r3, None)],
        hidden_in,
        grad_out,
        weights,
        (
            jnp.stack([b_out, gain_one, shift_one, b_down, gain_two, shift_two]),
            b_up.reshape(teams, hidden),
        ),
        lengths,
    )
    layer_out, near_rows, far_rows, turned = results[:4]
    backs = results[4 : 4 + teams]
    after_low, small = results[4 + teams :]
    ups = [backs[0]] + [swap(backs[s], s) for s in range(1, teams)]
    totals = [t0, t1, t2, t3]
    before = attend_backward(qkv, ups[:1], totals[:1], table, bias, heads, (0,))

    next_rows, next_turned = swap(far_rows, 1), swap(turned, 1)
    down_group = (
        [(turned, 1), (next_turned, 1)],
        [[(near_rows, 0), (near_rows, 1)], [(next_rows, 0), (next_rows, 1)]],
    )
    up_group = (
        [(turned, 0), (next_turned, 0)],
        [[(near_rows, 2), (near_rows, 3)], [(next_rows, 2), (next_rows, 3)]],
    )
    out_group = (
        [(turned, 2), (next_turned, 2)],
        [[(near_mixed, 0), (far_mixed, 0)], [(near_mixed, 1), (far_mixed, 1)]],
    )
    if halved:
        (down_gone,) = row_dot([down_group], 2, "far", (before[0], *ups[1:]))
        down_blocks = far_exchange(down_gone)
        up_quads = row_dot([up_group, out_group], 2, "quads", (down_gone,))
        up_gone = up_quads[3]
        up_away = [swap(up_quads[1], 2), dp_swap(up_quads[2], 1), swap_both(up_gone)]
        waited = (up_gone,)
    else:
        down_sums = row_dot([down_group], 2)[0].reshape(2, D, -1)
        up_sums = row_dot([up_group, out_group], 2)[0].reshape(2, D, -1)
        waited = ()
    results = attend_backward(
        qkv,
        ups[1:],
        totals[1:],
        table,
        bias,
        heads,
        (1, 2, 3),
        small,
        waited,
        (before[1], before[2], before[0]),
    )
    grads, tail = results[:4], results[4]
    qkv_group = ([(x[None], 0) for x in x_turned], [[(g[None], 0)] for g in grads])
    if halved:
        kept, gone = row_dot([qkv_group], 1, "bits", (), tail)
        away = dp_swap(gone, 1)
        parts = spread([grads[3], grads[1]], qkv_w, waited=(gone, *up_away))
        spread_away = swap(parts, 1)
        up_blocks = joined_sums([a[0, 0] for a in (up_quads[0], *up_away)], (parts,), True)
        up_part = up_blocks[0].astype(f32)
        for z in range(1, 4):
            up_part = up_part + dp_swap(up_blocks[z], 2 * z).astype(f32)
        beyond, here = spread([grads[2], grads[0]], qkv_w, spread_away, after_low, (up_blocks[0],))
        beyond_away = swap(beyond, 2)
        down_here, down_next = fold(down_blocks, (beyond,))
        down_away = swap(down_next, 2)
        blocks = joined_sums([kept[0, 0], away[0, 0]], (down_next,))
        arrived = far_exchange(blocks)
        qkv_part = jnp.sum(arrived.astype(f32), axis=0)
        down_here, down_next = plus(down_here, down_away, (blocks,), 2)
        down_away = dp_swap(down_next, 1)
        down_part = down_here[0].astype(f32) + down_away[0].astype(f32)
        qkv_part, small = qkv_part[:-16], qkv_part[-16:]
    else:
        blocks = row_dot([qkv_group], 1)[0].reshape(D, -1)
        qkv_part = dp_scatter_sum(blocks)
        small = lax.psum(tail.astype(f32), "dp")
        spread_away = swap(spread([grads[3], grads[1]], qkv_w), 1)
        beyond, here = spread([grads[2], grads[0]], qkv_w, spread_away, after_low)
        beyond_away = swap(beyond, 2)
        down_part = dp_scatter_sum(down_sums[0] + swap(down_sums[1], 2))
        up_part = dp_scatter_sum(up_sums[0] + swap(up_sums[1], 2))
    grad_in = here + beyond_away.astype(f32)

    bias_row = small[SUM_ROW]
    return (
        layer_out,
        grad_in,
        qkv_part[:, :width],
        bias_row[:width],
        qkv_part[:, PAD : PAD + width],
        qkv_part[:, 2 * PAD : 2 * PAD + width],
        bias_row[2 * PAD : 2 * PAD + width],
        up_part[:, hidden : hidden + width].T,
        small[5],
        small[3],
        small[4],
        up_part[:, :hidden],
        jnp.take(small[6 : 6 + teams], me, axis=0),
        down_part.T,
        small[2],
        small[0],
        small[1],
    )


def solution(mesh):
    in_specs = (
        P(("dp", "tensor"), None),
        P(("dp", "tensor"), None),
        P("dp", "tensor"),
        P("tensor"),
        P("dp", "tensor"),
        P("dp", "tensor"),
        P("tensor"),
        P("tensor", "dp"),
        P(),
        P(),
        P(),
        P("dp", "tensor"),
        P(),
        P("tensor", "dp"),
        P(),
        P(),
        P(),
        P("dp"),
        P("dp", None),
        P("dp", None, None),
    )
    out_specs = (
        P(("dp", "tensor"), None),
        P(("dp", "tensor"), None),
        P("dp", "tensor"),
        P("tensor"),
        P("dp", "tensor"),
        P("dp", "tensor"),
        P("tensor"),
        P("tensor", "dp"),
        P(),
        P(),
        P(),
        P("dp", "tensor"),
        P("tensor"),
        P("tensor", "dp"),
        P(),
        P(),
        P(),
    )
    return jax.shard_map(
        per_device, mesh=mesh, in_specs=in_specs, out_specs=out_specs, check_vma=False
    )
```
